32 devices in a mesh: seq: 4 (over x, core), fsdp: 8 (over z, y).
Axes of the slice: x: 2, y: 2, z: 4, core: 2. Of those that a mesh axis runs over, the one named last changes fastest.
Arguments:
- tokens: bfloat16 [8, 1536, 1536], P('fsdp', 'seq'), may hold values from -6 to 6
- out_grad: bfloat16 [8, 1536, 1536], P('fsdp', 'seq'), may hold values from -6 to 6
- attn_gain: bfloat16 [1536], P('fsdp'), may hold values from 0.5 to 1.5
- w_query: bfloat16 [1536, 768], P('fsdp'), may hold values from -0.0390625 to 0.0390625
- w_key: bfloat16 [1536, 768], P('fsdp'), may hold values from -0.15625 to 0.15625
- w_value: bfloat16 [1536, 768], P('fsdp'), may hold values from -0.15625 to 0.15625
- w_out: bfloat16 [768, 1536], P('fsdp'), may hold values from -0.875 to 0.875
- mix_gain: bfloat16 [1536], P('fsdp'), may hold values from 0.5 to 1.5
- w_gate: bfloat16 [1536, 3968], P('fsdp'), may hold values from -0.15625 to 0.15625
- w_up: bfloat16 [1536, 3968], P('fsdp'), may hold values from -0.15625 to 0.15625
- w_down: bfloat16 [3968, 1536], P('fsdp'), may hold values from -0.09375 to 0.09375
- rel_table: float32 [32, 12], replicated, may hold values from -4 to 4
- bucket_ids: int32 [3071], replicated, may hold values from 0 to 31
- cont_start: int32 [8, 2], P('fsdp'), may hold values from 1024 to 1279
Outputs:
- block_out: bfloat16 [8, 1536, 1536], P('fsdp', 'seq')
- in_grad: bfloat16 [8, 1536, 1536], P('fsdp', 'seq')
- attn_gain_grad: float32 [1536], P('fsdp')
- w_query_grad: float32 [1536, 768], P('fsdp')
- w_key_grad: float32 [1536, 768], P('fsdp')
- w_value_grad: float32 [1536, 768], P('fsdp')
- w_out_grad: float32 [768, 1536], P('fsdp')
- mix_gain_grad: float32 [1536], P('fsdp')
- w_gate_grad: float32 [1536, 3968], P('fsdp')
- w_up_grad: float32 [1536, 3968], P('fsdp')
- w_down_grad: float32 [3968, 1536], P('fsdp')
- rel_table_grad: float32 [32, 12], replicated
The draws below stay inside these ranges and needn't reach their ends.
Inputs may be any that keep to these rules, and one draw needn't show every extreme that they name: `cont_start`: a continuation's positions lie after all 1024 positions of the prompt.
All inputs are finite; a program needn't handle non-finite values.
Results may differ from the reference program's by a relative error of at most 0.018.
Values may be sent and summed in bfloat16 or wider, within the bound.
A program may use at most 320 MiB of HBM per device.

```python
import jax
import jax.numpy as jnp
from jax import lax

D = 1536
HEADS = 12
HEAD_DIM = 64
FF = 3968
BUCKETS = 32
PROMPT = 1024
CL = 256
CONT_N = 2
INNER = 768
GROUPS = 8
TOK_GROUP = 1536
MAXPOS = 1536
SPAN = 3071


def place_ends(entries, rng, smallest, largest):
    longest = entries.shape.index(max(entries.shape))
    spots = []
    for shift in (0, 1):
        where = [jax.random.randint(jax.random.fold_in(rng, axis), (), 0, length) for axis, length in enumerate(entries.shape)]
        where[longest] = (where[longest] + shift) % entries.shape[longest]
        spots.append(tuple(where))
    return entries.at[spots[0]].set(smallest).at[spots[1]].set(largest)


def steps_of(own_key, dims, shards, smallest, largest):
    factor_of, own = 1.0, jax.random.fold_in(own_key, 6)
    for position, parts in shards:
        draws = jnp.exp(jax.random.uniform(jax.random.fold_in(own, position), (parts,), jnp.float32, smallest / len(shards), largest / len(shards)))
        factor_of = factor_of * jnp.repeat(draws, dims[position] // parts).reshape([-1 if axis == position else 1 for axis in range(len(dims))])
    return factor_of


def centred(rng, dims, spread, reach, shards=(), held_as=jnp.bfloat16):
    values = spread * jax.random.normal(rng, dims, jnp.float32)
    if shards:
        values = values * steps_of(rng, dims, shards, -0.22, 0.18)
    return jnp.clip(values, -reach, reach).astype(held_as)


def setup_inputs(seed: int = 0) -> dict:
    seeds = jax.random.split(jax.random.key(seed), 15)
    return {
        "tokens": centred(seeds[0], (GROUPS, TOK_GROUP, D), 1.0, 6.0, ((0, 8), (1, 4))),
        "out_grad": centred(seeds[1], (GROUPS, TOK_GROUP, D), 1.0, 6.0, ((0, 8), (1, 4))),
        "attn_gain": jnp.clip(1.0 + 0.1 * jax.random.normal(seeds[2], (D,), jnp.float32), 0.5, 1.5).astype(jnp.bfloat16),
        "w_query": centred(seeds[3], (D, INNER), (16 * D) ** -0.5, 0.0390625, ((0, 8),)),
        "w_key": centred(seeds[4], (D, INNER), D ** -0.5, 0.15625, ((0, 8),)),
        "w_value": centred(seeds[5], (D, INNER), D ** -0.5, 0.15625, ((0, 8),)),
        "w_out": centred(seeds[6], (INNER, D), (INNER // 16) ** -0.5, 0.875, ((0, 8),)),
        "mix_gain": jnp.clip(1.0 + 0.1 * jax.random.normal(seeds[7], (D,), jnp.float32), 0.5, 1.5).astype(jnp.bfloat16),
        "w_gate": centred(seeds[8], (D, FF), D ** -0.5, 0.15625, ((0, 8),)),
        "w_up": centred(seeds[9], (D, FF), D ** -0.5, 0.15625, ((0, 8),)),
        "w_down": centred(seeds[10], (FF, D), FF ** -0.5, 0.09375, ((0, 8),)),
        "rel_table": centred(seeds[11], (BUCKETS, HEADS), 1.0, 4.0, (), jnp.float32),
        "bucket_ids": place_ends(jax.random.randint(seeds[12], (SPAN,), 0, BUCKETS), jax.random.fold_in(seeds[12], 1), 0, BUCKETS - 1).astype(jnp.int32),
        "cont_start": place_ends(jax.random.randint(seeds[13], (GROUPS, CONT_N), PROMPT, PROMPT + CL), jax.random.fold_in(seeds[13], 1), PROMPT, (PROMPT + CL) - 1).astype(jnp.int32),
    }


@jax.custom_vjp
def low(v):
    return lax.optimization_barrier(v.astype(jnp.bfloat16)).astype(jnp.float32)

@jax.custom_vjp
def low_back(v):
    return v

def low_keep(v):
    return (low(v), None)

def low_pass(kept, grad):
    return (grad,)

def back_keep(v):
    return (v, None)

def back_low(kept, grad):
    return (low(grad),)
low.defvjp(low_keep, low_pass)
low_back.defvjp(back_keep, back_low)
precise = lax.Precision.HIGHEST
epsilon = 1e-06

def both_ways(v):
    return low_back(low(v))

def rms_scaled(v, gain):
    return v * lax.rsqrt(lax.optimization_barrier(jnp.mean(v * v, axis=-1, keepdims=True)) + epsilon) * gain

def gelu_tanh(v):
    return 0.5 * v * (1.0 + jnp.tanh(0.7978845608028654 * (v + 0.044715 * v * v * v)))

def attend(query, keys, values, bias):
    scores = low_back(jnp.einsum('rhe,she->hrs', query, keys, precision=precise) + bias)
    weights = low(jax.nn.softmax(scores, axis=-1))
    return jnp.einsum('hrs,she->rhe', weights, values, precision=precise)

def layer(block, attn_gain, w_query, w_key, w_value, w_out, mix_gain, w_gate, w_up, w_down, rel_table, bucket_ids, cont_start):
    normed = low(rms_scaled(block, attn_gain))
    query = both_ways(jnp.dot(normed, w_query, precision=precise)).reshape(-1, HEADS, HEAD_DIM)
    keys = both_ways(jnp.dot(normed, w_key, precision=precise)).reshape(-1, HEADS, HEAD_DIM)
    values = both_ways(jnp.dot(normed, w_value, precision=precise)).reshape(-1, HEADS, HEAD_DIM)
    by_offset = rel_table[bucket_ids].T
    places = jnp.arange(PROMPT, dtype=jnp.int32)
    near = places[None, :] - places[:, None] + (MAXPOS - 1)
    prompt_bias = by_offset[:, near]
    step_attend = jax.checkpoint(attend)
    prompt_out = step_attend(query[:PROMPT], keys[:PROMPT], values[:PROMPT], prompt_bias)
    cont_query = query[PROMPT:].reshape(CONT_N, CL, HEADS, HEAD_DIM)
    prompt_keys = jnp.broadcast_to(keys[:PROMPT][None], (CONT_N, PROMPT, HEADS, HEAD_DIM))
    prompt_values = jnp.broadcast_to(values[:PROMPT][None], (CONT_N, PROMPT, HEADS, HEAD_DIM))
    cont_keys = jnp.concatenate([prompt_keys, keys[PROMPT:].reshape(CONT_N, CL, HEADS, HEAD_DIM)], axis=1)
    cont_values = jnp.concatenate([prompt_values, values[PROMPT:].reshape(CONT_N, CL, HEADS, HEAD_DIM)], axis=1)
    inside = jnp.arange(CL, dtype=jnp.int32)
    query_place = cont_start[:, None] + inside[None, :]
    key_place = jnp.concatenate([jnp.broadcast_to(places[None, :], (CONT_N, PROMPT)), query_place], axis=1)
    offsets = key_place[:, None, :] - query_place[:, :, None] + (MAXPOS - 1)
    cont_bias = jnp.moveaxis(by_offset[:, offsets], 0, 1)
    cont_out = jax.vmap(step_attend)(cont_query, cont_keys, cont_values, cont_bias)
    pieces = [prompt_out, cont_out.reshape(CONT_N * CL, HEADS, HEAD_DIM)]
    mixed = both_ways(jnp.concatenate(pieces, axis=0).reshape(-1, INNER))
    resid = block + low_back(jnp.dot(mixed, w_out, precision=precise))
    normed_two = low(rms_scaled(resid, mix_gain))
    gate = low_back(jnp.dot(normed_two, w_gate, precision=precise))
    upward = low_back(jnp.dot(normed_two, w_up, precision=precise))
    hidden = low(gelu_tanh(gate) * upward)
    return resid + jnp.dot(hidden, w_down, precision=precise)

def reference(tokens, out_grad, attn_gain, w_query, w_key, w_value, w_out, mix_gain, w_gate, w_up, w_down, rel_table, bucket_ids, cont_start):
    params = tuple((a.astype(jnp.float32) for a in (attn_gain, w_query, w_key, w_value, w_out, mix_gain, w_gate, w_up, w_down, rel_table)))
    run_layer = jax.checkpoint(layer)

    def whole(inputs, weights):

        def one_group(item):
            block, starts = item
            return run_layer(block, *weights, bucket_ids, starts)
        return lax.map(one_group, (inputs, cont_start))
    outputs, pull = jax.vjp(whole, tokens.astype(jnp.float32), params)
    input_grad, grads = pull(out_grad.astype(jnp.float32))
    return (outputs.astype(jnp.bfloat16), input_grad.astype(jnp.bfloat16), grads[0], grads[1], grads[2], grads[3], grads[4], grads[5], grads[6], grads[7], grads[8], grads[9])
```

```python
import functools
import jax
import jax.numpy as jnp
from jax import lax
from jax.experimental import pallas as pl
from jax.experimental.pallas import tpu as pltpu
from jax.sharding import PartitionSpec as P

HEAD_DIM = 64
PROMPT = 1024
CL = 256
F32 = jnp.float32
BF16 = jnp.bfloat16
epsilon = 1e-06
STRIP = 2 * PROMPT - 128
FARW = PROMPT - 128 + CL
KC = 256


def nt(a, b):
    return lax.dot_general(a, b, (((1,), (1,)), ((), ())), preferred_element_type=F32)


def nn(a, b):
    return lax.dot_general(a, b, (((1,), (0,)), ((), ())), preferred_element_type=F32)


def build_strips(heads, starts, table, ids, strip, far):
    length = ids.shape[1]
    half = 2 * PROMPT
    for h in range(heads):
        row = jnp.zeros(ids.shape, F32)
        for b in range(table.shape[0]):
            row = jnp.where(ids[...] == b, table[b, h], row)
        base = jnp.broadcast_to(row[:1, PROMPT // 2 : PROMPT // 2 + half], (128, half))
        strip[h] = pltpu.roll(base, 1, 1, stride=1, stride_axis=0)[:, 128:]
        for c in range(2):
            moved = pltpu.roll(row, length - PROMPT // 2 - starts[c], 1)
            base = jnp.broadcast_to(moved[:1, : FARW + 128], (128, FARW + 128))
            far[h, c] = pltpu.roll(base, 1, 1, stride=1, stride_axis=0)[:, 128:]


def head_masks(width, heads):
    lane = lax.broadcasted_iota(jnp.int32, (1, width), 1)
    return [(lane >= h * HEAD_DIM) & (lane < (h + 1) * HEAD_DIM) for h in range(heads)]


def masked_copies(src, dst, heads):
    masks = head_masks(src.shape[1], heads)
    for h in range(heads):
        dst[h] = jnp.where(masks[h], src[...], jnp.zeros((), src.dtype))


def bias_chunk(strip, far, h, first_q, kstart, kind, c):
    parts = []
    for r in range(KC // 128):
        m = PROMPT - 128 - (kstart + 128 * r)
        if kind == "far":
            parts.append(far[h, c, :, m : m + CL])
        else:
            parts.append(strip[h, :, pl.ds(pl.multiple_of(first_q + m, 128), CL)])
    return jnp.concatenate(parts, axis=0)


def attn_fwd_kernel(heads, starts, table, ids, q, k, v, o, lse, strip, far, kh, vt, ot, s, p):
    build_strips(heads, starts, table, ids, strip, far)
    masked_copies(k, kh, heads)
    vt[...] = v[...].astype(F32).T.astype(BF16)
    lse[...] = jnp.zeros(lse.shape, F32)

    def block(h, q0, bias_q0, chunks, c):
        qb = q[pl.ds(q0, CL), :]
        top = None
        for n, (k0, kind, kstart) in enumerate(chunks):
            sc = nt(kh[h, pl.ds(k0, KC), :], qb) + bias_chunk(strip, far, h, bias_q0, kstart, kind, c)
            s[n * KC : (n + 1) * KC, :] = sc
            m = jnp.max(sc, axis=0, keepdims=True)
            top = m if top is None else jnp.maximum(top, m)
        total = jnp.zeros((1, CL), F32)
        acc = jnp.zeros((HEAD_DIM, CL), F32)
        for n, (k0, kind, kstart) in enumerate(chunks):
            e = jnp.exp(s[n * KC : (n + 1) * KC, :] - top)
            total = total + jnp.sum(e, axis=0, keepdims=True)
            acc = acc + nn(vt[pl.ds(pl.multiple_of(h * HEAD_DIM, HEAD_DIM), HEAD_DIM), pl.ds(k0, KC)], e.astype(BF16))
        ot[pl.ds(pl.multiple_of(h * HEAD_DIM, HEAD_DIM), HEAD_DIM), pl.ds(q0, CL)] = acc / total
        lse[pl.ds(h, 1), pl.ds(q0, CL)] = top + jnp.log(total)

    nblk = PROMPT // CL

    def prompt_body(i, carry):
        h, blk = i // nblk, i % nblk
        q0 = pl.multiple_of(blk * CL, CL)
        block(h, q0, q0, [(j * KC, "strip", j * KC) for j in range(PROMPT // KC)], None)
        return carry

    lax.fori_loop(0, heads * nblk, prompt_body, 0)

    def cont_body(i, carry):
        h, c = i // 2, i % 2
        q0 = pl.multiple_of(PROMPT + c * CL, CL)
        chunks = [(j * KC, "far", j * KC) for j in range(PROMPT // KC)]
        chunks += [(q0 + j * KC, "strip", j * KC) for j in range(CL // KC)]
        block(h, q0, 0, chunks, c)
        return carry

    lax.fori_loop(0, heads * 2, cont_body, 0)
    o[...] = ot[...].T.astype(BF16)


def attn_fwd(starts, table, ids, q, k, v):
    rows, width = q.shape
    heads = width // HEAD_DIM
    smem = pl.BlockSpec(memory_space=pltpu.SMEM)
    vm = pl.BlockSpec(memory_space=pltpu.VMEM)
    return pl.pallas_call(
        functools.partial(attn_fwd_kernel, heads),
        out_shape=(
            jax.ShapeDtypeStruct((rows, width), BF16),
            jax.ShapeDtypeStruct((8, rows), F32),
        ),
        in_specs=[smem, smem, vm, vm, vm, vm],
        out_specs=(vm, vm),
        scratch_shapes=[
            pltpu.VMEM((heads, 128, STRIP), F32),
            pltpu.VMEM((heads, 2, 128, FARW), F32),
            pltpu.VMEM((heads, rows, width), BF16),
            pltpu.VMEM((width, rows), BF16),
            pltpu.VMEM((width, rows), F32),
            pltpu.VMEM((PROMPT + CL, CL), F32),
            pltpu.VMEM((PROMPT + CL, CL), BF16),
        ],
        compiler_params=pltpu.CompilerParams(vmem_limit_bytes=56 << 20),
        name="attend_forward",
    )(starts, table, ids, q, k, v)


def attn_bwd_kernel(
    heads, starts, table, ids, q, k, v, o, do, lse,
    dq, dk, dv, tgrad,
    strip, far, kh, vh, qh, doh, kt, delta, dqt, gstrip, gfar,
):
    build_strips(heads, starts, table, ids, strip, far)
    for src, dst in ((k, kh), (v, vh), (q, qh), (do, doh)):
        masked_copies(src, dst, heads)
    kt[...] = k[...].astype(F32).T.astype(BF16)
    prod = (o[...].astype(F32) * do[...].astype(F32)).T
    for h in range(heads):
        delta[h : h + 1, :] = jnp.sum(prod[h * HEAD_DIM : (h + 1) * HEAD_DIM, :], axis=0, keepdims=True)
    dk[...] = jnp.zeros(dk.shape, F32)
    dv[...] = jnp.zeros(dv.shape, F32)
    gstrip[...] = jnp.zeros(gstrip.shape, F32)
    gfar[...] = jnp.zeros(gfar.shape, F32)

    def block(h, q0, bias_q0, chunks, c):
        qb = q[pl.ds(q0, CL), :]
        dob = do[pl.ds(q0, CL), :]
        qhb = qh[h, pl.ds(q0, CL), :]
        dohb = doh[h, pl.ds(q0, CL), :]
        lrow = lse[pl.ds(h, 1), pl.ds(q0, CL)]
        drow = delta[pl.ds(h, 1), pl.ds(q0, CL)]
        acc = jnp.zeros((HEAD_DIM, CL), F32)
        for n, (k0, kind, kstart) in enumerate(chunks):
            ks = pl.ds(k0, KC)
            sc = nt(kh[h, ks, :], qb) + bias_chunk(strip, far, h, bias_q0, kstart, kind, c)
            pr = jnp.exp(sc - lrow)
            dp = nt(vh[h, ks, :], dob)
            ds = pr * (dp - drow)
            pl_ = pr.astype(BF16)
            dsl = ds.astype(BF16)
            dv[ks, :] += nn(pl_, dohb)
            dk[ks, :] += nn(dsl, qhb)
            acc = acc + nn(kt[pl.ds(pl.multiple_of(h * HEAD_DIM, HEAD_DIM), HEAD_DIM), ks], dsl)
            for r in range(KC // 128):
                m = PROMPT - 128 - (kstart + 128 * r)
                piece = ds[128 * r : 128 * (r + 1), :]
                if kind == "far":
                    gfar[h, c, :, m : m + CL] += piece
                else:
                    gstrip[h, :, pl.ds(pl.multiple_of(bias_q0 + m, 128), CL)] += piece
        dqt[pl.ds(pl.multiple_of(h * HEAD_DIM, HEAD_DIM), HEAD_DIM), pl.ds(q0, CL)] = acc

    nblk = PROMPT // CL

    def prompt_body(i, carry):
        h, blk = i // nblk, i % nblk
        q0 = pl.multiple_of(blk * CL, CL)
        block(h, q0, q0, [(j * KC, "strip", j * KC) for j in range(PROMPT // KC)], None)
        return carry

    lax.fori_loop(0, heads * nblk, prompt_body, 0)

    def cont_body(i, carry):
        h, c = i // 2, i % 2
        q0 = pl.multiple_of(PROMPT + c * CL, CL)
        chunks = [(j * KC, "far", j * KC) for j in range(PROMPT // KC)]
        chunks += [(q0 + j * KC, "strip", j * KC) for j in range(CL // KC)]
        block(h, q0, 0, chunks, c)
        return carry

    lax.fori_loop(0, heads * 2, cont_body, 0)
    dq[...] = dqt[...].T

    length = ids.shape[1]
    half = 2 * PROMPT
    lane8 = lax.broadcasted_iota(jnp.int32, (table.shape[0], length), 0)
    hot = ids[:1, :] == lane8
    for h in range(heads):
        def unskew(g, width):
            full = jnp.concatenate([jnp.zeros((128, 128), F32), g], axis=1)
            eight = full[:8]
            for a in range(1, 16):
                eight = eight + pltpu.roll(full[8 * a : 8 * a + 8], width - 8 * a, 1)
            vec = pltpu.roll(eight, width - 1, 1)[:1]
            for b in range(1, 8):
                vec = vec + pltpu.roll(eight, width - 1 - b, 1)[b : b + 1]
            return jnp.concatenate([vec, jnp.zeros((1, length - width), F32)], axis=1)

        total = jnp.broadcast_to(unskew(gstrip[h], half), (8, length))
        total = pltpu.roll(total, PROMPT // 2, 1)
        for c in range(2):
            piece = jnp.broadcast_to(unskew(gfar[h, c], FARW + 128), (8, length))
            total = total + pltpu.roll(piece, PROMPT // 2 + starts[c], 1)
        picked = jnp.where(hot, total[:1, :], 0.0)
        tgrad[h] = jnp.broadcast_to(jnp.sum(picked, axis=1, keepdims=True), tgrad.shape[1:])


def attn_bwd(starts, table, ids, q, k, v, o, do, lse):
    rows, width = q.shape
    heads = width // HEAD_DIM
    smem = pl.BlockSpec(memory_space=pltpu.SMEM)
    vm = pl.BlockSpec(memory_space=pltpu.VMEM)
    wide = jax.ShapeDtypeStruct((rows, width), F32)
    return pl.pallas_call(
        functools.partial(attn_bwd_kernel, heads),
        out_shape=(wide, wide, wide, jax.ShapeDtypeStruct((heads, table.shape[0], 128), F32)),
        in_specs=[smem, smem] + [vm] * 7,
        out_specs=(vm,) * 4,
        scratch_shapes=[
            pltpu.VMEM((heads, 128, STRIP), F32),
            pltpu.VMEM((heads, 2, 128, FARW), F32),
        ]
        + [pltpu.VMEM((heads, rows, width), BF16)] * 4
        + [
            pltpu.VMEM((width, rows), BF16),
            pltpu.VMEM((8, rows), F32),
            pltpu.VMEM((width, rows), F32),
            pltpu.VMEM((heads, 128, STRIP), F32),
            pltpu.VMEM((heads, 2, 128, FARW), F32),
        ],
        compiler_params=pltpu.CompilerParams(vmem_limit_bytes=60 << 20),
        name="attend_backward",
    )(starts, table, ids, q, k, v, o, do, lse)


def reversed_ids(bucket_ids):
    span = bucket_ids.shape[0]
    ids = jnp.concatenate([bucket_ids[::-1], jnp.full((1,), -1, jnp.int32)])
    return jnp.broadcast_to(ids[None, :], (8, span + 1))


def pack_columns(w, nseq, nfsdp, mine):
    depth, total = w.shape
    block = total // nfsdp
    piece = -(-block // (16 * nseq)) * 16
    w = jnp.pad(w.reshape(depth, nfsdp, block), ((0, 0), (0, 0), (0, nseq * piece - block)))
    w = w.reshape(depth, nfsdp, nseq, piece)
    w = lax.dynamic_index_in_dim(w, mine, 2, keepdims=False)
    return w.reshape(depth, nfsdp * piece)


def unpack_columns(parts, total, nfsdp):
    nseq, depth, width = parts.shape
    piece = width // nfsdp
    block = total // nfsdp
    w = parts.reshape(nseq, depth, nfsdp, piece).transpose(1, 2, 0, 3)
    return w.reshape(depth, nfsdp, nseq * piece)[:, :, :block].reshape(depth, total)


def pack_rows(w, nseq, mine):
    block, depth = w.shape
    piece = -(-block // (16 * nseq)) * 16
    w = jnp.pad(w, ((0, nseq * piece - block), (0, 0)))
    return lax.dynamic_slice_in_dim(w, mine * piece, piece, 0)


def dot32(a, b):
    return jnp.dot(a, b, preferred_element_type=F32)


def dot_tn(a, b):
    return lax.dot_general(a, b, (((0,), (0,)), ((), ())), preferred_element_type=F32)


def inverse_rms(v):
    return lax.rsqrt(jnp.mean(v * v, axis=-1, keepdims=True) + epsilon)


def gelu_both(u):
    inner = 0.7978845608028654 * (u + 0.044715 * u * u * u)
    t = jnp.tanh(inner)
    value = 0.5 * u * (1.0 + t)
    slope = 0.5 * (1.0 + t) + 0.5 * u * (1.0 - t * t) * 0.7978845608028654 * (1.0 + 3 * 0.044715 * u * u)
    return value, slope


def norm_back(grad, v, r, gain):
    scaled = grad * gain
    return r * scaled - v * (r * r * r) * jnp.mean(v * scaled, axis=-1, keepdims=True)


def body(
    tokens,
    out_grad,
    attn_gain,
    w_query,
    w_key,
    w_value,
    w_out,
    mix_gain,
    w_gate,
    w_up,
    w_down,
    rel_table,
    bucket_ids,
    cont_start,
):
    nseq = lax.axis_size("seq")
    nfsdp = lax.axis_size("fsdp")
    mine = lax.axis_index("seq")
    where = lax.axis_index("fsdp")
    rows, width = tokens.shape[1:]
    inner = w_query.shape[1]
    piece = inner // nseq
    heads = piece // HEAD_DIM
    hidden_all = w_gate.shape[1]

    def gather_f(a):
        return lax.all_gather(a, "fsdp", axis=0, tiled=True)

    def gather_s(a):
        return lax.all_gather(a, "seq", axis=0, tiled=True)

    def scatter_s(a):
        return lax.psum_scatter(a.astype(BF16), "seq", scatter_dimension=0, tiled=True).astype(F32)

    def scatter_f(a):
        return lax.psum_scatter(a.astype(BF16), "fsdp", scatter_dimension=0, tiled=True)

    local = [lax.dynamic_slice_in_dim(w, mine * piece, piece, 1) for w in (w_query, w_key, w_value)]
    gains = jnp.pad(jnp.stack([attn_gain, mix_gain], axis=1), ((0, 0), (0, 62)))
    first = gather_f(jnp.concatenate(local + [gains], axis=1))
    query_w, key_w, value_w = (first[:, i * piece : (i + 1) * piece] for i in range(3))
    gain_one = first[:, 3 * piece].astype(F32)
    gain_two = first[:, 3 * piece + 1].astype(F32)
    out_cols = width // nseq
    out_local = lax.dynamic_slice_in_dim(w_out, mine * out_cols, out_cols, 1)
    out_w = lax.all_to_all(gather_f(out_local), "seq", split_axis=0, concat_axis=1, tiled=True)
    gate_w = gather_f(pack_columns(w_gate, nseq, nfsdp, mine))
    up_w = gather_f(pack_columns(w_up, nseq, nfsdp, mine))
    down_w = gather_f(pack_rows(w_down, nseq, mine))

    block = tokens[0].astype(F32)
    r_one = inverse_rms(block)
    group = gather_s(tokens[0]).astype(F32)
    normed = (group * inverse_rms(group) * gain_one).astype(BF16)
    query = dot32(normed, query_w).astype(BF16)
    keys = dot32(normed, key_w).astype(BF16)
    values = dot32(normed, value_w).astype(BF16)
    table = lax.dynamic_slice_in_dim(rel_table, mine * heads, heads, 1)
    ids = reversed_ids(bucket_ids)
    starts = cont_start[0]
    mixed, lse = attn_fwd(starts, table, ids, query, keys, values)
    resid = block + scatter_s(dot32(mixed, out_w))
    r_two = inverse_rms(resid)
    normed_two = gather_s((resid * r_two * gain_two).astype(BF16))
    gate = dot32(normed_two, gate_w)
    upward = dot32(normed_two, up_w)
    active, slope = gelu_both(gate)
    hidden = (active * upward).astype(BF16)
    result = resid + scatter_s(dot32(hidden, down_w))
    cot = gather_s(out_grad[0])
    down_grad = scatter_f(dot_tn(hidden, cot))
    hidden_grad = lax.dot_general(cot, down_w, (((1,), (1,)), ((), ())), preferred_element_type=F32)
    gate_grad = (hidden_grad * upward * slope).astype(BF16)
    up_grad = (hidden_grad * active).astype(BF16)
    normed_two_grad = scatter_s(nt(gate_grad, gate_w) + nt(up_grad, up_w))
    gate_w_grad = scatter_f(dot_tn(normed_two, gate_grad))
    up_w_grad = scatter_f(dot_tn(normed_two, up_grad))
    gain_two_grad = jnp.sum(normed_two_grad * resid * r_two, axis=0)
    resid_grad = out_grad[0].astype(F32) + norm_back(normed_two_grad, resid, r_two, gain_two)
    attn_grad = gather_s(resid_grad.astype(BF16))
    out_w_grad = dot_tn(mixed, attn_grad).astype(BF16)
    mixed_grad = nt(attn_grad, out_w).astype(BF16)
    dq, dk, dv, tgrad = attn_bwd(starts, table, ids, query, keys, values, mixed, mixed_grad, lse)
    dq, dk, dv = (a.astype(BF16) for a in (dq, dk, dv))
    normed_grad = scatter_s(nt(dq, query_w) + nt(dk, key_w) + nt(dv, value_w))
    qkv_grad = scatter_f(dot_tn(normed, jnp.concatenate([dq, dk, dv], axis=1)))
    gain_one_grad = jnp.sum(normed_grad * block * r_one, axis=0)
    in_grad = resid_grad + norm_back(normed_grad, block, r_one, gain_one)

    out_grad_cols = lax.all_to_all(out_w_grad, "seq", split_axis=1, concat_axis=0, tiled=True)
    out_w_grad = lax.all_gather(scatter_f(out_grad_cols), "seq", axis=1, tiled=True)
    qkv_grad = lax.all_gather(qkv_grad, "seq", axis=0).reshape(nseq, -1, 3, piece)
    qkv_grad = qkv_grad.transpose(1, 2, 0, 3).reshape(-1, 3, inner).astype(F32)
    gate_w_grad = unpack_columns(lax.all_gather(gate_w_grad, "seq", axis=0), hidden_all, nfsdp)
    up_w_grad = unpack_columns(lax.all_gather(up_w_grad, "seq", axis=0), hidden_all, nfsdp)
    down_grad = gather_s(down_grad)[: w_down.shape[0]]

    buckets = rel_table.shape[0]
    table_full = jnp.zeros((nseq, heads, buckets), F32)
    table_full = lax.dynamic_update_slice(table_full, tgrad[None, :, :, 0], (mine, jnp.int32(0), jnp.int32(0)))
    table_grad, gain_one_all, gain_two_all = lax.psum((table_full, gain_one_grad, gain_two_grad), ("seq", "fsdp"))
    share = width // nfsdp
    gain_one_share = lax.dynamic_slice_in_dim(gain_one_all, where * share, share)
    gain_two_share = lax.dynamic_slice_in_dim(gain_two_all, where * share, share)
    return (
        result.astype(BF16)[None],
        in_grad.astype(BF16)[None],
        gain_one_share,
        qkv_grad[:, 0],
        qkv_grad[:, 1],
        qkv_grad[:, 2],
        out_w_grad.astype(F32),
        gain_two_share,
        gate_w_grad.astype(F32),
        up_w_grad.astype(F32),
        down_grad.astype(F32),
        table_grad.reshape(nseq * heads, buckets).T,
    )


def solution(mesh):
    placed = (
        P("fsdp", "seq", None),
        P("fsdp", "seq", None),
        P("fsdp"),
        P("fsdp", None),
        P("fsdp", None),
        P("fsdp", None),
        P("fsdp", None),
        P("fsdp"),
        P("fsdp", None),
        P("fsdp", None),
        P("fsdp", None),
        P(),
        P(),
        P("fsdp", None),
    )
    results = placed[:1] * 2 + placed[2:11] + (P(),)
    return jax.shard_map(body, mesh=mesh, in_specs=placed, out_specs=results, check_vma=False)
```

```python
import functools
import jax
import jax.numpy as jnp
from jax import lax
from jax.experimental import pallas as pl
from jax.experimental.pallas import tpu as pltpu
from jax.sharding import PartitionSpec as P

HEAD_DIM = 64
PROMPT = 1024
CL = 256
F32 = jnp.float32
BF16 = jnp.bfloat16
MESH = pl.DeviceIdType.MESH
epsilon = 1e-06
STRIP = 2 * PROMPT - 128
FARW = PROMPT - 128 + CL
KC = 256


def nt(a, b):
    return lax.dot_general(a, b, (((1,), (1,)), ((), ())), preferred_element_type=F32)


def nn(a, b):
    return lax.dot_general(a, b, (((1,), (0,)), ((), ())), preferred_element_type=F32)


class Wires:
    def __init__(self, send, recv):
        self.send, self.recv, self.used = send, recv, 0

    def copy(self, src, dst, where):
        i = self.used
        self.used += 1
        return pltpu.make_async_remote_copy(
            src_ref=src,
            dst_ref=dst,
            send_sem=self.send.at[i],
            recv_sem=self.recv.at[i],
            device_id=where,
            device_id_type=MESH,
        )

    def go(self, src, dst, where):
        c = self.copy(src, dst, where)
        c.start()
        return c


def seq_places():
    s = lax.axis_index("seq")
    near = s + 1 - 2 * lax.rem(s, 2)
    far = lax.rem(s + 2, 4)
    cross = lax.rem(near + 2, 4)
    return s, near, far, cross


def meet(places):
    barrier = pltpu.get_barrier_semaphore()
    for where in places:
        pl.semaphore_signal(barrier, inc=1, device_id=where, device_id_type=MESH)
    pl.semaphore_wait(barrier, len(places))


def rows_at(index, rows, offset=0, count=None):
    return pl.ds(pl.multiple_of(index * rows + offset, 16), rows if count is None else count)


class SeqGather:
    def __init__(self, wires, out_at, chunks):
        self.wires, self.out_at, self.chunks = wires, out_at, chunks
        self.s, self.near, self.far, self.cross = seq_places()
        self.there, self.here, self.onward = [], [], []

    def send(self, c, src):
        self.there.append(self.wires.go(src, self.out_at(self.s, c), {"seq": self.far}))
        self.here.append(self.wires.go(src, self.out_at(self.s, c), {"seq": self.near}))

    def forward(self, c):
        self.there[c].wait_recv()
        view = self.out_at(self.far, c)
        self.onward.append(self.wires.go(view, view, {"seq": self.near}))

    def finish(self):
        for a in self.here + self.onward:
            a.wait_recv()
        for a in self.there + self.here + self.onward:
            a.wait_send()


def vm_spec():
    return pl.BlockSpec(memory_space=pltpu.VMEM)


def any_spec():
    return pl.BlockSpec(memory_space=pl.ANY)


def wires_scratch(n):
    return [pltpu.SemaphoreType.DMA((n,)), pltpu.SemaphoreType.DMA((n,))]


def call_params(number, vmem=60):
    return pltpu.CompilerParams(collective_id=number, has_side_effects=True, vmem_limit_bytes=vmem << 20)


def inverse_rms(v):
    return lax.rsqrt(jnp.mean(v * v, axis=-1, keepdims=True) + epsilon)


def norm_back(grad, v, r, gain):
    scaled = grad * gain
    return r * scaled - v * (r * r * r) * jnp.mean(v * scaled, axis=-1, keepdims=True)


def tokens_gather_kernel(src, out, send, recv, local):
    rows = src.shape[0]
    s, near, far, cross = seq_places()
    meet([{"seq": near}, {"seq": far}])
    half = rows // 2
    ring = SeqGather(Wires(send, recv), lambda t, c: out.at[rows_at(t, rows, c * half, half), :], 2)
    own = pltpu.make_async_copy(src, out.at[rows_at(s, rows), :], local)
    own.start()
    for c in range(2):
        ring.send(c, src.at[pl.ds(c * half, half), :])
    for c in range(2):
        ring.forward(c)
    own.wait()
    ring.finish()


def tokens_gather(tokens, nseq):
    rows, width = tokens.shape
    return pl.pallas_call(
        tokens_gather_kernel,
        out_shape=jax.ShapeDtypeStruct((nseq * rows, width), BF16),
        in_specs=[any_spec()],
        out_specs=any_spec(),
        scratch_shapes=wires_scratch(6) + [pltpu.SemaphoreType.DMA],
        compiler_params=call_params(0, 4),
        name="tokens_gather",
    )(tokens)


def mix_kernel(o, out_w, tok, gain, obuf, resid, n2, send, recv, own, local):
    rows, width = tok.shape
    piece = o.shape[1]
    nseq = obuf.shape[0]
    s, near, far, cross = seq_places()
    meet([{"seq": near}, {"seq": far}, {"seq": cross}])
    wires = Wires(send, recv)
    trips = [wires.go(o.at[rows_at(t, rows), :], obuf.at[s], {"seq": t}) for t in (far, cross, near)]
    obuf[s] = o[rows_at(s, rows), :]
    half = rows // 2
    for a in trips:
        a.wait_recv()
    ring = SeqGather(wires, lambda t, c: n2.at[rows_at(t, rows, c * half, half), :], 2)
    for c in range(2):
        part = slice(c * half, (c + 1) * half)
        cols = out_w.shape[2]
        for u in range(nseq):
            acc = tok[part, u * cols : (u + 1) * cols].astype(F32)
            for t in range(nseq):
                acc = acc + nn(obuf[t, part, :], out_w[u, t * piece : (t + 1) * piece, :])
            resid[part, u * cols : (u + 1) * cols] = acc
        h = resid[part, :]
        own[part, :] = (h * inverse_rms(h) * gain[...]).astype(BF16)
        ring.send(c, own.at[pl.ds(c * half, half), :])
    mineblock = pltpu.make_async_copy(own, n2.at[rows_at(s, rows), :], local)
    mineblock.start()
    for c in range(2):
        ring.forward(c)
    mineblock.wait()
    ring.finish()
    for a in trips:
        a.wait_send()


def mix(o, out_w, tok, gain):
    nseq = out_w.shape[0]
    rows, width = tok.shape
    return pl.pallas_call(
        mix_kernel,
        out_shape=(
            jax.ShapeDtypeStruct((nseq, rows, o.shape[1]), BF16),
            jax.ShapeDtypeStruct((rows, width), F32),
            jax.ShapeDtypeStruct((nseq * rows, width), BF16),
        ),
        in_specs=[vm_spec()] * 4,
        out_specs=(vm_spec(), vm_spec(), any_spec()),
        scratch_shapes=wires_scratch(9) + [pltpu.VMEM((rows, width), BF16), pltpu.SemaphoreType.DMA],
        compiler_params=call_params(2, 32),
        name="mix",
    )(o, out_w, tok, gain)


class SeqScatter:
    def __init__(self, wires, to_near, from_near, to_far, from_far, to_own, from_own):
        self.s, self.near, self.far, self.cross = seq_places()
        self.wires = wires
        self.bufs = (to_near, from_near, to_far, from_far, to_own, from_own)
        self.first, self.second, self.third = [], [], []

    def cross_chunk(self, c, value):
        self.bufs[0][c] = value.astype(BF16)
        self.first.append(self.wires.go(self.bufs[0].at[c], self.bufs[1].at[c], {"seq": self.near}))

    def far_chunk(self, c, value):
        self.first[c].wait_recv()
        self.bufs[2][c] = (value + self.bufs[1][c].astype(F32)).astype(BF16)
        self.second.append(self.wires.go(self.bufs[2].at[c], self.bufs[3].at[c], {"seq": self.far}))

    def near_chunk(self, c, value):
        self.bufs[4][c] = value.astype(BF16)
        self.third.append(self.wires.go(self.bufs[4].at[c], self.bufs[5].at[c], {"seq": self.near}))

    def own_chunk(self, c, value):
        self.third[c].wait_recv()
        self.second[c].wait_recv()
        return value + self.bufs[5][c].astype(F32) + self.bufs[3][c].astype(F32)

    def finish(self):
        for a in self.first + self.second + self.third:
            a.wait_send()


def scatter_scratch(chunks, rows, width):
    return [pltpu.VMEM((chunks, rows, width), BF16)] * 6


def unmix_kernel(
    chunks, dg, du, gate_w, up_w, resid, gain, cot, out_w, obuf,
    rgrad, dmix, wgrad, ggrad,
    send, recv, b0, b1, b2, b3, b4, b5, attn, dob,
):
    rows, width = resid.shape
    nseq, _, piece = obuf.shape
    s, near, far, cross = seq_places()
    meet([{"seq": near}, {"seq": far}, {"seq": cross}])
    wires = Wires(send, recv)
    sums = SeqScatter(wires, b0, b1, b2, b3, b4, b5)
    size = rows // chunks

    def part(t, c):
        at = rows_at(t, rows, c * size, size)
        return nt(dg[at, :], gate_w[...]) + nt(du[at, :], up_w[...])

    for c in range(chunks):
        sums.cross_chunk(c, part(cross, c))
    for c in range(chunks):
        sums.far_chunk(c, part(far, c))
    for c in range(chunks):
        sums.near_chunk(c, part(near, c))
    for c in range(chunks):
        rgrad[c * size : (c + 1) * size, :] = part(s, c)
    total = jnp.zeros((1, width), F32)
    trips = []
    for c in range(chunks):
        at = slice(c * size, (c + 1) * size)
        dn = sums.own_chunk(c, rgrad[at, :])
        h = resid[at, :]
        r = inverse_rms(h)
        total = total + jnp.sum(dn * h * r, axis=0, keepdims=True)
        rg = cot[at, :].astype(F32) + norm_back(dn, h, r, gain[...])
        rgrad[at, :] = rg
        low = rg.astype(BF16)
        attn[at, :] = low
        cols = out_w.shape[2]
        for t in range(nseq):
            acc = jnp.zeros((size, piece), F32)
            for u in range(nseq):
                acc = acc + nt(low[:, u * cols : (u + 1) * cols], out_w[u, t * piece : (t + 1) * piece, :])
            dob[t, at, :] = acc.astype(BF16)
    ggrad[...] = jnp.broadcast_to(total, ggrad.shape)
    for t in (far, cross, near):
        trips.append(wires.go(dob.at[t], dmix.at[rows_at(s, rows), :], {"seq": t}))
    dmix[rows_at(s, rows), :] = dob[s]
    cols = out_w.shape[2]
    for t in range(nseq):
        for u in range(nseq):
            wgrad[u, t * piece : (t + 1) * piece, :] = lax.dot_general(
                obuf[t], attn[:, u * cols : (u + 1) * cols], (((0,), (0,)), ((), ())), preferred_element_type=F32
            ).astype(BF16)
    for a in trips:
        a.wait()
    sums.finish()


def unmix(dg, du, gate_w, up_w, resid, gain, cot, out_w, obuf, chunks=2):
    rows, width = resid.shape
    nseq, _, piece = obuf.shape
    return pl.pallas_call(
        functools.partial(unmix_kernel, chunks),
        out_shape=(
            jax.ShapeDtypeStruct((rows, width), F32),
            jax.ShapeDtypeStruct((nseq * rows, piece), BF16),
            jax.ShapeDtypeStruct(out_w.shape, BF16),
            jax.ShapeDtypeStruct((8, width), F32),
        ),
        in_specs=[vm_spec()] * 9,
        out_specs=(vm_spec(),) * 4,
        scratch_shapes=wires_scratch(3 * chunks + 3)
        + scatter_scratch(chunks, rows // chunks, width)
        + [pltpu.VMEM((rows, width), BF16), pltpu.VMEM((nseq, rows, piece), BF16)],
        compiler_params=call_params(4),
        name="unmix",
    )(dg, du, gate_w, up_w, resid, gain, cot, out_w, obuf)


def input_kernel(chunks, dqkv, qkv_w, tok, gain, rgrad, in_grad, ggrad, send, recv, b0, b1, b2, b3, b4, b5, hold):
    rows, width = tok.shape
    s, near, far, cross = seq_places()
    meet([{"seq": near}, {"seq": far}])
    wires = Wires(send, recv)
    sums = SeqScatter(wires, b0, b1, b2, b3, b4, b5)
    size = rows // chunks
    used = dqkv.shape[1]

    def part(t, c):
        return nt(dqkv[rows_at(t, rows, c * size, size), :], qkv_w[:, :used])

    for c in range(chunks):
        sums.cross_chunk(c, part(cross, c))
    for c in range(chunks):
        sums.far_chunk(c, part(far, c))
    for c in range(chunks):
        sums.near_chunk(c, part(near, c))
    for c in range(chunks):
        hold[c * size : (c + 1) * size, :] = part(s, c)
    total = jnp.zeros((1, width), F32)
    for c in range(chunks):
        at = slice(c * size, (c + 1) * size)
        dn = sums.own_chunk(c, hold[at, :])
        x = tok[at, :].astype(F32)
        r = inverse_rms(x)
        total = total + jnp.sum(dn * x * r, axis=0, keepdims=True)
        in_grad[at, :] = (rgrad[at, :] + norm_back(dn, x, r, gain[...])).astype(BF16)
    ggrad[...] = jnp.broadcast_to(total, ggrad.shape)
    sums.finish()


def input_grads(dqkv, qkv_w, tok, gain, rgrad, chunks=2):
    rows, width = tok.shape
    return pl.pallas_call(
        functools.partial(input_kernel, chunks),
        out_shape=(jax.ShapeDtypeStruct((rows, width), BF16), jax.ShapeDtypeStruct((8, width), F32)),
        in_specs=[vm_spec()] * 5,
        out_specs=(vm_spec(),) * 2,
        scratch_shapes=wires_scratch(3 * chunks)
        + scatter_scratch(chunks, rows // chunks, width)
        + [pltpu.VMEM((rows, width), F32)],
        compiler_params=call_params(6, 40),
        name="input_grads",
    )(dqkv, qkv_w, tok, gain, rgrad)


def build_strips(heads, starts, table, ids, strip, far):
    length = ids.shape[1]
    half = 2 * PROMPT
    for h in range(heads):
        row = jnp.zeros(ids.shape, F32)
        for b in range(table.shape[0]):
            row = jnp.where(ids[...] == b, table[b, h], row)
        base = jnp.broadcast_to(row[:1, PROMPT // 2 : PROMPT // 2 + half], (128, half))
        strip[h] = pltpu.roll(base, 1, 1, stride=1, stride_axis=0)[:, 128:]
        for c in range(2):
            moved = pltpu.roll(row, length - PROMPT // 2 - starts[c], 1)
            base = jnp.broadcast_to(moved[:1, : FARW + 128], (128, FARW + 128))
            far[h, c] = pltpu.roll(base, 1, 1, stride=1, stride_axis=0)[:, 128:]


def head_masks(width, heads):
    lane = lax.broadcasted_iota(jnp.int32, (1, width), 1)
    return [(lane >= h * HEAD_DIM) & (lane < (h + 1) * HEAD_DIM) for h in range(heads)]


def masked_copies(src, dst, heads):
    masks = head_masks(src.shape[1], heads)
    for h in range(heads):
        dst[h] = jnp.where(masks[h], src[...], jnp.zeros((), src.dtype))


def bias_chunk(strip, far, h, first_q, kstart, kind, c):
    parts = []
    for r in range(KC // 128):
        m = PROMPT - 128 - (kstart + 128 * r)
        if kind == "far":
            parts.append(far[h, c, :, m : m + CL])
        else:
            parts.append(strip[h, :, pl.ds(pl.multiple_of(first_q + m, 128), CL)])
    return jnp.concatenate(parts, axis=0)


def attn_fwd_kernel(
    heads, starts, table, ids, q, k, v, out_q, cot, o, lse, out_w, cots, strip, far, kh, vt, ot, s, send, recv, local
):
    rows = cot.shape[0]
    mine, near, other, cross = seq_places()
    meet([{"seq": near}, {"seq": other}])
    wires = Wires(send, recv)
    half = rows // 2
    wring = SeqGather(wires, lambda t, c: out_w.at[t], 1)
    cring = SeqGather(wires, lambda t, c: cots.at[rows_at(t, rows, c * half, half), :], 2)
    wring.send(0, out_q)
    for c in range(2):
        cring.send(c, cot.at[pl.ds(c * half, half), :])
    own = [
        pltpu.make_async_copy(out_q, out_w.at[mine], local.at[0]),
        pltpu.make_async_copy(cot, cots.at[rows_at(mine, rows), :], local.at[1]),
    ]
    for a in own:
        a.start()
    build_strips(heads, starts, table, ids, strip, far)
    masked_copies(k, kh, heads)
    vt[...] = v[...].astype(F32).T.astype(BF16)
    lse[...] = jnp.zeros(lse.shape, F32)

    def block(h, q0, bias_q0, chunks, c):
        qb = q[pl.ds(q0, CL), :]
        top = None
        for n, (k0, kind, kstart) in enumerate(chunks):
            sc = nt(kh[h, pl.ds(k0, KC), :], qb) + bias_chunk(strip, far, h, bias_q0, kstart, kind, c)
            s[n * KC : (n + 1) * KC, :] = sc
            m = jnp.max(sc, axis=0, keepdims=True)
            top = m if top is None else jnp.maximum(top, m)
        total = jnp.zeros((1, CL), F32)
        acc = jnp.zeros((HEAD_DIM, CL), F32)
        for n, (k0, kind, kstart) in enumerate(chunks):
            e = jnp.exp(s[n * KC : (n + 1) * KC, :] - top)
            total = total + jnp.sum(e, axis=0, keepdims=True)
            acc = acc + nn(vt[pl.ds(pl.multiple_of(h * HEAD_DIM, HEAD_DIM), HEAD_DIM), pl.ds(k0, KC)], e.astype(BF16))
        ot[pl.ds(pl.multiple_of(h * HEAD_DIM, HEAD_DIM), HEAD_DIM), pl.ds(q0, CL)] = acc / total
        lse[pl.ds(h, 1), pl.ds(q0, CL)] = top + jnp.log(total)

    nblk = PROMPT // CL

    def prompt_body(i, carry):
        h, blk = i // nblk, i % nblk
        q0 = pl.multiple_of(blk * CL, CL)
        block(h, q0, q0, [(j * KC, "strip", j * KC) for j in range(PROMPT // KC)], None)
        return carry

    lax.fori_loop(0, heads * nblk, prompt_body, 0)

    def cont_body(i, carry):
        h, c = i // 2, i % 2
        q0 = pl.multiple_of(PROMPT + c * CL, CL)
        chunks = [(j * KC, "far", j * KC) for j in range(PROMPT // KC)]
        chunks += [(q0 + j * KC, "strip", j * KC) for j in range(CL // KC)]
        block(h, q0, 0, chunks, c)
        return carry

    wring.forward(0)
    lax.fori_loop(0, heads * 2, cont_body, 0)
    o[...] = ot[...].T.astype(BF16)
    for c in range(2):
        cring.forward(c)
    for a in own:
        a.wait()
    wring.finish()
    cring.finish()


def attn_fwd(starts, table, ids, q, k, v, out_q, cot, nseq):
    rows, width = q.shape
    heads = width // HEAD_DIM
    smem = pl.BlockSpec(memory_space=pltpu.SMEM)
    vm = pl.BlockSpec(memory_space=pltpu.VMEM)
    return pl.pallas_call(
        functools.partial(attn_fwd_kernel, heads),
        out_shape=(
            jax.ShapeDtypeStruct((rows, width), BF16),
            jax.ShapeDtypeStruct((8, rows), F32),
            jax.ShapeDtypeStruct((nseq,) + out_q.shape, BF16),
            jax.ShapeDtypeStruct((rows, cot.shape[1]), BF16),
        ),
        in_specs=[smem, smem, vm, vm, vm, vm, any_spec(), any_spec()],
        out_specs=(vm, vm, any_spec(), any_spec()),
        scratch_shapes=[
            pltpu.VMEM((heads, 128, STRIP), F32),
            pltpu.VMEM((heads, 2, 128, FARW), F32),
            pltpu.VMEM((heads, rows, width), BF16),
            pltpu.VMEM((width, rows), BF16),
            pltpu.VMEM((width, rows), F32),
            pltpu.VMEM((PROMPT + CL, CL), F32),
        ]
        + wires_scratch(9)
        + [pltpu.SemaphoreType.DMA((2,))],
        compiler_params=call_params(1, 40),
        name="attend_forward",
    )(starts, table, ids, q, k, v, out_q, cot)


def attn_bwd_kernel(
    heads, starts, table, ids, q, k, v, o, do, lse, resid, ypart, wpart,
    dq, dk, dv, tgrad, y, wsum,
    strip, far, kh, vh, qh, doh, kt, delta, dqt, gstrip, gfar,
    send, recv, local, ybuf, wbuf,
):
    rows = resid.shape[0]
    mine, near, other, cross = seq_places()
    meet([{"seq": near}, {"seq": other}])
    wires = Wires(send, recv)

    def block_of(part, t):
        return part.at[rows_at(t, rows), :] if part is ypart else part.at[t]

    pairs = ((wpart, wbuf), (ypart, ybuf))
    hops = [wires.go(block_of(part, cross), buf.at[0], {"seq": near}) for part, buf in pairs]
    turns = [wires.go(block_of(part, near), buf.at[1], {"seq": near}) for part, buf in pairs]
    loads = []
    for n, (part, buf) in enumerate(pairs):
        loads.append(pltpu.make_async_copy(block_of(part, other), buf.at[2], local.at[2 * n]))
        loads.append(pltpu.make_async_copy(block_of(part, mine), buf.at[3], local.at[2 * n + 1]))
    for a in loads:
        a.start()
    build_strips(heads, starts, table, ids, strip, far)
    for src, dst in ((k, kh), (v, vh), (q, qh), (do, doh)):
        masked_copies(src, dst, heads)
    kt[...] = k[...].astype(F32).T.astype(BF16)
    far_hops = []
    for n, (part, buf) in enumerate(pairs):
        loads[2 * n].wait()
        hops[n].wait_recv()
        buf[2] = (buf[2].astype(F32) + buf[0].astype(F32)).astype(BF16)
    for part, buf in pairs:
        far_hops.append(wires.go(buf.at[2], buf.at[4], {"seq": other}))
    prod = (o[...].astype(F32) * do[...].astype(F32)).T
    for h in range(heads):
        delta[h : h + 1, :] = jnp.sum(prod[h * HEAD_DIM : (h + 1) * HEAD_DIM, :], axis=0, keepdims=True)
    dk[...] = jnp.zeros(dk.shape, F32)
    dv[...] = jnp.zeros(dv.shape, F32)
    gstrip[...] = jnp.zeros(gstrip.shape, F32)
    gfar[...] = jnp.zeros(gfar.shape, F32)

    def block(h, q0, bias_q0, chunks, c):
        qb = q[pl.ds(q0, CL), :]
        dob = do[pl.ds(q0, CL), :]
        qhb = qh[h, pl.ds(q0, CL), :]
        dohb = doh[h, pl.ds(q0, CL), :]
        lrow = lse[pl.ds(h, 1), pl.ds(q0, CL)]
        drow = delta[pl.ds(h, 1), pl.ds(q0, CL)]
        acc = jnp.zeros((HEAD_DIM, CL), F32)
        for n, (k0, kind, kstart) in enumerate(chunks):
            ks = pl.ds(k0, KC)
            sc = nt(kh[h, ks, :], qb) + bias_chunk(strip, far, h, bias_q0, kstart, kind, c)
            pr = jnp.exp(sc - lrow)
            dp = nt(vh[h, ks, :], dob)
            ds = pr * (dp - drow)
            pl_ = pr.astype(BF16)
            dsl = ds.astype(BF16)
            dv[ks, :] += nn(pl_, dohb)
            dk[ks, :] += nn(dsl, qhb)
            acc = acc + nn(kt[pl.ds(pl.multiple_of(h * HEAD_DIM, HEAD_DIM), HEAD_DIM), ks], dsl)
            for r in range(KC // 128):
                m = PROMPT - 128 - (kstart + 128 * r)
                piece = ds[128 * r : 128 * (r + 1), :]
                if kind == "far":
                    gfar[h, c, :, m : m + CL] += piece
                else:
                    gstrip[h, :, pl.ds(pl.multiple_of(bias_q0 + m, 128), CL)] += piece
        dqt[pl.ds(pl.multiple_of(h * HEAD_DIM, HEAD_DIM), HEAD_DIM), pl.ds(q0, CL)] = acc

    nblk = PROMPT // CL

    def prompt_body(i, carry):
        h, blk = i // nblk, i % nblk
        q0 = pl.multiple_of(blk * CL, CL)
        block(h, q0, q0, [(j * KC, "strip", j * KC) for j in range(PROMPT // KC)], None)
        return carry

    lax.fori_loop(0, heads * nblk, prompt_body, 0)

    def cont_body(i, carry):
        h, c = i // 2, i % 2
        q0 = pl.multiple_of(PROMPT + c * CL, CL)
        chunks = [(j * KC, "far", j * KC) for j in range(PROMPT // KC)]
        chunks += [(q0 + j * KC, "strip", j * KC) for j in range(CL // KC)]
        block(h, q0, 0, chunks, c)
        return carry

    lax.fori_loop(0, heads * 2, cont_body, 0)
    dq[...] = dqt[...].T

    length = ids.shape[1]
    half = 2 * PROMPT
    lane8 = lax.broadcasted_iota(jnp.int32, (table.shape[0], length), 0)
    hot = ids[:1, :] == lane8
    for h in range(heads):
        def unskew(g, width):
            full = jnp.concatenate([jnp.zeros((128, 128), F32), g], axis=1)
            eight = full[:8]
            for a in range(1, 16):
                eight = eight + pltpu.roll(full[8 * a : 8 * a + 8], width - 8 * a, 1)
            vec = pltpu.roll(eight, width - 1, 1)[:1]
            for b in range(1, 8):
                vec = vec + pltpu.roll(eight, width - 1 - b, 1)[b : b + 1]
            return jnp.concatenate([vec, jnp.zeros((1, length - width), F32)], axis=1)

        total = jnp.broadcast_to(unskew(gstrip[h], half), (8, length))
        total = pltpu.roll(total, PROMPT // 2, 1)
        for c in range(2):
            piece = jnp.broadcast_to(unskew(gfar[h, c], FARW + 128), (8, length))
            total = total + pltpu.roll(piece, PROMPT // 2 + starts[c], 1)
        picked = jnp.where(hot, total[:1, :], 0.0)
        tgrad[h] = jnp.broadcast_to(jnp.sum(picked, axis=1, keepdims=True), tgrad.shape[1:])
    sums = []
    for n, (part, buf) in enumerate(pairs):
        loads[2 * n + 1].wait()
        turns[n].wait_recv()
        far_hops[n].wait_recv()
        sums.append(buf[3].astype(F32) + buf[1].astype(F32) + buf[4].astype(F32))
    wsum[...] = sums[0].astype(BF16)
    y[...] = (resid[...] + sums[1]).astype(BF16)
    for a in hops + turns + far_hops:
        a.wait_send()


def attn_bwd(starts, table, ids, q, k, v, o, do, lse, resid, ypart, wpart):
    rows, width = q.shape
    heads = width // HEAD_DIM
    smem = pl.BlockSpec(memory_space=pltpu.SMEM)
    vm = pl.BlockSpec(memory_space=pltpu.VMEM)
    wide = jax.ShapeDtypeStruct((rows, width), F32)
    return pl.pallas_call(
        functools.partial(attn_bwd_kernel, heads),
        out_shape=(
            wide,
            wide,
            wide,
            jax.ShapeDtypeStruct((heads, table.shape[0], 128), F32),
            jax.ShapeDtypeStruct(resid.shape, BF16),
            jax.ShapeDtypeStruct(wpart.shape[1:], BF16),
        ),
        in_specs=[smem, smem] + [vm] * 8 + [any_spec()] * 2,
        out_specs=(vm,) * 6,
        scratch_shapes=[
            pltpu.VMEM((heads, 128, STRIP), F32),
            pltpu.VMEM((heads, 2, 128, FARW), F32),
        ]
        + [pltpu.VMEM((heads, rows, width), BF16)] * 4
        + [
            pltpu.VMEM((width, rows), BF16),
            pltpu.VMEM((8, rows), F32),
            pltpu.VMEM((width, rows), F32),
            pltpu.VMEM((heads, 128, STRIP), F32),
            pltpu.VMEM((heads, 2, 128, FARW), F32),
        ]
        + wires_scratch(6)
        + [
            pltpu.SemaphoreType.DMA((4,)),
            pltpu.VMEM((5,) + resid.shape, BF16),
            pltpu.VMEM((5,) + wpart.shape[1:], BF16),
        ],
        compiler_params=call_params(5),
        name="attend_backward",
    )(starts, table, ids, q, k, v, o, do, lse, resid, ypart, wpart)


def reversed_ids(bucket_ids):
    span = bucket_ids.shape[0]
    ids = jnp.concatenate([bucket_ids[::-1], jnp.full((1,), -1, jnp.int32)])
    return jnp.broadcast_to(ids[None, :], (8, span + 1))


def pack_columns(w, nseq, nfsdp, mine):
    depth, total = w.shape
    block = total // nfsdp
    piece = -(-block // (16 * nseq)) * 16
    w = jnp.pad(w.reshape(depth, nfsdp, block), ((0, 0), (0, 0), (0, nseq * piece - block)))
    w = w.reshape(depth, nfsdp, nseq, piece)
    w = lax.dynamic_index_in_dim(w, mine, 2, keepdims=False)
    return w.reshape(depth, nfsdp * piece)


def unpack_columns(parts, total, nfsdp):
    nseq, depth, width = parts.shape
    piece = width // nfsdp
    block = total // nfsdp
    w = parts.reshape(nseq, depth, nfsdp, piece).transpose(1, 2, 0, 3)
    return w.reshape(depth, nfsdp, nseq * piece)[:, :, :block].reshape(depth, total)


def pack_rows(w, nseq, mine):
    block, depth = w.shape
    piece = -(-block // (16 * nseq)) * 16
    w = jnp.pad(w, ((0, nseq * piece - block), (0, 0)))
    return lax.dynamic_slice_in_dim(w, mine * piece, piece, 0)


def dot32(a, b):
    return jnp.dot(a, b, preferred_element_type=F32)


def dot_tn(a, b):
    return lax.dot_general(a, b, (((0,), (0,)), ((), ())), preferred_element_type=F32)


def gelu_both(u):
    inner = 0.7978845608028654 * (u + 0.044715 * u * u * u)
    t = jnp.tanh(inner)
    value = 0.5 * u * (1.0 + t)
    slope = 0.5 * (1.0 + t) + 0.5 * u * (1.0 - t * t) * 0.7978845608028654 * (1.0 + 3 * 0.044715 * u * u)
    return value, slope


def body(
    tokens,
    out_grad,
    attn_gain,
    w_query,
    w_key,
    w_value,
    w_out,
    mix_gain,
    w_gate,
    w_up,
    w_down,
    rel_table,
    bucket_ids,
    cont_start,
):
    nseq = lax.axis_size("seq")
    nfsdp = lax.axis_size("fsdp")
    mine = lax.axis_index("seq")
    where = lax.axis_index("fsdp")
    rows, width = tokens.shape[1:]
    inner = w_query.shape[1]
    piece = inner // nseq
    heads = piece // HEAD_DIM
    hidden_all = w_gate.shape[1]

    def gather_f(a):
        return lax.all_gather(a, "fsdp", axis=0, tiled=True)

    def gather_s(a):
        return lax.all_gather(a, "seq", axis=0, tiled=True)

    def scatter_f(a):
        return lax.psum_scatter(a.astype(BF16), "fsdp", scatter_dimension=0, tiled=True)

    local = [lax.dynamic_slice_in_dim(w, mine * piece, piece, 1) for w in (w_query, w_key, w_value)]
    gains = jnp.pad(jnp.stack([attn_gain, mix_gain], axis=1), ((0, 0), (0, 62)))
    first = gather_f(jnp.concatenate(local + [gains], axis=1))
    query_w, key_w, value_w = (first[:, i * piece : (i + 1) * piece] for i in range(3))
    gain_one = first[:, 3 * piece].astype(F32)
    gain_two = first[:, 3 * piece + 1].astype(F32)
    out_cols = width // nseq
    out_local = lax.dynamic_slice_in_dim(w_out, mine * out_cols, out_cols, 1)
    out_q = gather_f(out_local)
    gate_w = gather_f(pack_columns(w_gate, nseq, nfsdp, mine))
    up_w = gather_f(pack_columns(w_up, nseq, nfsdp, mine))
    down_w = gather_f(pack_rows(w_down, nseq, mine))

    group = tokens_gather(tokens[0], nseq).astype(F32)
    normed = (group * inverse_rms(group) * gain_one).astype(BF16)
    query = dot32(normed, query_w).astype(BF16)
    keys = dot32(normed, key_w).astype(BF16)
    values = dot32(normed, value_w).astype(BF16)
    table = lax.dynamic_slice_in_dim(rel_table, mine * heads, heads, 1)
    ids = reversed_ids(bucket_ids)
    starts = cont_start[0]
    mixed, lse, out_w, cot = attn_fwd(starts, table, ids, query, keys, values, out_q, out_grad[0], nseq)
    mixed_rows, resid, normed_two = mix(mixed, out_w, tokens[0], gain_two[None])
    gate = dot32(normed_two, gate_w)
    upward = dot32(normed_two, up_w)
    active, slope = gelu_both(gate)
    hidden = (active * upward).astype(BF16)
    result = dot32(hidden, down_w).astype(BF16)
    down_grad = scatter_f(dot_tn(hidden, cot))
    hidden_grad = nt(cot, down_w)
    gate_grad = (hidden_grad * upward * slope).astype(BF16)
    up_grad = (hidden_grad * active).astype(BF16)
    resid_grad, mixed_grad, out_w_grad, gain_two_grad = unmix(
        gate_grad, up_grad, gate_w, up_w, resid, gain_two[None], out_grad[0], out_w, mixed_rows
    )
    gate_w_grad = scatter_f(dot_tn(normed_two, gate_grad))
    up_w_grad = scatter_f(dot_tn(normed_two, up_grad))
    dq, dk, dv, tgrad, block_out, out_w_grad = attn_bwd(
        starts, table, ids, query, keys, values, mixed, mixed_grad, lse, resid, result, out_w_grad
    )
    dqkv = jnp.concatenate([dq, dk, dv], axis=1).astype(BF16)
    qkv_grad = scatter_f(dot_tn(normed, dqkv))
    in_grad, gain_one_grad = input_grads(dqkv, first, tokens[0], gain_one[None], resid_grad)

    out_w_grad = lax.all_gather(scatter_f(out_w_grad), "seq", axis=1, tiled=True)
    qkv_grad = lax.all_gather(qkv_grad, "seq", axis=0).reshape(nseq, -1, 3, piece)
    qkv_grad = qkv_grad.transpose(1, 2, 0, 3).reshape(-1, 3, inner).astype(F32)
    gate_w_grad = unpack_columns(lax.all_gather(gate_w_grad, "seq", axis=0), hidden_all, nfsdp)
    up_w_grad = unpack_columns(lax.all_gather(up_w_grad, "seq", axis=0), hidden_all, nfsdp)
    down_grad = gather_s(down_grad)[: w_down.shape[0]]

    buckets = rel_table.shape[0]
    table_full = jnp.zeros((nseq, heads, buckets), F32)
    table_full = lax.dynamic_update_slice(table_full, tgrad[None, :, :, 0], (mine, jnp.int32(0), jnp.int32(0)))
    table_grad, gain_one_all, gain_two_all = lax.psum(
        (table_full, gain_one_grad[0], gain_two_grad[0]), ("seq", "fsdp")
    )
    share = width // nfsdp
    gain_one_share = lax.dynamic_slice_in_dim(gain_one_all, where * share, share)
    gain_two_share = lax.dynamic_slice_in_dim(gain_two_all, where * share, share)
    return (
        block_out[None],
        in_grad[None],
        gain_one_share,
        qkv_grad[:, 0],
        qkv_grad[:, 1],
        qkv_grad[:, 2],
        out_w_grad.astype(F32),
        gain_two_share,
        gate_w_grad.astype(F32),
        up_w_grad.astype(F32),
        down_grad.astype(F32),
        table_grad.reshape(nseq * heads, buckets).T,
    )


def solution(mesh):
    placed = (
        P("fsdp", "seq", None),
        P("fsdp", "seq", None),
        P("fsdp"),
        P("fsdp", None),
        P("fsdp", None),
        P("fsdp", None),
        P("fsdp", None),
        P("fsdp"),
        P("fsdp", None),
        P("fsdp", None),
        P("fsdp", None),
        P(),
        P(),
        P("fsdp", None),
    )
    results = placed[:1] * 2 + placed[2:11] + (P(),)
    return jax.shard_map(body, mesh=mesh, in_specs=placed, out_specs=results, check_vma=False)
```

```python
import functools
import jax
import jax.numpy as jnp
from jax import lax
from jax.experimental import pallas as pl
from jax.experimental.pallas import tpu as pltpu
from jax.sharding import PartitionSpec as P

HEAD_DIM = 64
PROMPT = 1024
CL = 256
F32 = jnp.float32
BF16 = jnp.bfloat16
MESH = pl.DeviceIdType.MESH
epsilon = 1e-06
STRIP = 2 * PROMPT - 128
FARW = PROMPT - 128 + CL
KC = 256


def nt(a, b):
    return lax.dot_general(a, b, (((1,), (1,)), ((), ())), preferred_element_type=F32)


def nn(a, b):
    return lax.dot_general(a, b, (((1,), (0,)), ((), ())), preferred_element_type=F32)


class Wires:
    def __init__(self, send, recv):
        self.send, self.recv, self.used = send, recv, 0

    def take(self, count):
        self.used += count
        return self.used - count

    def at(self, i, src, dst, where):
        return pltpu.make_async_remote_copy(
            src_ref=src,
            dst_ref=dst,
            send_sem=self.send.at[i],
            recv_sem=self.recv.at[i],
            device_id=where,
            device_id_type=MESH,
        )

    def go(self, src, dst, where):
        c = self.at(self.take(1), src, dst, where)
        c.start()
        return c


def seq_places():
    s = lax.axis_index("seq")
    near = s + 1 - 2 * lax.rem(s, 2)
    far = lax.rem(s + 2, 4)
    cross = lax.rem(near + 2, 4)
    return s, near, far, cross


def meet(places):
    barrier = pltpu.get_barrier_semaphore()
    for where in places:
        pl.semaphore_signal(barrier, inc=1, device_id=where, device_id_type=MESH)
    pl.semaphore_wait(barrier, len(places))


def rows_at(index, rows, offset=0, count=None):
    return pl.ds(pl.multiple_of(index * rows + offset, 16), rows if count is None else count)


class SeqGather:
    def __init__(self, wires, out_at, chunks):
        self.wires, self.out_at, self.chunks = wires, out_at, chunks
        self.s, self.near, self.far, self.cross = seq_places()
        self.base = wires.take(3 * chunks)

    def trip(self, kind, c, src=None):
        view = self.out_at(self.far if kind == 2 else self.s, c)
        where = {"seq": self.far if kind == 0 else self.near}
        return self.wires.at(self.base + 3 * c + kind, view if src is None else src, view, where)

    def send(self, c, src):
        self.trip(0, c, src).start()
        self.trip(1, c, src).start()

    def forward(self, c):
        self.trip(0, c).wait_recv()
        self.trip(2, c).start()

    def finish(self):
        for c in range(self.chunks):
            self.trip(1, c).wait_recv()
            self.trip(2, c).wait_recv()
            for kind in range(3):
                self.trip(kind, c).wait_send()


def fsdp_places():
    f = lax.axis_index("fsdp")
    return f // 2, lax.rem(f, 2), lax.axis_size("fsdp") // 2


def fsdp_peers():
    pair, side, pairs = fsdp_places()
    peers = [{"fsdp": lax.rem(pair + d, pairs) * 2 + side} for d in range(1, pairs)]
    return peers + [{"fsdp": pair * 2 + 1 - side}]


class FsdpGather:
    def __init__(self, wires, shard, full, local):
        self.wires, self.shard, self.full, self.local = wires, shard, full, local
        self.pair, self.side, self.pairs = fsdp_places()
        self.base = wires.take(2 * self.pairs)

    def view(self, d, side):
        return self.full.at[lax.rem(self.pair + d, self.pairs) * 2 + side]

    def out(self, d):
        own = self.view(0, self.side)
        if d == 0:
            return self.wires.at(self.base, self.shard, own, {"fsdp": self.pair * 2 + 1 - self.side})
        where = {"fsdp": lax.rem(self.pair + d, self.pairs) * 2 + self.side}
        return self.wires.at(self.base + d, self.shard, own, where)

    def onward(self, d):
        view = self.view(self.pairs - d, self.side)
        return self.wires.at(self.base + self.pairs + d, view, view, {"fsdp": self.pair * 2 + 1 - self.side})

    def keep(self):
        return pltpu.make_async_copy(self.shard, self.view(0, self.side), self.local)

    def start(self):
        self.out(0).start()
        for d in range(1, self.pairs):
            self.out(d).start()
        self.keep().start()

    def forward(self, d):
        self.out(d).wait_recv()
        self.onward(d).start()

    def finish(self):
        self.keep().wait()
        self.out(0).wait_recv()
        for d in range(1, self.pairs):
            self.onward(d).wait_recv()
        for d in range(self.pairs):
            self.out(d).wait_send()
        for d in range(1, self.pairs):
            self.onward(d).wait_send()


class FsdpScatter:
    def __init__(self, wires, parts, bufs, local, result):
        self.wires, self.parts, self.local, self.result = wires, parts, local, result
        self.mine, self.got, self.passed, self.landed = bufs
        self.pair, self.side, self.pairs = fsdp_places()
        self.base = wires.take(2 * self.pairs)

    def owner(self, d):
        return lax.rem(self.pair + d, self.pairs) * 2

    def load(self, d):
        return pltpu.make_async_copy(self.parts.at[self.owner(d) + self.side], self.mine.at[d], self.local.at[d])

    def swap(self, d):
        src = self.parts.at[self.owner(d) + 1 - self.side]
        return self.wires.at(self.base + d, src, self.got.at[d], {"fsdp": self.pair * 2 + 1 - self.side})

    def onward(self, d):
        where = {"fsdp": self.owner(d) + self.side}
        return self.wires.at(self.base + self.pairs + d, self.passed.at[d], self.landed.at[d], where)

    def order(self):
        return list(range(1, self.pairs)) + [0]

    def start(self):
        for d in self.order():
            self.swap(d).start()
            self.load(d).start()

    def step(self, d):
        self.load(d).wait()
        self.swap(d).wait_recv()
        self.passed[d] = (self.mine[d].astype(F32) + self.got[d].astype(F32)).astype(BF16)
        self.onward(d).start()

    def finish(self):
        self.load(0).wait()
        self.swap(0).wait_recv()
        total = self.mine[0].astype(F32) + self.got[0].astype(F32)
        for d in range(1, self.pairs):
            self.onward(d).wait_recv()
            total = total + self.landed[d].astype(F32)
        self.result[...] = total.astype(BF16)
        for d in range(self.pairs):
            self.swap(d).wait_send()
        for d in range(1, self.pairs):
            self.onward(d).wait_send()


def fsdp_scatter_scratch(parts):
    shape = (parts.shape[0] // 2,) + parts.shape[1:]
    return [pltpu.VMEM(shape, BF16)] * 4 + [pltpu.SemaphoreType.DMA((shape[0],))]


def blocks(a, count):
    return a.reshape((count, a.shape[0] // count) + a.shape[1:])


def vm_spec():
    return pl.BlockSpec(memory_space=pltpu.VMEM)


def any_spec():
    return pl.BlockSpec(memory_space=pl.ANY)


def wires_scratch(n):
    return [pltpu.SemaphoreType.DMA((n,)), pltpu.SemaphoreType.DMA((n,))]


def call_params(number, vmem=60):
    return pltpu.CompilerParams(collective_id=number, has_side_effects=True, vmem_limit_bytes=vmem << 20)


def inverse_rms(v):
    return lax.rsqrt(jnp.mean(v * v, axis=-1, keepdims=True) + epsilon)


def norm_back(grad, v, r, gain):
    scaled = grad * gain
    return r * scaled - v * (r * r * r) * jnp.mean(v * scaled, axis=-1, keepdims=True)


def tokens_gather_kernel(src, first_q, out_q, out, first, out_w, send, recv, local):
    rows = src.shape[0]
    s, near, far, cross = seq_places()
    meet([{"seq": near}, {"seq": far}] + fsdp_peers())
    half = rows // 2
    wires = Wires(send, recv)
    ring = SeqGather(wires, lambda t, c: out.at[rows_at(t, rows, c * half, half), :], 2)
    lead = FsdpGather(wires, first_q, first, local.at[1])
    late = FsdpGather(wires, out_q, out_w, local.at[2])
    own = pltpu.make_async_copy(src, out.at[rows_at(s, rows), :], local.at[0])
    lead.start()
    for c in range(2):
        ring.send(c, src.at[pl.ds(c * half, half), :])
    late.start()
    own.start()
    for d in range(1, lead.pairs):
        lead.forward(d)
        if d == lead.pairs // 2:
            ring.forward(0)
    for d in range(1, late.pairs):
        late.forward(d)
    ring.forward(1)
    own.wait()
    lead.finish()
    late.finish()
    ring.finish()


def tokens_gather(tokens, first_q, out_q, nseq, nfsdp):
    rows, width = tokens.shape
    return pl.pallas_call(
        tokens_gather_kernel,
        out_shape=(
            jax.ShapeDtypeStruct((nseq * rows, width), BF16),
            jax.ShapeDtypeStruct((nfsdp,) + first_q.shape, BF16),
            jax.ShapeDtypeStruct((nfsdp,) + out_q.shape, BF16),
        ),
        in_specs=[any_spec()] * 3,
        out_specs=(any_spec(),) * 3,
        scratch_shapes=wires_scratch(6 + 2 * nfsdp) + [pltpu.SemaphoreType.DMA((3,))],
        compiler_params=call_params(0, 4),
        name="tokens_gather",
    )(tokens, first_q, out_q)


def mix_kernel(o, out_w, tok, gain, up_q, down_q, obuf, resid, n2, up_w, down_w, send, recv, own, local):
    rows, width = tok.shape
    piece = o.shape[1]
    nseq = obuf.shape[0]
    s, near, far, cross = seq_places()
    meet([{"seq": near}, {"seq": far}, {"seq": cross}] + fsdp_peers())
    wires = Wires(send, recv)
    weights = [FsdpGather(wires, up_q, up_w, local.at[1]), FsdpGather(wires, down_q, down_w, local.at[2])]
    for a in weights:
        a.start()
    trips = [wires.go(o.at[rows_at(t, rows), :], obuf.at[s], {"seq": t}) for t in (far, cross, near)]
    obuf[s] = o[rows_at(s, rows), :]
    half = rows // 2
    for a in trips:
        a.wait_recv()
    ring = SeqGather(wires, lambda t, c: n2.at[rows_at(t, rows, c * half, half), :], 2)
    for c in range(2):
        part = slice(c * half, (c + 1) * half)
        cols = out_w.shape[2]
        for u in range(nseq):
            acc = tok[part, u * cols : (u + 1) * cols].astype(F32)
            for t in range(nseq):
                acc = acc + nn(obuf[t, part, :], out_w[u, t * piece : (t + 1) * piece, :])
            resid[part, u * cols : (u + 1) * cols] = acc
        h = resid[part, :]
        own[part, :] = (h * inverse_rms(h) * gain[...]).astype(BF16)
        ring.send(c, own.at[pl.ds(c * half, half), :])
    mineblock = pltpu.make_async_copy(own, n2.at[rows_at(s, rows), :], local.at[0])
    mineblock.start()
    pairs = weights[0].pairs
    weights[0].forward(1)
    ring.forward(0)
    for d in range(2, pairs):
        weights[0].forward(d)
    ring.forward(1)
    for d in range(1, pairs):
        weights[1].forward(d)
    for a in weights:
        a.finish()
    mineblock.wait()
    ring.finish()
    for a in trips:
        a.wait_send()


def mix(o, out_w, tok, gain, up_q, down_q, nfsdp):
    nseq = out_w.shape[0]
    rows, width = tok.shape
    return pl.pallas_call(
        mix_kernel,
        out_shape=(
            jax.ShapeDtypeStruct((nseq, rows, o.shape[1]), BF16),
            jax.ShapeDtypeStruct((rows, width), F32),
            jax.ShapeDtypeStruct((nseq * rows, width), BF16),
            jax.ShapeDtypeStruct((nfsdp,) + up_q.shape, BF16),
            jax.ShapeDtypeStruct((nfsdp,) + down_q.shape, BF16),
        ),
        in_specs=[vm_spec()] * 4 + [any_spec()] * 2,
        out_specs=(vm_spec(), vm_spec()) + (any_spec(),) * 3,
        scratch_shapes=wires_scratch(9 + 2 * nfsdp)
        + [pltpu.VMEM((rows, width), BF16), pltpu.SemaphoreType.DMA((3,))],
        compiler_params=call_params(2, 32),
        name="mix",
    )(o, out_w, tok, gain, up_q, down_q)


class SeqScatter:
    def __init__(self, wires, chunks, *bufs):
        self.s, self.near, self.far, self.cross = seq_places()
        self.wires, self.chunks, self.bufs = wires, chunks, bufs
        self.base = wires.take(3 * chunks)

    def trip(self, kind, c):
        where = {"seq": self.far if kind == 1 else self.near}
        src, dst = self.bufs[2 * kind].at[c], self.bufs[2 * kind + 1].at[c]
        return self.wires.at(self.base + 3 * c + kind, src, dst, where)

    def cross_chunk(self, c, value):
        self.bufs[0][c] = value.astype(BF16)
        self.trip(0, c).start()

    def far_chunk(self, c, value):
        self.trip(0, c).wait_recv()
        self.bufs[2][c] = (value + self.bufs[1][c].astype(F32)).astype(BF16)
        self.trip(1, c).start()

    def near_chunk(self, c, value):
        self.bufs[4][c] = value.astype(BF16)
        self.trip(2, c).start()

    def own_chunk(self, c, value):
        self.trip(2, c).wait_recv()
        self.trip(1, c).wait_recv()
        return value + self.bufs[5][c].astype(F32) + self.bufs[3][c].astype(F32)

    def finish(self):
        for c in range(self.chunks):
            for kind in range(3):
                self.trip(kind, c).wait_send()


def scatter_scratch(chunks, rows, width):
    return [pltpu.VMEM((chunks, rows, width), BF16)] * 6


def unmix_kernel(
    chunks, dg, du, gate_w, up_w, resid, gain, cot, out_w, obuf, parts,
    rgrad, dmix, wgrad, ggrad, shard,
    send, recv, b0, b1, b2, b3, b4, b5, attn, dob, p0, p1, p2, p3, local,
):
    rows, width = resid.shape
    nseq, _, piece = obuf.shape
    s, near, far, cross = seq_places()
    meet([{"seq": near}, {"seq": far}, {"seq": cross}] + fsdp_peers())
    wires = Wires(send, recv)
    grads = FsdpScatter(wires, parts, (p0, p1, p2, p3), local, shard)
    grads.start()
    sums = SeqScatter(wires, chunks, b0, b1, b2, b3, b4, b5)
    size = rows // chunks

    def part(t, c):
        at = rows_at(t, rows, c * size, size)
        return nt(dg[at, :], gate_w[...]) + nt(du[at, :], up_w[...])

    for c in range(chunks):
        sums.cross_chunk(c, part(cross, c))
    for c in range(chunks):
        sums.far_chunk(c, part(far, c))
    for c in range(chunks):
        sums.near_chunk(c, part(near, c))
    for c in range(chunks):
        rgrad[c * size : (c + 1) * size, :] = part(s, c)
    total = jnp.zeros((1, width), F32)
    trips = []
    grads.step(1)
    for c in range(chunks):
        at = slice(c * size, (c + 1) * size)
        dn = sums.own_chunk(c, rgrad[at, :])
        h = resid[at, :]
        r = inverse_rms(h)
        total = total + jnp.sum(dn * h * r, axis=0, keepdims=True)
        rg = cot[at, :].astype(F32) + norm_back(dn, h, r, gain[...])
        rgrad[at, :] = rg
        low = rg.astype(BF16)
        attn[at, :] = low
        cols = out_w.shape[2]
        for t in range(nseq):
            acc = jnp.zeros((size, piece), F32)
            for u in range(nseq):
                acc = acc + nt(low[:, u * cols : (u + 1) * cols], out_w[u, t * piece : (t + 1) * piece, :])
            dob[t, at, :] = acc.astype(BF16)
        if c == 0:
            for d in range(2, grads.pairs):
                grads.step(d)
    ggrad[...] = jnp.broadcast_to(total, ggrad.shape)
    for t in (far, cross, near):
        trips.append(wires.go(dob.at[t], dmix.at[rows_at(s, rows), :], {"seq": t}))
    dmix[rows_at(s, rows), :] = dob[s]
    cols = out_w.shape[2]
    for t in range(nseq):
        for u in range(nseq):
            wgrad[u, t * piece : (t + 1) * piece, :] = lax.dot_general(
                obuf[t], attn[:, u * cols : (u + 1) * cols], (((0,), (0,)), ((), ())), preferred_element_type=F32
            ).astype(BF16)
    for a in trips:
        a.wait()
    sums.finish()
    grads.finish()


def unmix(dg, du, gate_w, up_w, resid, gain, cot, out_w, obuf, parts, chunks=2):
    rows, width = resid.shape
    nseq, _, piece = obuf.shape
    return pl.pallas_call(
        functools.partial(unmix_kernel, chunks),
        out_shape=(
            jax.ShapeDtypeStruct((rows, width), F32),
            jax.ShapeDtypeStruct((nseq * rows, piece), BF16),
            jax.ShapeDtypeStruct(out_w.shape, BF16),
            jax.ShapeDtypeStruct((8, width), F32),
            jax.ShapeDtypeStruct(parts.shape[1:], BF16),
        ),
        in_specs=[vm_spec()] * 9 + [any_spec()],
        out_specs=(vm_spec(),) * 5,
        scratch_shapes=wires_scratch(3 * chunks + 3 + parts.shape[0])
        + scatter_scratch(chunks, rows // chunks, width)
        + [pltpu.VMEM((rows, width), BF16), pltpu.VMEM((nseq, rows, piece), BF16)]
        + fsdp_scatter_scratch(parts),
        compiler_params=call_params(4),
        name="unmix",
    )(dg, du, gate_w, up_w, resid, gain, cot, out_w, obuf, parts)


def input_kernel(
    chunks, dqkv, qkv_w, tok, gain, rgrad, parts, done0, done1,
    in_grad, ggrad, shard, full0, full1,
    send, recv, b0, b1, b2, b3, b4, b5, hold, p0, p1, p2, p3, plocal, local,
):
    rows, width = tok.shape
    s, near, far, cross = seq_places()
    meet([{"seq": near}, {"seq": far}] + fsdp_peers())
    wires = Wires(send, recv)
    grads = FsdpScatter(wires, parts, (p0, p1, p2, p3), plocal, shard)
    grads.start()
    sums = SeqScatter(wires, chunks, b0, b1, b2, b3, b4, b5)
    size = rows // chunks
    used = dqkv.shape[1]

    def part(t, c):
        return nt(dqkv[rows_at(t, rows, c * size, size), :], qkv_w[:, :used])

    for c in range(chunks):
        sums.cross_chunk(c, part(cross, c))
    for c in range(chunks):
        sums.far_chunk(c, part(far, c))
    for c in range(chunks):
        sums.near_chunk(c, part(near, c))
    for c in range(chunks):
        hold[c * size : (c + 1) * size, :] = part(s, c)
    total = jnp.zeros((1, width), F32)
    rings = []
    for n, (done, full) in enumerate(((done0, full0), (done1, full1))):
        ring = SeqGather(wires, lambda t, c, full=full: full.at[t], 1)
        ring.send(0, done)
        pltpu.make_async_copy(done, full.at[s], local.at[n]).start()
        rings.append(ring)
    grads.step(1)
    for c in range(chunks):
        at = slice(c * size, (c + 1) * size)
        dn = sums.own_chunk(c, hold[at, :])
        x = tok[at, :].astype(F32)
        r = inverse_rms(x)
        total = total + jnp.sum(dn * x * r, axis=0, keepdims=True)
        in_grad[at, :] = (rgrad[at, :] + norm_back(dn, x, r, gain[...])).astype(BF16)
        if c == 0:
            for d in range(2, grads.pairs):
                grads.step(d)
    ggrad[...] = jnp.broadcast_to(total, ggrad.shape)
    for ring in rings:
        ring.forward(0)
    sums.finish()
    grads.finish()
    for n, (done, full) in enumerate(((done0, full0), (done1, full1))):
        rings[n].finish()
        pltpu.make_async_copy(done, full.at[s], local.at[n]).wait()


def input_grads(dqkv, qkv_w, tok, gain, rgrad, parts, done0, done1, nseq, chunks=2):
    rows, width = tok.shape
    return pl.pallas_call(
        functools.partial(input_kernel, chunks),
        out_shape=(
            jax.ShapeDtypeStruct((rows, width), BF16),
            jax.ShapeDtypeStruct((8, width), F32),
            jax.ShapeDtypeStruct(parts.shape[1:], BF16),
            jax.ShapeDtypeStruct((nseq,) + done0.shape, BF16),
            jax.ShapeDtypeStruct((nseq,) + done1.shape, BF16),
        ),
        in_specs=[vm_spec()] * 5 + [any_spec()] * 3,
        out_specs=(vm_spec(),) * 3 + (any_spec(),) * 2,
        scratch_shapes=wires_scratch(3 * chunks + parts.shape[0] + 6)
        + scatter_scratch(chunks, rows // chunks, width)
        + [pltpu.VMEM((rows, width), F32)]
        + fsdp_scatter_scratch(parts)
        + [pltpu.SemaphoreType.DMA((2,))],
        compiler_params=call_params(6, 48),
        name="input_grads",
    )(dqkv, qkv_w, tok, gain, rgrad, parts, done0, done1)


def last_kernel(
    qkv_p, out_p, done, gain_a, gain_b, table,
    qkv_f, out_f, full, small,
    send, recv, local, qkv_s, out_s, held, stage, one, two, three, *bufs,
):
    s, near, far, cross = seq_places()
    pair, side, pairs = fsdp_places()
    meet([{"seq": near}, {"seq": far}, {"seq": cross}] + fsdp_peers())
    wires = Wires(send, recv)
    scatters = [
        FsdpScatter(wires, qkv_p, bufs[:4], bufs[4], qkv_s),
        FsdpScatter(wires, out_p, bufs[5:9], bufs[9], out_s),
    ]
    for a in scatters:
        a.start()
    ring = SeqGather(wires, lambda t, c: full.at[t], 1)
    ring.send(0, done)
    keep = pltpu.make_async_copy(done, full.at[s], local.at[0])
    keep.start()
    held[...] = jnp.zeros(held.shape, F32)
    lanes = held.shape[1]
    lines = gain_a.shape[1] // lanes
    for n in range(lines):
        held[n : n + 1, :] = gain_a[:1, n * lanes : (n + 1) * lanes]
        held[lines + n : lines + n + 1, :] = gain_b[:1, n * lanes : (n + 1) * lanes]
    heads = table.shape[0]
    held[pl.ds(2 * lines + s * 8, heads), :] = table[...]
    trips = [wires.go(held, one.at[n], {"seq": t}) for n, t in enumerate((near, far, cross))]
    scatters[0].step(1)
    for a in trips:
        a.wait_recv()
    stage[0] = held[...] + one[0] + one[1] + one[2]
    trips.append(wires.go(stage.at[0], two, {"fsdp": pair * 2 + 1 - side}))
    for d in range(2, pairs):
        scatters[0].step(d)
    trips[-1].wait_recv()
    stage[1] = stage[0] + two[...]
    zs = [
        wires.go(stage.at[1], three.at[d - 1], {"fsdp": lax.rem(pair + d, pairs) * 2 + side})
        for d in range(1, pairs)
    ]
    for d in range(1, pairs):
        scatters[1].step(d)
    ring.forward(0)
    scatters[0].finish()
    more = [SeqGather(wires, lambda t, c: qkv_f.at[t], 1), SeqGather(wires, lambda t, c: out_f.at[t], 1)]
    copies = [pltpu.make_async_copy(qkv_s, qkv_f.at[s], local.at[1]), pltpu.make_async_copy(out_s, out_f.at[s], local.at[2])]
    more[0].send(0, qkv_s)
    scatters[1].finish()
    more[1].send(0, out_s)
    total = stage[1]
    for d, a in enumerate(zs):
        a.wait_recv()
        total = total + three[d]
    small[...] = total
    for n in range(2):
        copies[n].start()
        more[n].forward(0)
    for n in range(2):
        more[n].finish()
        copies[n].wait()
    ring.finish()
    keep.wait()
    for a in trips + zs:
        a.wait_send()


def last_sums(qkv_p, out_p, done, gain_a, gain_b, table, nseq):
    nfsdp = qkv_p.shape[0]
    lines = -(-(2 * gain_a.shape[1] // 128 + 8 * nseq) // 8) * 8
    return pl.pallas_call(
        last_kernel,
        out_shape=(
            jax.ShapeDtypeStruct((nseq,) + qkv_p.shape[1:], BF16),
            jax.ShapeDtypeStruct((nseq,) + out_p.shape[1:], BF16),
            jax.ShapeDtypeStruct((nseq,) + done.shape, BF16),
            jax.ShapeDtypeStruct((lines, 128), F32),
        ),
        in_specs=[any_spec()] * 3 + [vm_spec()] * 3,
        out_specs=(any_spec(),) * 3 + (vm_spec(),),
        scratch_shapes=wires_scratch(2 * nfsdp + 9 + 4 + nfsdp // 2)
        + [
            pltpu.SemaphoreType.DMA((3,)),
            pltpu.VMEM(qkv_p.shape[1:], BF16),
            pltpu.VMEM(out_p.shape[1:], BF16),
            pltpu.VMEM((lines, 128), F32),
            pltpu.VMEM((2, lines, 128), F32),
            pltpu.VMEM((3, lines, 128), F32),
            pltpu.VMEM((lines, 128), F32),
            pltpu.VMEM((nfsdp // 2 - 1, lines, 128), F32),
        ]
        + fsdp_scatter_scratch(qkv_p)
        + fsdp_scatter_scratch(out_p),
        compiler_params=call_params(7, 32),
        name="last_sums",
    )(qkv_p, out_p, done, gain_a, gain_b, table)


def build_strips(heads, starts, table, ids, strip, far):
    length = ids.shape[1]
    half = 2 * PROMPT
    for h in range(heads):
        row = jnp.zeros(ids.shape, F32)
        for b in range(table.shape[0]):
            row = jnp.where(ids[...] == b, table[b, h], row)
        base = jnp.broadcast_to(row[:1, PROMPT // 2 : PROMPT // 2 + half], (128, half))
        strip[h] = pltpu.roll(base, 1, 1, stride=1, stride_axis=0)[:, 128:]
        for c in range(2):
            moved = pltpu.roll(row, length - PROMPT // 2 - starts[c], 1)
            base = jnp.broadcast_to(moved[:1, : FARW + 128], (128, FARW + 128))
            far[h, c] = pltpu.roll(base, 1, 1, stride=1, stride_axis=0)[:, 128:]


def head_masks(width, heads):
    lane = lax.broadcasted_iota(jnp.int32, (1, width), 1)
    return [(lane >= h * HEAD_DIM) & (lane < (h + 1) * HEAD_DIM) for h in range(heads)]


def masked_copies(src, dst, heads):
    masks = head_masks(src.shape[1], heads)
    for h in range(heads):
        dst[h] = jnp.where(masks[h], src[...], jnp.zeros((), src.dtype))


def bias_chunk(strip, far, h, first_q, kstart, kind, c):
    parts = []
    for r in range(KC // 128):
        m = PROMPT - 128 - (kstart + 128 * r)
        if kind == "far":
            parts.append(far[h, c, :, m : m + CL])
        else:
            parts.append(strip[h, :, pl.ds(pl.multiple_of(first_q + m, 128), CL)])
    return jnp.concatenate(parts, axis=0)


def attn_fwd_kernel(
    heads, starts, table, ids, q, k, v, out_q, cot, gate_q,
    o, lse, out_w, cots, gate_w,
    strip, far, kh, vt, ot, s, send, recv, local,
):
    rows = cot.shape[0]
    mine, near, other, cross = seq_places()
    meet([{"seq": near}, {"seq": other}] + fsdp_peers())
    wires = Wires(send, recv)
    half = rows // 2
    weight = FsdpGather(wires, gate_q, gate_w, local.at[2])
    weight.start()
    wring = SeqGather(wires, lambda t, c: out_w.at[t], 1)
    cring = SeqGather(wires, lambda t, c: cots.at[rows_at(t, rows, c * half, half), :], 2)
    wring.send(0, out_q)
    for c in range(2):
        cring.send(c, cot.at[pl.ds(c * half, half), :])
    own = [
        pltpu.make_async_copy(out_q, out_w.at[mine], local.at[0]),
        pltpu.make_async_copy(cot, cots.at[rows_at(mine, rows), :], local.at[1]),
    ]
    for a in own:
        a.start()
    build_strips(heads, starts, table, ids, strip, far)
    masked_copies(k, kh, heads)
    vt[...] = v[...].astype(F32).T.astype(BF16)
    lse[...] = jnp.zeros(lse.shape, F32)

    def block(h, q0, bias_q0, chunks, c):
        qb = q[pl.ds(q0, CL), :]
        top = None
        for n, (k0, kind, kstart) in enumerate(chunks):
            sc = nt(kh[h, pl.ds(k0, KC), :], qb) + bias_chunk(strip, far, h, bias_q0, kstart, kind, c)
            s[n * KC : (n + 1) * KC, :] = sc
            m = jnp.max(sc, axis=0, keepdims=True)
            top = m if top is None else jnp.maximum(top, m)
        total = jnp.zeros((1, CL), F32)
        acc = jnp.zeros((HEAD_DIM, CL), F32)
        for n, (k0, kind, kstart) in enumerate(chunks):
            e = jnp.exp(s[n * KC : (n + 1) * KC, :] - top)
            total = total + jnp.sum(e, axis=0, keepdims=True)
            acc = acc + nn(vt[pl.ds(pl.multiple_of(h * HEAD_DIM, HEAD_DIM), HEAD_DIM), pl.ds(k0, KC)], e.astype(BF16))
        ot[pl.ds(pl.multiple_of(h * HEAD_DIM, HEAD_DIM), HEAD_DIM), pl.ds(q0, CL)] = acc / total
        lse[pl.ds(h, 1), pl.ds(q0, CL)] = top + jnp.log(total)

    nblk = PROMPT // CL

    def prompt_body(i, carry):
        h, blk = i // nblk, i % nblk
        q0 = pl.multiple_of(blk * CL, CL)
        block(h, q0, q0, [(j * KC, "strip", j * KC) for j in range(PROMPT // KC)], None)

        @pl.when(i == 6)
        def _():
            weight.forward(1)

        return carry

    lax.fori_loop(0, heads * nblk, prompt_body, 0)

    def cont_body(i, carry):
        h, c = i // 2, i % 2
        q0 = pl.multiple_of(PROMPT + c * CL, CL)
        chunks = [(j * KC, "far", j * KC) for j in range(PROMPT // KC)]
        chunks += [(q0 + j * KC, "strip", j * KC) for j in range(CL // KC)]
        block(h, q0, 0, chunks, c)
        return carry

    wring.forward(0)
    lax.fori_loop(0, heads * 2, cont_body, 0)
    o[...] = ot[...].T.astype(BF16)
    cring.forward(0)
    for d in range(2, weight.pairs):
        weight.forward(d)
    cring.forward(1)
    for a in own:
        a.wait()
    weight.finish()
    wring.finish()
    cring.finish()


def attn_fwd(starts, table, ids, q, k, v, out_q, cot, gate_q, nseq, nfsdp):
    rows, width = q.shape
    heads = width // HEAD_DIM
    smem = pl.BlockSpec(memory_space=pltpu.SMEM)
    vm = pl.BlockSpec(memory_space=pltpu.VMEM)
    return pl.pallas_call(
        functools.partial(attn_fwd_kernel, heads),
        out_shape=(
            jax.ShapeDtypeStruct((rows, width), BF16),
            jax.ShapeDtypeStruct((8, rows), F32),
            jax.ShapeDtypeStruct((nseq,) + out_q.shape, BF16),
            jax.ShapeDtypeStruct((rows, cot.shape[1]), BF16),
            jax.ShapeDtypeStruct((nfsdp,) + gate_q.shape, BF16),
        ),
        in_specs=[smem, smem, vm, vm, vm, vm] + [any_spec()] * 3,
        out_specs=(vm, vm) + (any_spec(),) * 3,
        scratch_shapes=[
            pltpu.VMEM((heads, 128, STRIP), F32),
            pltpu.VMEM((heads, 2, 128, FARW), F32),
            pltpu.VMEM((heads, rows, width), BF16),
            pltpu.VMEM((width, rows), BF16),
            pltpu.VMEM((width, rows), F32),
            pltpu.VMEM((PROMPT + CL, CL), F32),
        ]
        + wires_scratch(9 + nfsdp)
        + [pltpu.SemaphoreType.DMA((3,))],
        compiler_params=call_params(1, 40),
        name="attend_forward",
    )(starts, table, ids, q, k, v, out_q, cot, gate_q)


def attn_bwd_kernel(
    heads, starts, table, ids, q, k, v, o, do, lse, resid, ypart, wpart, parts,
    dq, dk, dv, tgrad, y, wsum, shard,
    strip, far, kh, vh, qh, doh, kt, delta, dqt, gstrip, gfar,
    send, recv, local, ybuf, wbuf, p0, p1, p2, p3, plocal,
):
    rows = resid.shape[0]
    mine, near, other, cross = seq_places()
    meet([{"seq": near}, {"seq": other}] + fsdp_peers())
    wires = Wires(send, recv)
    grads = FsdpScatter(wires, parts, (p0, p1, p2, p3), plocal, shard)
    grads.start()

    def block_of(part, t):
        return part.at[rows_at(t, rows), :] if part is ypart else part.at[t]

    pairs = ((wpart, wbuf), (ypart, ybuf))
    hops = [wires.go(block_of(part, cross), buf.at[0], {"seq": near}) for part, buf in pairs]
    turns = [wires.go(block_of(part, near), buf.at[1], {"seq": near}) for part, buf in pairs]
    loads = []
    for n, (part, buf) in enumerate(pairs):
        loads.append(pltpu.make_async_copy(block_of(part, other), buf.at[2], local.at[2 * n]))
        loads.append(pltpu.make_async_copy(block_of(part, mine), buf.at[3], local.at[2 * n + 1]))
    for a in loads:
        a.start()
    build_strips(heads, starts, table, ids, strip, far)
    for src, dst in ((k, kh), (v, vh), (q, qh), (do, doh)):
        masked_copies(src, dst, heads)
    kt[...] = k[...].astype(F32).T.astype(BF16)
    far_hops = []
    for n, (part, buf) in enumerate(pairs):
        loads[2 * n].wait()
        hops[n].wait_recv()
        buf[2] = (buf[2].astype(F32) + buf[0].astype(F32)).astype(BF16)
    for part, buf in pairs:
        far_hops.append(wires.go(buf.at[2], buf.at[4], {"seq": other}))
    prod = (o[...].astype(F32) * do[...].astype(F32)).T
    for h in range(heads):
        delta[h : h + 1, :] = jnp.sum(prod[h * HEAD_DIM : (h + 1) * HEAD_DIM, :], axis=0, keepdims=True)
    dk[...] = jnp.zeros(dk.shape, F32)
    dv[...] = jnp.zeros(dv.shape, F32)
    gstrip[...] = jnp.zeros(gstrip.shape, F32)
    gfar[...] = jnp.zeros(gfar.shape, F32)

    def block(h, q0, bias_q0, chunks, c):
        qb = q[pl.ds(q0, CL), :]
        dob = do[pl.ds(q0, CL), :]
        qhb = qh[h, pl.ds(q0, CL), :]
        dohb = doh[h, pl.ds(q0, CL), :]
        lrow = lse[pl.ds(h, 1), pl.ds(q0, CL)]
        drow = delta[pl.ds(h, 1), pl.ds(q0, CL)]
        acc = jnp.zeros((HEAD_DIM, CL), F32)
        for n, (k0, kind, kstart) in enumerate(chunks):
            ks = pl.ds(k0, KC)
            sc = nt(kh[h, ks, :], qb) + bias_chunk(strip, far, h, bias_q0, kstart, kind, c)
            pr = jnp.exp(sc - lrow)
            dp = nt(vh[h, ks, :], dob)
            ds = pr * (dp - drow)
            pl_ = pr.astype(BF16)
            dsl = ds.astype(BF16)
            dv[ks, :] += nn(pl_, dohb)
            dk[ks, :] += nn(dsl, qhb)
            acc = acc + nn(kt[pl.ds(pl.multiple_of(h * HEAD_DIM, HEAD_DIM), HEAD_DIM), ks], dsl)
            for r in range(KC // 128):
                m = PROMPT - 128 - (kstart + 128 * r)
                piece = ds[128 * r : 128 * (r + 1), :]
                if kind == "far":
                    gfar[h, c, :, m : m + CL] += piece
                else:
                    gstrip[h, :, pl.ds(pl.multiple_of(bias_q0 + m, 128), CL)] += piece
        dqt[pl.ds(pl.multiple_of(h * HEAD_DIM, HEAD_DIM), HEAD_DIM), pl.ds(q0, CL)] = acc

    nblk = PROMPT // CL

    def prompt_body(i, carry):
        h, blk = i // nblk, i % nblk
        q0 = pl.multiple_of(blk * CL, CL)
        block(h, q0, q0, [(j * KC, "strip", j * KC) for j in range(PROMPT // KC)], None)

        @pl.when(i == 3)
        def _():
            grads.step(1)

        return carry

    lax.fori_loop(0, heads * nblk, prompt_body, 0)

    for d in range(2, grads.pairs - 1):
        grads.step(d)

    def cont_body(i, carry):
        h, c = i // 2, i % 2
        q0 = pl.multiple_of(PROMPT + c * CL, CL)
        chunks = [(j * KC, "far", j * KC) for j in range(PROMPT // KC)]
        chunks += [(q0 + j * KC, "strip", j * KC) for j in range(CL // KC)]
        block(h, q0, 0, chunks, c)
        return carry

    lax.fori_loop(0, heads * 2, cont_body, 0)
    if grads.pairs > 2:
        grads.step(grads.pairs - 1)
    dq[...] = dqt[...].T

    length = ids.shape[1]
    half = 2 * PROMPT
    lane8 = lax.broadcasted_iota(jnp.int32, (table.shape[0], length), 0)
    hot = ids[:1, :] == lane8
    for h in range(heads):
        def unskew(g, width):
            full = jnp.concatenate([jnp.zeros((128, 128), F32), g], axis=1)
            eight = full[:8]
            for a in range(1, 16):
                eight = eight + pltpu.roll(full[8 * a : 8 * a + 8], width - 8 * a, 1)
            vec = pltpu.roll(eight, width - 1, 1)[:1]
            for b in range(1, 8):
                vec = vec + pltpu.roll(eight, width - 1 - b, 1)[b : b + 1]
            return jnp.concatenate([vec, jnp.zeros((1, length - width), F32)], axis=1)

        total = jnp.broadcast_to(unskew(gstrip[h], half), (8, length))
        total = pltpu.roll(total, PROMPT // 2, 1)
        for c in range(2):
            piece = jnp.broadcast_to(unskew(gfar[h, c], FARW + 128), (8, length))
            total = total + pltpu.roll(piece, PROMPT // 2 + starts[c], 1)
        picked = jnp.where(hot, total[:1, :], 0.0)
        tgrad[h] = jnp.broadcast_to(jnp.sum(picked, axis=1, keepdims=True), tgrad.shape[1:])
    sums = []
    for n, (part, buf) in enumerate(pairs):
        loads[2 * n + 1].wait()
        turns[n].wait_recv()
        far_hops[n].wait_recv()
        sums.append(buf[3].astype(F32) + buf[1].astype(F32) + buf[4].astype(F32))
    wsum[...] = sums[0].astype(BF16)
    y[...] = (resid[...] + sums[1]).astype(BF16)
    for a in hops + turns + far_hops:
        a.wait_send()
    grads.finish()


def attn_bwd(starts, table, ids, q, k, v, o, do, lse, resid, ypart, wpart, parts):
    rows, width = q.shape
    heads = width // HEAD_DIM
    smem = pl.BlockSpec(memory_space=pltpu.SMEM)
    vm = pl.BlockSpec(memory_space=pltpu.VMEM)
    wide = jax.ShapeDtypeStruct((rows, width), F32)
    return pl.pallas_call(
        functools.partial(attn_bwd_kernel, heads),
        out_shape=(
            wide,
            wide,
            wide,
            jax.ShapeDtypeStruct((heads, table.shape[0], 128), F32),
            jax.ShapeDtypeStruct(resid.shape, BF16),
            jax.ShapeDtypeStruct(wpart.shape[1:], BF16),
            jax.ShapeDtypeStruct(parts.shape[1:], BF16),
        ),
        in_specs=[smem, smem] + [vm] * 8 + [any_spec()] * 3,
        out_specs=(vm,) * 7,
        scratch_shapes=[
            pltpu.VMEM((heads, 128, STRIP), F32),
            pltpu.VMEM((heads, 2, 128, FARW), F32),
        ]
        + [pltpu.VMEM((heads, rows, width), BF16)] * 4
        + [
            pltpu.VMEM((width, rows), BF16),
            pltpu.VMEM((8, rows), F32),
            pltpu.VMEM((width, rows), F32),
            pltpu.VMEM((heads, 128, STRIP), F32),
            pltpu.VMEM((heads, 2, 128, FARW), F32),
        ]
        + wires_scratch(6 + parts.shape[0])
        + [
            pltpu.SemaphoreType.DMA((4,)),
            pltpu.VMEM((5,) + resid.shape, BF16),
            pltpu.VMEM((5,) + wpart.shape[1:], BF16),
        ]
        + fsdp_scatter_scratch(parts),
        compiler_params=call_params(5),
        name="attend_backward",
    )(starts, table, ids, q, k, v, o, do, lse, resid, ypart, wpart, parts)


def reversed_ids(bucket_ids):
    span = bucket_ids.shape[0]
    ids = jnp.concatenate([bucket_ids[::-1], jnp.full((1,), -1, jnp.int32)])
    return jnp.broadcast_to(ids[None, :], (8, span + 1))


def pack_columns(w, nseq, nfsdp, mine):
    depth, total = w.shape
    block = total // nfsdp
    piece = -(-block // (16 * nseq)) * 16
    w = jnp.pad(w.reshape(depth, nfsdp, block), ((0, 0), (0, 0), (0, nseq * piece - block)))
    w = w.reshape(depth, nfsdp, nseq, piece)
    w = lax.dynamic_index_in_dim(w, mine, 2, keepdims=False)
    return w.reshape(depth, nfsdp * piece)


def unpack_columns(parts, total, nfsdp):
    nseq, depth, width = parts.shape
    piece = width // nfsdp
    block = total // nfsdp
    w = parts.reshape(nseq, depth, nfsdp, piece).transpose(1, 2, 0, 3)
    return w.reshape(depth, nfsdp, nseq * piece)[:, :, :block].reshape(depth, total)


def pack_rows(w, nseq, mine):
    block, depth = w.shape
    piece = -(-block // (16 * nseq)) * 16
    w = jnp.pad(w, ((0, nseq * piece - block), (0, 0)))
    return lax.dynamic_slice_in_dim(w, mine * piece, piece, 0)


def dot32(a, b):
    return jnp.dot(a, b, preferred_element_type=F32)


def dot_tn(a, b):
    return lax.dot_general(a, b, (((0,), (0,)), ((), ())), preferred_element_type=F32)


def gelu_both(u):
    inner = 0.7978845608028654 * (u + 0.044715 * u * u * u)
    t = jnp.tanh(inner)
    value = 0.5 * u * (1.0 + t)
    slope = 0.5 * (1.0 + t) + 0.5 * u * (1.0 - t * t) * 0.7978845608028654 * (1.0 + 3 * 0.044715 * u * u)
    return value, slope


def body(
    tokens,
    out_grad,
    attn_gain,
    w_query,
    w_key,
    w_value,
    w_out,
    mix_gain,
    w_gate,
    w_up,
    w_down,
    rel_table,
    bucket_ids,
    cont_start,
):
    nseq = lax.axis_size("seq")
    nfsdp = lax.axis_size("fsdp")
    mine = lax.axis_index("seq")
    where = lax.axis_index("fsdp")
    rows, width = tokens.shape[1:]
    inner = w_query.shape[1]
    piece = inner // nseq
    heads = piece // HEAD_DIM
    hidden_all = w_gate.shape[1]

    local = [lax.dynamic_slice_in_dim(w, mine * piece, piece, 1) for w in (w_query, w_key, w_value)]
    gains = jnp.pad(jnp.stack([attn_gain, mix_gain], axis=1), ((0, 0), (0, 62)))
    out_cols = width // nseq
    out_local = lax.dynamic_slice_in_dim(w_out, mine * out_cols, out_cols, 1)
    group, first, out_q = tokens_gather(
        tokens[0], jnp.concatenate(local + [gains], axis=1), out_local, nseq, nfsdp
    )
    first = first.reshape(width, -1)
    out_q = out_q.reshape(inner, out_cols)
    query_w, key_w, value_w = (first[:, i * piece : (i + 1) * piece] for i in range(3))
    gain_one = first[:, 3 * piece].astype(F32)
    gain_two = first[:, 3 * piece + 1].astype(F32)
    group = group.astype(F32)
    normed = (group * inverse_rms(group) * gain_one).astype(BF16)
    query = dot32(normed, query_w).astype(BF16)
    keys = dot32(normed, key_w).astype(BF16)
    values = dot32(normed, value_w).astype(BF16)
    table = lax.dynamic_slice_in_dim(rel_table, mine * heads, heads, 1)
    ids = reversed_ids(bucket_ids)
    starts = cont_start[0]
    gate_q = pack_columns(w_gate, nseq, nfsdp, mine)
    up_q = pack_columns(w_up, nseq, nfsdp, mine)
    down_q = pack_rows(w_down, nseq, mine)
    mixed, lse, out_w, cot, gate_w = attn_fwd(
        starts, table, ids, query, keys, values, out_q, out_grad[0], gate_q, nseq, nfsdp
    )
    mixed_rows, resid, normed_two, up_w, down_w = mix(
        mixed, out_w, tokens[0], gain_two[None], up_q, down_q, nfsdp
    )
    gate_w = gate_w.reshape(width, -1)
    up_w = up_w.reshape(width, -1)
    down_w = down_w.reshape(-1, width)
    gate = dot32(normed_two, gate_w)
    upward = dot32(normed_two, up_w)
    active, slope = gelu_both(gate)
    hidden = (active * upward).astype(BF16)
    result = dot32(hidden, down_w).astype(BF16)
    down_grad = dot_tn(hidden, cot).astype(BF16)
    hidden_grad = nt(cot, down_w)
    gate_grad = (hidden_grad * upward * slope).astype(BF16)
    up_grad = (hidden_grad * active).astype(BF16)
    resid_grad, mixed_grad, out_w_grad, gain_two_grad, down_grad = unmix(
        gate_grad,
        up_grad,
        gate_w,
        up_w,
        resid,
        gain_two[None],
        out_grad[0],
        out_w,
        mixed_rows,
        blocks(down_grad, nfsdp),
    )
    gate_w_grad = dot_tn(normed_two, gate_grad).astype(BF16)
    up_w_grad = dot_tn(normed_two, up_grad).astype(BF16)
    dq, dk, dv, tgrad, block_out, out_w_grad, gate_w_grad = attn_bwd(
        starts,
        table,
        ids,
        query,
        keys,
        values,
        mixed,
        mixed_grad,
        lse,
        resid,
        result,
        out_w_grad,
        blocks(gate_w_grad, nfsdp),
    )
    dqkv = jnp.concatenate([dq, dk, dv], axis=1).astype(BF16)
    qkv_grad = dot_tn(normed, dqkv).astype(BF16)
    in_grad, gain_one_grad, up_w_grad, down_grad, gate_w_grad = input_grads(
        dqkv,
        first,
        tokens[0],
        gain_one[None],
        resid_grad,
        blocks(up_w_grad, nfsdp),
        down_grad,
        gate_w_grad,
        nseq,
    )
    buckets = rel_table.shape[0]
    tpad = jnp.pad(tgrad[:, :, 0], ((0, 0), (0, 128 - buckets)))
    qkv_grad, out_w_grad, up_w_grad, small = last_sums(
        blocks(qkv_grad, nfsdp),
        blocks(out_w_grad, nfsdp),
        up_w_grad,
        gain_one_grad,
        gain_two_grad,
        tpad,
        nseq,
    )
    qkv_grad = qkv_grad.reshape(nseq, -1, 3, piece).transpose(1, 2, 0, 3).reshape(-1, 3, inner).astype(F32)
    out_w_grad = out_w_grad.transpose(1, 0, 2).reshape(-1, width)
    gate_w_grad = unpack_columns(gate_w_grad, hidden_all, nfsdp)
    up_w_grad = unpack_columns(up_w_grad, hidden_all, nfsdp)
    down_grad = down_grad.reshape(-1, width)[: w_down.shape[0]]
    lines = width // 128
    share = width // nfsdp
    gain_one_share = lax.dynamic_slice_in_dim(small[:lines].reshape(-1), where * share, share)
    gain_two_share = lax.dynamic_slice_in_dim(small[lines : 2 * lines].reshape(-1), where * share, share)
    tables = small[2 * lines : 2 * lines + 8 * nseq].reshape(nseq, 8, 128)[:, :heads, :buckets]
    table_grad = tables.reshape(nseq * heads, buckets).T
    return (
        block_out[None],
        in_grad[None],
        gain_one_share,
        qkv_grad[:, 0],
        qkv_grad[:, 1],
        qkv_grad[:, 2],
        out_w_grad.astype(F32),
        gain_two_share,
        gate_w_grad.astype(F32),
        up_w_grad.astype(F32),
        down_grad.astype(F32),
        table_grad,
    )


def solution(mesh):
    placed = (
        P("fsdp", "seq", None),
        P("fsdp", "seq", None),
        P("fsdp"),
        P("fsdp", None),
        P("fsdp", None),
        P("fsdp", None),
        P("fsdp", None),
        P("fsdp"),
        P("fsdp", None),
        P("fsdp", None),
        P("fsdp", None),
        P(),
        P(),
        P("fsdp", None),
    )
    results = placed[:1] * 2 + placed[2:11] + (P(),)
    return jax.shard_map(body, mesh=mesh, in_specs=placed, out_specs=results, check_vma=False)
```

```python
import functools
import jax
import jax.numpy as jnp
from jax import lax
from jax.experimental import pallas as pl
from jax.experimental.pallas import tpu as pltpu
from jax.sharding import PartitionSpec as P

HEAD_DIM = 64
PROMPT = 1024
CL = 256
F32 = jnp.float32
BF16 = jnp.bfloat16
MESH = pl.DeviceIdType.MESH
epsilon = 1e-06
STRIP = 2 * PROMPT - 128
FARW = PROMPT - 128 + CL
KC = 256


def nt(a, b):
    return lax.dot_general(a, b, (((1,), (1,)), ((), ())), preferred_element_type=F32)


def nn(a, b):
    return lax.dot_general(a, b, (((1,), (0,)), ((), ())), preferred_element_type=F32)


class Wires:
    def __init__(self, send, recv):
        self.send, self.recv, self.used = send, recv, 0

    def take(self, count):
        self.used += count
        return self.used - count

    def at(self, i, src, dst, where):
        return pltpu.make_async_remote_copy(
            src_ref=src,
            dst_ref=dst,
            send_sem=self.send.at[i],
            recv_sem=self.recv.at[i],
            device_id=where,
            device_id_type=MESH,
        )

    def go(self, src, dst, where):
        c = self.at(self.take(1), src, dst, where)
        c.start()
        return c


def seq_places():
    s = lax.axis_index("seq")
    near = s + 1 - 2 * lax.rem(s, 2)
    far = lax.rem(s + 2, 4)
    cross = lax.rem(near + 2, 4)
    return s, near, far, cross


def meet(places):
    barrier = pltpu.get_barrier_semaphore()
    for where in places:
        pl.semaphore_signal(barrier, inc=1, device_id=where, device_id_type=MESH)
    pl.semaphore_wait(barrier, len(places))


def rows_at(index, rows, offset=0, count=None):
    return pl.ds(pl.multiple_of(index * rows + offset, 16), rows if count is None else count)


class SeqGather:
    def __init__(self, wires, out_at, chunks):
        self.wires, self.out_at, self.chunks = wires, out_at, chunks
        self.s, self.near, self.far, self.cross = seq_places()
        self.base = wires.take(3 * chunks)

    def trip(self, kind, c, src=None):
        view = self.out_at(self.far if kind == 2 else self.s, c)
        where = {"seq": self.far if kind == 0 else self.near}
        return self.wires.at(self.base + 3 * c + kind, view if src is None else src, view, where)

    def send(self, c, src):
        self.trip(0, c, src).start()
        self.trip(1, c, src).start()

    def forward(self, c):
        self.trip(0, c).wait_recv()
        self.trip(2, c).start()

    def got_near(self, c):
        self.trip(1, c).wait_recv()

    def got_cross(self, c):
        self.trip(2, c).wait_recv()

    def drain(self):
        for c in range(self.chunks):
            for kind in range(3):
                self.trip(kind, c).wait_send()

    def finish(self):
        for c in range(self.chunks):
            self.got_near(c)
            self.got_cross(c)
        self.drain()


def fsdp_places():
    f = lax.axis_index("fsdp")
    return f // 2, lax.rem(f, 2), lax.axis_size("fsdp") // 2


def fsdp_peers():
    pair, side, pairs = fsdp_places()
    peers = [{"fsdp": lax.rem(pair + d, pairs) * 2 + side} for d in range(1, pairs)]
    return peers + [{"fsdp": pair * 2 + 1 - side}]


class FsdpGather:
    def __init__(self, wires, shard, full_at, local):
        self.wires, self.shard, self.full_at, self.local = wires, shard, full_at, local
        self.pair, self.side, self.pairs = fsdp_places()
        self.base = wires.take(2 * self.pairs)

    def source(self, d):
        return lax.rem(self.pair + self.pairs - d, self.pairs)

    def out(self, d):
        own = self.full_at(self.pair * 2 + self.side)
        if d == 0:
            return self.wires.at(self.base, self.shard, own, {"fsdp": self.pair * 2 + 1 - self.side})
        where = {"fsdp": lax.rem(self.pair + d, self.pairs) * 2 + self.side}
        return self.wires.at(self.base + d, self.shard, own, where)

    def onward(self, d):
        view = self.full_at(self.source(d) * 2 + self.side)
        return self.wires.at(self.base + self.pairs + d, view, view, {"fsdp": self.pair * 2 + 1 - self.side})

    def keep(self):
        return pltpu.make_async_copy(self.shard, self.full_at(self.pair * 2 + self.side), self.local)

    def start(self):
        self.out(0).start()
        for d in range(1, self.pairs):
            self.out(d).start()
        self.keep().start()

    def forward(self, d):
        self.out(d).wait_recv()
        self.onward(d).start()

    def complete(self, d):
        if d == 0:
            self.keep().wait()
            self.out(0).wait_recv()
        else:
            self.onward(d).wait_recv()

    def drain(self):
        for d in range(self.pairs):
            self.out(d).wait_send()
        for d in range(1, self.pairs):
            self.onward(d).wait_send()

    def finish(self):
        for d in range(self.pairs):
            self.complete(d)
        self.drain()


class FsdpScatter:
    def __init__(self, wires, parts, bufs, local, result):
        self.wires, self.parts, self.local, self.result = wires, parts, local, result
        self.mine, self.got, self.passed, self.landed = bufs
        self.pair, self.side, self.pairs = fsdp_places()
        self.base = wires.take(2 * self.pairs)

    def owner(self, d):
        return lax.rem(self.pair + d, self.pairs) * 2

    def load(self, d):
        return pltpu.make_async_copy(self.parts.at[self.owner(d) + self.side], self.mine.at[d], self.local.at[d])

    def swap(self, d):
        src = self.parts.at[self.owner(d) + 1 - self.side]
        return self.wires.at(self.base + d, src, self.got.at[d], {"fsdp": self.pair * 2 + 1 - self.side})

    def onward(self, d):
        where = {"fsdp": self.owner(d) + self.side}
        return self.wires.at(self.base + self.pairs + d, self.passed.at[d], self.landed.at[d], where)

    def order(self):
        return list(range(1, self.pairs)) + [0]

    def start(self):
        for d in self.order():
            self.swap(d).start()
            self.load(d).start()

    def step(self, d):
        self.load(d).wait()
        self.swap(d).wait_recv()
        self.passed[d] = (self.mine[d].astype(F32) + self.got[d].astype(F32)).astype(BF16)
        self.onward(d).start()

    def finish(self):
        self.load(0).wait()
        self.swap(0).wait_recv()
        total = self.mine[0].astype(F32) + self.got[0].astype(F32)
        for d in range(1, self.pairs):
            self.onward(d).wait_recv()
            total = total + self.landed[d].astype(F32)
        self.result[...] = total.astype(BF16)
        for d in range(self.pairs):
            self.swap(d).wait_send()
        for d in range(1, self.pairs):
            self.onward(d).wait_send()


def fsdp_scatter_scratch(parts):
    shape = (parts.shape[0] // 2,) + parts.shape[1:]
    return [pltpu.VMEM(shape, BF16)] * 4 + [pltpu.SemaphoreType.DMA((shape[0],))]


def blocks(a, count):
    return a.reshape((count, a.shape[0] // count) + a.shape[1:])


def shard_rows(f, size):
    return pl.ds(pl.multiple_of(f * size, 16 if size % 16 == 0 else 8 if size % 8 == 0 else size), size)


def vm_spec():
    return pl.BlockSpec(memory_space=pltpu.VMEM)


def any_spec():
    return pl.BlockSpec(memory_space=pl.ANY)


def wires_scratch(n):
    return [pltpu.SemaphoreType.DMA((n,)), pltpu.SemaphoreType.DMA((n,))]


def call_params(number, vmem=60):
    return pltpu.CompilerParams(collective_id=number, has_side_effects=True, vmem_limit_bytes=vmem << 20)


def inverse_rms(v):
    return lax.rsqrt(jnp.mean(v * v, axis=-1, keepdims=True) + epsilon)


def norm_back(grad, v, r, gain):
    scaled = grad * gain
    return r * scaled - v * (r * r * r) * jnp.mean(v * scaled, axis=-1, keepdims=True)


def middle_kernel(
    o, out_w, tok, gains, up_q, down_q, gate_h, cot_h,
    obuf, resid, n2_h, hid_h, dg_h, du_h, up_h, down_h, parts_h,
    send, recv, local, own, n2, cot, gate_w, up_w, down_w, ga, ub, hid, dg, du, parts,
):
    rows, width = tok.shape
    piece = o.shape[1]
    nseq = obuf.shape[0]
    units = gate_w.shape[1]
    nfsdp = parts.shape[0]
    s, near, far, cross = seq_places()
    loads = [pltpu.make_async_copy(gate_h, gate_w, local.at[0]), pltpu.make_async_copy(cot_h, cot, local.at[1])]
    for a in loads:
        a.start()
    meet([{"seq": near}, {"seq": far}, {"seq": cross}] + fsdp_peers())
    wires = Wires(send, recv)
    trips = [wires.go(o.at[rows_at(t, rows), :], obuf.at[s], {"seq": t}) for t in (far, cross, near)]
    up_size, down_size = up_q.shape[0], down_q.shape[0]
    ups = FsdpGather(wires, up_q, lambda f: up_w.at[shard_rows(f, up_size), :], local.at[2])
    downs = FsdpGather(wires, down_q, lambda f: down_w.at[shard_rows(f, down_size), :], local.at[3])
    ups.start()
    downs.start()
    obuf[s] = o[rows_at(s, rows), :]
    half = rows // 2
    for a in trips:
        a.wait_recv()
    ring = SeqGather(wires, lambda t, c: n2.at[rows_at(t, rows, c * half, half), :], 2)
    cols = out_w.shape[2]
    for c in range(2):
        part = slice(c * half, (c + 1) * half)
        for u in range(nseq):
            acc = tok[part, u * cols : (u + 1) * cols].astype(F32)
            for t in range(nseq):
                acc = acc + nn(obuf[t, part, :], out_w[u, t * piece : (t + 1) * piece, :])
            resid[part, u * cols : (u + 1) * cols] = acc
        h = resid[part, :]
        low = (h * inverse_rms(h) * gains[1:2, :]).astype(BF16)
        own[part, :] = low
        n2[rows_at(s, rows, c * half, half), :] = low
        ring.send(c, own.at[pl.ds(c * half, half), :])
    loads[0].wait()

    def gate_rows(t):
        ga[rows_at(t, rows), :] = nn(n2[rows_at(t, rows), :], gate_w[...])

    def act_rows(t):
        up = nn(n2[rows_at(t, rows), :], up_w[...])
        active, slope = gelu_both(ga[rows_at(t, rows), :])
        hid[rows_at(t, rows), :] = (active * up).astype(BF16)
        ga[rows_at(t, rows), :] = slope * up
        ub[rows_at(t, rows), :] = active

    pairs = ups.pairs
    ups.forward(1)
    gate_rows(s)
    ring.got_near(0)
    ring.got_near(1)
    gate_rows(near)
    for d in range(2, pairs):
        ups.forward(d)
        if d == 2:
            ring.forward(0)
    ring.forward(1)
    downs.forward(1)
    gate_rows(far)
    for c in range(2):
        ring.got_cross(c)
    gate_rows(cross)
    saves = [pltpu.make_async_copy(n2, n2_h, local.at[4])]
    saves[0].start()
    for d in range(pairs):
        ups.complete(d)
    saves.append(pltpu.make_async_copy(up_w, up_h, local.at[5]))
    saves[1].start()
    for t in (s, near):
        act_rows(t)
    downs.forward(2) if pairs > 2 else None
    for t in (far, cross):
        act_rows(t)
    saves.append(pltpu.make_async_copy(hid, hid_h, local.at[6]))
    saves[2].start()
    loads[1].wait()
    width_f = units // nfsdp
    wide = max(256 // width_f, 1)

    def down_part(n):
        got = dot_tn(hid[:, n * wide * width_f : (n + 1) * wide * width_f], cot[...]).astype(BF16)
        for m in range(wide):
            parts[n * wide + m] = got[m * width_f : (m + 1) * width_f, :]

    for n in range(nfsdp // wide):
        down_part(n)
        if n == 1:
            for d in range(3, pairs):
                downs.forward(d)
    saves.append(pltpu.make_async_copy(parts, parts_h, local.at[7]))
    saves[3].start()

    def back_cols(at, units_at):
        for t in range(nseq):
            band = slice(t * rows, (t + 1) * rows)
            dh = nt(cot[band, :], down_w[units_at, :])
            dg[band, at] = (dh * ga[band, at]).astype(BF16)
            du[band, at] = (dh * ub[band, at]).astype(BF16)

    if (2 * width_f) % 128 == 0:
        for d in range(pairs):
            downs.complete(d)
            at = pl.ds(pl.multiple_of(downs.source(d) * 2 * width_f, 2 * width_f), 2 * width_f)
            back_cols(at, at)
    else:
        for d in range(pairs):
            downs.complete(d)
        for n in range(units // 256):
            at = slice(n * 256, (n + 1) * 256)
            back_cols(at, at)
    saves.append(pltpu.make_async_copy(down_w, down_h, local.at[8]))
    saves.append(pltpu.make_async_copy(dg, dg_h, local.at[9]))
    saves.append(pltpu.make_async_copy(du, du_h, local.at[10]))
    for a in saves[4:]:
        a.start()
    ring.drain()
    ups.drain()
    downs.drain()
    for a in trips:
        a.wait_send()
    for a in saves:
        a.wait()


def middle(o, out_w, tok, gains, up_q, down_q, gate_w, cot, nfsdp):
    nseq = out_w.shape[0]
    rows, width = tok.shape
    units = gate_w.shape[1]
    tall = nseq * rows
    return pl.pallas_call(
        middle_kernel,
        out_shape=(
            jax.ShapeDtypeStruct((nseq, rows, o.shape[1]), BF16),
            jax.ShapeDtypeStruct((rows, width), F32),
            jax.ShapeDtypeStruct((tall, width), BF16),
            jax.ShapeDtypeStruct((tall, units), BF16),
            jax.ShapeDtypeStruct((tall, units), BF16),
            jax.ShapeDtypeStruct((tall, units), BF16),
            jax.ShapeDtypeStruct((width, units), BF16),
            jax.ShapeDtypeStruct((units, width), BF16),
            jax.ShapeDtypeStruct((nfsdp, units // nfsdp, width), BF16),
        ),
        in_specs=[vm_spec()] * 4 + [any_spec()] * 4,
        out_specs=(vm_spec(), vm_spec()) + (any_spec(),) * 7,
        scratch_shapes=wires_scratch(9 + 2 * nfsdp)
        + [
            pltpu.SemaphoreType.DMA((11,)),
            pltpu.VMEM((rows, width), BF16),
            pltpu.VMEM((tall, width), BF16),
            pltpu.VMEM((tall, width), BF16),
            pltpu.VMEM((width, units), BF16),
            pltpu.VMEM((width, units), BF16),
            pltpu.VMEM((units, width), BF16),
            pltpu.VMEM((tall, units), F32),
            pltpu.VMEM((tall, units), F32),
            pltpu.VMEM((tall, units), BF16),
            pltpu.VMEM((tall, units), BF16),
            pltpu.VMEM((tall, units), BF16),
            pltpu.VMEM((nfsdp, units // nfsdp, width), BF16),
        ],
        compiler_params=call_params(2, 63),
        name="middle",
    )(o, out_w, tok, gains, up_q, down_q, gate_w, cot)


class SeqScatter:
    def __init__(self, wires, chunks, *bufs):
        self.s, self.near, self.far, self.cross = seq_places()
        self.wires, self.chunks, self.bufs = wires, chunks, bufs
        self.base = wires.take(3 * chunks)

    def trip(self, kind, c):
        where = {"seq": self.far if kind == 1 else self.near}
        src, dst = self.bufs[2 * kind].at[c], self.bufs[2 * kind + 1].at[c]
        return self.wires.at(self.base + 3 * c + kind, src, dst, where)

    def cross_chunk(self, c, value):
        self.bufs[0][c] = value.astype(BF16)
        self.trip(0, c).start()

    def far_chunk(self, c, value):
        self.trip(0, c).wait_recv()
        self.bufs[2][c] = (value + self.bufs[1][c].astype(F32)).astype(BF16)
        self.trip(1, c).start()

    def near_chunk(self, c, value):
        self.bufs[4][c] = value.astype(BF16)
        self.trip(2, c).start()

    def own_chunk(self, c, value):
        self.trip(2, c).wait_recv()
        self.trip(1, c).wait_recv()
        return value + self.bufs[5][c].astype(F32) + self.bufs[3][c].astype(F32)

    def finish(self):
        for c in range(self.chunks):
            for kind in range(3):
                self.trip(kind, c).wait_send()


def scatter_scratch(chunks, rows, width):
    return [pltpu.VMEM((chunks, rows, width), BF16)] * 6


def unmix_kernel(
    chunks, dg, du, gate_w, up_w, resid, gain, cot, out_w, obuf, parts,
    rgrad, dmix, wgrad, ggrad, shard,
    send, recv, b0, b1, b2, b3, b4, b5, attn, dob, p0, p1, p2, p3, local,
):
    rows, width = resid.shape
    nseq, _, piece = obuf.shape
    s, near, far, cross = seq_places()
    meet([{"seq": near}, {"seq": far}, {"seq": cross}] + fsdp_peers())
    wires = Wires(send, recv)
    grads = FsdpScatter(wires, parts, (p0, p1, p2, p3), local, shard)
    grads.start()
    sums = SeqScatter(wires, chunks, b0, b1, b2, b3, b4, b5)
    size = rows // chunks

    def part(t, c):
        at = rows_at(t, rows, c * size, size)
        return nt(dg[at, :], gate_w[...]) + nt(du[at, :], up_w[...])

    for c in range(chunks):
        sums.cross_chunk(c, part(cross, c))
    for c in range(chunks):
        sums.far_chunk(c, part(far, c))
    for c in range(chunks):
        sums.near_chunk(c, part(near, c))
    for c in range(chunks):
        rgrad[c * size : (c + 1) * size, :] = part(s, c)
    total = jnp.zeros((1, width), F32)
    trips = []
    grads.step(1)
    for c in range(chunks):
        at = slice(c * size, (c + 1) * size)
        dn = sums.own_chunk(c, rgrad[at, :])
        h = resid[at, :]
        r = inverse_rms(h)
        total = total + jnp.sum(dn * h * r, axis=0, keepdims=True)
        rg = cot[at, :].astype(F32) + norm_back(dn, h, r, gain[...])
        rgrad[at, :] = rg
        low = rg.astype(BF16)
        attn[at, :] = low
        cols = out_w.shape[2]
        for t in range(nseq):
            acc = jnp.zeros((size, piece), F32)
            for u in range(nseq):
                acc = acc + nt(low[:, u * cols : (u + 1) * cols], out_w[u, t * piece : (t + 1) * piece, :])
            dob[t, at, :] = acc.astype(BF16)
        if c == 0:
            for d in range(2, grads.pairs):
                grads.step(d)
    ggrad[...] = jnp.broadcast_to(total, ggrad.shape)
    for t in (far, cross, near):
        trips.append(wires.go(dob.at[t], dmix.at[rows_at(s, rows), :], {"seq": t}))
    dmix[rows_at(s, rows), :] = dob[s]
    cols = out_w.shape[2]
    for t in range(nseq):
        for u in range(nseq):
            wgrad[u, t * piece : (t + 1) * piece, :] = lax.dot_general(
                obuf[t], attn[:, u * cols : (u + 1) * cols], (((0,), (0,)), ((), ())), preferred_element_type=F32
            ).astype(BF16)
    for a in trips:
        a.wait()
    sums.finish()
    grads.finish()


def unmix(dg, du, gate_w, up_w, resid, gain, cot, out_w, obuf, parts, chunks=2):
    rows, width = resid.shape
    nseq, _, piece = obuf.shape
    return pl.pallas_call(
        functools.partial(unmix_kernel, chunks),
        out_shape=(
            jax.ShapeDtypeStruct((rows, width), F32),
            jax.ShapeDtypeStruct((nseq * rows, piece), BF16),
            jax.ShapeDtypeStruct(out_w.shape, BF16),
            jax.ShapeDtypeStruct((8, width), F32),
            jax.ShapeDtypeStruct(parts.shape[1:], BF16),
        ),
        in_specs=[vm_spec()] * 9 + [any_spec()],
        out_specs=(vm_spec(),) * 5,
        scratch_shapes=wires_scratch(3 * chunks + 3 + parts.shape[0])
        + scatter_scratch(chunks, rows // chunks, width)
        + [pltpu.VMEM((rows, width), BF16), pltpu.VMEM((nseq, rows, piece), BF16)]
        + fsdp_scatter_scratch(parts),
        compiler_params=call_params(4),
        name="unmix",
    )(dg, du, gate_w, up_w, resid, gain, cot, out_w, obuf, parts)


def input_kernel(
    chunks, dqkv, qkv_w, tok, gain, rgrad, parts, done0, done1,
    in_grad, ggrad, shard, full0, full1,
    send, recv, b0, b1, b2, b3, b4, b5, hold, p0, p1, p2, p3, plocal, local,
):
    rows, width = tok.shape
    s, near, far, cross = seq_places()
    meet([{"seq": near}, {"seq": far}] + fsdp_peers())
    wires = Wires(send, recv)
    grads = FsdpScatter(wires, parts, (p0, p1, p2, p3), plocal, shard)
    grads.start()
    sums = SeqScatter(wires, chunks, b0, b1, b2, b3, b4, b5)
    size = rows // chunks
    used = dqkv.shape[1]

    def part(t, c):
        return nt(dqkv[rows_at(t, rows, c * size, size), :], qkv_w[:, :used])

    for c in range(chunks):
        sums.cross_chunk(c, part(cross, c))
    for c in range(chunks):
        sums.far_chunk(c, part(far, c))
    for c in range(chunks):
        sums.near_chunk(c, part(near, c))
    for c in range(chunks):
        hold[c * size : (c + 1) * size, :] = part(s, c)
    total = jnp.zeros((1, width), F32)
    rings = []
    for n, (done, full) in enumerate(((done0, full0), (done1, full1))):
        ring = SeqGather(wires, lambda t, c, full=full: full.at[t], 1)
        ring.send(0, done)
        pltpu.make_async_copy(done, full.at[s], local.at[n]).start()
        rings.append(ring)
    grads.step(1)
    for c in range(chunks):
        at = slice(c * size, (c + 1) * size)
        dn = sums.own_chunk(c, hold[at, :])
        x = tok[at, :].astype(F32)
        r = inverse_rms(x)
        total = total + jnp.sum(dn * x * r, axis=0, keepdims=True)
        in_grad[at, :] = (rgrad[at, :] + norm_back(dn, x, r, gain[...])).astype(BF16)
        if c == 0:
            for d in range(2, grads.pairs):
                grads.step(d)
    ggrad[...] = jnp.broadcast_to(total, ggrad.shape)
    for ring in rings:
        ring.forward(0)
    sums.finish()
    grads.finish()
    for n, (done, full) in enumerate(((done0, full0), (done1, full1))):
        rings[n].finish()
        pltpu.make_async_copy(done, full.at[s], local.at[n]).wait()


def input_grads(dqkv, qkv_w, tok, gain, rgrad, parts, done0, done1, nseq, chunks=2):
    rows, width = tok.shape
    return pl.pallas_call(
        functools.partial(input_kernel, chunks),
        out_shape=(
            jax.ShapeDtypeStruct((rows, width), BF16),
            jax.ShapeDtypeStruct((8, width), F32),
            jax.ShapeDtypeStruct(parts.shape[1:], BF16),
            jax.ShapeDtypeStruct((nseq,) + done0.shape, BF16),
            jax.ShapeDtypeStruct((nseq,) + done1.shape, BF16),
        ),
        in_specs=[vm_spec()] * 5 + [any_spec()] * 3,
        out_specs=(vm_spec(),) * 3 + (any_spec(),) * 2,
        scratch_shapes=wires_scratch(3 * chunks + parts.shape[0] + 6)
        + scatter_scratch(chunks, rows // chunks, width)
        + [pltpu.VMEM((rows, width), F32)]
        + fsdp_scatter_scratch(parts)
        + [pltpu.SemaphoreType.DMA((2,))],
        compiler_params=call_params(6, 48),
        name="input_grads",
    )(dqkv, qkv_w, tok, gain, rgrad, parts, done0, done1)


def last_kernel(
    qkv_p, out_p, done, gain_a, gain_b, table,
    qkv_f, out_f, full, small,
    send, recv, local, qkv_s, out_s, held, stage, one, two, three, *bufs,
):
    s, near, far, cross = seq_places()
    pair, side, pairs = fsdp_places()
    meet([{"seq": near}, {"seq": far}, {"seq": cross}] + fsdp_peers())
    wires = Wires(send, recv)
    scatters = [
        FsdpScatter(wires, qkv_p, bufs[:4], bufs[4], qkv_s),
        FsdpScatter(wires, out_p, bufs[5:9], bufs[9], out_s),
    ]
    for a in scatters:
        a.start()
    ring = SeqGather(wires, lambda t, c: full.at[t], 1)
    ring.send(0, done)
    keep = pltpu.make_async_copy(done, full.at[s], local.at[0])
    keep.start()
    held[...] = jnp.zeros(held.shape, F32)
    lanes = held.shape[1]
    lines = gain_a.shape[1] // lanes
    for n in range(lines):
        held[n : n + 1, :] = gain_a[:1, n * lanes : (n + 1) * lanes]
        held[lines + n : lines + n + 1, :] = gain_b[:1, n * lanes : (n + 1) * lanes]
    heads = table.shape[0]
    held[pl.ds(2 * lines + s * 8, heads), :] = table[...]
    trips = [wires.go(held, one.at[n], {"seq": t}) for n, t in enumerate((near, far, cross))]
    scatters[0].step(1)
    for a in trips:
        a.wait_recv()
    stage[0] = held[...] + one[0] + one[1] + one[2]
    trips.append(wires.go(stage.at[0], two, {"fsdp": pair * 2 + 1 - side}))
    for d in range(2, pairs):
        scatters[0].step(d)
    trips[-1].wait_recv()
    stage[1] = stage[0] + two[...]
    zs = [
        wires.go(stage.at[1], three.at[d - 1], {"fsdp": lax.rem(pair + d, pairs) * 2 + side})
        for d in range(1, pairs)
    ]
    for d in range(1, pairs):
        scatters[1].step(d)
    ring.forward(0)
    scatters[0].finish()
    more = [SeqGather(wires, lambda t, c: qkv_f.at[t], 1), SeqGather(wires, lambda t, c: out_f.at[t], 1)]
    copies = [pltpu.make_async_copy(qkv_s, qkv_f.at[s], local.at[1]), pltpu.make_async_copy(out_s, out_f.at[s], local.at[2])]
    more[0].send(0, qkv_s)
    scatters[1].finish()
    more[1].send(0, out_s)
    total = stage[1]
    for d, a in enumerate(zs):
        a.wait_recv()
        total = total + three[d]
    small[...] = total
    for n in range(2):
        copies[n].start()
        more[n].forward(0)
    for n in range(2):
        more[n].finish()
        copies[n].wait()
    ring.finish()
    keep.wait()
    for a in trips + zs:
        a.wait_send()


def last_sums(qkv_p, out_p, done, gain_a, gain_b, table, nseq):
    nfsdp = qkv_p.shape[0]
    lines = -(-(2 * gain_a.shape[1] // 128 + 8 * nseq) // 8) * 8
    return pl.pallas_call(
        last_kernel,
        out_shape=(
            jax.ShapeDtypeStruct((nseq,) + qkv_p.shape[1:], BF16),
            jax.ShapeDtypeStruct((nseq,) + out_p.shape[1:], BF16),
            jax.ShapeDtypeStruct((nseq,) + done.shape, BF16),
            jax.ShapeDtypeStruct((lines, 128), F32),
        ),
        in_specs=[any_spec()] * 3 + [vm_spec()] * 3,
        out_specs=(any_spec(),) * 3 + (vm_spec(),),
        scratch_shapes=wires_scratch(2 * nfsdp + 9 + 4 + nfsdp // 2)
        + [
            pltpu.SemaphoreType.DMA((3,)),
            pltpu.VMEM(qkv_p.shape[1:], BF16),
            pltpu.VMEM(out_p.shape[1:], BF16),
            pltpu.VMEM((lines, 128), F32),
            pltpu.VMEM((2, lines, 128), F32),
            pltpu.VMEM((3, lines, 128), F32),
            pltpu.VMEM((lines, 128), F32),
            pltpu.VMEM((nfsdp // 2 - 1, lines, 128), F32),
        ]
        + fsdp_scatter_scratch(qkv_p)
        + fsdp_scatter_scratch(out_p),
        compiler_params=call_params(7, 32),
        name="last_sums",
    )(qkv_p, out_p, done, gain_a, gain_b, table)


def build_strips(heads, starts, table, ids, strip, far):
    length = ids.shape[1]
    half = 2 * PROMPT
    for h in range(heads):
        row = jnp.zeros(ids.shape, F32)
        for b in range(table.shape[0]):
            row = jnp.where(ids[...] == b, table[b, h], row)
        base = jnp.broadcast_to(row[:1, PROMPT // 2 : PROMPT // 2 + half], (128, half))
        strip[h] = pltpu.roll(base, 1, 1, stride=1, stride_axis=0)[:, 128:]
        for c in range(2):
            moved = pltpu.roll(row, length - PROMPT // 2 - starts[c], 1)
            base = jnp.broadcast_to(moved[:1, : FARW + 128], (128, FARW + 128))
            far[h, c] = pltpu.roll(base, 1, 1, stride=1, stride_axis=0)[:, 128:]


def head_masks(width, heads):
    lane = lax.broadcasted_iota(jnp.int32, (1, width), 1)
    return [(lane >= h * HEAD_DIM) & (lane < (h + 1) * HEAD_DIM) for h in range(heads)]


def masked_copies(src, dst, heads):
    masks = head_masks(src.shape[1], heads)
    for h in range(heads):
        dst[h] = jnp.where(masks[h], src[...], jnp.zeros((), src.dtype))


def bias_chunk(strip, far, h, first_q, kstart, kind, c):
    parts = []
    for r in range(KC // 128):
        m = PROMPT - 128 - (kstart + 128 * r)
        if kind == "far":
            parts.append(far[h, c, :, m : m + CL])
        else:
            parts.append(strip[h, :, pl.ds(pl.multiple_of(first_q + m, 128), CL)])
    return jnp.concatenate(parts, axis=0)


def pack_piece(units, nfsdp, nseq):
    block = units // nfsdp
    return block, -(-block // (16 * nseq)) * 16


def pack_front(t, raw, first_q, out_q, gains):
    r_q, r_k, r_v, r_o = raw
    piece = first_q.shape[1] * 3 // 10
    depth = first_q.shape[0]
    cut = slice(t * piece, (t + 1) * piece)
    first_q[...] = jnp.concatenate(
        [r_q[:, cut], r_k[:, cut], r_v[:, cut], gains, jnp.zeros((depth, first_q.shape[1] - 3 * piece - 8), BF16)], axis=1
    )
    cols = out_q.shape[1]
    out_q[...] = r_o[:, t * cols : (t + 1) * cols]


def pack_cols(t, nseq, nfsdp, raw, packed):
    block, piece = pack_piece(raw.shape[1], nfsdp, nseq)
    pieces = []
    for f in range(nfsdp):
        begin = f * block + t * piece
        end = min(begin + piece, (f + 1) * block)
        pieces.append(raw[:, begin:end])
        if end - begin < piece:
            pieces.append(jnp.zeros((raw.shape[0], piece - end + begin), BF16))
    packed[...] = jnp.concatenate(pieces, axis=1)


def pack_down(t, raw, packed):
    piece = packed.shape[0]
    begin = t * piece
    end = min(begin + piece, raw.shape[0])
    packed[: end - begin, :] = raw[begin:end, :]
    if end - begin < piece:
        packed[end - begin :, :] = jnp.zeros((piece - end + begin, raw.shape[1]), BF16)


def front_kernel(
    heads, nseq, starts, table, ids, gain_a, gain_b, tok, w_q, w_k, w_v, w_o, w_g, w_u, w_d, cot,
    q, k, v, o, lse, gains, n1_h, first_h, out_w, cots, gate_w, up_q, down_q,
    send, recv, local, r_q, r_k, r_v, r_o, r_g, r_u, r_d, first_q, out_q, gate_q, up_s, down_s,
    group, n1, first, strip, far, kh, vt, ot, s,
):
    rows, width = tok.shape
    mine, near, other, cross = seq_places()
    pair, side, pairs = fsdp_places()
    nfsdp = 2 * pairs
    loads = [
        pltpu.make_async_copy(src, dst, local.at[n])
        for n, (src, dst) in enumerate(
            ((w_q, r_q), (w_k, r_k), (w_v, r_v), (w_o, r_o), (w_g, r_g), (w_u, r_u), (w_d, r_d))
        )
    ]
    for a in loads:
        a.start()
    meet([{"seq": near}, {"seq": other}] + fsdp_peers())
    wires = Wires(send, recv)
    half = rows // 2
    ring = SeqGather(wires, lambda t, c: group.at[rows_at(t, rows, c * half, half), :], 2)
    size = first_q.shape[0]
    lead = FsdpGather(wires, first_q, lambda f: first.at[shard_rows(f, size), :], local.at[7])
    late = FsdpGather(wires, out_q, lambda f: out_w.at[mine, f], local.at[8])
    gate_size = gate_q.shape[0]
    weight = FsdpGather(wires, gate_q, lambda f: gate_w.at[shard_rows(f, gate_size), :], local.at[9])
    wring = SeqGather(wires, lambda t, c: out_w.at[t], 1)
    cring = SeqGather(wires, lambda t, c: cots.at[rows_at(t, rows, c * half, half), :], 2)
    own = [
        pltpu.make_async_copy(tok, group.at[rows_at(mine, rows), :], local.at[10]),
        pltpu.make_async_copy(cot, cots.at[rows_at(mine, rows), :], local.at[11]),
    ]
    for c in range(2):
        ring.send(c, tok.at[pl.ds(c * half, half), :])
    for a in own:
        a.start()
    for a in loads[:4]:
        a.wait()
    both = jnp.concatenate([gain_a[...], gain_b[...], jnp.zeros((6, gain_a.shape[1]), BF16)], axis=0)
    both = both.astype(F32).T.astype(BF16)
    for t in range(nseq):

        @pl.when(mine == t)
        def _():
            pack_front(t, (r_q, r_k, r_v, r_o), first_q, out_q, both)

    for a in loads[4:]:
        a.wait()
    lead.start()
    for t in range(nseq):

        @pl.when(mine == t)
        def _():
            pack_cols(t, nseq, nfsdp, r_g, gate_q)

    late.start()
    for t in range(nseq):

        @pl.when(mine == t)
        def _():
            pack_cols(t, nseq, nfsdp, r_u, up_s)
            pack_down(t, r_d, down_s)

    weight.start()
    for c in range(2):
        cring.send(c, cot.at[pl.ds(c * half, half), :])
    saves = [pltpu.make_async_copy(up_s, up_q, local.at[12]), pltpu.make_async_copy(down_s, down_q, local.at[13])]
    for a in saves:
        a.start()
    build_strips(heads, starts, table, ids, strip, far)
    lse[...] = jnp.zeros(lse.shape, F32)
    for d in range(1, pairs):
        lead.forward(d)
        if d == pairs // 2:
            ring.forward(0)
    for d in range(1, pairs):
        late.forward(d)
    ring.forward(1)
    lead.finish()
    saves.append(pltpu.make_async_copy(first, first_h, local.at[14]))
    saves[2].start()
    piece = q.shape[1]
    column = 3 * piece
    gains[...] = jnp.zeros(gains.shape, F32)
    for b in range(width // 256):
        band = first[b * 256 : (b + 1) * 256, column // 128 * 128 : column // 128 * 128 + 128].astype(F32).T
        for n in range(2):
            line = column % 128 + n
            gains[n : n + 1, b * 256 : (b + 1) * 256] = band[line : line + 1, :]

    def project(t):
        at = rows_at(t, rows)
        x = group[at, :].astype(F32)
        low = (x * inverse_rms(x) * gains[0:1, :]).astype(BF16)
        n1[at, :] = low
        r = nn(low, first[:, :column])
        q[at, :] = r[:, :piece].astype(BF16)
        k[at, :] = r[:, piece : 2 * piece].astype(BF16)
        v[at, :] = r[:, 2 * piece :].astype(BF16)

    own[0].wait()
    project(mine)
    for c in range(2):
        ring.got_near(c)
    project(near)
    project(other)
    for c in range(2):
        ring.got_cross(c)
    project(cross)
    saves.append(pltpu.make_async_copy(n1, n1_h, local.at[15]))
    saves[3].start()
    for d in range(pairs):
        late.complete(d)
    wring.send(0, out_w.at[mine])
    masked_copies(k, kh, heads)
    vt[...] = v[...].astype(F32).T.astype(BF16)

    def block(h, q0, bias_q0, chunks, c):
        qb = q[pl.ds(q0, CL), :]
        top = None
        for n, (k0, kind, kstart) in enumerate(chunks):
            sc = nt(kh[h, pl.ds(k0, KC), :], qb) + bias_chunk(strip, far, h, bias_q0, kstart, kind, c)
            s[n * KC : (n + 1) * KC, :] = sc
            m = jnp.max(sc, axis=0, keepdims=True)
            top = m if top is None else jnp.maximum(top, m)
        total = jnp.zeros((1, CL), F32)
        acc = jnp.zeros((HEAD_DIM, CL), F32)
        for n, (k0, kind, kstart) in enumerate(chunks):
            e = jnp.exp(s[n * KC : (n + 1) * KC, :] - top)
            total = total + jnp.sum(e, axis=0, keepdims=True)
            acc = acc + nn(vt[pl.ds(pl.multiple_of(h * HEAD_DIM, HEAD_DIM), HEAD_DIM), pl.ds(k0, KC)], e.astype(BF16))
        ot[pl.ds(pl.multiple_of(h * HEAD_DIM, HEAD_DIM), HEAD_DIM), pl.ds(q0, CL)] = acc / total
        lse[pl.ds(h, 1), pl.ds(q0, CL)] = top + jnp.log(total)

    nblk = PROMPT // CL

    def prompt_body(i, carry):
        h, blk = i // nblk, i % nblk
        q0 = pl.multiple_of(blk * CL, CL)
        block(h, q0, q0, [(j * KC, "strip", j * KC) for j in range(PROMPT // KC)], None)
        for d in range(1, pairs - 1):

            @pl.when(i == heads * nblk * d // pairs)
            def _():
                weight.forward(d)

        return carry

    lax.fori_loop(0, heads * nblk, prompt_body, 0)

    def cont_body(i, carry):
        h, c = i // 2, i % 2
        q0 = pl.multiple_of(PROMPT + c * CL, CL)
        chunks = [(j * KC, "far", j * KC) for j in range(PROMPT // KC)]
        chunks += [(q0 + j * KC, "strip", j * KC) for j in range(CL // KC)]
        block(h, q0, 0, chunks, c)
        return carry

    cring.forward(0)
    lax.fori_loop(0, heads * 2, cont_body, 0)
    o[...] = ot[...].T.astype(BF16)
    weight.forward(pairs - 1)
    cring.forward(1)
    wring.forward(0)
    for a in own[1:] + saves:
        a.wait()
    weight.finish()
    late.drain()
    wring.finish()
    cring.finish()
    ring.drain()


def front(starts, table, ids, gain_a, gain_b, tok, w_q, w_k, w_v, w_o, w_g, w_u, w_d, cot, nseq, nfsdp):
    rows, width = tok.shape
    inner = w_q.shape[1]
    piece = inner // nseq
    heads = piece // HEAD_DIM
    tall = nseq * rows
    size = w_q.shape[0]
    units = pack_piece(w_g.shape[1], nfsdp, nseq)[1]
    cols = width // nseq
    lead = piece * 10 // 3
    smem = pl.BlockSpec(memory_space=pltpu.SMEM)
    return pl.pallas_call(
        functools.partial(front_kernel, heads, nseq),
        out_shape=(
            jax.ShapeDtypeStruct((tall, piece), BF16),
            jax.ShapeDtypeStruct((tall, piece), BF16),
            jax.ShapeDtypeStruct((tall, piece), BF16),
            jax.ShapeDtypeStruct((tall, piece), BF16),
            jax.ShapeDtypeStruct((8, tall), F32),
            jax.ShapeDtypeStruct((8, width), F32),
            jax.ShapeDtypeStruct((tall, width), BF16),
            jax.ShapeDtypeStruct((width, lead), BF16),
            jax.ShapeDtypeStruct((nseq, nfsdp, w_o.shape[0], cols), BF16),
            jax.ShapeDtypeStruct((tall, width), BF16),
            jax.ShapeDtypeStruct((width, nfsdp * units), BF16),
            jax.ShapeDtypeStruct((size, nfsdp * units), BF16),
            jax.ShapeDtypeStruct((nseq * units // nseq, width), BF16),
        ),
        in_specs=[smem, smem, vm_spec(), vm_spec(), vm_spec()] + [any_spec()] * 9,
        out_specs=(vm_spec(),) * 6 + (any_spec(),) * 7,
        scratch_shapes=wires_scratch(15 + 3 * nfsdp)
        + [
            pltpu.SemaphoreType.DMA((16,)),
            pltpu.VMEM(w_q.shape, BF16),
            pltpu.VMEM(w_k.shape, BF16),
            pltpu.VMEM(w_v.shape, BF16),
            pltpu.VMEM(w_o.shape, BF16),
            pltpu.VMEM(w_g.shape, BF16),
            pltpu.VMEM(w_u.shape, BF16),
            pltpu.VMEM(w_d.shape, BF16),
            pltpu.VMEM((size, lead), BF16),
            pltpu.VMEM((w_o.shape[0], cols), BF16),
            pltpu.VMEM((size, nfsdp * units), BF16),
            pltpu.VMEM((size, nfsdp * units), BF16),
            pltpu.VMEM((units, width), BF16),
            pltpu.VMEM((tall, width), BF16),
            pltpu.VMEM((tall, width), BF16),
            pltpu.VMEM((width, lead), BF16),
            pltpu.VMEM((heads, 128, STRIP), F32),
            pltpu.VMEM((heads, 2, 128, FARW), F32),
            pltpu.VMEM((heads, tall, piece), BF16),
            pltpu.VMEM((piece, tall), BF16),
            pltpu.VMEM((piece, tall), F32),
            pltpu.VMEM((PROMPT + CL, CL), F32),
        ],
        compiler_params=call_params(1, 60),
        name="front",
    )(starts, table, ids, gain_a, gain_b, tok, w_q, w_k, w_v, w_o, w_g, w_u, w_d, cot)


def attn_bwd_kernel(
    heads, starts, table, ids, q, k, v, o, do, lse, resid, ypart, wpart, parts,
    dq, dk, dv, tgrad, y, wsum, shard,
    strip, far, kh, vh, qh, doh, kt, delta, dqt, gstrip, gfar,
    send, recv, local, ybuf, wbuf, p0, p1, p2, p3, plocal,
):
    rows = resid.shape[0]
    mine, near, other, cross = seq_places()
    meet([{"seq": near}, {"seq": other}] + fsdp_peers())
    wires = Wires(send, recv)
    grads = FsdpScatter(wires, parts, (p0, p1, p2, p3), plocal, shard)
    grads.start()

    def block_of(part, t):
        return part.at[rows_at(t, rows), :] if part is ypart else part.at[t]

    pairs = ((wpart, wbuf), (ypart, ybuf))
    hops = [wires.go(block_of(part, cross), buf.at[0], {"seq": near}) for part, buf in pairs]
    turns = [wires.go(block_of(part, near), buf.at[1], {"seq": near}) for part, buf in pairs]
    loads = []
    for n, (part, buf) in enumerate(pairs):
        loads.append(pltpu.make_async_copy(block_of(part, other), buf.at[2], local.at[2 * n]))
        loads.append(pltpu.make_async_copy(block_of(part, mine), buf.at[3], local.at[2 * n + 1]))
    for a in loads:
        a.start()
    build_strips(heads, starts, table, ids, strip, far)
    for src, dst in ((k, kh), (v, vh), (q, qh), (do, doh)):
        masked_copies(src, dst, heads)
    kt[...] = k[...].astype(F32).T.astype(BF16)
    far_hops = []
    for n, (part, buf) in enumerate(pairs):
        loads[2 * n].wait()
        hops[n].wait_recv()
        buf[2] = (buf[2].astype(F32) + buf[0].astype(F32)).astype(BF16)
    for part, buf in pairs:
        far_hops.append(wires.go(buf.at[2], buf.at[4], {"seq": other}))
    prod = (o[...].astype(F32) * do[...].astype(F32)).T
    for h in range(heads):
        delta[h : h + 1, :] = jnp.sum(prod[h * HEAD_DIM : (h + 1) * HEAD_DIM, :], axis=0, keepdims=True)
    dk[...] = jnp.zeros(dk.shape, F32)
    dv[...] = jnp.zeros(dv.shape, F32)
    gstrip[...] = jnp.zeros(gstrip.shape, F32)
    gfar[...] = jnp.zeros(gfar.shape, F32)

    def block(h, q0, bias_q0, chunks, c):
        qb = q[pl.ds(q0, CL), :]
        dob = do[pl.ds(q0, CL), :]
        qhb = qh[h, pl.ds(q0, CL), :]
        dohb = doh[h, pl.ds(q0, CL), :]
        lrow = lse[pl.ds(h, 1), pl.ds(q0, CL)]
        drow = delta[pl.ds(h, 1), pl.ds(q0, CL)]
        acc = jnp.zeros((HEAD_DIM, CL), F32)
        for n, (k0, kind, kstart) in enumerate(chunks):
            ks = pl.ds(k0, KC)
            sc = nt(kh[h, ks, :], qb) + bias_chunk(strip, far, h, bias_q0, kstart, kind, c)
            pr = jnp.exp(sc - lrow)
            dp = nt(vh[h, ks, :], dob)
            ds = pr * (dp - drow)
            pl_ = pr.astype(BF16)
            dsl = ds.astype(BF16)
            dv[ks, :] += nn(pl_, dohb)
            dk[ks, :] += nn(dsl, qhb)
            acc = acc + nn(kt[pl.ds(pl.multiple_of(h * HEAD_DIM, HEAD_DIM), HEAD_DIM), ks], dsl)
            for r in range(KC // 128):
                m = PROMPT - 128 - (kstart + 128 * r)
                piece = ds[128 * r : 128 * (r + 1), :]
                if kind == "far":
                    gfar[h, c, :, m : m + CL] += piece
                else:
                    gstrip[h, :, pl.ds(pl.multiple_of(bias_q0 + m, 128), CL)] += piece
        dqt[pl.ds(pl.multiple_of(h * HEAD_DIM, HEAD_DIM), HEAD_DIM), pl.ds(q0, CL)] = acc

    nblk = PROMPT // CL

    def prompt_body(i, carry):
        h, blk = i // nblk, i % nblk
        q0 = pl.multiple_of(blk * CL, CL)
        block(h, q0, q0, [(j * KC, "strip", j * KC) for j in range(PROMPT // KC)], None)

        @pl.when(i == 3)
        def _():
            grads.step(1)

        return carry

    lax.fori_loop(0, heads * nblk, prompt_body, 0)

    for d in range(2, grads.pairs - 1):
        grads.step(d)

    def cont_body(i, carry):
        h, c = i // 2, i % 2
        q0 = pl.multiple_of(PROMPT + c * CL, CL)
        chunks = [(j * KC, "far", j * KC) for j in range(PROMPT // KC)]
        chunks += [(q0 + j * KC, "strip", j * KC) for j in range(CL // KC)]
        block(h, q0, 0, chunks, c)
        return carry

    lax.fori_loop(0, heads * 2, cont_body, 0)
    if grads.pairs > 2:
        grads.step(grads.pairs - 1)
    dq[...] = dqt[...].T

    length = ids.shape[1]
    half = 2 * PROMPT
    lane8 = lax.broadcasted_iota(jnp.int32, (table.shape[0], length), 0)
    hot = ids[:1, :] == lane8
    for h in range(heads):
        def unskew(g, width):
            full = jnp.concatenate([jnp.zeros((128, 128), F32), g], axis=1)
            eight = full[:8]
            for a in range(1, 16):
                eight = eight + pltpu.roll(full[8 * a : 8 * a + 8], width - 8 * a, 1)
            vec = pltpu.roll(eight, width - 1, 1)[:1]
            for b in range(1, 8):
                vec = vec + pltpu.roll(eight, width - 1 - b, 1)[b : b + 1]
            return jnp.concatenate([vec, jnp.zeros((1, length - width), F32)], axis=1)

        total = jnp.broadcast_to(unskew(gstrip[h], half), (8, length))
        total = pltpu.roll(total, PROMPT // 2, 1)
        for c in range(2):
            piece = jnp.broadcast_to(unskew(gfar[h, c], FARW + 128), (8, length))
            total = total + pltpu.roll(piece, PROMPT // 2 + starts[c], 1)
        picked = jnp.where(hot, total[:1, :], 0.0)
        tgrad[h] = jnp.broadcast_to(jnp.sum(picked, axis=1, keepdims=True), tgrad.shape[1:])
    sums = []
    for n, (part, buf) in enumerate(pairs):
        loads[2 * n + 1].wait()
        turns[n].wait_recv()
        far_hops[n].wait_recv()
        sums.append(buf[3].astype(F32) + buf[1].astype(F32) + buf[4].astype(F32))
    wsum[...] = sums[0].astype(BF16)
    y[...] = (resid[...] + sums[1]).astype(BF16)
    for a in hops + turns + far_hops:
        a.wait_send()
    grads.finish()


def attn_bwd(starts, table, ids, q, k, v, o, do, lse, resid, ypart, wpart, parts):
    rows, width = q.shape
    heads = width // HEAD_DIM
    smem = pl.BlockSpec(memory_space=pltpu.SMEM)
    vm = pl.BlockSpec(memory_space=pltpu.VMEM)
    wide = jax.ShapeDtypeStruct((rows, width), F32)
    return pl.pallas_call(
        functools.partial(attn_bwd_kernel, heads),
        out_shape=(
            wide,
            wide,
            wide,
            jax.ShapeDtypeStruct((heads, table.shape[0], 128), F32),
            jax.ShapeDtypeStruct(resid.shape, BF16),
            jax.ShapeDtypeStruct(wpart.shape[1:], BF16),
            jax.ShapeDtypeStruct(parts.shape[1:], BF16),
        ),
        in_specs=[smem, smem] + [vm] * 8 + [any_spec()] * 3,
        out_specs=(vm,) * 7,
        scratch_shapes=[
            pltpu.VMEM((heads, 128, STRIP), F32),
            pltpu.VMEM((heads, 2, 128, FARW), F32),
        ]
        + [pltpu.VMEM((heads, rows, width), BF16)] * 4
        + [
            pltpu.VMEM((width, rows), BF16),
            pltpu.VMEM((8, rows), F32),
            pltpu.VMEM((width, rows), F32),
            pltpu.VMEM((heads, 128, STRIP), F32),
            pltpu.VMEM((heads, 2, 128, FARW), F32),
        ]
        + wires_scratch(6 + parts.shape[0])
        + [
            pltpu.SemaphoreType.DMA((4,)),
            pltpu.VMEM((5,) + resid.shape, BF16),
            pltpu.VMEM((5,) + wpart.shape[1:], BF16),
        ]
        + fsdp_scatter_scratch(parts),
        compiler_params=call_params(5),
        name="attend_backward",
    )(starts, table, ids, q, k, v, o, do, lse, resid, ypart, wpart, parts)


def reversed_ids(bucket_ids):
    span = bucket_ids.shape[0]
    ids = jnp.concatenate([bucket_ids[::-1], jnp.full((1,), -1, jnp.int32)])
    return jnp.broadcast_to(ids[None, :], (8, span + 1))


def unpack_columns(parts, total, nfsdp):
    nseq, depth, width = parts.shape
    piece = width // nfsdp
    block = total // nfsdp
    w = parts.reshape(nseq, depth, nfsdp, piece).transpose(1, 2, 0, 3)
    return w.reshape(depth, nfsdp, nseq * piece)[:, :, :block].reshape(depth, total)


def dot32(a, b):
    return jnp.dot(a, b, preferred_element_type=F32)


def dot_tn(a, b):
    return lax.dot_general(a, b, (((0,), (0,)), ((), ())), preferred_element_type=F32)


def gelu_both(u):
    inner = 0.7978845608028654 * (u + 0.044715 * u * u * u)
    t = jnp.tanh(inner)
    value = 0.5 * u * (1.0 + t)
    slope = 0.5 * (1.0 + t) + 0.5 * u * (1.0 - t * t) * 0.7978845608028654 * (1.0 + 3 * 0.044715 * u * u)
    return value, slope


def body(
    tokens,
    out_grad,
    attn_gain,
    w_query,
    w_key,
    w_value,
    w_out,
    mix_gain,
    w_gate,
    w_up,
    w_down,
    rel_table,
    bucket_ids,
    cont_start,
):
    nseq = lax.axis_size("seq")
    nfsdp = lax.axis_size("fsdp")
    mine = lax.axis_index("seq")
    where = lax.axis_index("fsdp")
    rows, width = tokens.shape[1:]
    inner = w_query.shape[1]
    piece = inner // nseq
    heads = piece // HEAD_DIM
    hidden_all = w_gate.shape[1]

    table = lax.dynamic_slice_in_dim(rel_table, mine * heads, heads, 1)
    ids = reversed_ids(bucket_ids)
    starts = cont_start[0]
    query, keys, values, mixed, lse, gains, normed, first, out_w, cot, gate_w, up_q, down_q = front(
        starts,
        table,
        ids,
        attn_gain[None],
        mix_gain[None],
        tokens[0],
        w_query,
        w_key,
        w_value,
        w_out,
        w_gate,
        w_up,
        w_down,
        out_grad[0],
        nseq,
        nfsdp,
    )
    out_w = out_w.reshape(nseq, inner, -1)
    mixed_rows, resid, normed_two, hidden, gate_grad, up_grad, up_w, down_w, down_grad = middle(
        mixed, out_w, tokens[0], gains, up_q, down_q, gate_w, cot, nfsdp
    )
    gain_one, gain_two = gains[0], gains[1]
    result = dot32(hidden, down_w).astype(BF16)
    resid_grad, mixed_grad, out_w_grad, gain_two_grad, down_grad = unmix(
        gate_grad,
        up_grad,
        gate_w,
        up_w,
        resid,
        gain_two[None],
        out_grad[0],
        out_w,
        mixed_rows,
        down_grad,
    )
    gate_w_grad = dot_tn(normed_two, gate_grad).astype(BF16)
    up_w_grad = dot_tn(normed_two, up_grad).astype(BF16)
    dq, dk, dv, tgrad, block_out, out_w_grad, gate_w_grad = attn_bwd(
        starts,
        table,
        ids,
        query,
        keys,
        values,
        mixed,
        mixed_grad,
        lse,
        resid,
        result,
        out_w_grad,
        blocks(gate_w_grad, nfsdp),
    )
    dqkv = jnp.concatenate([dq, dk, dv], axis=1).astype(BF16)
    qkv_grad = dot_tn(normed, dqkv).astype(BF16)
    in_grad, gain_one_grad, up_w_grad, down_grad, gate_w_grad = input_grads(
        dqkv,
        first,
        tokens[0],
        gain_one[None],
        resid_grad,
        blocks(up_w_grad, nfsdp),
        down_grad,
        gate_w_grad,
        nseq,
    )
    buckets = rel_table.shape[0]
    tpad = jnp.pad(tgrad[:, :, 0], ((0, 0), (0, 128 - buckets)))
    qkv_grad, out_w_grad, up_w_grad, small = last_sums(
        blocks(qkv_grad, nfsdp),
        blocks(out_w_grad, nfsdp),
        up_w_grad,
        gain_one_grad,
        gain_two_grad,
        tpad,
        nseq,
    )
    qkv_grad = qkv_grad.reshape(nseq, -1, 3, piece).transpose(1, 2, 0, 3).reshape(-1, 3, inner).astype(F32)
    out_w_grad = out_w_grad.transpose(1, 0, 2).reshape(-1, width)
    gate_w_grad = unpack_columns(gate_w_grad, hidden_all, nfsdp)
    up_w_grad = unpack_columns(up_w_grad, hidden_all, nfsdp)
    down_grad = down_grad.reshape(-1, width)[: w_down.shape[0]]
    lines = width // 128
    share = width // nfsdp
    gain_one_share = lax.dynamic_slice_in_dim(small[:lines].reshape(-1), where * share, share)
    gain_two_share = lax.dynamic_slice_in_dim(small[lines : 2 * lines].reshape(-1), where * share, share)
    tables = small[2 * lines : 2 * lines + 8 * nseq].reshape(nseq, 8, 128)[:, :heads, :buckets]
    table_grad = tables.reshape(nseq * heads, buckets).T
    return (
        block_out[None],
        in_grad[None],
        gain_one_share,
        qkv_grad[:, 0],
        qkv_grad[:, 1],
        qkv_grad[:, 2],
        out_w_grad.astype(F32),
        gain_two_share,
        gate_w_grad.astype(F32),
        up_w_grad.astype(F32),
        down_grad.astype(F32),
        table_grad,
    )


def solution(mesh):
    placed = (
        P("fsdp", "seq", None),
        P("fsdp", "seq", None),
        P("fsdp"),
        P("fsdp", None),
        P("fsdp", None),
        P("fsdp", None),
        P("fsdp", None),
        P("fsdp"),
        P("fsdp", None),
        P("fsdp", None),
        P("fsdp", None),
        P(),
        P(),
        P("fsdp", None),
    )
    results = placed[:1] * 2 + placed[2:11] + (P(),)
    return jax.shard_map(body, mesh=mesh, in_specs=placed, out_specs=results, check_vma=False)
```

```python
import functools
import jax
import jax.numpy as jnp
from jax import lax
from jax.experimental import pallas as pl
from jax.experimental.pallas import tpu as pltpu
from jax.sharding import PartitionSpec as P

HEAD_DIM = 64
PROMPT = 1024
CL = 256
F32 = jnp.float32
BF16 = jnp.bfloat16
MESH = pl.DeviceIdType.MESH
epsilon = 1e-06
STRIP = 2 * PROMPT - 128
FARW = PROMPT - 128 + CL
KC = 256


def nt(a, b):
    return lax.dot_general(a, b, (((1,), (1,)), ((), ())), preferred_element_type=F32)


def nn(a, b):
    return lax.dot_general(a, b, (((1,), (0,)), ((), ())), preferred_element_type=F32)


class Wires:
    def __init__(self, send, recv):
        self.send, self.recv, self.used = send, recv, 0

    def take(self, count):
        self.used += count
        return self.used - count

    def at(self, i, src, dst, where):
        return pltpu.make_async_remote_copy(
            src_ref=src,
            dst_ref=dst,
            send_sem=self.send.at[i],
            recv_sem=self.recv.at[i],
            device_id=where,
            device_id_type=MESH,
        )

    def go(self, src, dst, where):
        c = self.at(self.take(1), src, dst, where)
        c.start()
        return c


def seq_places():
    s = lax.axis_index("seq")
    near = s + 1 - 2 * lax.rem(s, 2)
    far = lax.rem(s + 2, 4)
    cross = lax.rem(near + 2, 4)
    return s, near, far, cross


def meet(places):
    barrier = pltpu.get_barrier_semaphore()
    for where in places:
        pl.semaphore_signal(barrier, inc=1, device_id=where, device_id_type=MESH)
    pl.semaphore_wait(barrier, len(places))


def rows_at(index, rows, offset=0, count=None):
    return pl.ds(pl.multiple_of(index * rows + offset, 16), rows if count is None else count)


class SeqGather:
    def __init__(self, wires, out_at, chunks):
        self.wires, self.out_at, self.chunks = wires, out_at, chunks
        self.s, self.near, self.far, self.cross = seq_places()
        self.base = wires.take(3 * chunks)

    def trip(self, kind, c, src=None):
        view = self.out_at(self.far if kind == 2 else self.s, c)
        where = {"seq": self.far if kind == 0 else self.near}
        return self.wires.at(self.base + 3 * c + kind, view if src is None else src, view, where)

    def send(self, c, src):
        self.trip(0, c, src).start()
        self.trip(1, c, src).start()

    def forward(self, c):
        self.trip(0, c).wait_recv()
        self.trip(2, c).start()

    def got_near(self, c):
        self.trip(1, c).wait_recv()

    def got_cross(self, c):
        self.trip(2, c).wait_recv()

    def drain(self):
        for c in range(self.chunks):
            for kind in range(3):
                self.trip(kind, c).wait_send()

    def finish(self):
        for c in range(self.chunks):
            self.got_near(c)
            self.got_cross(c)
        self.drain()


def fsdp_places():
    f = lax.axis_index("fsdp")
    return f // 2, lax.rem(f, 2), lax.axis_size("fsdp") // 2


def fsdp_peers():
    pair, side, pairs = fsdp_places()
    peers = [{"fsdp": lax.rem(pair + d, pairs) * 2 + side} for d in range(1, pairs)]
    return peers + [{"fsdp": pair * 2 + 1 - side}]


class FsdpGather:
    def __init__(self, wires, shard, full_at, local):
        self.wires, self.shard, self.full_at, self.local = wires, shard, full_at, local
        self.pair, self.side, self.pairs = fsdp_places()
        self.base = wires.take(2 * self.pairs)

    def source(self, d):
        return lax.rem(self.pair + self.pairs - d, self.pairs)

    def out(self, d):
        own = self.full_at(self.pair * 2 + self.side)
        if d == 0:
            return self.wires.at(self.base, self.shard, own, {"fsdp": self.pair * 2 + 1 - self.side})
        where = {"fsdp": lax.rem(self.pair + d, self.pairs) * 2 + self.side}
        return self.wires.at(self.base + d, self.shard, own, where)

    def onward(self, d):
        view = self.full_at(self.source(d) * 2 + self.side)
        return self.wires.at(self.base + self.pairs + d, view, view, {"fsdp": self.pair * 2 + 1 - self.side})

    def keep(self):
        return pltpu.make_async_copy(self.shard, self.full_at(self.pair * 2 + self.side), self.local)

    def start(self):
        self.out(0).start()
        for d in range(1, self.pairs):
            self.out(d).start()
        self.keep().start()

    def forward(self, d):
        self.out(d).wait_recv()
        self.onward(d).start()

    def complete(self, d):
        if d == 0:
            self.keep().wait()
            self.out(0).wait_recv()
        else:
            self.onward(d).wait_recv()

    def drain(self):
        for d in range(self.pairs):
            self.out(d).wait_send()
        for d in range(1, self.pairs):
            self.onward(d).wait_send()

    def finish(self):
        for d in range(self.pairs):
            self.complete(d)
        self.drain()


class FsdpScatter:
    def __init__(self, wires, parts, bufs, result):
        self.wires, self.parts, self.result = wires, parts, result
        self.mine, self.got, self.landed, self.local = bufs
        self.pair, self.side, self.pairs = fsdp_places()
        self.base = wires.take(2 * self.pairs)

    def owner(self, d):
        return lax.rem(self.pair + d, self.pairs) * 2

    def load(self, d):
        slot = d % 2
        return pltpu.make_async_copy(self.parts.at[self.owner(d) + self.side], self.mine.at[slot], self.local.at[slot])

    def swap(self, d):
        src = self.parts.at[self.owner(d) + 1 - self.side]
        return self.wires.at(self.base + d, src, self.got.at[d], {"fsdp": self.pair * 2 + 1 - self.side})

    def onward(self, d):
        where = {"fsdp": self.owner(d) + self.side}
        return self.wires.at(self.base + self.pairs + d, self.got.at[d], self.landed.at[d - 1], where)

    def start(self):
        for d in list(range(1, self.pairs)) + [0]:
            self.swap(d).start()
        self.load(1).start()

    def step(self, d):
        self.load((d + 1) % self.pairs).start()
        self.load(d).wait()
        self.swap(d).wait_recv()
        self.got[d] = (self.mine[d % 2].astype(F32) + self.got[d].astype(F32)).astype(BF16)
        self.onward(d).start()

    def finish(self):
        self.load(0).wait()
        self.swap(0).wait_recv()
        total = self.mine[0].astype(F32) + self.got[0].astype(F32)
        for d in range(1, self.pairs):
            self.onward(d).wait_recv()
            total = total + self.landed[d - 1].astype(F32)
        self.result[...] = total.astype(BF16)

    def drain(self):
        for d in range(self.pairs):
            self.swap(d).wait_send()
        for d in range(1, self.pairs):
            self.onward(d).wait_send()


def fsdp_scatter_scratch(shape):
    pairs = shape[0] // 2
    return [
        pltpu.VMEM((2,) + shape[1:], BF16),
        pltpu.VMEM((pairs,) + shape[1:], BF16),
        pltpu.VMEM((pairs - 1,) + shape[1:], BF16),
        pltpu.SemaphoreType.DMA((2,)),
    ]


def blocks(a, count):
    return a.reshape((count, a.shape[0] // count) + a.shape[1:])


def shard_rows(f, size):
    return pl.ds(pl.multiple_of(f * size, 16 if size % 16 == 0 else 8 if size % 8 == 0 else size), size)


def vm_spec():
    return pl.BlockSpec(memory_space=pltpu.VMEM)


def any_spec():
    return pl.BlockSpec(memory_space=pl.ANY)


def wires_scratch(n):
    return [pltpu.SemaphoreType.DMA((n,)), pltpu.SemaphoreType.DMA((n,))]


def call_params(number, vmem=60):
    return pltpu.CompilerParams(collective_id=number, has_side_effects=True, vmem_limit_bytes=min(vmem << 20, 67043328))


def inverse_rms(v):
    return lax.rsqrt(jnp.mean(v * v, axis=-1, keepdims=True) + epsilon)


def norm_back(grad, v, r, gain):
    scaled = grad * gain
    return r * scaled - v * (r * r * r) * jnp.mean(v * scaled, axis=-1, keepdims=True)


def middle_kernel(
    o, out_w, tok, gains, up_q, down_q, gate_h, cot_h,
    obuf, resid, n2_h, hid_h, dg_h, du_h, up_h, down_h, parts_h,
    send, recv, local, own, n2, cot, gate_w, up_w, down_w, ga, ub, hid, dg, du, parts,
):
    rows, width = tok.shape
    piece = o.shape[1]
    nseq = obuf.shape[0]
    units = gate_w.shape[1]
    nfsdp = parts.shape[0]
    s, near, far, cross = seq_places()
    loads = [pltpu.make_async_copy(gate_h, gate_w, local.at[0]), pltpu.make_async_copy(cot_h, cot, local.at[1])]
    for a in loads:
        a.start()
    meet([{"seq": near}, {"seq": far}, {"seq": cross}] + fsdp_peers())
    wires = Wires(send, recv)
    trips = [wires.go(o.at[rows_at(t, rows), :], obuf.at[s], {"seq": t}) for t in (far, cross, near)]
    up_size, down_size = up_q.shape[0], down_q.shape[0]
    ups = FsdpGather(wires, up_q, lambda f: up_w.at[shard_rows(f, up_size), :], local.at[2])
    downs = FsdpGather(wires, down_q, lambda f: down_w.at[shard_rows(f, down_size), :], local.at[3])
    ups.start()
    downs.start()
    obuf[s] = o[rows_at(s, rows), :]
    half = rows // 2
    for a in trips:
        a.wait_recv()
    ring = SeqGather(wires, lambda t, c: n2.at[rows_at(t, rows, c * half, half), :], 2)
    cols = out_w.shape[2]
    for c in range(2):
        part = slice(c * half, (c + 1) * half)
        for u in range(nseq):
            acc = tok[part, u * cols : (u + 1) * cols].astype(F32)
            for t in range(nseq):
                acc = acc + nn(obuf[t, part, :], out_w[u, t * piece : (t + 1) * piece, :])
            resid[part, u * cols : (u + 1) * cols] = acc
        h = resid[part, :]
        low = (h * inverse_rms(h) * gains[1:2, :]).astype(BF16)
        own[part, :] = low
        n2[rows_at(s, rows, c * half, half), :] = low
        ring.send(c, own.at[pl.ds(c * half, half), :])
    loads[0].wait()

    def gate_rows(t):
        ga[rows_at(t, rows), :] = nn(n2[rows_at(t, rows), :], gate_w[...])

    def act_rows(t):
        up = nn(n2[rows_at(t, rows), :], up_w[...])
        active, slope = gelu_both(ga[rows_at(t, rows), :])
        hid[rows_at(t, rows), :] = (active * up).astype(BF16)
        ga[rows_at(t, rows), :] = slope * up
        ub[rows_at(t, rows), :] = active

    pairs = ups.pairs
    ups.forward(1)
    gate_rows(s)
    ring.got_near(0)
    ring.got_near(1)
    gate_rows(near)
    for d in range(2, pairs):
        ups.forward(d)
        if d == 2:
            ring.forward(0)
    ring.forward(1)
    downs.forward(1)
    gate_rows(far)
    for c in range(2):
        ring.got_cross(c)
    gate_rows(cross)
    saves = [pltpu.make_async_copy(n2, n2_h, local.at[4])]
    saves[0].start()
    for d in range(pairs):
        ups.complete(d)
    saves.append(pltpu.make_async_copy(up_w, up_h, local.at[5]))
    saves[1].start()
    for t in (s, near):
        act_rows(t)
    downs.forward(2) if pairs > 2 else None
    for t in (far, cross):
        act_rows(t)
    saves.append(pltpu.make_async_copy(hid, hid_h, local.at[6]))
    saves[2].start()
    loads[1].wait()
    width_f = units // nfsdp
    wide = max(256 // width_f, 1)

    def down_part(n):
        got = dot_tn(hid[:, n * wide * width_f : (n + 1) * wide * width_f], cot[...]).astype(BF16)
        for m in range(wide):
            parts[n * wide + m] = got[m * width_f : (m + 1) * width_f, :]

    for n in range(nfsdp // wide):
        down_part(n)
        if n == 1:
            for d in range(3, pairs):
                downs.forward(d)
    saves.append(pltpu.make_async_copy(parts, parts_h, local.at[7]))
    saves[3].start()

    def back_cols(at, units_at):
        for t in range(nseq):
            band = slice(t * rows, (t + 1) * rows)
            dh = nt(cot[band, :], down_w[units_at, :])
            dg[band, at] = (dh * ga[band, at]).astype(BF16)
            du[band, at] = (dh * ub[band, at]).astype(BF16)

    if (2 * width_f) % 128 == 0:
        for d in range(pairs):
            downs.complete(d)
            at = pl.ds(pl.multiple_of(downs.source(d) * 2 * width_f, 2 * width_f), 2 * width_f)
            back_cols(at, at)
    else:
        for d in range(pairs):
            downs.complete(d)
        for n in range(units // 256):
            at = slice(n * 256, (n + 1) * 256)
            back_cols(at, at)
    saves.append(pltpu.make_async_copy(down_w, down_h, local.at[8]))
    saves.append(pltpu.make_async_copy(dg, dg_h, local.at[9]))
    saves.append(pltpu.make_async_copy(du, du_h, local.at[10]))
    for a in saves[4:]:
        a.start()
    ring.drain()
    ups.drain()
    downs.drain()
    for a in trips:
        a.wait_send()
    for a in saves:
        a.wait()


def middle(o, out_w, tok, gains, up_q, down_q, gate_w, cot, nfsdp):
    nseq = out_w.shape[0]
    rows, width = tok.shape
    units = gate_w.shape[1]
    tall = nseq * rows
    return pl.pallas_call(
        middle_kernel,
        out_shape=(
            jax.ShapeDtypeStruct((nseq, rows, o.shape[1]), BF16),
            jax.ShapeDtypeStruct((rows, width), F32),
            jax.ShapeDtypeStruct((tall, width), BF16),
            jax.ShapeDtypeStruct((tall, units), BF16),
            jax.ShapeDtypeStruct((tall, units), BF16),
            jax.ShapeDtypeStruct((tall, units), BF16),
            jax.ShapeDtypeStruct((width, units), BF16),
            jax.ShapeDtypeStruct((units, width), BF16),
            jax.ShapeDtypeStruct((nfsdp, units // nfsdp, width), BF16),
        ),
        in_specs=[vm_spec()] * 4 + [any_spec()] * 4,
        out_specs=(vm_spec(), vm_spec()) + (any_spec(),) * 7,
        scratch_shapes=wires_scratch(9 + 2 * nfsdp)
        + [
            pltpu.SemaphoreType.DMA((11,)),
            pltpu.VMEM((rows, width), BF16),
            pltpu.VMEM((tall, width), BF16),
            pltpu.VMEM((tall, width), BF16),
            pltpu.VMEM((width, units), BF16),
            pltpu.VMEM((width, units), BF16),
            pltpu.VMEM((units, width), BF16),
            pltpu.VMEM((tall, units), F32),
            pltpu.VMEM((tall, units), F32),
            pltpu.VMEM((tall, units), BF16),
            pltpu.VMEM((tall, units), BF16),
            pltpu.VMEM((tall, units), BF16),
            pltpu.VMEM((nfsdp, units // nfsdp, width), BF16),
        ],
        compiler_params=call_params(2, 63),
        name="middle",
    )(o, out_w, tok, gains, up_q, down_q, gate_w, cot)


class SeqScatter:
    def __init__(self, wires, chunks, *bufs):
        self.s, self.near, self.far, self.cross = seq_places()
        self.wires, self.chunks, self.bufs = wires, chunks, bufs
        self.base = wires.take(3 * chunks)

    def trip(self, kind, c):
        where = {"seq": self.far if kind == 1 else self.near}
        src, dst = self.bufs[2 * kind].at[c], self.bufs[2 * kind + 1].at[c]
        return self.wires.at(self.base + 3 * c + kind, src, dst, where)

    def cross_chunk(self, c, value):
        self.bufs[0][c] = value.astype(BF16)
        self.trip(0, c).start()

    def far_chunk(self, c, value):
        self.trip(0, c).wait_recv()
        self.bufs[2][c] = (value + self.bufs[1][c].astype(F32)).astype(BF16)
        self.trip(1, c).start()

    def near_chunk(self, c, value):
        self.bufs[4][c] = value.astype(BF16)
        self.trip(2, c).start()

    def own_chunk(self, c, value):
        self.trip(2, c).wait_recv()
        self.trip(1, c).wait_recv()
        return value + self.bufs[5][c].astype(F32) + self.bufs[3][c].astype(F32)

    def finish(self):
        for c in range(self.chunks):
            for kind in range(3):
                self.trip(kind, c).wait_send()


def scatter_scratch(chunks, rows, width):
    return [pltpu.VMEM((chunks, rows, width), BF16)] * 6


def unmix_kernel(
    chunks, gains, obuf, resid, cot, down_p, dg_h, du_h, gate_h, up_h, out_h, n2_h, hid_h, dw_h,
    rgrad, dmix, ggrad, shard, wgrad_h, gate_p, up_p, y_h,
    send, recv, b0, b1, b2, b3, b4, b5, attn, dob, p0, p1, p2, p3,
    local, dg, du, gate_w, up_w, out_w, n2, hid, down_w, wgrad, stage, ystage, sems,
):
    rows, width = resid.shape
    nseq, _, piece = obuf.shape
    nfsdp = gate_p.shape[0]
    units = dg.shape[1]
    s, near, far, cross = seq_places()
    loads = [
        pltpu.make_async_copy(src, dst, local.at[n])
        for n, (src, dst) in enumerate(
            (
                (gate_h, gate_w),
                (up_h, up_w),
                (dg_h, dg),
                (du_h, du),
                (n2_h, n2),
                (out_h, out_w),
                (hid_h, hid),
                (dw_h, down_w),
            )
        )
    ]
    for a in loads:
        a.start()
    meet([{"seq": near}, {"seq": far}, {"seq": cross}] + fsdp_peers())
    wires = Wires(send, recv)
    grads = FsdpScatter(wires, down_p, (p0, p1, p2, p3), shard)
    grads.start()
    pairs = grads.pairs
    sums = SeqScatter(wires, chunks, b0, b1, b2, b3, b4, b5)
    size = rows // chunks
    for a in loads[:4]:
        a.wait()

    def part(t, c):
        at = rows_at(t, rows, c * size, size)
        return nt(dg[at, :], gate_w[...]) + nt(du[at, :], up_w[...])

    for c in range(chunks):
        sums.cross_chunk(c, part(cross, c))
    for c in range(chunks):
        sums.far_chunk(c, part(far, c))
    for c in range(chunks):
        sums.near_chunk(c, part(near, c))
    for c in range(chunks):
        rgrad[c * size : (c + 1) * size, :] = part(s, c)
    grads.step(1)
    loads[4].wait()
    depth = width // nfsdp
    wide = 384
    saves = []

    def weight_parts(side, out, begin, end):
        for n in range(begin, end):
            slot = n % 2
            copies = [
                pltpu.make_async_copy(
                    stage.at[slot], out.at[pl.ds(n * (wide // depth), wide // depth)], sems.at[3 + slot]
                )
            ]
            for a in saves[-2:-1] if len(saves) > 1 else []:
                for b in a:
                    b.wait()
            got = dot_tn(n2[:, n * wide : (n + 1) * wide], side[...])
            for m in range(wide // depth):
                stage[slot, m] = got[m * depth : (m + 1) * depth, :].astype(BF16)
            for a in copies:
                a.start()
            saves.append(copies)

    weight_parts(dg, gate_p, 0, width // wide)
    if pairs > 2:
        grads.step(2)
    loads[5].wait()
    cols = out_w.shape[2]

    def own_rows(c, total):
        at = slice(c * size, (c + 1) * size)
        dn = sums.own_chunk(c, rgrad[at, :])
        h = resid[at, :]
        r = inverse_rms(h)
        rg = cot[at, :].astype(F32) + norm_back(dn, h, r, gains[1:2, :])
        rgrad[at, :] = rg
        low = rg.astype(BF16)
        attn[at, :] = low
        for t in range(nseq):
            acc = jnp.zeros((size, piece), F32)
            for u in range(nseq):
                acc = acc + nt(low[:, u * cols : (u + 1) * cols], out_w[u, t * piece : (t + 1) * piece, :])
            dob[t, at, :] = acc.astype(BF16)
        return total + jnp.sum(dn * h * r, axis=0, keepdims=True)

    base = wires.take(3 * chunks)

    def trip(n, t, c):
        at = pl.ds(c * size, size)
        return wires.at(base + 3 * c + n, dob.at[t, at, :], dmix.at[rows_at(s, rows, c * size, size), :], {"seq": t})

    total = jnp.zeros((1, width), F32)
    for c in range(chunks):
        total = own_rows(c, total)
        if c == 0:
            weight_parts(du, up_p, 0, 1)
        for n, t in enumerate((far, cross, near)):
            trip(n, t, c).start()
        dmix[rows_at(s, rows, c * size, size), :] = dob[s, pl.ds(c * size, size), :]
        if c == 0:
            weight_parts(du, up_p, 1, width // wide)
            for d in range(3, pairs):
                grads.step(d)
    ggrad[...] = jnp.broadcast_to(total, ggrad.shape)
    for t in range(nseq):
        for u in range(nseq):
            wgrad[u, t * piece : (t + 1) * piece, :] = dot_tn(obuf[t], attn[:, u * cols : (u + 1) * cols]).astype(BF16)
    last = pltpu.make_async_copy(wgrad, wgrad_h, sems.at[2])
    last.start()
    for a in loads[6:]:
        a.wait()
    ycopies = []
    for t in range(nseq):
        slot = t % 2
        if t > 1:
            ycopies[t - 2].wait()
        at = slice(t * rows, (t + 1) * rows)
        ystage[slot] = nn(hid[at, :], down_w[...]).astype(BF16)
        ycopies.append(pltpu.make_async_copy(ystage.at[slot], y_h.at[at, :], sems.at[slot]))
        ycopies[t].start()
    for c in range(chunks):
        for n, t in enumerate((far, cross, near)):
            trip(n, t, c).wait()
    grads.finish()
    sums.finish()
    grads.drain()
    for a in saves[-2:]:
        for b in a:
            b.wait()
    for a in ycopies[-2:] + [last]:
        a.wait()


def unmix(gains, obuf, resid, cot, down_p, dg, du, gate_w, up_w, out_w, n2, hid, down_w, chunks=2):
    rows, width = resid.shape
    nseq, _, piece = obuf.shape
    nfsdp = down_p.shape[0]
    units = dg.shape[1]
    grad_shape = (nfsdp, width // nfsdp, units)
    return pl.pallas_call(
        functools.partial(unmix_kernel, chunks),
        out_shape=(
            jax.ShapeDtypeStruct((rows, width), F32),
            jax.ShapeDtypeStruct((nseq * rows, piece), BF16),
            jax.ShapeDtypeStruct((8, width), F32),
            jax.ShapeDtypeStruct(down_p.shape[1:], BF16),
            jax.ShapeDtypeStruct(out_w.shape, BF16),
            jax.ShapeDtypeStruct(grad_shape, BF16),
            jax.ShapeDtypeStruct(grad_shape, BF16),
            jax.ShapeDtypeStruct(n2.shape, BF16),
        ),
        in_specs=[vm_spec()] * 4 + [any_spec()] * 9,
        out_specs=(vm_spec(),) * 4 + (any_spec(),) * 4,
        scratch_shapes=wires_scratch(6 * chunks + nfsdp)
        + scatter_scratch(chunks, rows // chunks, width)
        + [pltpu.VMEM((rows, width), BF16), pltpu.VMEM((nseq, rows, piece), BF16)]
        + fsdp_scatter_scratch(down_p.shape)
        + [
            pltpu.SemaphoreType.DMA((8,)),
            pltpu.VMEM(dg.shape, BF16),
            pltpu.VMEM(du.shape, BF16),
            pltpu.VMEM(gate_w.shape, BF16),
            pltpu.VMEM(up_w.shape, BF16),
            pltpu.VMEM(out_w.shape, BF16),
            pltpu.VMEM(n2.shape, BF16),
            pltpu.VMEM(hid.shape, BF16),
            pltpu.VMEM(down_w.shape, BF16),
            pltpu.VMEM(out_w.shape, BF16),
            pltpu.VMEM((2, 384 * nfsdp // width, width // nfsdp, units), BF16),
            pltpu.VMEM((2, rows, width), BF16),
            pltpu.SemaphoreType.DMA((5,)),
        ],
        compiler_params=call_params(4, 63),
        name="unmix",
    )(gains, obuf, resid, cot, down_p, dg, du, gate_w, up_w, out_w, n2, hid, down_w)


def build_strips(heads, starts, table, ids, strip, far):
    length = ids.shape[1]
    half = 2 * PROMPT
    for h in range(heads):
        row = jnp.zeros(ids.shape, F32)
        for b in range(table.shape[0]):
            row = jnp.where(ids[...] == b, table[b, h], row)
        base = jnp.broadcast_to(row[:1, PROMPT // 2 : PROMPT // 2 + half], (128, half))
        strip[h] = pltpu.roll(base, 1, 1, stride=1, stride_axis=0)[:, 128:]
        for c in range(2):
            moved = pltpu.roll(row, length - PROMPT // 2 - starts[c], 1)
            base = jnp.broadcast_to(moved[:1, : FARW + 128], (128, FARW + 128))
            far[h, c] = pltpu.roll(base, 1, 1, stride=1, stride_axis=0)[:, 128:]


def head_masks(width, heads):
    lane = lax.broadcasted_iota(jnp.int32, (1, width), 1)
    return [(lane >= h * HEAD_DIM) & (lane < (h + 1) * HEAD_DIM) for h in range(heads)]


def masked_copies(src, dst, heads):
    masks = head_masks(src.shape[1], heads)
    for h in range(heads):
        dst[h] = jnp.where(masks[h], src[...], jnp.zeros((), src.dtype))


def bias_chunk(strip, far, h, first_q, kstart, kind, c):
    parts = []
    for r in range(KC // 128):
        m = PROMPT - 128 - (kstart + 128 * r)
        if kind == "far":
            parts.append(far[h, c, :, m : m + CL])
        else:
            parts.append(strip[h, :, pl.ds(pl.multiple_of(first_q + m, 128), CL)])
    return jnp.concatenate(parts, axis=0)


def pack_piece(units, nfsdp, nseq):
    block = units // nfsdp
    return block, -(-block // (16 * nseq)) * 16


def pack_front(t, raw, first_q, out_q, gains):
    r_q, r_k, r_v, r_o = raw
    piece = first_q.shape[1] * 3 // 10
    depth = first_q.shape[0]
    cut = slice(t * piece, (t + 1) * piece)
    first_q[...] = jnp.concatenate(
        [r_q[:, cut], r_k[:, cut], r_v[:, cut], gains, jnp.zeros((depth, first_q.shape[1] - 3 * piece - 8), BF16)], axis=1
    )
    cols = out_q.shape[1]
    out_q[...] = r_o[:, t * cols : (t + 1) * cols]


def pack_cols(t, nseq, nfsdp, raw, packed):
    block, piece = pack_piece(raw.shape[1], nfsdp, nseq)
    pieces = []
    for f in range(nfsdp):
        begin = f * block + t * piece
        end = min(begin + piece, (f + 1) * block)
        pieces.append(raw[:, begin:end])
        if end - begin < piece:
            pieces.append(jnp.zeros((raw.shape[0], piece - end + begin), BF16))
    packed[...] = jnp.concatenate(pieces, axis=1)


def pack_down(t, raw, packed):
    piece = packed.shape[0]
    begin = t * piece
    end = min(begin + piece, raw.shape[0])
    packed[: end - begin, :] = raw[begin:end, :]
    if end - begin < piece:
        packed[end - begin :, :] = jnp.zeros((piece - end + begin, raw.shape[1]), BF16)


def front_kernel(
    heads, nseq, starts, table, ids, gain_a, gain_b, tok, w_q, w_k, w_v, w_o, w_g, w_u, w_d, cot,
    q, k, v, o, lse, gains, n1_h, first_h, out_w, cots, gate_w, up_q, down_q,
    send, recv, local, r_q, r_k, r_v, r_o, r_g, r_u, r_d, first_q, out_q, gate_q, up_s, down_s,
    group, n1, first, strip, far, kh, vt, ot, s,
):
    rows, width = tok.shape
    mine, near, other, cross = seq_places()
    pair, side, pairs = fsdp_places()
    nfsdp = 2 * pairs
    loads = [
        pltpu.make_async_copy(src, dst, local.at[n])
        for n, (src, dst) in enumerate(
            ((w_q, r_q), (w_k, r_k), (w_v, r_v), (w_o, r_o), (w_g, r_g), (w_u, r_u), (w_d, r_d))
        )
    ]
    for a in loads:
        a.start()
    meet([{"seq": near}, {"seq": other}] + fsdp_peers())
    wires = Wires(send, recv)
    half = rows // 2
    ring = SeqGather(wires, lambda t, c: group.at[rows_at(t, rows, c * half, half), :], 2)
    size = first_q.shape[0]
    lead = FsdpGather(wires, first_q, lambda f: first.at[shard_rows(f, size), :], local.at[7])
    late = FsdpGather(wires, out_q, lambda f: out_w.at[mine, f], local.at[8])
    gate_size = gate_q.shape[0]
    weight = FsdpGather(wires, gate_q, lambda f: gate_w.at[shard_rows(f, gate_size), :], local.at[9])
    wring = SeqGather(wires, lambda t, c: out_w.at[t], 1)
    cring = SeqGather(wires, lambda t, c: cots.at[rows_at(t, rows, c * half, half), :], 2)
    own = [
        pltpu.make_async_copy(tok, group.at[rows_at(mine, rows), :], local.at[10]),
        pltpu.make_async_copy(cot, cots.at[rows_at(mine, rows), :], local.at[11]),
    ]
    for c in range(2):
        ring.send(c, tok.at[pl.ds(c * half, half), :])
    for a in own:
        a.start()
    for a in loads[:4]:
        a.wait()
    both = jnp.concatenate([gain_a[...], gain_b[...], jnp.zeros((6, gain_a.shape[1]), BF16)], axis=0)
    both = both.astype(F32).T.astype(BF16)
    for t in range(nseq):

        @pl.when(mine == t)
        def _():
            pack_front(t, (r_q, r_k, r_v, r_o), first_q, out_q, both)

    for a in loads[4:]:
        a.wait()
    lead.start()
    for t in range(nseq):

        @pl.when(mine == t)
        def _():
            pack_cols(t, nseq, nfsdp, r_g, gate_q)

    late.start()
    for t in range(nseq):

        @pl.when(mine == t)
        def _():
            pack_cols(t, nseq, nfsdp, r_u, up_s)
            pack_down(t, r_d, down_s)

    weight.start()
    for c in range(2):
        cring.send(c, cot.at[pl.ds(c * half, half), :])
    saves = [pltpu.make_async_copy(up_s, up_q, local.at[12]), pltpu.make_async_copy(down_s, down_q, local.at[13])]
    for a in saves:
        a.start()
    build_strips(heads, starts, table, ids, strip, far)
    lse[...] = jnp.zeros(lse.shape, F32)
    for d in range(1, pairs):
        lead.forward(d)
        if d == pairs // 2:
            ring.forward(0)
    for d in range(1, pairs):
        late.forward(d)
    ring.forward(1)
    lead.finish()
    saves.append(pltpu.make_async_copy(first, first_h, local.at[14]))
    saves[2].start()
    piece = q.shape[1]
    column = 3 * piece
    gains[...] = jnp.zeros(gains.shape, F32)
    for b in range(width // 256):
        band = first[b * 256 : (b + 1) * 256, column // 128 * 128 : column // 128 * 128 + 128].astype(F32).T
        for n in range(2):
            line = column % 128 + n
            gains[n : n + 1, b * 256 : (b + 1) * 256] = band[line : line + 1, :]

    def project(t):
        at = rows_at(t, rows)
        x = group[at, :].astype(F32)
        low = (x * inverse_rms(x) * gains[0:1, :]).astype(BF16)
        n1[at, :] = low
        r = nn(low, first[:, :column])
        q[at, :] = r[:, :piece].astype(BF16)
        k[at, :] = r[:, piece : 2 * piece].astype(BF16)
        v[at, :] = r[:, 2 * piece :].astype(BF16)

    own[0].wait()
    project(mine)
    for c in range(2):
        ring.got_near(c)
    project(near)
    project(other)
    for c in range(2):
        ring.got_cross(c)
    project(cross)
    saves.append(pltpu.make_async_copy(n1, n1_h, local.at[15]))
    saves[3].start()
    for d in range(pairs):
        late.complete(d)
    wring.send(0, out_w.at[mine])
    masked_copies(k, kh, heads)
    vt[...] = v[...].astype(F32).T.astype(BF16)

    def block(h, q0, bias_q0, chunks, c):
        qb = q[pl.ds(q0, CL), :]
        top = None
        for n, (k0, kind, kstart) in enumerate(chunks):
            sc = nt(kh[h, pl.ds(k0, KC), :], qb) + bias_chunk(strip, far, h, bias_q0, kstart, kind, c)
            s[n * KC : (n + 1) * KC, :] = sc
            m = jnp.max(sc, axis=0, keepdims=True)
            top = m if top is None else jnp.maximum(top, m)
        total = jnp.zeros((1, CL), F32)
        acc = jnp.zeros((HEAD_DIM, CL), F32)
        for n, (k0, kind, kstart) in enumerate(chunks):
            e = jnp.exp(s[n * KC : (n + 1) * KC, :] - top)
            total = total + jnp.sum(e, axis=0, keepdims=True)
            acc = acc + nn(vt[pl.ds(pl.multiple_of(h * HEAD_DIM, HEAD_DIM), HEAD_DIM), pl.ds(k0, KC)], e.astype(BF16))
        ot[pl.ds(pl.multiple_of(h * HEAD_DIM, HEAD_DIM), HEAD_DIM), pl.ds(q0, CL)] = acc / total
        lse[pl.ds(h, 1), pl.ds(q0, CL)] = top + jnp.log(total)

    nblk = PROMPT // CL

    def prompt_body(i, carry):
        h, blk = i // nblk, i % nblk
        q0 = pl.multiple_of(blk * CL, CL)
        block(h, q0, q0, [(j * KC, "strip", j * KC) for j in range(PROMPT // KC)], None)
        for d in range(1, pairs - 1):

            @pl.when(i == heads * nblk * d // pairs)
            def _():
                weight.forward(d)

        return carry

    lax.fori_loop(0, heads * nblk, prompt_body, 0)

    def cont_body(i, carry):
        h, c = i // 2, i % 2
        q0 = pl.multiple_of(PROMPT + c * CL, CL)
        chunks = [(j * KC, "far", j * KC) for j in range(PROMPT // KC)]
        chunks += [(q0 + j * KC, "strip", j * KC) for j in range(CL // KC)]
        block(h, q0, 0, chunks, c)
        return carry

    cring.forward(0)
    lax.fori_loop(0, heads * 2, cont_body, 0)
    o[...] = ot[...].T.astype(BF16)
    weight.forward(pairs - 1)
    cring.forward(1)
    wring.forward(0)
    for a in own[1:] + saves:
        a.wait()
    weight.finish()
    late.drain()
    wring.finish()
    cring.finish()
    ring.drain()


def front(starts, table, ids, gain_a, gain_b, tok, w_q, w_k, w_v, w_o, w_g, w_u, w_d, cot, nseq, nfsdp):
    rows, width = tok.shape
    inner = w_q.shape[1]
    piece = inner // nseq
    heads = piece // HEAD_DIM
    tall = nseq * rows
    size = w_q.shape[0]
    units = pack_piece(w_g.shape[1], nfsdp, nseq)[1]
    cols = width // nseq
    lead = piece * 10 // 3
    smem = pl.BlockSpec(memory_space=pltpu.SMEM)
    return pl.pallas_call(
        functools.partial(front_kernel, heads, nseq),
        out_shape=(
            jax.ShapeDtypeStruct((tall, piece), BF16),
            jax.ShapeDtypeStruct((tall, piece), BF16),
            jax.ShapeDtypeStruct((tall, piece), BF16),
            jax.ShapeDtypeStruct((tall, piece), BF16),
            jax.ShapeDtypeStruct((8, tall), F32),
            jax.ShapeDtypeStruct((8, width), F32),
            jax.ShapeDtypeStruct((tall, width), BF16),
            jax.ShapeDtypeStruct((width, lead), BF16),
            jax.ShapeDtypeStruct((nseq, nfsdp, w_o.shape[0], cols), BF16),
            jax.ShapeDtypeStruct((tall, width), BF16),
            jax.ShapeDtypeStruct((width, nfsdp * units), BF16),
            jax.ShapeDtypeStruct((size, nfsdp * units), BF16),
            jax.ShapeDtypeStruct((nseq * units // nseq, width), BF16),
        ),
        in_specs=[smem, smem, vm_spec(), vm_spec(), vm_spec()] + [any_spec()] * 9,
        out_specs=(vm_spec(),) * 6 + (any_spec(),) * 7,
        scratch_shapes=wires_scratch(15 + 3 * nfsdp)
        + [
            pltpu.SemaphoreType.DMA((16,)),
            pltpu.VMEM(w_q.shape, BF16),
            pltpu.VMEM(w_k.shape, BF16),
            pltpu.VMEM(w_v.shape, BF16),
            pltpu.VMEM(w_o.shape, BF16),
            pltpu.VMEM(w_g.shape, BF16),
            pltpu.VMEM(w_u.shape, BF16),
            pltpu.VMEM(w_d.shape, BF16),
            pltpu.VMEM((size, lead), BF16),
            pltpu.VMEM((w_o.shape[0], cols), BF16),
            pltpu.VMEM((size, nfsdp * units), BF16),
            pltpu.VMEM((size, nfsdp * units), BF16),
            pltpu.VMEM((units, width), BF16),
            pltpu.VMEM((tall, width), BF16),
            pltpu.VMEM((tall, width), BF16),
            pltpu.VMEM((width, lead), BF16),
            pltpu.VMEM((heads, 128, STRIP), F32),
            pltpu.VMEM((heads, 2, 128, FARW), F32),
            pltpu.VMEM((heads, tall, piece), BF16),
            pltpu.VMEM((piece, tall), BF16),
            pltpu.VMEM((piece, tall), F32),
            pltpu.VMEM((PROMPT + CL, CL), F32),
        ],
        compiler_params=call_params(1, 60),
        name="front",
    )(starts, table, ids, gain_a, gain_b, tok, w_q, w_k, w_v, w_o, w_g, w_u, w_d, cot)


def back_kernel(
    heads, chunks, starts, table, ids, gains, lse, gain_b, q, k, v, o, do,
    resid_h, rgrad_h, tok_h, y_p, w_p, gate_p, up_p, done_h, n1_h, first_h,
    small, y_h, in_h, down_f, gate_f, up_f, qkv_f, out_f,
    send, recv, local, ybuf, wbuf, out_p, qkv_p, b0, b1, b2, b3, b4, b5,
    g0, g1, g2, g3, u0, u1, u2, u3, q0_, q1_, q2_, q3_, o0, o1, o2, o3,
    gate_s, up_s, qkv_s, out_s, dqkv, tok, held, stage, one, two, three, tgrad,
):
    rows, width = tok.shape
    nseq = w_p.shape[0]
    piece = q.shape[1]
    nfsdp = gate_p.shape[0]
    s, near, far_d, cross = seq_places()
    pair, side, pairs = fsdp_places()

    def y_block(t):
        return y_p.at[rows_at(t, rows), :]

    def w_block(t):
        return w_p.at[t]

    sides = ((w_block, wbuf), (y_block, ybuf))
    loads = []
    for n, (block_of, buf) in enumerate(sides):
        loads.append(pltpu.make_async_copy(block_of(far_d), buf.at[2], local.at[2 * n]))
        loads.append(pltpu.make_async_copy(block_of(s), buf.at[3], local.at[2 * n + 1]))
    loads.append(pltpu.make_async_copy(tok_h, tok, local.at[5]))
    for a in loads:
        a.start()
    meet([{"seq": near}, {"seq": far_d}, {"seq": cross}] + fsdp_peers())
    wires = Wires(send, recv)
    hops = [wires.go(block_of(cross), buf.at[0], {"seq": near}) for block_of, buf in sides]
    turns = [wires.go(block_of(near), buf.at[1], {"seq": near}) for block_of, buf in sides]
    gates = FsdpScatter(wires, gate_p, (g0, g1, g2, g3), gate_s)
    ups = FsdpScatter(wires, up_p, (u0, u1, u2, u3), up_s)
    gates.start()
    ups.start()
    down_ring = SeqGather(wires, lambda t, c: down_f.at[t], 1)
    gate_ring = SeqGather(wires, lambda t, c: gate_f.at[t], 1)
    up_ring = SeqGather(wires, lambda t, c: up_f.at[t], 1)
    qkv_ring = SeqGather(wires, lambda t, c: qkv_f.at[t], 1)
    out_ring = SeqGather(wires, lambda t, c: out_f.at[t], 1)
    qkvs = FsdpScatter(wires, qkv_p, (q0_, q1_, q2_, q3_), qkv_s)
    outs = FsdpScatter(wires, out_p, (o0, o1, o2, o3), out_s)
    far_base = wires.take(2)

    def far_hop(n):
        buf = sides[n][1]
        return wires.at(far_base + n, buf.at[2], buf.at[4], {"seq": far_d})

    def add_far(n):
        buf = sides[n][1]
        loads[2 * n].wait()
        hops[n].wait_recv()
        buf[2] = (buf[2].astype(F32) + buf[0].astype(F32)).astype(BF16)

    def total_of(n):
        buf = sides[n][1]
        loads[2 * n + 1].wait()
        turns[n].wait_recv()
        far_hop(n).wait_recv()
        return buf[3].astype(F32) + buf[1].astype(F32) + buf[4].astype(F32)

    down_keep = pltpu.make_async_copy(done_h, down_f.at[s], local.at[6])
    down_keep.start()
    down_ring.send(0, done_h)
    length = ids.shape[1]
    half = 2 * PROMPT

    def attend_back(strip, far, kh, vh, kt, delta, dqt, dk, dv, gstrip, gfar):
        build_strips(heads, starts, table, ids, strip, far)
        add_far(0)
        add_far(1)
        for src, dst in ((k, kh), (v, vh)):
            masked_copies(src, dst, heads)
        far_hop(0).start()
        far_hop(1).start()
        kt[...] = k[...].astype(F32).T.astype(BF16)
        prod = (o[...].astype(F32) * do[...].astype(F32)).T
        for h in range(heads):
            delta[h : h + 1, :] = jnp.sum(prod[h * HEAD_DIM : (h + 1) * HEAD_DIM, :], axis=0, keepdims=True)
        dk[...] = jnp.zeros(dk.shape, F32)
        dv[...] = jnp.zeros(dv.shape, F32)
        gstrip[...] = jnp.zeros(gstrip.shape, F32)
        gfar[...] = jnp.zeros(gfar.shape, F32)
        lane = lax.broadcasted_iota(jnp.int32, (1, piece), 1)

        def block(h, q0, bias_q0, chunk_list, c):
            qb = q[pl.ds(q0, CL), :]
            dob = do[pl.ds(q0, CL), :]
            keep = lane // HEAD_DIM == h
            qhb = jnp.where(keep, qb, jnp.zeros((), BF16))
            dohb = jnp.where(keep, dob, jnp.zeros((), BF16))
            lrow = lse[pl.ds(h, 1), pl.ds(q0, CL)]
            drow = delta[pl.ds(h, 1), pl.ds(q0, CL)]
            acc = jnp.zeros((HEAD_DIM, CL), F32)
            for n, (k0, kind, kstart) in enumerate(chunk_list):
                ks = pl.ds(k0, KC)
                sc = nt(kh[h, ks, :], qb) + bias_chunk(strip, far, h, bias_q0, kstart, kind, c)
                pr = jnp.exp(sc - lrow)
                dp = nt(vh[h, ks, :], dob)
                ds = pr * (dp - drow)
                dsl = ds.astype(BF16)
                dv[ks, :] += nn(pr.astype(BF16), dohb)
                dk[ks, :] += nn(dsl, qhb)
                acc = acc + nn(kt[pl.ds(pl.multiple_of(h * HEAD_DIM, HEAD_DIM), HEAD_DIM), ks], dsl)
                for r in range(KC // 128):
                    m = PROMPT - 128 - (kstart + 128 * r)
                    part = ds[128 * r : 128 * (r + 1), :]
                    if kind == "far":
                        gfar[h, c, :, m : m + CL] += part
                    else:
                        gstrip[h, :, pl.ds(pl.multiple_of(bias_q0 + m, 128), CL)] += part
            dqt[pl.ds(pl.multiple_of(h * HEAD_DIM, HEAD_DIM), HEAD_DIM), pl.ds(q0, CL)] = acc

        nblk = PROMPT // CL

        def prompt_body(i, carry):
            h, blk = i // nblk, i % nblk
            q0 = pl.multiple_of(blk * CL, CL)
            block(h, q0, q0, [(j * KC, "strip", j * KC) for j in range(PROMPT // KC)], None)

            @pl.when(i == 3)
            def _():
                gates.step(1)

            return carry

        lax.fori_loop(0, heads * nblk, prompt_body, 0)
        for d in range(2, pairs - 1):
            gates.step(d)

        def cont_body(i, carry):
            h, c = i // 2, i % 2
            q0 = pl.multiple_of(PROMPT + c * CL, CL)
            chunk_list = [(j * KC, "far", j * KC) for j in range(PROMPT // KC)]
            chunk_list += [(q0 + j * KC, "strip", j * KC) for j in range(CL // KC)]
            block(h, q0, 0, chunk_list, c)
            return carry

        lax.fori_loop(0, heads * 2, cont_body, 0)
        if pairs > 2:
            gates.step(pairs - 1)
        dqkv[...] = jnp.concatenate([dqt[...].T, dk[...], dv[...]], axis=1).astype(BF16)
        lines8 = lax.broadcasted_iota(jnp.int32, (table.shape[0], length), 0)
        hot = ids[:1, :] == lines8
        tgrad[...] = jnp.zeros(tgrad.shape, F32)
        for h in range(heads):

            def unskew(g, span):
                full = jnp.concatenate([jnp.zeros((128, 128), F32), g], axis=1)
                eight = full[:8]
                for a in range(1, 16):
                    eight = eight + pltpu.roll(full[8 * a : 8 * a + 8], span - 8 * a, 1)
                vec = pltpu.roll(eight, span - 1, 1)[:1]
                for b in range(1, 8):
                    vec = vec + pltpu.roll(eight, span - 1 - b, 1)[b : b + 1]
                return jnp.concatenate([vec, jnp.zeros((1, length - span), F32)], axis=1)

            whole = jnp.broadcast_to(unskew(gstrip[h], half), (8, length))
            whole = pltpu.roll(whole, PROMPT // 2, 1)
            for c in range(2):
                moved = jnp.broadcast_to(unskew(gfar[h, c], FARW + 128), (8, length))
                whole = whole + pltpu.roll(moved, PROMPT // 2 + starts[c], 1)
            picked = jnp.where(hot, whole[:1, :], 0.0)
            column = jnp.broadcast_to(jnp.sum(picked, axis=1, keepdims=True), (table.shape[0], 128))
            tgrad[h : h + 1, : table.shape[0]] = column.T[:1, :]

    tall = nseq * rows
    pl.run_scoped(
        attend_back,
        pltpu.VMEM((heads, 128, STRIP), F32),
        pltpu.VMEM((heads, 2, 128, FARW), F32),
        pltpu.VMEM((heads, tall, piece), BF16),
        pltpu.VMEM((heads, tall, piece), BF16),
        pltpu.VMEM((piece, tall), BF16),
        pltpu.VMEM((8, tall), F32),
        pltpu.VMEM((piece, tall), F32),
        pltpu.VMEM((tall, piece), F32),
        pltpu.VMEM((tall, piece), F32),
        pltpu.VMEM((heads, 128, STRIP), F32),
        pltpu.VMEM((heads, 2, 128, FARW), F32),
    )

    def rest(n1, hold, rgrad, resid, first):
        later = [
            pltpu.make_async_copy(n1_h, n1, local.at[7]),
            pltpu.make_async_copy(rgrad_h, rgrad, local.at[8]),
            pltpu.make_async_copy(resid_h, resid, local.at[9]),
        ]
        ready = pltpu.make_async_copy(first_h, first, local.at[4])
        ready.start()
        for a in later:
            a.start()
        sums = SeqScatter(wires, chunks, b0, b1, b2, b3, b4, b5)
        size = rows // chunks
        ready.wait()

        def part(t, c):
            return nt(dqkv[rows_at(t, rows, c * size, size), :], first[:, : 3 * piece])

        for c in range(chunks):
            sums.cross_chunk(c, part(cross, c))
        for c in range(chunks):
            sums.far_chunk(c, part(far_d, c))
        ups.step(1)
        later[0].wait()
        depth = width // nfsdp
        wide = 384
        for n in range(width // wide):
            got = dot_tn(n1[:, n * wide : (n + 1) * wide], dqkv[...])
            for m in range(wide // depth):
                qkv_p[n * (wide // depth) + m] = got[m * depth : (m + 1) * depth, :].astype(BF16)
        for c in range(chunks):
            sums.near_chunk(c, part(near, c))
        for c in range(chunks):
            hold[c * size : (c + 1) * size, :] = part(s, c)
        wsum = total_of(0).astype(BF16)
        lines_f = out_p.shape[1]
        for f in range(nfsdp):
            out_p[f] = wsum[f * lines_f : (f + 1) * lines_f, :]
        qkvs.start()
        gates.finish()
        outs.start()
        gate_keep = pltpu.make_async_copy(gate_s, gate_f.at[s], local.at[11])
        gate_keep.start()
        gate_ring.send(0, gate_s)
        down_ring.forward(0)
        if pairs > 2:
            ups.step(2)
        later[2].wait()
        ybuf[3] = (resid[...] + total_of(1)).astype(BF16)
        loads[4].wait()
        later[1].wait()
        gsum = jnp.zeros((1, width), F32)
        y_keep = pltpu.make_async_copy(ybuf.at[3], y_h, local.at[12])
        y_keep.start()
        for c in range(chunks):
            at = slice(c * size, (c + 1) * size)
            dn = sums.own_chunk(c, hold[at, :])
            x = tok[at, :].astype(F32)
            r = inverse_rms(x)
            gsum = gsum + jnp.sum(dn * x * r, axis=0, keepdims=True)
            tok[at, :] = (rgrad[at, :] + norm_back(dn, x, r, gains[0:1, :])).astype(BF16)
            if c == 0:
                for d in range(3, pairs):
                    ups.step(d)
        in_keep = pltpu.make_async_copy(tok, in_h, local.at[13])
        in_keep.start()
        held[...] = jnp.zeros(held.shape, F32)
        lanes = held.shape[1]
        lines = width // lanes
        for n in range(lines):
            held[n : n + 1, :] = gsum[:, n * lanes : (n + 1) * lanes]
            held[lines + n : lines + n + 1, :] = gain_b[:1, n * lanes : (n + 1) * lanes]
        held[pl.ds(2 * lines + s * 8, 8), :] = tgrad[...]
        ups.finish()
        trips = [wires.go(held, one.at[n], {"seq": t}) for n, t in enumerate((near, far_d, cross))]
        up_keep = pltpu.make_async_copy(up_s, up_f.at[s], local.at[14])
        up_keep.start()
        up_ring.send(0, up_s)
        gate_ring.forward(0)
        qkvs.step(1)
        for a in trips:
            a.wait_recv()
        stage[0] = held[...] + one[0] + one[1] + one[2]
        for d in range(2, pairs):
            qkvs.step(d)
        trips.append(wires.go(stage.at[0], two, {"fsdp": pair * 2 + 1 - side}))
        for d in range(1, pairs):
            outs.step(d)
        trips[-1].wait_recv()
        stage[1] = stage[0] + two[...]
        up_ring.forward(0)
        zs = [
            wires.go(stage.at[1], three.at[d - 1], {"fsdp": lax.rem(pair + d, pairs) * 2 + side})
            for d in range(1, pairs)
        ]
        qkvs.finish()
        qkv_keep = pltpu.make_async_copy(qkv_s, qkv_f.at[s], local.at[15])
        qkv_keep.start()
        qkv_ring.send(0, qkv_s)
        outs.finish()
        out_keep = pltpu.make_async_copy(out_s, out_f.at[s], local.at[16])
        out_keep.start()
        out_ring.send(0, out_s)
        total = stage[1]
        for d, a in enumerate(zs):
            a.wait_recv()
            total = total + three[d]
        small[...] = total
        qkv_ring.forward(0)
        out_ring.forward(0)
        for a in (down_ring, gate_ring, up_ring, qkv_ring, out_ring):
            a.finish()
        sums.finish()
        for a in (gates, ups, qkvs, outs):
            a.drain()
        for a in (gate_keep, up_keep, qkv_keep, out_keep, y_keep, in_keep, down_keep):
            a.wait()
        for a in trips + zs + hops + turns + [far_hop(0), far_hop(1)]:
            a.wait_send()

    pl.run_scoped(
        rest,
        pltpu.VMEM((tall, width), BF16),
        pltpu.VMEM((rows, width), F32),
        pltpu.VMEM((rows, width), F32),
        pltpu.VMEM((rows, width), F32),
        pltpu.VMEM(first_h.shape, BF16),
    )


def back(starts, table, ids, gains, lse, gain_b, q, k, v, o, do, resid, rgrad, tok, y_p, w_p, gate_p, up_p, done, n1, first, chunks=2):
    tall, piece = q.shape
    heads = piece // HEAD_DIM
    rows, width = tok.shape
    nseq = w_p.shape[0]
    nfsdp = gate_p.shape[0]
    pairs = nfsdp // 2
    lines = -(-(2 * width // 128 + 8 * nseq) // 8) * 8
    qkv_shape = (nfsdp, width // nfsdp, 3 * piece)
    out_shape = (nfsdp, w_p.shape[1] // nfsdp, w_p.shape[2])
    smem = pl.BlockSpec(memory_space=pltpu.SMEM)

    def full(a):
        return jax.ShapeDtypeStruct((nseq,) + tuple(a), BF16)

    return pl.pallas_call(
        functools.partial(back_kernel, heads, chunks),
        out_shape=(
            jax.ShapeDtypeStruct((lines, 128), F32),
            jax.ShapeDtypeStruct((rows, width), BF16),
            jax.ShapeDtypeStruct((rows, width), BF16),
            full(done.shape),
            full(gate_p.shape[1:]),
            full(up_p.shape[1:]),
            full(qkv_shape[1:]),
            full(out_shape[1:]),
        ),
        in_specs=[smem, smem] + [vm_spec()] * 9 + [any_spec()] * 10,
        out_specs=(vm_spec(),) + (any_spec(),) * 7,
        scratch_shapes=wires_scratch(6 + 4 * nfsdp + 15 + 3 * chunks + 4 + pairs)
        + [
            pltpu.SemaphoreType.DMA((17,)),
            pltpu.VMEM((5, rows, width), BF16),
            pltpu.VMEM((5,) + w_p.shape[1:], BF16),
            pltpu.VMEM(out_shape, BF16),
            pltpu.VMEM(qkv_shape, BF16),
        ]
        + scatter_scratch(chunks, rows // chunks, width)
        + fsdp_scatter_scratch(gate_p.shape)
        + fsdp_scatter_scratch(up_p.shape)
        + fsdp_scatter_scratch(qkv_shape)
        + fsdp_scatter_scratch(out_shape)
        + [
            pltpu.VMEM(gate_p.shape[1:], BF16),
            pltpu.VMEM(up_p.shape[1:], BF16),
            pltpu.VMEM(qkv_shape[1:], BF16),
            pltpu.VMEM(out_shape[1:], BF16),
            pltpu.VMEM((tall, 3 * piece), BF16),
            pltpu.VMEM((rows, width), BF16),
            pltpu.VMEM((lines, 128), F32),
            pltpu.VMEM((2, lines, 128), F32),
            pltpu.VMEM((3, lines, 128), F32),
            pltpu.VMEM((lines, 128), F32),
            pltpu.VMEM((pairs - 1, lines, 128), F32),
            pltpu.VMEM((8, 128), F32),
        ],
        compiler_params=call_params(5, 64),
        name="back",
    )(starts, table, ids, gains, lse, gain_b, q, k, v, o, do, resid, rgrad, tok, y_p, w_p, gate_p, up_p, done, n1, first)


def unpack_kernel(
    nseq, nfsdp, gate_f, up_f, down_f, qkv_f, out_f, gq, gk, gv, go, gg, gu, gd, sems, tq, tk, tv, to, tg, tu, td
):
    copies = []

    def save(src, dst):
        copies.append(pltpu.make_async_copy(src, dst, sems.at[len(copies)]))
        copies[-1].start()

    total = tg.shape[1]
    block, piece = pack_piece(total, nfsdp, nseq)
    for full, dst, out in ((gate_f, tg, gg), (up_f, tu, gu)):
        parts = []
        for f in range(nfsdp):
            for t in range(nseq):
                size = min(piece, block - t * piece)
                parts.append(full[t, :, f * piece : f * piece + size].astype(F32))
        dst[...] = jnp.concatenate(parts, axis=1)
        save(dst, out)
    size = down_f.shape[1]
    for t in range(nseq):
        count = min(size, td.shape[0] - t * size)
        td[t * size : t * size + count, :] = down_f[t, :count, :].astype(F32)
    save(td, gd)
    width = qkv_f.shape[2] // 3
    for n, (dst, out) in enumerate(((tq, gq), (tk, gk), (tv, gv))):
        dst[...] = jnp.concatenate([qkv_f[t, :, n * width : (n + 1) * width] for t in range(nseq)], axis=1).astype(F32)
        save(dst, out)
    to[...] = jnp.concatenate([out_f[t] for t in range(nseq)], axis=1).astype(F32)
    save(to, go)
    for a in copies:
        a.wait()


def unpack(gate_f, up_f, down_f, qkv_f, out_f, like, nfsdp):
    nseq = gate_f.shape[0]
    return pl.pallas_call(
        functools.partial(unpack_kernel, nseq, nfsdp),
        out_shape=tuple(jax.ShapeDtypeStruct(a.shape, F32) for a in like),
        in_specs=[vm_spec()] * 5,
        out_specs=(any_spec(),) * 7,
        scratch_shapes=[pltpu.SemaphoreType.DMA((7,))] + [pltpu.VMEM(a.shape, F32) for a in like],
        compiler_params=pltpu.CompilerParams(vmem_limit_bytes=32 << 20),
        name="unpack",
    )(gate_f, up_f, down_f, qkv_f, out_f)


def reversed_ids(bucket_ids):
    span = bucket_ids.shape[0]
    ids = jnp.concatenate([bucket_ids[::-1], jnp.full((1,), -1, jnp.int32)])
    return jnp.broadcast_to(ids[None, :], (8, span + 1))


def dot32(a, b):
    return jnp.dot(a, b, preferred_element_type=F32)


def dot_tn(a, b):
    return lax.dot_general(a, b, (((0,), (0,)), ((), ())), preferred_element_type=F32)


def gelu_both(u):
    inner = 0.7978845608028654 * (u + 0.044715 * u * u * u)
    t = jnp.tanh(inner)
    value = 0.5 * u * (1.0 + t)
    slope = 0.5 * (1.0 + t) + 0.5 * u * (1.0 - t * t) * 0.7978845608028654 * (1.0 + 3 * 0.044715 * u * u)
    return value, slope


def body(
    tokens,
    out_grad,
    attn_gain,
    w_query,
    w_key,
    w_value,
    w_out,
    mix_gain,
    w_gate,
    w_up,
    w_down,
    rel_table,
    bucket_ids,
    cont_start,
):
    nseq = lax.axis_size("seq")
    nfsdp = lax.axis_size("fsdp")
    mine = lax.axis_index("seq")
    where = lax.axis_index("fsdp")
    rows, width = tokens.shape[1:]
    inner = w_query.shape[1]
    piece = inner // nseq
    heads = piece // HEAD_DIM

    table = lax.dynamic_slice_in_dim(rel_table, mine * heads, heads, 1)
    ids = reversed_ids(bucket_ids)
    starts = cont_start[0]
    query, keys, values, mixed, lse, gains, normed, first, out_w, cot, gate_w, up_q, down_q = front(
        starts,
        table,
        ids,
        attn_gain[None],
        mix_gain[None],
        tokens[0],
        w_query,
        w_key,
        w_value,
        w_out,
        w_gate,
        w_up,
        w_down,
        out_grad[0],
        nseq,
        nfsdp,
    )
    out_w = out_w.reshape(nseq, inner, -1)
    mixed_rows, resid, normed_two, hidden, gate_grad, up_grad, up_w, down_w, down_grad = middle(
        mixed, out_w, tokens[0], gains, up_q, down_q, gate_w, cot, nfsdp
    )
    resid_grad, mixed_grad, gain_two_grad, down_grad, out_w_grad, gate_w_grad, up_w_grad, result = unmix(
        gains, mixed_rows, resid, out_grad[0], down_grad, gate_grad, up_grad, gate_w, up_w, out_w, normed_two, hidden, down_w
    )
    small, block_out, in_grad, down_grad, gate_w_grad, up_w_grad, qkv_grad, out_w_grad = back(
        starts,
        table,
        ids,
        gains,
        lse,
        gain_two_grad,
        query,
        keys,
        values,
        mixed,
        mixed_grad,
        resid,
        resid_grad,
        tokens[0],
        result,
        out_w_grad,
        gate_w_grad,
        up_w_grad,
        down_grad,
        normed,
        first,
    )
    buckets = rel_table.shape[0]
    shards = unpack(
        gate_w_grad,
        up_w_grad,
        down_grad,
        qkv_grad,
        out_w_grad,
        (w_query, w_key, w_value, w_out, w_gate, w_up, w_down),
        nfsdp,
    )
    lines = width // 128
    share = width // nfsdp
    gain_one_share = lax.dynamic_slice_in_dim(small[:lines].reshape(-1), where * share, share)
    gain_two_share = lax.dynamic_slice_in_dim(small[lines : 2 * lines].reshape(-1), where * share, share)
    tables = small[2 * lines : 2 * lines + 8 * nseq].reshape(nseq, 8, 128)[:, :heads, :buckets]
    table_grad = tables.reshape(nseq * heads, buckets).T
    return (
        block_out[None],
        in_grad[None],
        gain_one_share,
        *shards[:4],
        gain_two_share,
        *shards[4:],
        table_grad,
    )


def solution(mesh):
    placed = (
        P("fsdp", "seq", None),
        P("fsdp", "seq", None),
        P("fsdp"),
        P("fsdp", None),
        P("fsdp", None),
        P("fsdp", None),
        P("fsdp", None),
        P("fsdp"),
        P("fsdp", None),
        P("fsdp", None),
        P("fsdp", None),
        P(),
        P(),
        P("fsdp", None),
    )
    results = placed[:1] * 2 + placed[2:11] + (P(),)
    return jax.shard_map(body, mesh=mesh, in_specs=placed, out_specs=results, check_vma=False)
```

```python
import functools
import jax
import jax.numpy as jnp
from jax import lax
from jax.experimental import pallas as pl
from jax.experimental.pallas import tpu as pltpu
from jax.sharding import PartitionSpec as P

HEAD_DIM = 64
PROMPT = 1024
CL = 256
F32 = jnp.float32
BF16 = jnp.bfloat16
MESH = pl.DeviceIdType.MESH
epsilon = 1e-06
STRIP = 2 * PROMPT - 128
FARW = PROMPT - 128 + CL
KC = 256


def nt(a, b):
    return lax.dot_general(a, b, (((1,), (1,)), ((), ())), preferred_element_type=F32)


def nn(a, b):
    return lax.dot_general(a, b, (((1,), (0,)), ((), ())), preferred_element_type=F32)


class Wires:
    def __init__(self, send, recv):
        self.send, self.recv, self.used = send, recv, 0

    def take(self, count):
        self.used += count
        return self.used - count

    def at(self, i, src, dst, where):
        return pltpu.make_async_remote_copy(
            src_ref=src,
            dst_ref=dst,
            send_sem=self.send.at[i],
            recv_sem=self.recv.at[i],
            device_id=where,
            device_id_type=MESH,
        )

    def go(self, src, dst, where):
        c = self.at(self.take(1), src, dst, where)
        c.start()
        return c


def seq_places():
    s = lax.axis_index("seq")
    near = s + 1 - 2 * lax.rem(s, 2)
    far = lax.rem(s + 2, 4)
    cross = lax.rem(near + 2, 4)
    return s, near, far, cross


def meet(places):
    barrier = pltpu.get_barrier_semaphore()
    for where in places:
        pl.semaphore_signal(barrier, inc=1, device_id=where, device_id_type=MESH)
    pl.semaphore_wait(barrier, len(places))


def rows_at(index, rows, offset=0, count=None):
    return pl.ds(pl.multiple_of(index * rows + offset, 16), rows if count is None else count)


class SeqGather:
    def __init__(self, wires, out_at, chunks):
        self.wires, self.out_at, self.chunks = wires, out_at, chunks
        self.s, self.near, self.far, self.cross = seq_places()
        self.base = wires.take(3 * chunks)

    def trip(self, kind, c, src=None):
        view = self.out_at(self.far if kind == 2 else self.s, c)
        where = {"seq": self.far if kind == 0 else self.near}
        return self.wires.at(self.base + 3 * c + kind, view if src is None else src, view, where)

    def send(self, c, src):
        self.trip(0, c, src).start()
        self.trip(1, c, src).start()

    def forward(self, c):
        self.trip(0, c).wait_recv()
        self.trip(2, c).start()

    def got_near(self, c):
        self.trip(1, c).wait_recv()

    def got_cross(self, c):
        self.trip(2, c).wait_recv()

    def drain(self):
        for c in range(self.chunks):
            for kind in range(3):
                self.trip(kind, c).wait_send()

    def finish(self):
        for c in range(self.chunks):
            self.got_near(c)
            self.got_cross(c)
        self.drain()


def fsdp_places():
    f = lax.axis_index("fsdp")
    return f // 2, lax.rem(f, 2), lax.axis_size("fsdp") // 2


def fsdp_peers():
    pair, side, pairs = fsdp_places()
    peers = [{"fsdp": lax.rem(pair + d, pairs) * 2 + side} for d in range(1, pairs)]
    return peers + [{"fsdp": pair * 2 + 1 - side}]


class FsdpGather:
    def __init__(self, wires, shard, full_at, local):
        self.wires, self.shard, self.full_at, self.local = wires, shard, full_at, local
        self.pair, self.side, self.pairs = fsdp_places()
        self.base = wires.take(2 * self.pairs)

    def source(self, d):
        return lax.rem(self.pair + self.pairs - d, self.pairs)

    def out(self, d):
        own = self.full_at(self.pair * 2 + self.side)
        if d == 0:
            return self.wires.at(self.base, self.shard, own, {"fsdp": self.pair * 2 + 1 - self.side})
        where = {"fsdp": lax.rem(self.pair + d, self.pairs) * 2 + self.side}
        return self.wires.at(self.base + d, self.shard, own, where)

    def onward(self, d):
        view = self.full_at(self.source(d) * 2 + self.side)
        return self.wires.at(self.base + self.pairs + d, view, view, {"fsdp": self.pair * 2 + 1 - self.side})

    def keep(self):
        return pltpu.make_async_copy(self.shard, self.full_at(self.pair * 2 + self.side), self.local)

    def start(self):
        self.out(0).start()
        for d in range(1, self.pairs):
            self.out(d).start()
        self.keep().start()

    def forward(self, d):
        self.out(d).wait_recv()
        self.onward(d).start()

    def complete(self, d):
        if d == 0:
            self.keep().wait()
            self.out(0).wait_recv()
        else:
            self.onward(d).wait_recv()

    def drain(self):
        for d in range(self.pairs):
            self.out(d).wait_send()
        for d in range(1, self.pairs):
            self.onward(d).wait_send()

    def finish(self):
        for d in range(self.pairs):
            self.complete(d)
        self.drain()


def gather_halves(wires, shard, full, size, local):
    half = shard.shape[1] // 2

    def one(n):
        cut = slice(n * half, (n + 1) * half)
        return FsdpGather(wires, shard.at[:, cut], lambda f: full.at[shard_rows(f, size), cut], local[n])

    return [one(0), one(1)]


class FsdpScatter:
    def __init__(self, wires, parts, bufs, result):
        self.wires, self.parts_at, self.result = wires, lambda f: parts.at[f], result
        self.mine, self.got, self.landed, self.local = bufs
        self.pair, self.side, self.pairs = fsdp_places()
        self.base = wires.take(2 * self.pairs)

    def owner(self, d):
        return lax.rem(self.pair + d, self.pairs) * 2

    def load(self, d):
        slot = d % 2
        return pltpu.make_async_copy(self.parts_at(self.owner(d) + self.side), self.mine.at[slot], self.local.at[slot])

    def swap(self, d):
        src = self.parts_at(self.owner(d) + 1 - self.side)
        return self.wires.at(self.base + d, src, self.got.at[d], {"fsdp": self.pair * 2 + 1 - self.side})

    def onward(self, d):
        where = {"fsdp": self.owner(d) + self.side}
        return self.wires.at(self.base + self.pairs + d, self.got.at[d], self.landed.at[d - 1], where)

    def start(self):
        for d in list(range(1, self.pairs)) + [0]:
            self.swap(d).start()
        self.load(1).start()

    def step(self, d):
        self.load((d + 1) % self.pairs).start()
        self.load(d).wait()
        self.swap(d).wait_recv()
        self.got[d] = (self.mine[d % 2].astype(F32) + self.got[d].astype(F32)).astype(BF16)
        self.onward(d).start()

    def finish(self):
        self.load(0).wait()
        self.swap(0).wait_recv()
        total = self.mine[0].astype(F32) + self.got[0].astype(F32)
        for d in range(1, self.pairs):
            self.onward(d).wait_recv()
            total = total + self.landed[d - 1].astype(F32)
        self.result[...] = total.astype(BF16)

    def drain(self):
        for d in range(self.pairs):
            self.swap(d).wait_send()
        for d in range(1, self.pairs):
            self.onward(d).wait_send()


def fsdp_scatter_scratch(shape):
    pairs = shape[0] // 2
    return [
        pltpu.VMEM((2,) + shape[1:], BF16),
        pltpu.VMEM((pairs,) + shape[1:], BF16),
        pltpu.VMEM((pairs - 1,) + shape[1:], BF16),
        pltpu.SemaphoreType.DMA((2,)),
    ]


def blocks(a, count):
    return a.reshape((count, a.shape[0] // count) + a.shape[1:])


def shard_rows(f, size):
    return pl.ds(pl.multiple_of(f * size, 16 if size % 16 == 0 else 8 if size % 8 == 0 else size), size)


def vm_spec():
    return pl.BlockSpec(memory_space=pltpu.VMEM)


def any_spec():
    return pl.BlockSpec(memory_space=pl.ANY)


def wires_scratch(n):
    return [pltpu.SemaphoreType.DMA((n,)), pltpu.SemaphoreType.DMA((n,))]


def call_params(number, vmem=60):
    return pltpu.CompilerParams(collective_id=number, has_side_effects=True, vmem_limit_bytes=min(vmem << 20, 67043328))


def inverse_rms(v):
    return lax.rsqrt(jnp.mean(v * v, axis=-1, keepdims=True) + epsilon)


def norm_back(grad, v, r, gain):
    scaled = grad * gain
    return r * scaled - v * (r * r * r) * jnp.mean(v * scaled, axis=-1, keepdims=True)


def middle_kernel(
    o, out_w, tok, gains, up_q, down_q, gate_h, cot_h,
    obuf, resid, n2_h, hid_h, dg_h, du_h, up_h, down_h, parts_h,
    send, recv, local, own, n2, cot, gate_w, up_w, down_w, ga, ub, hid, dg, du, parts,
):
    rows, width = tok.shape
    piece = o.shape[1]
    nseq = obuf.shape[0]
    units = gate_w.shape[1]
    nfsdp = parts.shape[0]
    s, near, far, cross = seq_places()
    loads = [pltpu.make_async_copy(gate_h, gate_w, local.at[0]), pltpu.make_async_copy(cot_h, cot, local.at[1])]
    for a in loads:
        a.start()
    meet([{"seq": near}, {"seq": far}, {"seq": cross}] + fsdp_peers())
    wires = Wires(send, recv)
    trips = [wires.go(o.at[rows_at(t, rows), :], obuf.at[s], {"seq": t}) for t in (far, cross, near)]
    up_size, down_size = up_q.shape[0], down_q.shape[0]
    ups = gather_halves(wires, up_q, up_w, up_size, (local.at[2], local.at[11]))
    downs = gather_halves(wires, down_q, down_w, down_size, (local.at[3], local.at[12]))
    for a in ups + downs:
        a.start()
    pairs = ups[0].pairs
    todo = [(a, d) for a in ups + downs for d in range(1, pairs)]

    def pass_on(share):
        while todo and len(todo) > round((1 - share) * 4 * (pairs - 1)):
            a, d = todo.pop(0)
            a.forward(d)

    obuf[s] = o[rows_at(s, rows), :]
    half = rows // 2
    for a in trips:
        a.wait_recv()
    pass_on(1 / 12)
    ring = SeqGather(wires, lambda t, c: n2.at[rows_at(t, rows, c * half, half), :], 2)
    cols = out_w.shape[2]
    for c in range(2):
        part = slice(c * half, (c + 1) * half)
        for u in range(nseq):
            acc = tok[part, u * cols : (u + 1) * cols].astype(F32)
            for t in range(nseq):
                acc = acc + nn(obuf[t, part, :], out_w[u, t * piece : (t + 1) * piece, :])
            resid[part, u * cols : (u + 1) * cols] = acc
        h = resid[part, :]
        low = (h * inverse_rms(h) * gains[1:2, :]).astype(BF16)
        own[part, :] = low
        n2[rows_at(s, rows, c * half, half), :] = low
        ring.send(c, own.at[pl.ds(c * half, half), :])
    loads[0].wait()

    def gate_rows(t):
        ga[rows_at(t, rows), :] = nn(n2[rows_at(t, rows), :], gate_w[...])

    def act_rows(t):
        up = nn(n2[rows_at(t, rows), :], up_w[...])
        active, slope = gelu_both(ga[rows_at(t, rows), :])
        hid[rows_at(t, rows), :] = (active * up).astype(BF16)
        ga[rows_at(t, rows), :] = slope * up
        ub[rows_at(t, rows), :] = active

    pass_on(2 / 12)
    gate_rows(s)
    ring.got_near(0)
    ring.got_near(1)
    pass_on(3 / 12)
    gate_rows(near)
    pass_on(5 / 12)
    ring.forward(0)
    pass_on(6 / 12)
    ring.forward(1)
    pass_on(7 / 12)
    gate_rows(far)
    for c in range(2):
        ring.got_cross(c)
    gate_rows(cross)
    saves = [pltpu.make_async_copy(n2, n2_h, local.at[4])]
    saves[0].start()
    for a in ups:
        for d in range(pairs):
            a.complete(d)
    saves.append(pltpu.make_async_copy(up_w, up_h, local.at[5]))
    saves[1].start()
    pass_on(8 / 12)
    for t in (s, near):
        act_rows(t)
    pass_on(9 / 12)
    for t in (far, cross):
        act_rows(t)
    saves.append(pltpu.make_async_copy(hid, hid_h, local.at[6]))
    saves[2].start()
    loads[1].wait()
    pass_on(10 / 12)
    width_f = units // nfsdp
    wide = max(256 // width_f, 1)

    def down_part(n):
        got = dot_tn(hid[:, n * wide * width_f : (n + 1) * wide * width_f], cot[...]).astype(BF16)
        for m in range(wide):
            parts[n * wide + m] = got[m * width_f : (m + 1) * width_f, :]

    for n in range(nfsdp // wide):
        down_part(n)
        if n == 1:
            pass_on(11 / 12)
    saves.append(pltpu.make_async_copy(parts, parts_h, local.at[7]))
    saves[3].start()
    pass_on(1)

    def back_cols(at, units_at):
        for t in range(nseq):
            band = slice(t * rows, (t + 1) * rows)
            dh = nt(cot[band, :], down_w[units_at, :])
            dg[band, at] = (dh * ga[band, at]).astype(BF16)
            du[band, at] = (dh * ub[band, at]).astype(BF16)

    if (2 * width_f) % 128 == 0:
        for d in range(pairs):
            for a in downs:
                a.complete(d)
            at = pl.ds(pl.multiple_of(downs[0].source(d) * 2 * width_f, 2 * width_f), 2 * width_f)
            back_cols(at, at)
    else:
        for d in range(pairs):
            for a in downs:
                a.complete(d)
        for n in range(units // 256):
            at = slice(n * 256, (n + 1) * 256)
            back_cols(at, at)
    saves.append(pltpu.make_async_copy(down_w, down_h, local.at[8]))
    saves.append(pltpu.make_async_copy(dg, dg_h, local.at[9]))
    saves.append(pltpu.make_async_copy(du, du_h, local.at[10]))
    for a in saves[4:]:
        a.start()
    ring.drain()
    for a in ups + downs:
        a.drain()
    for a in trips:
        a.wait_send()
    for a in saves:
        a.wait()


def middle(o, out_w, tok, gains, up_q, down_q, gate_w, cot, nfsdp):
    nseq = out_w.shape[0]
    rows, width = tok.shape
    units = gate_w.shape[1]
    tall = nseq * rows
    return pl.pallas_call(
        middle_kernel,
        out_shape=(
            jax.ShapeDtypeStruct((nseq, rows, o.shape[1]), BF16),
            jax.ShapeDtypeStruct((rows, width), F32),
            jax.ShapeDtypeStruct((tall, width), BF16),
            jax.ShapeDtypeStruct((tall, units), BF16),
            jax.ShapeDtypeStruct((tall, units), BF16),
            jax.ShapeDtypeStruct((tall, units), BF16),
            jax.ShapeDtypeStruct((width, units), BF16),
            jax.ShapeDtypeStruct((units, width), BF16),
            jax.ShapeDtypeStruct((nfsdp, units // nfsdp, width), BF16),
        ),
        in_specs=[vm_spec()] * 4 + [any_spec()] * 4,
        out_specs=(vm_spec(), vm_spec()) + (any_spec(),) * 7,
        scratch_shapes=wires_scratch(9 + 4 * nfsdp)
        + [
            pltpu.SemaphoreType.DMA((13,)),
            pltpu.VMEM((rows, width), BF16),
            pltpu.VMEM((tall, width), BF16),
            pltpu.VMEM((tall, width), BF16),
            pltpu.VMEM((width, units), BF16),
            pltpu.VMEM((width, units), BF16),
            pltpu.VMEM((units, width), BF16),
            pltpu.VMEM((tall, units), F32),
            pltpu.VMEM((tall, units), F32),
            pltpu.VMEM((tall, units), BF16),
            pltpu.VMEM((tall, units), BF16),
            pltpu.VMEM((tall, units), BF16),
            pltpu.VMEM((nfsdp, units // nfsdp, width), BF16),
        ],
        compiler_params=call_params(2, 63),
        name="middle",
    )(o, out_w, tok, gains, up_q, down_q, gate_w, cot)


class SeqScatter:
    def __init__(self, wires, chunks, *bufs):
        self.s, self.near, self.far, self.cross = seq_places()
        self.wires, self.chunks, self.bufs = wires, chunks, bufs
        self.base = wires.take(3 * chunks)

    def trip(self, kind, c):
        where = {"seq": self.far if kind == 1 else self.near}
        src, dst = self.bufs[2 * kind].at[c], self.bufs[2 * kind + 1].at[c]
        return self.wires.at(self.base + 3 * c + kind, src, dst, where)

    def cross_chunk(self, c, value):
        self.bufs[0][c] = value.astype(BF16)
        self.trip(0, c).start()

    def far_chunk(self, c, value):
        self.trip(0, c).wait_recv()
        self.bufs[2][c] = (value + self.bufs[1][c].astype(F32)).astype(BF16)
        self.trip(1, c).start()

    def near_chunk(self, c, value):
        self.bufs[4][c] = value.astype(BF16)
        self.trip(2, c).start()

    def own_chunk(self, c, value):
        self.trip(2, c).wait_recv()
        self.trip(1, c).wait_recv()
        return value + self.bufs[5][c].astype(F32) + self.bufs[3][c].astype(F32)

    def finish(self):
        for c in range(self.chunks):
            for kind in range(3):
                self.trip(kind, c).wait_send()


def scatter_scratch(chunks, rows, width):
    return [pltpu.VMEM((chunks, rows, width), BF16)] * 6


def unmix_kernel(
    chunks, gains, obuf, resid, cot, down_p, dg_h, du_h, gate_h, up_h, out_h, n2_h, hid_h, dw_h,
    rgrad, dmix, ggrad, shard, lead_s, wgrad_h, gate_p, up_p, y_h,
    send, recv, b0, b1, b2, b3, b4, b5, attn, dob, p0, p1, p2, p3, l0, l1, l2, l3, lead_p,
    local, dg, du, gate_w, up_w, out_w, n2, hid, down_w, wgrad, stage, ystage, sems,
):
    rows, width = resid.shape
    nseq, _, piece = obuf.shape
    nfsdp = gate_p.shape[0]
    units = dg.shape[1]
    first_half = units // 2
    s, near, far, cross = seq_places()
    loads = [
        pltpu.make_async_copy(src, dst, local.at[n])
        for n, (src, dst) in enumerate(
            (
                (gate_h, gate_w),
                (up_h, up_w),
                (dg_h, dg),
                (du_h, du),
                (n2_h, n2),
                (out_h, out_w),
                (hid_h, hid),
                (dw_h, down_w),
            )
        )
    ]
    for a in loads:
        a.start()
    meet([{"seq": near}, {"seq": far}, {"seq": cross}] + fsdp_peers())
    wires = Wires(send, recv)
    grads = FsdpScatter(wires, down_p, (p0, p1, p2, p3), shard)
    grads.start()
    leads = FsdpScatter(wires, lead_p, (l0, l1, l2, l3), lead_s)
    pairs = grads.pairs
    sums = SeqScatter(wires, chunks, b0, b1, b2, b3, b4, b5)
    size = rows // chunks
    for a in loads[:4]:
        a.wait()

    def part(t, c):
        at = rows_at(t, rows, c * size, size)
        return nt(dg[at, :], gate_w[...]) + nt(du[at, :], up_w[...])

    for c in range(chunks):
        sums.cross_chunk(c, part(cross, c))
    for c in range(chunks):
        sums.far_chunk(c, part(far, c))
    for c in range(chunks):
        sums.near_chunk(c, part(near, c))
    for c in range(chunks):
        rgrad[c * size : (c + 1) * size, :] = part(s, c)
    grads.step(1)
    loads[4].wait()
    depth = width // nfsdp
    wide = 384
    saves = []

    def weight_parts(side, out, begin, end, cut):
        for n in range(begin, end):
            slot = n % 2
            group = pl.ds(n * (wide // depth), wide // depth)
            if len(saves) > 1:
                saves[-2].wait()
            got = dot_tn(n2[:, n * wide : (n + 1) * wide], side[...])
            for m in range(wide // depth):
                low = got[m * depth : (m + 1) * depth, :].astype(BF16)
                if cut:
                    lead_p[n * (wide // depth) + m] = low[:, :cut]
                stage[slot, m, :, : units - cut] = low[:, cut:]
            a = pltpu.make_async_copy(stage.at[slot, :, :, : units - cut], out.at[group], sems.at[3 + slot])
            a.start()
            saves.append(a)

    weight_parts(dg, gate_p, 0, width // wide, first_half)
    if pairs > 2:
        grads.step(2)
    loads[5].wait()
    cols = out_w.shape[2]

    def own_rows(c, total):
        at = slice(c * size, (c + 1) * size)
        dn = sums.own_chunk(c, rgrad[at, :])
        h = resid[at, :]
        r = inverse_rms(h)
        rg = cot[at, :].astype(F32) + norm_back(dn, h, r, gains[1:2, :])
        rgrad[at, :] = rg
        low = rg.astype(BF16)
        attn[at, :] = low
        for t in range(nseq):
            acc = jnp.zeros((size, piece), F32)
            for u in range(nseq):
                acc = acc + nt(low[:, u * cols : (u + 1) * cols], out_w[u, t * piece : (t + 1) * piece, :])
            dob[t, at, :] = acc.astype(BF16)
        return total + jnp.sum(dn * h * r, axis=0, keepdims=True)

    base = wires.take(3 * chunks)

    def trip(n, t, c):
        at = pl.ds(c * size, size)
        return wires.at(base + 3 * c + n, dob.at[t, at, :], dmix.at[rows_at(s, rows, c * size, size), :], {"seq": t})

    total = jnp.zeros((1, width), F32)
    for c in range(chunks):
        total = own_rows(c, total)
        if c == 0:
            weight_parts(du, up_p, 0, 1, 0)
            leads.start()
        for n, t in enumerate((far, cross, near)):
            trip(n, t, c).start()
        dmix[rows_at(s, rows, c * size, size), :] = dob[s, pl.ds(c * size, size), :]
        if c == 0:
            weight_parts(du, up_p, 1, width // wide, 0)
            for d in range(3, pairs):
                grads.step(d)
    ggrad[...] = jnp.broadcast_to(total, ggrad.shape)
    for t in range(nseq):
        for u in range(nseq):
            wgrad[u, t * piece : (t + 1) * piece, :] = dot_tn(obuf[t], attn[:, u * cols : (u + 1) * cols]).astype(BF16)
    last = pltpu.make_async_copy(wgrad, wgrad_h, sems.at[2])
    last.start()
    leads.step(1)
    for a in loads[6:]:
        a.wait()
    ycopies = []
    for t in range(nseq):
        slot = t % 2
        if t > 1:
            ycopies[t - 2].wait()
        at = slice(t * rows, (t + 1) * rows)
        ystage[slot] = nn(hid[at, :], down_w[...]).astype(BF16)
        ycopies.append(pltpu.make_async_copy(ystage.at[slot], y_h.at[at, :], sems.at[slot]))
        ycopies[t].start()
        if t == 1:
            grads.finish()
            for d in range(2, pairs - 1):
                leads.step(d)
    for c in range(chunks):
        for n, t in enumerate((far, cross, near)):
            trip(n, t, c).wait()
    if pairs > 2:
        leads.step(pairs - 1)
    sums.finish()
    grads.drain()
    leads.finish()
    leads.drain()
    for a in saves[-2:]:
        a.wait()
    for a in ycopies[-2:] + [last]:
        a.wait()


def unmix(gains, obuf, resid, cot, down_p, dg, du, gate_w, up_w, out_w, n2, hid, down_w, chunks=2):
    rows, width = resid.shape
    nseq, _, piece = obuf.shape
    nfsdp = down_p.shape[0]
    units = dg.shape[1]
    grad_shape = (nfsdp, width // nfsdp, units)
    half_shape = (nfsdp, width // nfsdp, units // 2)
    return pl.pallas_call(
        functools.partial(unmix_kernel, chunks),
        out_shape=(
            jax.ShapeDtypeStruct((rows, width), F32),
            jax.ShapeDtypeStruct((nseq * rows, piece), BF16),
            jax.ShapeDtypeStruct((8, width), F32),
            jax.ShapeDtypeStruct(down_p.shape[1:], BF16),
            jax.ShapeDtypeStruct(half_shape[1:], BF16),
            jax.ShapeDtypeStruct(out_w.shape, BF16),
            jax.ShapeDtypeStruct(half_shape, BF16),
            jax.ShapeDtypeStruct(grad_shape, BF16),
            jax.ShapeDtypeStruct(n2.shape, BF16),
        ),
        in_specs=[vm_spec()] * 4 + [any_spec()] * 9,
        out_specs=(vm_spec(),) * 5 + (any_spec(),) * 4,
        scratch_shapes=wires_scratch(6 * chunks + 2 * nfsdp)
        + scatter_scratch(chunks, rows // chunks, width)
        + [pltpu.VMEM((rows, width), BF16), pltpu.VMEM((nseq, rows, piece), BF16)]
        + fsdp_scatter_scratch(down_p.shape)
        + fsdp_scatter_scratch(half_shape)
        + [
            pltpu.VMEM(half_shape, BF16),
            pltpu.SemaphoreType.DMA((8,)),
            pltpu.VMEM(dg.shape, BF16),
            pltpu.VMEM(du.shape, BF16),
            pltpu.VMEM(gate_w.shape, BF16),
            pltpu.VMEM(up_w.shape, BF16),
            pltpu.VMEM(out_w.shape, BF16),
            pltpu.VMEM(n2.shape, BF16),
            pltpu.VMEM(hid.shape, BF16),
            pltpu.VMEM(down_w.shape, BF16),
            pltpu.VMEM(out_w.shape, BF16),
            pltpu.VMEM((2, 384 * nfsdp // width, width // nfsdp, units), BF16),
            pltpu.VMEM((2, rows, width), BF16),
            pltpu.SemaphoreType.DMA((5,)),
        ],
        compiler_params=call_params(4, 63),
        name="unmix",
    )(gains, obuf, resid, cot, down_p, dg, du, gate_w, up_w, out_w, n2, hid, down_w)


def build_strips(heads, first_head, starts, table, ids, strip, far):
    length = ids.shape[1]
    half = 2 * PROMPT
    for h in range(heads):
        row = jnp.zeros(ids.shape, F32)
        for b in range(table.shape[0]):
            row = jnp.where(ids[...] == b, table[b, first_head + h], row)
        row = jnp.broadcast_to(row, (8, length))
        base = jnp.broadcast_to(row[:1, PROMPT // 2 : PROMPT // 2 + half], (128, half))
        strip[h] = pltpu.roll(base, 1, 1, stride=1, stride_axis=0)[:, 128:]
        for c in range(2):
            moved = pltpu.roll(row, length - PROMPT // 2 - starts[c], 1)
            base = jnp.broadcast_to(moved[:1, : FARW + 128], (128, FARW + 128))
            far[h, c] = pltpu.roll(base, 1, 1, stride=1, stride_axis=0)[:, 128:]


def head_masks(width, heads):
    lane = lax.broadcasted_iota(jnp.int32, (1, width), 1)
    return [(lane >= h * HEAD_DIM) & (lane < (h + 1) * HEAD_DIM) for h in range(heads)]


def masked_copies(src, dst, heads):
    masks = head_masks(src.shape[1], heads)
    for h in range(heads):
        dst[h] = jnp.where(masks[h], src[...], jnp.zeros((), src.dtype))


def bias_chunk(strip, far, h, first_q, kstart, kind, c):
    parts = []
    for r in range(KC // 128):
        m = PROMPT - 128 - (kstart + 128 * r)
        if kind == "far":
            parts.append(far[h, c, :, m : m + CL])
        else:
            parts.append(strip[h, :, pl.ds(pl.multiple_of(first_q + m, 128), CL)])
    return jnp.concatenate(parts, axis=0)


def pack_piece(units, nfsdp, nseq):
    block = units // nfsdp
    return block, -(-block // (16 * nseq)) * 16


def pack_front(t, raw, first_q, out_q, gains):
    r_q, r_k, r_v, r_o = raw
    piece = first_q.shape[1] * 3 // 10
    depth = first_q.shape[0]
    cut = slice(t * piece, (t + 1) * piece)
    first_q[...] = jnp.concatenate(
        [r_q[:, cut], r_k[:, cut], r_v[:, cut], gains, jnp.zeros((depth, first_q.shape[1] - 3 * piece - 8), BF16)], axis=1
    )
    cols = out_q.shape[1]
    out_q[...] = r_o[:, t * cols : (t + 1) * cols]


def pack_cols(t, nseq, nfsdp, raw, packed):
    block, piece = pack_piece(raw.shape[1], nfsdp, nseq)
    pieces = []
    for f in range(nfsdp):
        begin = f * block + t * piece
        end = min(begin + piece, (f + 1) * block)
        pieces.append(raw[:, begin:end])
        if end - begin < piece:
            pieces.append(jnp.zeros((raw.shape[0], piece - end + begin), BF16))
    packed[...] = jnp.concatenate(pieces, axis=1)


def pack_down(t, raw, packed):
    piece = packed.shape[0]
    begin = t * piece
    end = min(begin + piece, raw.shape[0])
    packed[: end - begin, :] = raw[begin:end, :]
    if end - begin < piece:
        packed[end - begin :, :] = jnp.zeros((piece - end + begin, raw.shape[1]), BF16)


def front_kernel(
    heads, nseq, starts, table, ids, gain_q, tok, w_q, w_k, w_v, w_o, w_g, w_u, w_d, cot,
    q, k, v, o, lse, gains, n1_h, first_h, out_w, cots, gate_w, up_q, down_q,
    send, recv, local, r_q, r_k, r_v, r_o, r_g, r_u, r_d, first_q, out_q, gate_q, up_s, down_s,
    group, n1, first, strip, far, kh, vt, ot, s,
):
    rows, width = tok.shape
    mine, near, other, cross = seq_places()
    pair, side, pairs = fsdp_places()
    nfsdp = 2 * pairs
    loads = [
        pltpu.make_async_copy(src, dst, local.at[n])
        for n, (src, dst) in enumerate(
            ((w_q, r_q), (w_k, r_k), (w_v, r_v), (w_o, r_o), (w_g, r_g), (w_u, r_u), (w_d, r_d))
        )
    ]
    for a in loads:
        a.start()
    meet([{"seq": near}, {"seq": other}] + fsdp_peers())
    wires = Wires(send, recv)
    half = rows // 2
    ring = SeqGather(wires, lambda t, c: group.at[rows_at(t, rows, c * half, half), :], 2)
    size = first_q.shape[0]
    lead = FsdpGather(wires, first_q, lambda f: first.at[shard_rows(f, size), :], local.at[7])
    late = FsdpGather(wires, out_q, lambda f: out_w.at[mine, f], local.at[8])
    gate_size = gate_q.shape[0]
    weights = gather_halves(wires, gate_q, gate_w, gate_size, (local.at[9], local.at[16]))
    wring = SeqGather(wires, lambda t, c: out_w.at[t], 1)
    cring = SeqGather(wires, lambda t, c: cots.at[rows_at(t, rows, c * half, half), :], 2)
    own = [
        pltpu.make_async_copy(tok, group.at[rows_at(mine, rows), :], local.at[10]),
        pltpu.make_async_copy(cot, cots.at[rows_at(mine, rows), :], local.at[11]),
    ]
    for c in range(2):
        ring.send(c, tok.at[pl.ds(c * half, half), :])
    for a in own:
        a.start()
    for a in loads[:4]:
        a.wait()
    both = jnp.concatenate([gain_q[...], jnp.zeros((6, gain_q.shape[1]), F32)], axis=0).T.astype(BF16)
    for t in range(nseq):

        @pl.when(mine == t)
        def _():
            pack_front(t, (r_q, r_k, r_v, r_o), first_q, out_q, both)

    for a in loads[4:]:
        a.wait()
    lead.start()
    for t in range(nseq):

        @pl.when(mine == t)
        def _():
            pack_cols(t, nseq, nfsdp, r_g, gate_q)

    late.start()
    for t in range(nseq):

        @pl.when(mine == t)
        def _():
            pack_cols(t, nseq, nfsdp, r_u, up_s)
            pack_down(t, r_d, down_s)

    for a in weights:
        a.start()
    for c in range(2):
        cring.send(c, cot.at[pl.ds(c * half, half), :])
    saves = [pltpu.make_async_copy(up_s, up_q, local.at[12]), pltpu.make_async_copy(down_s, down_q, local.at[13])]
    for a in saves:
        a.start()
    build_strips(heads, mine * heads, starts, table, ids, strip, far)
    lse[...] = jnp.zeros(lse.shape, F32)
    for d in range(1, pairs):
        lead.forward(d)
        if d == pairs // 2:
            ring.forward(0)
    for d in range(1, pairs):
        late.forward(d)
    ring.forward(1)
    lead.finish()
    saves.append(pltpu.make_async_copy(first, first_h, local.at[14]))
    saves[2].start()
    piece = q.shape[1]
    column = 3 * piece
    gains[...] = jnp.zeros(gains.shape, F32)
    for b in range(width // 256):
        band = first[b * 256 : (b + 1) * 256, column // 128 * 128 : column // 128 * 128 + 128].astype(F32).T
        for n in range(2):
            line = column % 128 + n
            gains[n : n + 1, b * 256 : (b + 1) * 256] = band[line : line + 1, :]

    def project(t):
        at = rows_at(t, rows)
        x = group[at, :].astype(F32)
        low = (x * inverse_rms(x) * gains[0:1, :]).astype(BF16)
        n1[at, :] = low
        r = nn(low, first[:, :column])
        q[at, :] = r[:, :piece].astype(BF16)
        k[at, :] = r[:, piece : 2 * piece].astype(BF16)
        v[at, :] = r[:, 2 * piece :].astype(BF16)

    own[0].wait()
    project(mine)
    for c in range(2):
        ring.got_near(c)
    project(near)
    project(other)
    for c in range(2):
        ring.got_cross(c)
    project(cross)
    saves.append(pltpu.make_async_copy(n1, n1_h, local.at[15]))
    saves[3].start()
    for d in range(pairs):
        late.complete(d)
    wring.send(0, out_w.at[mine])
    masked_copies(k, kh, heads)
    vt[...] = v[...].astype(F32).T.astype(BF16)

    def block(h, q0, bias_q0, chunks, c):
        qb = q[pl.ds(q0, CL), :]
        top = None
        for n, (k0, kind, kstart) in enumerate(chunks):
            sc = nt(kh[h, pl.ds(k0, KC), :], qb) + bias_chunk(strip, far, h, bias_q0, kstart, kind, c)
            s[n * KC : (n + 1) * KC, :] = sc
            m = jnp.max(sc, axis=0, keepdims=True)
            top = m if top is None else jnp.maximum(top, m)
        total = jnp.zeros((1, CL), F32)
        acc = jnp.zeros((HEAD_DIM, CL), F32)
        for n, (k0, kind, kstart) in enumerate(chunks):
            e = jnp.exp(s[n * KC : (n + 1) * KC, :] - top)
            total = total + jnp.sum(e, axis=0, keepdims=True)
            acc = acc + nn(vt[pl.ds(pl.multiple_of(h * HEAD_DIM, HEAD_DIM), HEAD_DIM), pl.ds(k0, KC)], e.astype(BF16))
        ot[pl.ds(pl.multiple_of(h * HEAD_DIM, HEAD_DIM), HEAD_DIM), pl.ds(q0, CL)] = acc / total
        lse[pl.ds(h, 1), pl.ds(q0, CL)] = top + jnp.log(total)

    nblk = PROMPT // CL
    hooks = [(n, d) for n in range(2) for d in range(1, pairs)]

    def prompt_body(i, carry):
        h, blk = i // nblk, i % nblk
        q0 = pl.multiple_of(blk * CL, CL)
        block(h, q0, q0, [(j * KC, "strip", j * KC) for j in range(PROMPT // KC)], None)
        for n, (half_n, d) in enumerate(hooks[:-2]):

            @pl.when(i == heads * nblk * n // (len(hooks) - 2))
            def _():
                weights[half_n].forward(d)

        return carry

    lax.fori_loop(0, heads * nblk, prompt_body, 0)

    def cont_body(i, carry):
        h, c = i // 2, i % 2
        q0 = pl.multiple_of(PROMPT + c * CL, CL)
        chunks = [(j * KC, "far", j * KC) for j in range(PROMPT // KC)]
        chunks += [(q0 + j * KC, "strip", j * KC) for j in range(CL // KC)]
        block(h, q0, 0, chunks, c)
        return carry

    for n, d in hooks[-2:-1]:
        weights[n].forward(d)
    cring.forward(0)
    lax.fori_loop(0, heads * 2, cont_body, 0)
    o[...] = ot[...].T.astype(BF16)
    weights[1].forward(pairs - 1)
    cring.forward(1)
    wring.forward(0)
    for a in own[1:] + saves:
        a.wait()
    for a in weights:
        a.finish()
    late.drain()
    wring.finish()
    cring.finish()
    ring.drain()


def front(starts, table, ids, gain_q, tok, w_q, w_k, w_v, w_o, w_g, w_u, w_d, cot, nseq, nfsdp):
    rows, width = tok.shape
    inner = w_q.shape[1]
    piece = inner // nseq
    heads = piece // HEAD_DIM
    tall = nseq * rows
    size = w_q.shape[0]
    units = pack_piece(w_g.shape[1], nfsdp, nseq)[1]
    cols = width // nseq
    lead = piece * 10 // 3
    smem = pl.BlockSpec(memory_space=pltpu.SMEM)
    return pl.pallas_call(
        functools.partial(front_kernel, heads, nseq),
        out_shape=(
            jax.ShapeDtypeStruct((tall, piece), BF16),
            jax.ShapeDtypeStruct((tall, piece), BF16),
            jax.ShapeDtypeStruct((tall, piece), BF16),
            jax.ShapeDtypeStruct((tall, piece), BF16),
            jax.ShapeDtypeStruct((8, tall), F32),
            jax.ShapeDtypeStruct((8, width), F32),
            jax.ShapeDtypeStruct((tall, width), BF16),
            jax.ShapeDtypeStruct((width, lead), BF16),
            jax.ShapeDtypeStruct((nseq, nfsdp, w_o.shape[0], cols), BF16),
            jax.ShapeDtypeStruct((tall, width), BF16),
            jax.ShapeDtypeStruct((width, nfsdp * units), BF16),
            jax.ShapeDtypeStruct((size, nfsdp * units), BF16),
            jax.ShapeDtypeStruct((nseq * units // nseq, width), BF16),
        ),
        in_specs=[smem, smem, vm_spec(), vm_spec()] + [any_spec()] * 9,
        out_specs=(vm_spec(),) * 6 + (any_spec(),) * 7,
        scratch_shapes=wires_scratch(15 + 4 * nfsdp)
        + [
            pltpu.SemaphoreType.DMA((17,)),
            pltpu.VMEM(w_q.shape, BF16),
            pltpu.VMEM(w_k.shape, BF16),
            pltpu.VMEM(w_v.shape, BF16),
            pltpu.VMEM(w_o.shape, BF16),
            pltpu.VMEM(w_g.shape, BF16),
            pltpu.VMEM(w_u.shape, BF16),
            pltpu.VMEM(w_d.shape, BF16),
            pltpu.VMEM((size, lead), BF16),
            pltpu.VMEM((w_o.shape[0], cols), BF16),
            pltpu.VMEM((size, nfsdp * units), BF16),
            pltpu.VMEM((size, nfsdp * units), BF16),
            pltpu.VMEM((units, width), BF16),
            pltpu.VMEM((tall, width), BF16),
            pltpu.VMEM((tall, width), BF16),
            pltpu.VMEM((width, lead), BF16),
            pltpu.VMEM((heads, 128, STRIP), F32),
            pltpu.VMEM((heads, 2, 128, FARW), F32),
            pltpu.VMEM((heads, tall, piece), BF16),
            pltpu.VMEM((piece, tall), BF16),
            pltpu.VMEM((piece, tall), F32),
            pltpu.VMEM((PROMPT + CL, CL), F32),
        ],
        compiler_params=call_params(1, 60),
        name="front",
    )(starts, table, ids, gain_q, tok, w_q, w_k, w_v, w_o, w_g, w_u, w_d, cot)


def back_kernel(
    heads, chunks, starts, table, ids, gains, lse, gain_b, q, k, v, o, do,
    resid_h, rgrad_h, tok_h, y_p, w_p, gate_p, up_p, done_h, lead_h, n1_h, first_h,
    small, y_h, in_h, down_f, lead_f, gate_f, up_f, qkv_f, out_f,
    send, recv, local, ybuf, wbuf, out_p, qkv_p, b0, b1, b2, b3, b4, b5,
    g0, g1, g2, g3, u0, u1, u2, u3, q0_, q1_, q2_, q3_, o0, o1, o2, o3,
    gate_s, up_s, qkv_s, out_s, dqkv, tok, held, stage, one, two, three, tgrad,
):
    rows, width = tok.shape
    nseq = w_p.shape[0]
    piece = q.shape[1]
    nfsdp = gate_p.shape[0]
    s, near, far_d, cross = seq_places()
    pair, side, pairs = fsdp_places()

    def y_block(t):
        return y_p.at[rows_at(t, rows), :]

    def w_block(t):
        return w_p.at[t]

    sides = ((w_block, wbuf), (y_block, ybuf))
    loads = []
    for n, (block_of, buf) in enumerate(sides):
        loads.append(pltpu.make_async_copy(block_of(far_d), buf.at[2], local.at[2 * n]))
        loads.append(pltpu.make_async_copy(block_of(s), buf.at[3], local.at[2 * n + 1]))
    loads.append(pltpu.make_async_copy(tok_h, tok, local.at[5]))
    for a in loads:
        a.start()
    meet([{"seq": near}, {"seq": far_d}, {"seq": cross}] + fsdp_peers())
    wires = Wires(send, recv)
    hops = [wires.go(block_of(cross), buf.at[0], {"seq": near}) for block_of, buf in sides]
    turns = [wires.go(block_of(near), buf.at[1], {"seq": near}) for block_of, buf in sides]
    gates = FsdpScatter(wires, gate_p, (g0, g1, g2, g3), gate_s)
    ups = FsdpScatter(wires, up_p, (u0, u1, u2, u3), up_s)
    gates.start()
    ups.start()
    down_ring = SeqGather(wires, lambda t, c: down_f.at[t], 1)
    lead_ring = SeqGather(wires, lambda t, c: lead_f.at[t], 1)
    gate_ring = SeqGather(wires, lambda t, c: gate_f.at[t], 1)
    up_ring = SeqGather(wires, lambda t, c: up_f.at[t], 1)
    qkv_ring = SeqGather(wires, lambda t, c: qkv_f.at[t], 1)
    out_ring = SeqGather(wires, lambda t, c: out_f.at[t], 1)
    qkvs = FsdpScatter(wires, qkv_p, (q0_, q1_, q2_, q3_), qkv_s)
    outs = FsdpScatter(wires, out_p, (o0, o1, o2, o3), out_s)
    far_base = wires.take(2)

    def far_hop(n):
        buf = sides[n][1]
        return wires.at(far_base + n, buf.at[2], buf.at[4], {"seq": far_d})

    def add_far(n):
        buf = sides[n][1]
        loads[2 * n].wait()
        hops[n].wait_recv()
        buf[2] = (buf[2].astype(F32) + buf[0].astype(F32)).astype(BF16)

    def total_of(n):
        buf = sides[n][1]
        loads[2 * n + 1].wait()
        turns[n].wait_recv()
        far_hop(n).wait_recv()
        return buf[3].astype(F32) + buf[1].astype(F32) + buf[4].astype(F32)

    down_keep = pltpu.make_async_copy(done_h, down_f.at[s], local.at[6])
    down_keep.start()
    down_ring.send(0, done_h)
    lead_keep = pltpu.make_async_copy(lead_h, lead_f.at[s], local.at[10])
    lead_keep.start()
    lead_ring.send(0, lead_h)
    length = ids.shape[1]
    half = 2 * PROMPT

    def attend_back(strip, far, kh, vh, kt, delta, dqt, dk, dv, gstrip, gfar):
        build_strips(heads, s * heads, starts, table, ids, strip, far)
        add_far(0)
        add_far(1)
        for src, dst in ((k, kh), (v, vh)):
            masked_copies(src, dst, heads)
        far_hop(0).start()
        far_hop(1).start()
        kt[...] = k[...].astype(F32).T.astype(BF16)
        prod = (o[...].astype(F32) * do[...].astype(F32)).T
        for h in range(heads):
            delta[h : h + 1, :] = jnp.sum(prod[h * HEAD_DIM : (h + 1) * HEAD_DIM, :], axis=0, keepdims=True)
        dk[...] = jnp.zeros(dk.shape, F32)
        dv[...] = jnp.zeros(dv.shape, F32)
        gstrip[...] = jnp.zeros(gstrip.shape, F32)
        gfar[...] = jnp.zeros(gfar.shape, F32)
        lane = lax.broadcasted_iota(jnp.int32, (1, piece), 1)

        def block(h, q0, bias_q0, chunk_list, c):
            qb = q[pl.ds(q0, CL), :]
            dob = do[pl.ds(q0, CL), :]
            keep = lane // HEAD_DIM == h
            qhb = jnp.where(keep, qb, jnp.zeros((), BF16))
            dohb = jnp.where(keep, dob, jnp.zeros((), BF16))
            lrow = lse[pl.ds(h, 1), pl.ds(q0, CL)]
            drow = delta[pl.ds(h, 1), pl.ds(q0, CL)]
            acc = jnp.zeros((HEAD_DIM, CL), F32)
            for n, (k0, kind, kstart) in enumerate(chunk_list):
                ks = pl.ds(k0, KC)
                sc = nt(kh[h, ks, :], qb) + bias_chunk(strip, far, h, bias_q0, kstart, kind, c)
                pr = jnp.exp(sc - lrow)
                dp = nt(vh[h, ks, :], dob)
                ds = pr * (dp - drow)
                dsl = ds.astype(BF16)
                dv[ks, :] += nn(pr.astype(BF16), dohb)
                dk[ks, :] += nn(dsl, qhb)
                acc = acc + nn(kt[pl.ds(pl.multiple_of(h * HEAD_DIM, HEAD_DIM), HEAD_DIM), ks], dsl)
                for r in range(KC // 128):
                    m = PROMPT - 128 - (kstart + 128 * r)
                    part = ds[128 * r : 128 * (r + 1), :]
                    if kind == "far":
                        gfar[h, c, :, m : m + CL] += part
                    else:
                        gstrip[h, :, pl.ds(pl.multiple_of(bias_q0 + m, 128), CL)] += part
            dqt[pl.ds(pl.multiple_of(h * HEAD_DIM, HEAD_DIM), HEAD_DIM), pl.ds(q0, CL)] = acc

        nblk = PROMPT // CL

        def prompt_body(i, carry):
            h, blk = i // nblk, i % nblk
            q0 = pl.multiple_of(blk * CL, CL)
            block(h, q0, q0, [(j * KC, "strip", j * KC) for j in range(PROMPT // KC)], None)

            @pl.when(i == 3)
            def _():
                gates.step(1)

            return carry

        lax.fori_loop(0, heads * nblk, prompt_body, 0)
        for d in range(2, pairs - 1):
            gates.step(d)

        def cont_body(i, carry):
            h, c = i // 2, i % 2
            q0 = pl.multiple_of(PROMPT + c * CL, CL)
            chunk_list = [(j * KC, "far", j * KC) for j in range(PROMPT // KC)]
            chunk_list += [(q0 + j * KC, "strip", j * KC) for j in range(CL // KC)]
            block(h, q0, 0, chunk_list, c)
            return carry

        lax.fori_loop(0, heads * 2, cont_body, 0)
        if pairs > 2:
            gates.step(pairs - 1)
        dqkv[...] = jnp.concatenate([dqt[...].T, dk[...], dv[...]], axis=1).astype(BF16)
        lines8 = lax.broadcasted_iota(jnp.int32, (table.shape[0], length), 0)
        hot = ids[:1, :] == lines8
        tgrad[...] = jnp.zeros(tgrad.shape, F32)
        for h in range(heads):

            def unskew(g, span):
                full = jnp.concatenate([jnp.zeros((128, 128), F32), g], axis=1)
                eight = full[:8]
                for a in range(1, 16):
                    eight = eight + pltpu.roll(full[8 * a : 8 * a + 8], span - 8 * a, 1)
                vec = pltpu.roll(eight, span - 1, 1)[:1]
                for b in range(1, 8):
                    vec = vec + pltpu.roll(eight, span - 1 - b, 1)[b : b + 1]
                return jnp.concatenate([vec, jnp.zeros((1, length - span), F32)], axis=1)

            whole = jnp.broadcast_to(unskew(gstrip[h], half), (8, length))
            whole = pltpu.roll(whole, PROMPT // 2, 1)
            for c in range(2):
                moved = jnp.broadcast_to(unskew(gfar[h, c], FARW + 128), (8, length))
                whole = whole + pltpu.roll(moved, PROMPT // 2 + starts[c], 1)
            picked = jnp.where(hot, whole[:1, :], 0.0)
            column = jnp.broadcast_to(jnp.sum(picked, axis=1, keepdims=True), (table.shape[0], 128))
            tgrad[h : h + 1, : table.shape[0]] = column.T[:1, :]

    tall = nseq * rows
    pl.run_scoped(
        attend_back,
        pltpu.VMEM((heads, 128, STRIP), F32),
        pltpu.VMEM((heads, 2, 128, FARW), F32),
        pltpu.VMEM((heads, tall, piece), BF16),
        pltpu.VMEM((heads, tall, piece), BF16),
        pltpu.VMEM((piece, tall), BF16),
        pltpu.VMEM((8, tall), F32),
        pltpu.VMEM((piece, tall), F32),
        pltpu.VMEM((tall, piece), F32),
        pltpu.VMEM((tall, piece), F32),
        pltpu.VMEM((heads, 128, STRIP), F32),
        pltpu.VMEM((heads, 2, 128, FARW), F32),
    )

    def rest(n1, hold, rgrad, resid, first):
        later = [
            pltpu.make_async_copy(n1_h, n1, local.at[7]),
            pltpu.make_async_copy(rgrad_h, rgrad, local.at[8]),
            pltpu.make_async_copy(resid_h, resid, local.at[9]),
        ]
        ready = pltpu.make_async_copy(first_h, first, local.at[4])
        ready.start()
        for a in later:
            a.start()
        sums = SeqScatter(wires, chunks, b0, b1, b2, b3, b4, b5)
        size = rows // chunks
        ready.wait()

        def part(t, c):
            return nt(dqkv[rows_at(t, rows, c * size, size), :], first[:, : 3 * piece])

        for c in range(chunks):
            sums.cross_chunk(c, part(cross, c))
        for c in range(chunks):
            sums.far_chunk(c, part(far_d, c))
        ups.step(1)
        later[0].wait()
        depth = width // nfsdp
        wide = 384
        for n in range(width // wide):
            got = dot_tn(n1[:, n * wide : (n + 1) * wide], dqkv[...])
            for m in range(wide // depth):
                qkv_p[n * (wide // depth) + m] = got[m * depth : (m + 1) * depth, :].astype(BF16)
        for c in range(chunks):
            sums.near_chunk(c, part(near, c))
        for c in range(chunks):
            hold[c * size : (c + 1) * size, :] = part(s, c)
        wsum = total_of(0).astype(BF16)
        lines_f = out_p.shape[1]
        for f in range(nfsdp):
            out_p[f] = wsum[f * lines_f : (f + 1) * lines_f, :]
        qkvs.start()
        gates.finish()
        outs.start()
        gate_keep = pltpu.make_async_copy(gate_s, gate_f.at[s], local.at[11])
        gate_keep.start()
        gate_ring.send(0, gate_s)
        down_ring.forward(0)
        lead_ring.forward(0)
        if pairs > 2:
            ups.step(2)
        later[2].wait()
        ybuf[3] = (resid[...] + total_of(1)).astype(BF16)
        loads[4].wait()
        later[1].wait()
        gsum = jnp.zeros((1, width), F32)
        y_keep = pltpu.make_async_copy(ybuf.at[3], y_h, local.at[12])
        y_keep.start()
        for c in range(chunks):
            at = slice(c * size, (c + 1) * size)
            dn = sums.own_chunk(c, hold[at, :])
            x = tok[at, :].astype(F32)
            r = inverse_rms(x)
            gsum = gsum + jnp.sum(dn * x * r, axis=0, keepdims=True)
            tok[at, :] = (rgrad[at, :] + norm_back(dn, x, r, gains[0:1, :])).astype(BF16)
            if c == 0:
                for d in range(3, pairs):
                    ups.step(d)
        in_keep = pltpu.make_async_copy(tok, in_h, local.at[13])
        in_keep.start()
        held[...] = jnp.zeros(held.shape, F32)
        lanes = held.shape[1]
        lines = width // lanes
        for n in range(lines):
            held[n : n + 1, :] = gsum[:, n * lanes : (n + 1) * lanes]
            held[lines + n : lines + n + 1, :] = gain_b[:1, n * lanes : (n + 1) * lanes]
        held[pl.ds(2 * lines + s * 8, 8), :] = tgrad[...]
        ups.finish()
        trips = [wires.go(held, one.at[n], {"seq": t}) for n, t in enumerate((near, far_d, cross))]
        up_keep = pltpu.make_async_copy(up_s, up_f.at[s], local.at[14])
        up_keep.start()
        up_ring.send(0, up_s)
        gate_ring.forward(0)
        qkvs.step(1)
        for a in trips:
            a.wait_recv()
        stage[0] = held[...] + one[0] + one[1] + one[2]
        for d in range(2, pairs):
            qkvs.step(d)
        trips.append(wires.go(stage.at[0], two, {"fsdp": pair * 2 + 1 - side}))
        for d in range(1, pairs):
            outs.step(d)
        trips[-1].wait_recv()
        stage[1] = stage[0] + two[...]
        up_ring.forward(0)
        zs = [
            wires.go(stage.at[1], three.at[d - 1], {"fsdp": lax.rem(pair + d, pairs) * 2 + side})
            for d in range(1, pairs)
        ]
        qkvs.finish()
        qkv_keep = pltpu.make_async_copy(qkv_s, qkv_f.at[s], local.at[15])
        qkv_keep.start()
        qkv_ring.send(0, qkv_s)
        outs.finish()
        out_keep = pltpu.make_async_copy(out_s, out_f.at[s], local.at[16])
        out_keep.start()
        out_ring.send(0, out_s)
        total = stage[1]
        for d, a in enumerate(zs):
            a.wait_recv()
            total = total + three[d]
        small[...] = total
        qkv_ring.forward(0)
        out_ring.forward(0)
        for a in (down_ring, lead_ring, gate_ring, up_ring, qkv_ring, out_ring):
            a.finish()
        sums.finish()
        for a in (gates, ups, qkvs, outs):
            a.drain()
        for a in (gate_keep, up_keep, qkv_keep, out_keep, y_keep, in_keep, down_keep, lead_keep):
            a.wait()
        for a in trips + zs + hops + turns + [far_hop(0), far_hop(1)]:
            a.wait_send()

    pl.run_scoped(
        rest,
        pltpu.VMEM((tall, width), BF16),
        pltpu.VMEM((rows, width), F32),
        pltpu.VMEM((rows, width), F32),
        pltpu.VMEM((rows, width), F32),
        pltpu.VMEM(first_h.shape, BF16),
    )


def back(starts, table, ids, gains, lse, gain_b, q, k, v, o, do, resid, rgrad, tok, y_p, w_p, gate_p, up_p, done, lead, n1, first, chunks=2):
    tall, piece = q.shape
    heads = piece // HEAD_DIM
    rows, width = tok.shape
    nseq = w_p.shape[0]
    nfsdp = gate_p.shape[0]
    pairs = nfsdp // 2
    lines = -(-(2 * width // 128 + 8 * nseq) // 8) * 8
    qkv_shape = (nfsdp, width // nfsdp, 3 * piece)
    out_shape = (nfsdp, w_p.shape[1] // nfsdp, w_p.shape[2])
    smem = pl.BlockSpec(memory_space=pltpu.SMEM)

    def full(a):
        return jax.ShapeDtypeStruct((nseq,) + tuple(a), BF16)

    return pl.pallas_call(
        functools.partial(back_kernel, heads, chunks),
        out_shape=(
            jax.ShapeDtypeStruct((lines, 128), F32),
            jax.ShapeDtypeStruct((rows, width), BF16),
            jax.ShapeDtypeStruct((rows, width), BF16),
            full(done.shape),
            full(lead.shape),
            full(gate_p.shape[1:]),
            full(up_p.shape[1:]),
            full(qkv_shape[1:]),
            full(out_shape[1:]),
        ),
        in_specs=[smem, smem] + [vm_spec()] * 9 + [any_spec()] * 11,
        out_specs=(vm_spec(),) + (any_spec(),) * 8,
        scratch_shapes=wires_scratch(6 + 4 * nfsdp + 18 + 3 * chunks + 4 + pairs)
        + [
            pltpu.SemaphoreType.DMA((17,)),
            pltpu.VMEM((5, rows, width), BF16),
            pltpu.VMEM((5,) + w_p.shape[1:], BF16),
            pltpu.VMEM(out_shape, BF16),
            pltpu.VMEM(qkv_shape, BF16),
        ]
        + scatter_scratch(chunks, rows // chunks, width)
        + fsdp_scatter_scratch(gate_p.shape)
        + fsdp_scatter_scratch(up_p.shape)
        + fsdp_scatter_scratch(qkv_shape)
        + fsdp_scatter_scratch(out_shape)
        + [
            pltpu.VMEM(gate_p.shape[1:], BF16),
            pltpu.VMEM(up_p.shape[1:], BF16),
            pltpu.VMEM(qkv_shape[1:], BF16),
            pltpu.VMEM(out_shape[1:], BF16),
            pltpu.VMEM((tall, 3 * piece), BF16),
            pltpu.VMEM((rows, width), BF16),
            pltpu.VMEM((lines, 128), F32),
            pltpu.VMEM((2, lines, 128), F32),
            pltpu.VMEM((3, lines, 128), F32),
            pltpu.VMEM((lines, 128), F32),
            pltpu.VMEM((pairs - 1, lines, 128), F32),
            pltpu.VMEM((8, 128), F32),
        ],
        compiler_params=call_params(5, 64),
        name="back",
    )(starts, table, ids, gains, lse, gain_b, q, k, v, o, do, resid, rgrad, tok, y_p, w_p, gate_p, up_p, done, lead, n1, first)


def unpack_kernel(nseq, nfsdp, heads, *refs):
    srcs, small, outs = refs[:8], refs[8], refs[9:18]
    ga, gb, table, ins, offs = refs[18:23]
    vs, ts = refs[23:31], refs[31:]
    loads = [pltpu.make_async_copy(a, b, ins.at[n]) for n, (a, b) in enumerate(zip(srcs, vs))]
    for a in loads:
        a.start()
    lead_f, gate_f, up_f, down_f, qkv_f, out_f, y, dx = vs
    tq, tk, tv, to, tg, tu, td = ts
    gq, gk, gv, go, gg, gu, gd, gy, gx = outs
    copies = []

    def save(src, dst):
        copies.append(pltpu.make_async_copy(src, dst, offs.at[len(copies)]))
        copies[-1].start()

    block, piece = pack_piece(tg.shape[1], nfsdp, nseq)
    half = nfsdp // 2

    def columns(get):
        parts = []
        for f in range(nfsdp):
            for t in range(nseq):
                size = min(piece, block - t * piece)
                full, f_at = get(f)
                parts.append(full[t, :, f_at * piece : f_at * piece + size].astype(F32))
        return jnp.concatenate(parts, axis=1)

    loads[0].wait()
    loads[1].wait()
    tg[...] = columns(lambda f: (lead_f, f) if f < half else (gate_f, f - half))
    save(tg, gg)
    loads[2].wait()
    tu[...] = columns(lambda f: (up_f, f))
    save(tu, gu)
    loads[3].wait()
    size = down_f.shape[1]
    for t in range(nseq):
        n = min(size, td.shape[0] - t * size)
        td[t * size : t * size + n, :] = down_f[t, :n, :].astype(F32)
    save(td, gd)
    loads[4].wait()
    width = qkv_f.shape[2] // 3
    for n, (dst, out) in enumerate(((tq, gq), (tk, gk), (tv, gv))):
        dst[...] = jnp.concatenate([qkv_f[t, :, n * width : (n + 1) * width] for t in range(nseq)], axis=1).astype(F32)
        save(dst, out)
    loads[5].wait()
    to[...] = jnp.concatenate([out_f[t] for t in range(nseq)], axis=1).astype(F32)
    save(to, go)
    for n, (src, dst) in enumerate(((y, gy), (dx, gx))):
        loads[6 + n].wait()
        save(src, dst)
    where = lax.axis_index("fsdp")
    share = ga.shape[1]
    lines = nfsdp * share // 128
    for n, dst in enumerate((ga, gb)):
        line = jnp.concatenate([small[n * lines + a : n * lines + a + 1, :] for a in range(lines)], axis=1)
        for f in range(nfsdp):

            @pl.when(where == f)
            def _():
                dst[...] = line[:, f * share : (f + 1) * share]

    turned = small[2 * lines : 2 * lines + 8 * nseq, :].T
    table[...] = jnp.concatenate([turned[: table.shape[0], 8 * t : 8 * t + heads] for t in range(nseq)], axis=1)
    for a in copies:
        a.wait()


def unpack(srcs, small, like, blocks_like, table, nfsdp):
    nseq = srcs[0].shape[0]
    share = like[0].shape[0]
    vm = [vm_spec()] * 3
    return pl.pallas_call(
        functools.partial(unpack_kernel, nseq, nfsdp, table.shape[1] // nseq),
        out_shape=tuple(jax.ShapeDtypeStruct(a.shape, F32) for a in like)
        + tuple(jax.ShapeDtypeStruct(a.shape, BF16) for a in blocks_like)
        + (
            jax.ShapeDtypeStruct((1, share), F32),
            jax.ShapeDtypeStruct((1, share), F32),
            jax.ShapeDtypeStruct(table.shape, F32),
        ),
        in_specs=[any_spec()] * 8 + [vm_spec()],
        out_specs=tuple([any_spec()] * 9 + vm),
        scratch_shapes=[pltpu.SemaphoreType.DMA((8,)), pltpu.SemaphoreType.DMA((9,))]
        + [pltpu.VMEM(a.shape, BF16) for a in srcs]
        + [pltpu.VMEM(a.shape, F32) for a in like],
        compiler_params=pltpu.CompilerParams(vmem_limit_bytes=40 << 20),
        name="unpack",
    )(*srcs, small)


def reversed_ids(bucket_ids):
    span = bucket_ids.shape[0]
    ids = jnp.concatenate([bucket_ids[::-1], jnp.full((1,), -1, jnp.int32)])
    return ids[None, :]


def dot32(a, b):
    return jnp.dot(a, b, preferred_element_type=F32)


def dot_tn(a, b):
    return lax.dot_general(a, b, (((0,), (0,)), ((), ())), preferred_element_type=F32)


def gelu_both(u):
    inner = 0.7978845608028654 * (u + 0.044715 * u * u * u)
    t = jnp.tanh(inner)
    value = 0.5 * u * (1.0 + t)
    slope = 0.5 * (1.0 + t) + 0.5 * u * (1.0 - t * t) * 0.7978845608028654 * (1.0 + 3 * 0.044715 * u * u)
    return value, slope


def body(
    tokens,
    out_grad,
    attn_gain,
    w_query,
    w_key,
    w_value,
    w_out,
    mix_gain,
    w_gate,
    w_up,
    w_down,
    rel_table,
    bucket_ids,
    cont_start,
):
    nseq = lax.axis_size("seq")
    nfsdp = lax.axis_size("fsdp")
    inner = w_query.shape[1]

    ids = reversed_ids(bucket_ids)
    starts = cont_start[0]
    query, keys, values, mixed, lse, gains, normed, first, out_w, cot, gate_w, up_q, down_q = front(
        starts,
        rel_table,
        ids,
        jnp.stack([attn_gain.astype(F32), mix_gain.astype(F32)]),
        tokens[0],
        w_query,
        w_key,
        w_value,
        w_out,
        w_gate,
        w_up,
        w_down,
        out_grad[0],
        nseq,
        nfsdp,
    )
    out_w = out_w.reshape(nseq, inner, -1)
    mixed_rows, resid, normed_two, hidden, gate_grad, up_grad, up_w, down_w, down_grad = middle(
        mixed, out_w, tokens[0], gains, up_q, down_q, gate_w, cot, nfsdp
    )
    resid_grad, mixed_grad, gain_two_grad, down_grad, lead_grad, out_w_grad, gate_w_grad, up_w_grad, result = unmix(
        gains, mixed_rows, resid, out_grad[0], down_grad, gate_grad, up_grad, gate_w, up_w, out_w, normed_two, hidden, down_w
    )
    small, block_out, in_grad, down_grad, lead_grad, gate_w_grad, up_w_grad, qkv_grad, out_w_grad = back(
        starts,
        rel_table,
        ids,
        gains,
        lse,
        gain_two_grad,
        query,
        keys,
        values,
        mixed,
        mixed_grad,
        resid,
        resid_grad,
        tokens[0],
        result,
        out_w_grad,
        gate_w_grad,
        up_w_grad,
        down_grad,
        lead_grad,
        normed,
        first,
    )
    *shards, block_out, in_grad, gain_one_share, gain_two_share, table_grad = unpack(
        (lead_grad, gate_w_grad, up_w_grad, down_grad, qkv_grad, out_w_grad, block_out, in_grad),
        small,
        (w_query, w_key, w_value, w_out, w_gate, w_up, w_down),
        (block_out, in_grad),
        rel_table,
        nfsdp,
    )
    return (
        block_out[None],
        in_grad[None],
        gain_one_share[0],
        *shards[:4],
        gain_two_share[0],
        *shards[4:],
        table_grad,
    )


def solution(mesh):
    placed = (
        P("fsdp", "seq", None),
        P("fsdp", "seq", None),
        P("fsdp"),
        P("fsdp", None),
        P("fsdp", None),
        P("fsdp", None),
        P("fsdp", None),
        P("fsdp"),
        P("fsdp", None),
        P("fsdp", None),
        P("fsdp", None),
        P(),
        P(),
        P("fsdp", None),
    )
    results = placed[:1] * 2 + placed[2:11] + (P(),)
    return jax.shard_map(body, mesh=mesh, in_specs=placed, out_specs=results, check_vma=False)
```

```python
import functools
import jax
import jax.numpy as jnp
from jax import lax
from jax.experimental import pallas as pl
from jax.experimental.pallas import tpu as pltpu
from jax.sharding import PartitionSpec as P

HEAD_DIM = 64
PROMPT = 1024
CL = 256
F32 = jnp.float32
BF16 = jnp.bfloat16
MESH = pl.DeviceIdType.MESH
epsilon = 1e-06
STRIP = 2 * PROMPT - 128
FARW = PROMPT - 128 + CL
KC = 256


def nt(a, b):
    return lax.dot_general(a, b, (((1,), (1,)), ((), ())), preferred_element_type=F32)


def nn(a, b):
    return lax.dot_general(a, b, (((1,), (0,)), ((), ())), preferred_element_type=F32)


class Wires:
    def __init__(self, send, recv):
        self.send, self.recv, self.used = send, recv, 0

    def take(self, count):
        self.used += count
        return self.used - count

    def at(self, i, src, dst, where):
        return pltpu.make_async_remote_copy(
            src_ref=src,
            dst_ref=dst,
            send_sem=self.send.at[i],
            recv_sem=self.recv.at[i],
            device_id=where,
            device_id_type=MESH,
        )

    def go(self, src, dst, where):
        c = self.at(self.take(1), src, dst, where)
        c.start()
        return c


def seq_places():
    s = lax.axis_index("seq")
    near = s + 1 - 2 * lax.rem(s, 2)
    far = lax.rem(s + 2, 4)
    cross = lax.rem(near + 2, 4)
    return s, near, far, cross


def meet(places):
    barrier = pltpu.get_barrier_semaphore()
    for where in places:
        pl.semaphore_signal(barrier, inc=1, device_id=where, device_id_type=MESH)
    pl.semaphore_wait(barrier, len(places))


def rows_at(index, rows, offset=0, count=None):
    return pl.ds(pl.multiple_of(index * rows + offset, 16), rows if count is None else count)


class SeqGather:
    def __init__(self, wires, out_at, chunks):
        self.wires, self.out_at, self.chunks = wires, out_at, chunks
        self.s, self.near, self.far, self.cross = seq_places()
        self.base = wires.take(3 * chunks)

    def trip(self, kind, c, src=None):
        view = self.out_at(self.far if kind == 2 else self.s, c)
        where = {"seq": self.far if kind == 0 else self.near}
        return self.wires.at(self.base + 3 * c + kind, view if src is None else src, view, where)

    def send(self, c, src):
        self.trip(0, c, src).start()
        self.trip(1, c, src).start()

    def forward(self, c):
        self.trip(0, c).wait_recv()
        self.trip(2, c).start()

    def got_near(self, c):
        self.trip(1, c).wait_recv()

    def got_cross(self, c):
        self.trip(2, c).wait_recv()

    def drain(self):
        for c in range(self.chunks):
            for kind in range(3):
                self.trip(kind, c).wait_send()

    def finish(self):
        for c in range(self.chunks):
            self.got_near(c)
            self.got_cross(c)
        self.drain()


def fsdp_places():
    f = lax.axis_index("fsdp")
    return f // 2, lax.rem(f, 2), lax.axis_size("fsdp") // 2


def far_first(k):
    pair, _, pairs = fsdp_places()
    if pairs != 4:
        return k + 1
    first, second = 3 - (pair + 1) // 2, 1 + lax.rem(pair + 1, 3)
    return (first, second, 6 - first - second)[k]


def near_first(k):
    pairs = lax.axis_size("fsdp") // 2
    return pairs - far_first(pairs - 2 - k) if pairs == 4 else k + 1


def fsdp_peers():
    pair, side, pairs = fsdp_places()
    peers = [{"fsdp": lax.rem(pair + d, pairs) * 2 + side} for d in range(1, pairs)]
    return peers + [{"fsdp": pair * 2 + 1 - side}]


class FsdpGather:
    def __init__(self, wires, shard, full_at, local):
        self.wires, self.shard, self.full_at, self.local = wires, shard, full_at, local
        self.pair, self.side, self.pairs = fsdp_places()
        self.base = wires.take(2 * self.pairs)

    def source(self, d):
        return lax.rem(self.pair + self.pairs - d, self.pairs)

    def over(self):
        own = self.full_at(self.pair * 2 + self.side)
        return self.wires.at(self.base, self.shard, own, {"fsdp": self.pair * 2 + 1 - self.side})

    def out(self, d):
        own = self.full_at(self.pair * 2 + self.side)
        where = {"fsdp": lax.rem(self.pair + d, self.pairs) * 2 + self.side}
        return self.wires.at(self.base + d, self.shard, own, where)

    def onward(self, d):
        view = self.full_at(self.source(d) * 2 + self.side)
        return self.wires.at(self.base + self.pairs + d, view, view, {"fsdp": self.pair * 2 + 1 - self.side})

    def keep(self):
        return pltpu.make_async_copy(self.shard, self.full_at(self.pair * 2 + self.side), self.local)

    def start(self):
        self.over().start()
        for k in range(self.pairs - 1):
            self.out(far_first(k)).start()
        self.keep().start()

    def forward(self, k):
        d = near_first(k - 1)
        self.out(d).wait_recv()
        self.onward(d).start()

    def place(self, k):
        return 0 if k == 0 else near_first(k - 1)

    def complete(self, k):
        if k == 0:
            self.keep().wait()
            self.over().wait_recv()
        else:
            self.onward(near_first(k - 1)).wait_recv()

    def drain(self):
        self.over().wait_send()
        for d in range(1, self.pairs):
            self.out(d).wait_send()
            self.onward(d).wait_send()

    def finish(self):
        for k in range(self.pairs):
            self.complete(k)
        self.drain()


def gather_halves(wires, shard, full, size, local):
    half = shard.shape[1] // 2

    def one(n):
        cut = slice(n * half, (n + 1) * half)
        return FsdpGather(wires, shard.at[:, cut], lambda f: full.at[shard_rows(f, size), cut], local[n])

    return [one(0), one(1)]


class FsdpScatter:
    def __init__(self, wires, parts, bufs, result):
        self.wires, self.parts, self.result = wires, parts, result
        self.mine, self.got, self.landed, self.local = bufs
        self.pair, self.side, self.pairs = fsdp_places()
        self.base = wires.take(2 * self.pairs)

    def step_to(self, k):
        return far_first(k) if k < self.pairs - 1 else 0

    def owner(self, d):
        return lax.rem(self.pair + d, self.pairs) * 2

    def load(self, k):
        part = self.parts.at[self.owner(self.step_to(k)) + self.side]
        return pltpu.make_async_copy(part, self.mine.at[k % 2], self.local.at[k % 2])

    def swap(self, d):
        src = self.parts.at[self.owner(d) + 1 - self.side]
        return self.wires.at(self.base + d, src, self.got.at[d], {"fsdp": self.pair * 2 + 1 - self.side})

    def onward(self, d):
        where = {"fsdp": self.owner(d) + self.side}
        return self.wires.at(self.base + self.pairs + d, self.got.at[d], self.landed.at[d - 1], where)

    def start(self):
        for k in range(self.pairs):
            self.swap(self.step_to(k)).start()
        self.load(0).start()

    def step(self, k):
        d = self.step_to(k - 1)
        self.load(k).start()
        self.load(k - 1).wait()
        self.swap(d).wait_recv()
        self.got[d] = (self.mine[(k - 1) % 2].astype(F32) + self.got[d].astype(F32)).astype(BF16)
        self.onward(d).start()

    def finish(self):
        self.load(self.pairs - 1).wait()
        self.swap(0).wait_recv()
        total = self.mine[(self.pairs - 1) % 2].astype(F32) + self.got[0].astype(F32)
        for d in range(1, self.pairs):
            self.onward(d).wait_recv()
            total = total + self.landed[d - 1].astype(F32)
        self.result[...] = total.astype(BF16)

    def drain(self):
        for d in range(self.pairs):
            self.swap(d).wait_send()
        for d in range(1, self.pairs):
            self.onward(d).wait_send()


def fsdp_scatter_scratch(shape):
    pairs = shape[0] // 2
    return [
        pltpu.VMEM((2,) + shape[1:], BF16),
        pltpu.VMEM((pairs,) + shape[1:], BF16),
        pltpu.VMEM((pairs - 1,) + shape[1:], BF16),
        pltpu.SemaphoreType.DMA((2,)),
    ]


def blocks(a, count):
    return a.reshape((count, a.shape[0] // count) + a.shape[1:])


def shard_rows(f, size):
    return pl.ds(pl.multiple_of(f * size, 16 if size % 16 == 0 else 8 if size % 8 == 0 else size), size)


def vm_spec():
    return pl.BlockSpec(memory_space=pltpu.VMEM)


def any_spec():
    return pl.BlockSpec(memory_space=pl.ANY)


def wires_scratch(n):
    return [pltpu.SemaphoreType.DMA((n,)), pltpu.SemaphoreType.DMA((n,))]


def call_params(number, vmem=60):
    return pltpu.CompilerParams(collective_id=number, has_side_effects=True, vmem_limit_bytes=min(vmem << 20, 67043328))


def inverse_rms(v):
    return lax.rsqrt(jnp.mean(v * v, axis=-1, keepdims=True) + epsilon)


def norm_back(grad, v, r, gain):
    scaled = grad * gain
    return r * scaled - v * (r * r * r) * jnp.mean(v * scaled, axis=-1, keepdims=True)


def middle_kernel(
    o, out_w, tok, gains, up_q, down_q, gate_h, cot_h,
    obuf, resid, n2_h, hid_h, dg_h, du_h, up_h, down_h, parts_h,
    send, recv, local, own, n2, cot, gate_w, up_w, down_w, ga, ub, hid, dg, du, parts,
):
    rows, width = tok.shape
    piece = o.shape[1]
    nseq = obuf.shape[0]
    units = gate_w.shape[1]
    nfsdp = parts.shape[0]
    s, near, far, cross = seq_places()
    loads = [pltpu.make_async_copy(gate_h, gate_w, local.at[0]), pltpu.make_async_copy(cot_h, cot, local.at[1])]
    for a in loads:
        a.start()
    meet([{"seq": near}, {"seq": far}, {"seq": cross}] + fsdp_peers())
    wires = Wires(send, recv)
    trips = [wires.go(o.at[rows_at(t, rows), :], obuf.at[s], {"seq": t}) for t in (far, cross, near)]
    up_size, down_size = up_q.shape[0], down_q.shape[0]
    ups = gather_halves(wires, up_q, up_w, up_size, (local.at[2], local.at[11]))
    downs = gather_halves(wires, down_q, down_w, down_size, (local.at[3], local.at[12]))
    for a in ups + downs:
        a.start()
    pairs = ups[0].pairs
    todo = [(a, d) for a in ups + downs for d in range(1, pairs)]

    def pass_on(share):
        while todo and len(todo) > round((1 - share) * 4 * (pairs - 1)):
            a, d = todo.pop(0)
            a.forward(d)

    obuf[s] = o[rows_at(s, rows), :]
    half = rows // 2
    for a in trips:
        a.wait_recv()
    pass_on(1 / 12)
    ring = SeqGather(wires, lambda t, c: n2.at[rows_at(t, rows, c * half, half), :], 2)
    cols = out_w.shape[2]
    for c in range(2):
        part = slice(c * half, (c + 1) * half)
        for u in range(nseq):
            acc = tok[part, u * cols : (u + 1) * cols].astype(F32)
            for t in range(nseq):
                acc = acc + nn(obuf[t, part, :], out_w[u, t * piece : (t + 1) * piece, :])
            resid[part, u * cols : (u + 1) * cols] = acc
        h = resid[part, :]
        low = (h * inverse_rms(h) * gains[1:2, :]).astype(BF16)
        own[part, :] = low
        n2[rows_at(s, rows, c * half, half), :] = low
        ring.send(c, own.at[pl.ds(c * half, half), :])
    loads[0].wait()

    def gate_rows(t):
        ga[rows_at(t, rows), :] = nn(n2[rows_at(t, rows), :], gate_w[...])

    def act_rows(t):
        up = nn(n2[rows_at(t, rows), :], up_w[...])
        active, slope = gelu_both(ga[rows_at(t, rows), :])
        hid[rows_at(t, rows), :] = (active * up).astype(BF16)
        ga[rows_at(t, rows), :] = slope * up
        ub[rows_at(t, rows), :] = active

    pass_on(2 / 12)
    gate_rows(s)
    ring.got_near(0)
    ring.got_near(1)
    pass_on(3 / 12)
    gate_rows(near)
    pass_on(5 / 12)
    ring.forward(0)
    pass_on(6 / 12)
    ring.forward(1)
    pass_on(7 / 12)
    gate_rows(far)
    for c in range(2):
        ring.got_cross(c)
    gate_rows(cross)
    saves = [pltpu.make_async_copy(n2, n2_h, local.at[4])]
    saves[0].start()
    for a in ups:
        for d in range(pairs):
            a.complete(d)
    saves.append(pltpu.make_async_copy(up_w, up_h, local.at[5]))
    saves[1].start()
    pass_on(8 / 12)
    for t in (s, near):
        act_rows(t)
    pass_on(9 / 12)
    for t in (far, cross):
        act_rows(t)
    saves.append(pltpu.make_async_copy(hid, hid_h, local.at[6]))
    saves[2].start()
    loads[1].wait()
    pass_on(10 / 12)
    width_f = units // nfsdp
    wide = max(256 // width_f, 1)

    def down_part(n):
        got = dot_tn(hid[:, n * wide * width_f : (n + 1) * wide * width_f], cot[...]).astype(BF16)
        for m in range(wide):
            parts[n * wide + m] = got[m * width_f : (m + 1) * width_f, :]

    for n in range(nfsdp // wide):
        down_part(n)
        if n == 1:
            pass_on(11 / 12)
    saves.append(pltpu.make_async_copy(parts, parts_h, local.at[7]))
    saves[3].start()
    pass_on(1)

    def back_cols(at, units_at):
        for t in range(nseq):
            band = slice(t * rows, (t + 1) * rows)
            dh = nt(cot[band, :], down_w[units_at, :])
            dg[band, at] = (dh * ga[band, at]).astype(BF16)
            du[band, at] = (dh * ub[band, at]).astype(BF16)

    if (2 * width_f) % 128 == 0:
        for d in range(pairs):
            for a in downs:
                a.complete(d)
            at = pl.ds(pl.multiple_of(downs[0].source(downs[0].place(d)) * 2 * width_f, 2 * width_f), 2 * width_f)
            back_cols(at, at)
    else:
        for d in range(pairs):
            for a in downs:
                a.complete(d)
        for n in range(units // 256):
            at = slice(n * 256, (n + 1) * 256)
            back_cols(at, at)
    saves.append(pltpu.make_async_copy(down_w, down_h, local.at[8]))
    saves.append(pltpu.make_async_copy(dg, dg_h, local.at[9]))
    saves.append(pltpu.make_async_copy(du, du_h, local.at[10]))
    for a in saves[4:]:
        a.start()
    ring.drain()
    for a in ups + downs:
        a.drain()
    for a in trips:
        a.wait_send()
    for a in saves:
        a.wait()


def middle(o, out_w, tok, gains, up_q, down_q, gate_w, cot, nfsdp):
    nseq = out_w.shape[0]
    rows, width = tok.shape
    units = gate_w.shape[1]
    tall = nseq * rows
    return pl.pallas_call(
        middle_kernel,
        out_shape=(
            jax.ShapeDtypeStruct((nseq, rows, o.shape[1]), BF16),
            jax.ShapeDtypeStruct((rows, width), F32),
            jax.ShapeDtypeStruct((tall, width), BF16),
            jax.ShapeDtypeStruct((tall, units), BF16),
            jax.ShapeDtypeStruct((tall, units), BF16),
            jax.ShapeDtypeStruct((tall, units), BF16),
            jax.ShapeDtypeStruct((width, units), BF16),
            jax.ShapeDtypeStruct((units, width), BF16),
            jax.ShapeDtypeStruct((nfsdp, units // nfsdp, width), BF16),
        ),
        in_specs=[vm_spec()] * 4 + [any_spec()] * 4,
        out_specs=(vm_spec(), vm_spec()) + (any_spec(),) * 7,
        scratch_shapes=wires_scratch(9 + 4 * nfsdp)
        + [
            pltpu.SemaphoreType.DMA((13,)),
            pltpu.VMEM((rows, width), BF16),
            pltpu.VMEM((tall, width), BF16),
            pltpu.VMEM((tall, width), BF16),
            pltpu.VMEM((width, units), BF16),
            pltpu.VMEM((width, units), BF16),
            pltpu.VMEM((units, width), BF16),
            pltpu.VMEM((tall, units), F32),
            pltpu.VMEM((tall, units), F32),
            pltpu.VMEM((tall, units), BF16),
            pltpu.VMEM((tall, units), BF16),
            pltpu.VMEM((tall, units), BF16),
            pltpu.VMEM((nfsdp, units // nfsdp, width), BF16),
        ],
        compiler_params=call_params(2, 63),
        name="middle",
    )(o, out_w, tok, gains, up_q, down_q, gate_w, cot)


class SeqScatter:
    def __init__(self, wires, chunks, *bufs):
        self.s, self.near, self.far, self.cross = seq_places()
        self.wires, self.chunks, self.bufs = wires, chunks, bufs
        self.base = wires.take(3 * chunks)

    def trip(self, kind, c):
        where = {"seq": self.far if kind == 1 else self.near}
        src, dst = self.bufs[2 * kind].at[c], self.bufs[2 * kind + 1].at[c]
        return self.wires.at(self.base + 3 * c + kind, src, dst, where)

    def cross_chunk(self, c, value):
        self.bufs[0][c] = value.astype(BF16)
        self.trip(0, c).start()

    def far_chunk(self, c, value):
        self.trip(0, c).wait_recv()
        self.bufs[2][c] = (value + self.bufs[1][c].astype(F32)).astype(BF16)
        self.trip(1, c).start()

    def near_chunk(self, c, value):
        self.bufs[4][c] = value.astype(BF16)
        self.trip(2, c).start()

    def own_chunk(self, c, value):
        self.trip(2, c).wait_recv()
        self.trip(1, c).wait_recv()
        return value + self.bufs[5][c].astype(F32) + self.bufs[3][c].astype(F32)

    def finish(self):
        for c in range(self.chunks):
            for kind in range(3):
                self.trip(kind, c).wait_send()


def scatter_scratch(chunks, rows, width):
    return [pltpu.VMEM((chunks, rows, width), BF16)] * 6


def unmix_kernel(
    chunks, gains, obuf, resid, cot, down_p, dg_h, du_h, gate_h, up_h, out_h, n2_h, hid_h, dw_h,
    rgrad, dmix, ggrad, shard, lead_s, out_p, gate_p, up_p, y_h,
    send, recv, b0, b1, b2, b3, b4, b5, attn, dob, p0, p1, p2, p3, l0, l1, l2, l3, lead_p,
    local, dg, du, gate_w, up_w, out_w, n2, hid, down_w, wgrad, wbuf, stage, ystage, sems,
):
    rows, width = resid.shape
    nseq, _, piece = obuf.shape
    nfsdp = gate_p.shape[0]
    units = dg.shape[1]
    first_half = units // 2
    s, near, far, cross = seq_places()
    loads = [
        pltpu.make_async_copy(src, dst, local.at[n])
        for n, (src, dst) in enumerate(
            (
                (gate_h, gate_w),
                (up_h, up_w),
                (dg_h, dg),
                (du_h, du),
                (n2_h, n2),
                (out_h, out_w),
                (hid_h, hid),
                (dw_h, down_w),
            )
        )
    ]
    for a in loads:
        a.start()
    meet([{"seq": near}, {"seq": far}, {"seq": cross}] + fsdp_peers())
    wires = Wires(send, recv)
    grads = FsdpScatter(wires, down_p, (p0, p1, p2, p3), shard)
    grads.start()
    leads = FsdpScatter(wires, lead_p, (l0, l1, l2, l3), lead_s)
    pairs = grads.pairs
    sums = SeqScatter(wires, chunks, b0, b1, b2, b3, b4, b5)
    size = rows // chunks
    for a in loads[:4]:
        a.wait()

    def part(t, c):
        at = rows_at(t, rows, c * size, size)
        return nt(dg[at, :], gate_w[...]) + nt(du[at, :], up_w[...])

    for c in range(chunks):
        sums.cross_chunk(c, part(cross, c))
    for c in range(chunks):
        sums.far_chunk(c, part(far, c))
    for c in range(chunks):
        sums.near_chunk(c, part(near, c))
    for c in range(chunks):
        rgrad[c * size : (c + 1) * size, :] = part(s, c)
    grads.step(1)
    loads[4].wait()
    depth = width // nfsdp
    wide = 384
    saves = []

    def weight_parts(side, out, begin, end, cut):
        for n in range(begin, end):
            slot = n % 2
            group = pl.ds(n * (wide // depth), wide // depth)
            if len(saves) > 1:
                saves[-2].wait()
            got = dot_tn(n2[:, n * wide : (n + 1) * wide], side[...])
            for m in range(wide // depth):
                low = got[m * depth : (m + 1) * depth, :].astype(BF16)
                if cut:
                    lead_p[n * (wide // depth) + m] = low[:, :cut]
                stage[slot, m, :, : units - cut] = low[:, cut:]
            a = pltpu.make_async_copy(stage.at[slot, :, :, : units - cut], out.at[group], sems.at[3 + slot])
            a.start()
            saves.append(a)

    weight_parts(dg, gate_p, 0, width // wide, first_half)
    if pairs > 2:
        grads.step(2)
    loads[5].wait()
    cols = out_w.shape[2]

    def own_rows(c, total):
        at = slice(c * size, (c + 1) * size)
        dn = sums.own_chunk(c, rgrad[at, :])
        h = resid[at, :]
        r = inverse_rms(h)
        rg = cot[at, :].astype(F32) + norm_back(dn, h, r, gains[1:2, :])
        rgrad[at, :] = rg
        low = rg.astype(BF16)
        attn[at, :] = low
        for t in range(nseq):
            acc = jnp.zeros((size, piece), F32)
            for u in range(nseq):
                acc = acc + nt(low[:, u * cols : (u + 1) * cols], out_w[u, t * piece : (t + 1) * piece, :])
            dob[t, at, :] = acc.astype(BF16)
        return total + jnp.sum(dn * h * r, axis=0, keepdims=True)

    base = wires.take(3 * chunks)

    def trip(n, t, c):
        at = pl.ds(c * size, size)
        return wires.at(base + 3 * c + n, dob.at[t, at, :], dmix.at[rows_at(s, rows, c * size, size), :], {"seq": t})

    total = jnp.zeros((1, width), F32)
    for c in range(chunks):
        total = own_rows(c, total)
        if c == 0:
            weight_parts(du, up_p, 0, 1, 0)
            leads.start()
        for n, t in enumerate((far, cross, near)):
            trip(n, t, c).start()
        dmix[rows_at(s, rows, c * size, size), :] = dob[s, pl.ds(c * size, size), :]
        if c == 0:
            weight_parts(du, up_p, 1, width // wide, 0)
            for d in range(3, pairs):
                grads.step(d)
    ggrad[...] = jnp.broadcast_to(total, ggrad.shape)
    wbase = wires.take(3)

    def wtrip(n):
        u = (cross, far, near)[n]
        return wires.at(wbase + n, wgrad.at[u], wbuf.at[n], {"seq": far if n == 1 else near})

    def wblock(u):
        for t in range(nseq):
            at = pl.ds(pl.multiple_of(u * cols, 128), cols)
            wgrad[u, t * piece : (t + 1) * piece, :] = dot_tn(obuf[t], attn[:, at]).astype(BF16)

    wblock(cross)
    wblock(far)
    wtrip(0).start()
    wblock(near)
    wtrip(0).wait_recv()
    wgrad[far] = (wgrad[far].astype(F32) + wbuf[0].astype(F32)).astype(BF16)
    wblock(s)
    wtrip(1).start()
    wtrip(2).start()
    leads.step(1)
    for a in loads[6:]:
        a.wait()
    ycopies = []
    for t in range(nseq):
        slot = t % 2
        if t > 1:
            ycopies[t - 2].wait()
        at = slice(t * rows, (t + 1) * rows)
        ystage[slot] = nn(hid[at, :], down_w[...]).astype(BF16)
        ycopies.append(pltpu.make_async_copy(ystage.at[slot], y_h.at[at, :], sems.at[slot]))
        ycopies[t].start()
        if t == 0:
            for d in range(2, pairs - 1):
                leads.step(d)
        if t == 1 and pairs > 2:
            leads.step(pairs - 1)
    for c in range(chunks):
        for n, t in enumerate((far, cross, near)):
            trip(n, t, c).wait()
    grads.finish()
    for n in range(1, 3):
        wtrip(n).wait_recv()
    wsum = wgrad[s].astype(F32) + wbuf[1].astype(F32) + wbuf[2].astype(F32)
    lines = out_p.shape[1]
    for f in range(nfsdp):
        out_p[f] = wsum[f * lines : (f + 1) * lines, :].astype(BF16)
    for n in range(3):
        wtrip(n).wait_send()
    sums.finish()
    grads.drain()
    leads.finish()
    leads.drain()
    for a in saves[-2:]:
        a.wait()
    for a in ycopies[-2:]:
        a.wait()


def unmix(gains, obuf, resid, cot, down_p, dg, du, gate_w, up_w, out_w, n2, hid, down_w, chunks=2):
    rows, width = resid.shape
    nseq, _, piece = obuf.shape
    nfsdp = down_p.shape[0]
    units = dg.shape[1]
    grad_shape = (nfsdp, width // nfsdp, units)
    half_shape = (nfsdp, width // nfsdp, units // 2)
    return pl.pallas_call(
        functools.partial(unmix_kernel, chunks),
        out_shape=(
            jax.ShapeDtypeStruct((rows, width), F32),
            jax.ShapeDtypeStruct((nseq * rows, piece), BF16),
            jax.ShapeDtypeStruct((8, width), F32),
            jax.ShapeDtypeStruct(down_p.shape[1:], BF16),
            jax.ShapeDtypeStruct(half_shape[1:], BF16),
            jax.ShapeDtypeStruct((nfsdp, out_w.shape[1] // nfsdp, out_w.shape[2]), BF16),
            jax.ShapeDtypeStruct(half_shape, BF16),
            jax.ShapeDtypeStruct(grad_shape, BF16),
            jax.ShapeDtypeStruct(n2.shape, BF16),
        ),
        in_specs=[vm_spec()] * 4 + [any_spec()] * 9,
        out_specs=(vm_spec(),) * 6 + (any_spec(),) * 3,
        scratch_shapes=wires_scratch(6 * chunks + 2 * nfsdp + 3)
        + scatter_scratch(chunks, rows // chunks, width)
        + [pltpu.VMEM((rows, width), BF16), pltpu.VMEM((nseq, rows, piece), BF16)]
        + fsdp_scatter_scratch(down_p.shape)
        + fsdp_scatter_scratch(half_shape)
        + [
            pltpu.VMEM(half_shape, BF16),
            pltpu.SemaphoreType.DMA((8,)),
            pltpu.VMEM(dg.shape, BF16),
            pltpu.VMEM(du.shape, BF16),
            pltpu.VMEM(gate_w.shape, BF16),
            pltpu.VMEM(up_w.shape, BF16),
            pltpu.VMEM(out_w.shape, BF16),
            pltpu.VMEM(n2.shape, BF16),
            pltpu.VMEM(hid.shape, BF16),
            pltpu.VMEM(down_w.shape, BF16),
            pltpu.VMEM(out_w.shape, BF16),
            pltpu.VMEM((3,) + out_w.shape[1:], BF16),
            pltpu.VMEM((2, 384 * nfsdp // width, width // nfsdp, units), BF16),
            pltpu.VMEM((2, rows, width), BF16),
            pltpu.SemaphoreType.DMA((5,)),
        ],
        compiler_params=call_params(4, 63),
        name="unmix",
    )(gains, obuf, resid, cot, down_p, dg, du, gate_w, up_w, out_w, n2, hid, down_w)


def build_strips(heads, first_head, starts, table, ids, strip, far):
    length = ids.shape[1]
    half = 2 * PROMPT
    for h in range(heads):
        row = jnp.zeros(ids.shape, F32)
        for b in range(table.shape[0]):
            row = jnp.where(ids[...] == b, table[b, first_head + h], row)
        row = jnp.broadcast_to(row, (8, length))
        base = jnp.broadcast_to(row[:1, PROMPT // 2 : PROMPT // 2 + half], (128, half))
        strip[h] = pltpu.roll(base, 1, 1, stride=1, stride_axis=0)[:, 128:]
        for c in range(2):
            moved = pltpu.roll(row, length - PROMPT // 2 - starts[c], 1)
            base = jnp.broadcast_to(moved[:1, : FARW + 128], (128, FARW + 128))
            far[h, c] = pltpu.roll(base, 1, 1, stride=1, stride_axis=0)[:, 128:]


def head_masks(width, heads):
    lane = lax.broadcasted_iota(jnp.int32, (1, width), 1)
    return [(lane >= h * HEAD_DIM) & (lane < (h + 1) * HEAD_DIM) for h in range(heads)]


def masked_copies(src, dst, heads):
    masks = head_masks(src.shape[1], heads)
    for h in range(heads):
        dst[h] = jnp.where(masks[h], src[...], jnp.zeros((), src.dtype))


def bias_chunk(strip, far, h, first_q, kstart, kind, c):
    parts = []
    for r in range(KC // 128):
        m = PROMPT - 128 - (kstart + 128 * r)
        if kind == "far":
            parts.append(far[h, c, :, m : m + CL])
        else:
            parts.append(strip[h, :, pl.ds(pl.multiple_of(first_q + m, 128), CL)])
    return jnp.concatenate(parts, axis=0)


def pack_piece(units, nfsdp, nseq):
    block = units // nfsdp
    return block, -(-block // (16 * nseq)) * 16


def pack_front(t, raw, first_q, out_q, gains):
    r_q, r_k, r_v, r_o = raw
    piece = first_q.shape[1] * 3 // 10
    depth = first_q.shape[0]
    cut = slice(t * piece, (t + 1) * piece)
    first_q[...] = jnp.concatenate(
        [r_q[:, cut], r_k[:, cut], r_v[:, cut], gains, jnp.zeros((depth, first_q.shape[1] - 3 * piece - 8), BF16)], axis=1
    )
    cols = out_q.shape[1]
    out_q[...] = r_o[:, t * cols : (t + 1) * cols]


def pack_cols(t, nseq, nfsdp, raw, packed):
    block, piece = pack_piece(raw.shape[1], nfsdp, nseq)
    pieces = []
    for f in range(nfsdp):
        begin = f * block + t * piece
        end = min(begin + piece, (f + 1) * block)
        pieces.append(raw[:, begin:end])
        if end - begin < piece:
            pieces.append(jnp.zeros((raw.shape[0], piece - end + begin), BF16))
    packed[...] = jnp.concatenate(pieces, axis=1)


def pack_down(t, raw, packed):
    piece = packed.shape[0]
    begin = t * piece
    end = min(begin + piece, raw.shape[0])
    packed[: end - begin, :] = raw[begin:end, :]
    if end - begin < piece:
        packed[end - begin :, :] = jnp.zeros((piece - end + begin, raw.shape[1]), BF16)


def front_kernel(
    heads, nseq, starts, table, ids, gain_q, tok, w_q, w_k, w_v, w_o, w_g, w_u, w_d, cot,
    q, k, v, o, lse, gains, n1_h, first_h, out_w, cots, gate_w, up_q, down_q,
    send, recv, local, r_q, r_k, r_v, r_o, r_g, r_u, r_d, first_q, out_q, gate_q, up_s, down_s,
    group, n1, first, strip, far, kh, vt, ot, s,
):
    rows, width = tok.shape
    mine, near, other, cross = seq_places()
    pair, side, pairs = fsdp_places()
    nfsdp = 2 * pairs
    loads = [
        pltpu.make_async_copy(src, dst, local.at[n])
        for n, (src, dst) in enumerate(
            ((w_q, r_q), (w_k, r_k), (w_v, r_v), (w_o, r_o), (w_g, r_g), (w_u, r_u), (w_d, r_d))
        )
    ]
    for a in loads:
        a.start()
    meet([{"seq": near}, {"seq": other}] + fsdp_peers())
    wires = Wires(send, recv)
    half = rows // 2
    ring = SeqGather(wires, lambda t, c: group.at[rows_at(t, rows, c * half, half), :], 2)
    size = first_q.shape[0]
    lead = FsdpGather(wires, first_q, lambda f: first.at[shard_rows(f, size), :], local.at[7])
    late = FsdpGather(wires, out_q, lambda f: out_w.at[mine, f], local.at[8])
    gate_size = gate_q.shape[0]
    weights = gather_halves(wires, gate_q, gate_w, gate_size, (local.at[9], local.at[16]))
    wring = SeqGather(wires, lambda t, c: out_w.at[t], 1)
    cring = SeqGather(wires, lambda t, c: cots.at[rows_at(t, rows, c * half, half), :], 2)
    own = [
        pltpu.make_async_copy(tok, group.at[rows_at(mine, rows), :], local.at[10]),
        pltpu.make_async_copy(cot, cots.at[rows_at(mine, rows), :], local.at[11]),
    ]
    for c in range(2):
        ring.send(c, tok.at[pl.ds(c * half, half), :])
    for a in own:
        a.start()
    for a in loads[:4]:
        a.wait()
    both = jnp.concatenate([gain_q[...], jnp.zeros((6, gain_q.shape[1]), F32)], axis=0).T.astype(BF16)
    for t in range(nseq):

        @pl.when(mine == t)
        def _():
            pack_front(t, (r_q, r_k, r_v, r_o), first_q, out_q, both)

    for a in loads[4:]:
        a.wait()
    lead.start()
    for t in range(nseq):

        @pl.when(mine == t)
        def _():
            pack_cols(t, nseq, nfsdp, r_g, gate_q)

    late.start()
    for t in range(nseq):

        @pl.when(mine == t)
        def _():
            pack_cols(t, nseq, nfsdp, r_u, up_s)
            pack_down(t, r_d, down_s)

    for a in weights:
        a.start()
    for c in range(2):
        cring.send(c, cot.at[pl.ds(c * half, half), :])
    saves = [pltpu.make_async_copy(up_s, up_q, local.at[12]), pltpu.make_async_copy(down_s, down_q, local.at[13])]
    for a in saves:
        a.start()
    build_strips(heads, mine * heads, starts, table, ids, strip, far)
    lse[...] = jnp.zeros(lse.shape, F32)
    for d in range(1, pairs):
        lead.forward(d)
        if d == pairs // 2:
            ring.forward(0)
    for d in range(1, pairs):
        late.forward(d)
    ring.forward(1)
    lead.finish()
    saves.append(pltpu.make_async_copy(first, first_h, local.at[14]))
    saves[2].start()
    piece = q.shape[1]
    column = 3 * piece
    gains[...] = jnp.zeros(gains.shape, F32)
    for b in range(width // 256):
        band = first[b * 256 : (b + 1) * 256, column // 128 * 128 : column // 128 * 128 + 128].astype(F32).T
        for n in range(2):
            line = column % 128 + n
            gains[n : n + 1, b * 256 : (b + 1) * 256] = band[line : line + 1, :]

    def project(t):
        at = rows_at(t, rows)
        x = group[at, :].astype(F32)
        low = (x * inverse_rms(x) * gains[0:1, :]).astype(BF16)
        n1[at, :] = low
        r = nn(low, first[:, :column])
        q[at, :] = r[:, :piece].astype(BF16)
        k[at, :] = r[:, piece : 2 * piece].astype(BF16)
        v[at, :] = r[:, 2 * piece :].astype(BF16)

    own[0].wait()
    project(mine)
    for c in range(2):
        ring.got_near(c)
    project(near)
    project(other)
    for c in range(2):
        ring.got_cross(c)
    project(cross)
    saves.append(pltpu.make_async_copy(n1, n1_h, local.at[15]))
    saves[3].start()
    for d in range(pairs):
        late.complete(d)
    wring.send(0, out_w.at[mine])
    masked_copies(k, kh, heads)
    vt[...] = v[...].astype(F32).T.astype(BF16)

    def block(h, q0, bias_q0, chunks, c):
        qb = q[pl.ds(q0, CL), :]
        top = None
        for n, (k0, kind, kstart) in enumerate(chunks):
            sc = nt(kh[h, pl.ds(k0, KC), :], qb) + bias_chunk(strip, far, h, bias_q0, kstart, kind, c)
            s[n * KC : (n + 1) * KC, :] = sc
            m = jnp.max(sc, axis=0, keepdims=True)
            top = m if top is None else jnp.maximum(top, m)
        total = jnp.zeros((1, CL), F32)
        acc = jnp.zeros((HEAD_DIM, CL), F32)
        for n, (k0, kind, kstart) in enumerate(chunks):
            e = jnp.exp(s[n * KC : (n + 1) * KC, :] - top)
            total = total + jnp.sum(e, axis=0, keepdims=True)
            acc = acc + nn(vt[pl.ds(pl.multiple_of(h * HEAD_DIM, HEAD_DIM), HEAD_DIM), pl.ds(k0, KC)], e.astype(BF16))
        ot[pl.ds(pl.multiple_of(h * HEAD_DIM, HEAD_DIM), HEAD_DIM), pl.ds(q0, CL)] = acc / total
        lse[pl.ds(h, 1), pl.ds(q0, CL)] = top + jnp.log(total)

    nblk = PROMPT // CL
    hooks = [(n, d) for n in range(2) for d in range(1, pairs)]

    def prompt_body(i, carry):
        h, blk = i // nblk, i % nblk
        q0 = pl.multiple_of(blk * CL, CL)
        block(h, q0, q0, [(j * KC, "strip", j * KC) for j in range(PROMPT // KC)], None)
        for n, (half_n, d) in enumerate(hooks[:-2]):

            @pl.when(i == heads * nblk * n // (len(hooks) - 2))
            def _():
                weights[half_n].forward(d)

        return carry

    lax.fori_loop(0, heads * nblk, prompt_body, 0)

    def cont_body(i, carry):
        h, c = i // 2, i % 2
        q0 = pl.multiple_of(PROMPT + c * CL, CL)
        chunks = [(j * KC, "far", j * KC) for j in range(PROMPT // KC)]
        chunks += [(q0 + j * KC, "strip", j * KC) for j in range(CL // KC)]
        block(h, q0, 0, chunks, c)
        return carry

    for n, d in hooks[-2:-1]:
        weights[n].forward(d)
    cring.forward(0)
    lax.fori_loop(0, heads * 2, cont_body, 0)
    o[...] = ot[...].T.astype(BF16)
    weights[1].forward(pairs - 1)
    cring.forward(1)
    wring.forward(0)
    for a in own[1:] + saves:
        a.wait()
    for a in weights:
        a.finish()
    late.drain()
    wring.finish()
    cring.finish()
    ring.drain()


def front(starts, table, ids, gain_q, tok, w_q, w_k, w_v, w_o, w_g, w_u, w_d, cot, nseq, nfsdp):
    rows, width = tok.shape
    inner = w_q.shape[1]
    piece = inner // nseq
    heads = piece // HEAD_DIM
    tall = nseq * rows
    size = w_q.shape[0]
    units = pack_piece(w_g.shape[1], nfsdp, nseq)[1]
    cols = width // nseq
    lead = piece * 10 // 3
    smem = pl.BlockSpec(memory_space=pltpu.SMEM)
    return pl.pallas_call(
        functools.partial(front_kernel, heads, nseq),
        out_shape=(
            jax.ShapeDtypeStruct((tall, piece), BF16),
            jax.ShapeDtypeStruct((tall, piece), BF16),
            jax.ShapeDtypeStruct((tall, piece), BF16),
            jax.ShapeDtypeStruct((tall, piece), BF16),
            jax.ShapeDtypeStruct((8, tall), F32),
            jax.ShapeDtypeStruct((8, width), F32),
            jax.ShapeDtypeStruct((tall, width), BF16),
            jax.ShapeDtypeStruct((width, lead), BF16),
            jax.ShapeDtypeStruct((nseq, nfsdp, w_o.shape[0], cols), BF16),
            jax.ShapeDtypeStruct((tall, width), BF16),
            jax.ShapeDtypeStruct((width, nfsdp * units), BF16),
            jax.ShapeDtypeStruct((size, nfsdp * units), BF16),
            jax.ShapeDtypeStruct((nseq * units // nseq, width), BF16),
        ),
        in_specs=[smem, smem, vm_spec(), vm_spec()] + [any_spec()] * 9,
        out_specs=(vm_spec(),) * 6 + (any_spec(),) * 7,
        scratch_shapes=wires_scratch(15 + 4 * nfsdp)
        + [
            pltpu.SemaphoreType.DMA((17,)),
            pltpu.VMEM(w_q.shape, BF16),
            pltpu.VMEM(w_k.shape, BF16),
            pltpu.VMEM(w_v.shape, BF16),
            pltpu.VMEM(w_o.shape, BF16),
            pltpu.VMEM(w_g.shape, BF16),
            pltpu.VMEM(w_u.shape, BF16),
            pltpu.VMEM(w_d.shape, BF16),
            pltpu.VMEM((size, lead), BF16),
            pltpu.VMEM((w_o.shape[0], cols), BF16),
            pltpu.VMEM((size, nfsdp * units), BF16),
            pltpu.VMEM((size, nfsdp * units), BF16),
            pltpu.VMEM((units, width), BF16),
            pltpu.VMEM((tall, width), BF16),
            pltpu.VMEM((tall, width), BF16),
            pltpu.VMEM((width, lead), BF16),
            pltpu.VMEM((heads, 128, STRIP), F32),
            pltpu.VMEM((heads, 2, 128, FARW), F32),
            pltpu.VMEM((heads, tall, piece), BF16),
            pltpu.VMEM((piece, tall), BF16),
            pltpu.VMEM((piece, tall), F32),
            pltpu.VMEM((PROMPT + CL, CL), F32),
        ],
        compiler_params=call_params(1, 60),
        name="front",
    )(starts, table, ids, gain_q, tok, w_q, w_k, w_v, w_o, w_g, w_u, w_d, cot)


def back_kernel(
    heads, chunks, starts, table, ids, gains, lse, gain_b, q, k, v, o, do,
    resid_h, rgrad_h, tok_h, y_p, out_p, gate_p, up_p, done_h, lead_h, n1_h, first_h,
    small, y_h, in_h, down_f, lead_f, gate_f, up_f, qkv_f, out_f,
    send, recv, local, ybuf, qkv_p, b0, b1, b2, b3, b4, b5,
    g0, g1, g2, g3, u0, u1, u2, u3, q0_, q1_, q2_, q3_, o0, o1, o2, o3,
    gate_s, up_s, qkv_s, out_s, dqkv, tok, held, stage, one, two, three, tgrad,
):
    rows, width = tok.shape
    nseq = q.shape[0] // rows
    piece = q.shape[1]
    nfsdp = gate_p.shape[0]
    s, near, far_d, cross = seq_places()
    pair, side, pairs = fsdp_places()

    def y_block(t):
        return y_p.at[rows_at(t, rows), :]

    loads = [
        pltpu.make_async_copy(y_block(far_d), ybuf.at[2], local.at[0]),
        pltpu.make_async_copy(y_block(s), ybuf.at[3], local.at[1]),
    ]
    loads.append(pltpu.make_async_copy(tok_h, tok, local.at[5]))
    for a in loads:
        a.start()
    meet([{"seq": near}, {"seq": far_d}, {"seq": cross}] + fsdp_peers())
    wires = Wires(send, recv)
    hop = wires.go(y_block(cross), ybuf.at[0], {"seq": near})
    turn = wires.go(y_block(near), ybuf.at[1], {"seq": near})
    gates = FsdpScatter(wires, gate_p, (g0, g1, g2, g3), gate_s)
    ups = FsdpScatter(wires, up_p, (u0, u1, u2, u3), up_s)
    gates.start()
    ups.start()
    down_ring = SeqGather(wires, lambda t, c: down_f.at[t], 1)
    lead_ring = SeqGather(wires, lambda t, c: lead_f.at[t], 1)
    gate_ring = SeqGather(wires, lambda t, c: gate_f.at[t], 1)
    up_ring = SeqGather(wires, lambda t, c: up_f.at[t], 1)
    qkv_ring = SeqGather(wires, lambda t, c: qkv_f.at[t], 1)
    out_ring = SeqGather(wires, lambda t, c: out_f.at[t], 1)
    qkvs = FsdpScatter(wires, qkv_p, (q0_, q1_, q2_, q3_), qkv_s)
    outs = FsdpScatter(wires, out_p, (o0, o1, o2, o3), out_s)
    far_hop = wires.at(wires.take(1), ybuf.at[2], ybuf.at[4], {"seq": far_d})
    down_keep = pltpu.make_async_copy(done_h, down_f.at[s], local.at[6])
    down_keep.start()
    down_ring.send(0, done_h)
    lead_keep = pltpu.make_async_copy(lead_h, lead_f.at[s], local.at[10])
    lead_keep.start()
    lead_ring.send(0, lead_h)
    length = ids.shape[1]
    half = 2 * PROMPT

    def attend_back(strip, far, kh, vh, kt, delta, dqt, dk, dv, gstrip, gfar):
        build_strips(heads, s * heads, starts, table, ids, strip, far)
        loads[0].wait()
        hop.wait_recv()
        ybuf[2] = (ybuf[2].astype(F32) + ybuf[0].astype(F32)).astype(BF16)
        for src, dst in ((k, kh), (v, vh)):
            masked_copies(src, dst, heads)
        far_hop.start()
        kt[...] = k[...].astype(F32).T.astype(BF16)
        prod = (o[...].astype(F32) * do[...].astype(F32)).T
        for h in range(heads):
            delta[h : h + 1, :] = jnp.sum(prod[h * HEAD_DIM : (h + 1) * HEAD_DIM, :], axis=0, keepdims=True)
        dk[...] = jnp.zeros(dk.shape, F32)
        dv[...] = jnp.zeros(dv.shape, F32)
        gstrip[...] = jnp.zeros(gstrip.shape, F32)
        gfar[...] = jnp.zeros(gfar.shape, F32)
        lane = lax.broadcasted_iota(jnp.int32, (1, piece), 1)

        def block(h, q0, bias_q0, chunk_list, c):
            qb = q[pl.ds(q0, CL), :]
            dob = do[pl.ds(q0, CL), :]
            keep = lane // HEAD_DIM == h
            qhb = jnp.where(keep, qb, jnp.zeros((), BF16))
            dohb = jnp.where(keep, dob, jnp.zeros((), BF16))
            lrow = lse[pl.ds(h, 1), pl.ds(q0, CL)]
            drow = delta[pl.ds(h, 1), pl.ds(q0, CL)]
            acc = jnp.zeros((HEAD_DIM, CL), F32)
            for n, (k0, kind, kstart) in enumerate(chunk_list):
                ks = pl.ds(k0, KC)
                sc = nt(kh[h, ks, :], qb) + bias_chunk(strip, far, h, bias_q0, kstart, kind, c)
                pr = jnp.exp(sc - lrow)
                dp = nt(vh[h, ks, :], dob)
                ds = pr * (dp - drow)
                dsl = ds.astype(BF16)
                dv[ks, :] += nn(pr.astype(BF16), dohb)
                dk[ks, :] += nn(dsl, qhb)
                acc = acc + nn(kt[pl.ds(pl.multiple_of(h * HEAD_DIM, HEAD_DIM), HEAD_DIM), ks], dsl)
                for r in range(KC // 128):
                    m = PROMPT - 128 - (kstart + 128 * r)
                    part = ds[128 * r : 128 * (r + 1), :]
                    if kind == "far":
                        gfar[h, c, :, m : m + CL] += part
                    else:
                        gstrip[h, :, pl.ds(pl.multiple_of(bias_q0 + m, 128), CL)] += part
            dqt[pl.ds(pl.multiple_of(h * HEAD_DIM, HEAD_DIM), HEAD_DIM), pl.ds(q0, CL)] = acc

        nblk = PROMPT // CL

        def prompt_body(i, carry):
            h, blk = i // nblk, i % nblk
            q0 = pl.multiple_of(blk * CL, CL)
            block(h, q0, q0, [(j * KC, "strip", j * KC) for j in range(PROMPT // KC)], None)

            for k in range(1, pairs):

                @pl.when(i == heads * nblk * k // pairs)
                def _():
                    gates.step(k)

            return carry

        lax.fori_loop(0, heads * nblk, prompt_body, 0)

        def cont_body(i, carry):
            h, c = i // 2, i % 2
            q0 = pl.multiple_of(PROMPT + c * CL, CL)
            chunk_list = [(j * KC, "far", j * KC) for j in range(PROMPT // KC)]
            chunk_list += [(q0 + j * KC, "strip", j * KC) for j in range(CL // KC)]
            block(h, q0, 0, chunk_list, c)

            @pl.when(i == heads)
            def _():
                ups.step(1)

            return carry

        lax.fori_loop(0, heads * 2, cont_body, 0)
        dqkv[...] = jnp.concatenate([dqt[...].T, dk[...], dv[...]], axis=1).astype(BF16)
        lines8 = lax.broadcasted_iota(jnp.int32, (table.shape[0], length), 0)
        hot = ids[:1, :] == lines8
        tgrad[...] = jnp.zeros(tgrad.shape, F32)
        for h in range(heads):

            def unskew(g, span):
                full = jnp.concatenate([jnp.zeros((128, 128), F32), g], axis=1)
                eight = full[:8]
                for a in range(1, 16):
                    eight = eight + pltpu.roll(full[8 * a : 8 * a + 8], span - 8 * a, 1)
                vec = pltpu.roll(eight, span - 1, 1)[:1]
                for b in range(1, 8):
                    vec = vec + pltpu.roll(eight, span - 1 - b, 1)[b : b + 1]
                return jnp.concatenate([vec, jnp.zeros((1, length - span), F32)], axis=1)

            whole = jnp.broadcast_to(unskew(gstrip[h], half), (8, length))
            whole = pltpu.roll(whole, PROMPT // 2, 1)
            for c in range(2):
                moved = jnp.broadcast_to(unskew(gfar[h, c], FARW + 128), (8, length))
                whole = whole + pltpu.roll(moved, PROMPT // 2 + starts[c], 1)
            picked = jnp.where(hot, whole[:1, :], 0.0)
            column = jnp.broadcast_to(jnp.sum(picked, axis=1, keepdims=True), (table.shape[0], 128))
            tgrad[h : h + 1, : table.shape[0]] = column.T[:1, :]

    tall = nseq * rows
    pl.run_scoped(
        attend_back,
        pltpu.VMEM((heads, 128, STRIP), F32),
        pltpu.VMEM((heads, 2, 128, FARW), F32),
        pltpu.VMEM((heads, tall, piece), BF16),
        pltpu.VMEM((heads, tall, piece), BF16),
        pltpu.VMEM((piece, tall), BF16),
        pltpu.VMEM((8, tall), F32),
        pltpu.VMEM((piece, tall), F32),
        pltpu.VMEM((tall, piece), F32),
        pltpu.VMEM((tall, piece), F32),
        pltpu.VMEM((heads, 128, STRIP), F32),
        pltpu.VMEM((heads, 2, 128, FARW), F32),
    )

    def rest(n1, hold, rgrad, resid, first):
        later = [
            pltpu.make_async_copy(n1_h, n1, local.at[7]),
            pltpu.make_async_copy(rgrad_h, rgrad, local.at[8]),
            pltpu.make_async_copy(resid_h, resid, local.at[9]),
        ]
        ready = pltpu.make_async_copy(first_h, first, local.at[4])
        ready.start()
        for a in later:
            a.start()
        sums = SeqScatter(wires, chunks, b0, b1, b2, b3, b4, b5)
        size = rows // chunks
        ready.wait()

        def part(t, c):
            return nt(dqkv[rows_at(t, rows, c * size, size), :], first[:, : 3 * piece])

        for c in range(chunks):
            sums.cross_chunk(c, part(cross, c))
        for c in range(chunks):
            sums.far_chunk(c, part(far_d, c))
        for k in range(2, pairs - 1):
            ups.step(k)
        later[0].wait()
        depth = width // nfsdp
        wide = 384
        for n in range(width // wide):
            got = dot_tn(n1[:, n * wide : (n + 1) * wide], dqkv[...])
            for m in range(wide // depth):
                qkv_p[n * (wide // depth) + m] = got[m * depth : (m + 1) * depth, :].astype(BF16)
        for c in range(chunks):
            sums.near_chunk(c, part(near, c))
        for c in range(chunks):
            hold[c * size : (c + 1) * size, :] = part(s, c)
        qkvs.start()
        if pairs > 2:
            ups.step(pairs - 1)
        gates.finish()
        outs.start()
        gate_keep = pltpu.make_async_copy(gate_s, gate_f.at[s], local.at[11])
        gate_keep.start()
        gate_ring.send(0, gate_s)
        down_ring.forward(0)
        lead_ring.forward(0)
        later[2].wait()
        loads[1].wait()
        turn.wait_recv()
        far_hop.wait_recv()
        total = ybuf[3].astype(F32) + ybuf[1].astype(F32) + ybuf[4].astype(F32)
        ybuf[3] = (resid[...] + total).astype(BF16)
        qkvs.step(1)
        loads[2].wait()
        later[1].wait()
        gsum = jnp.zeros((1, width), F32)
        y_keep = pltpu.make_async_copy(ybuf.at[3], y_h, local.at[12])
        y_keep.start()
        for c in range(chunks):
            at = slice(c * size, (c + 1) * size)
            dn = sums.own_chunk(c, hold[at, :])
            x = tok[at, :].astype(F32)
            r = inverse_rms(x)
            gsum = gsum + jnp.sum(dn * x * r, axis=0, keepdims=True)
            tok[at, :] = (rgrad[at, :] + norm_back(dn, x, r, gains[0:1, :])).astype(BF16)
            if c == 0:
                for k in range(2, pairs - 1):
                    qkvs.step(k)
                ups.finish()
                up_keep = pltpu.make_async_copy(up_s, up_f.at[s], local.at[14])
                up_keep.start()
                up_ring.send(0, up_s)
                if pairs > 2:
                    qkvs.step(pairs - 1)
        in_keep = pltpu.make_async_copy(tok, in_h, local.at[13])
        in_keep.start()
        held[...] = jnp.zeros(held.shape, F32)
        lanes = held.shape[1]
        lines = width // lanes
        for n in range(lines):
            held[n : n + 1, :] = gsum[:, n * lanes : (n + 1) * lanes]
            held[lines + n : lines + n + 1, :] = gain_b[:1, n * lanes : (n + 1) * lanes]
        held[pl.ds(2 * lines + s * 8, 8), :] = tgrad[...]
        outs.step(1)
        trips = [wires.go(held, one.at[n], {"seq": t}) for n, t in enumerate((near, far_d, cross))]
        gate_ring.forward(0)
        for k in range(2, pairs):
            outs.step(k)
        for a in trips:
            a.wait_recv()
        stage[0] = held[...] + one[0] + one[1] + one[2]
        up_ring.forward(0)
        trips.append(wires.go(stage.at[0], two, {"fsdp": pair * 2 + 1 - side}))
        trips[-1].wait_recv()
        stage[1] = stage[0] + two[...]
        zs = [
            wires.go(stage.at[1], three.at[d - 1], {"fsdp": lax.rem(pair + d, pairs) * 2 + side})
            for d in range(1, pairs)
        ]
        qkvs.finish()
        qkv_keep = pltpu.make_async_copy(qkv_s, qkv_f.at[s], local.at[15])
        qkv_keep.start()
        qkv_ring.send(0, qkv_s)
        outs.finish()
        out_keep = pltpu.make_async_copy(out_s, out_f.at[s], local.at[16])
        out_keep.start()
        out_ring.send(0, out_s)
        total = stage[1]
        for d, a in enumerate(zs):
            a.wait_recv()
            total = total + three[d]
        small[...] = total
        qkv_ring.forward(0)
        out_ring.forward(0)
        for a in (down_ring, lead_ring, gate_ring, up_ring, qkv_ring, out_ring):
            a.finish()
        sums.finish()
        for a in (gates, ups, qkvs, outs):
            a.drain()
        for a in (gate_keep, up_keep, qkv_keep, out_keep, y_keep, in_keep, down_keep, lead_keep):
            a.wait()
        for a in trips + zs + [hop, turn, far_hop]:
            a.wait_send()

    pl.run_scoped(
        rest,
        pltpu.VMEM((tall, width), BF16),
        pltpu.VMEM((rows, width), F32),
        pltpu.VMEM((rows, width), F32),
        pltpu.VMEM((rows, width), F32),
        pltpu.VMEM(first_h.shape, BF16),
    )


def back(starts, table, ids, gains, lse, gain_b, q, k, v, o, do, resid, rgrad, tok, y_p, out_p, gate_p, up_p, done, lead, n1, first, chunks=2):
    tall, piece = q.shape
    heads = piece // HEAD_DIM
    rows, width = tok.shape
    nseq = tall // rows
    nfsdp = gate_p.shape[0]
    pairs = nfsdp // 2
    lines = -(-(2 * width // 128 + 8 * nseq) // 8) * 8
    qkv_shape = (nfsdp, width // nfsdp, 3 * piece)
    out_shape = out_p.shape
    smem = pl.BlockSpec(memory_space=pltpu.SMEM)

    def full(a):
        return jax.ShapeDtypeStruct((nseq,) + tuple(a), BF16)

    return pl.pallas_call(
        functools.partial(back_kernel, heads, chunks),
        out_shape=(
            jax.ShapeDtypeStruct((lines, 128), F32),
            jax.ShapeDtypeStruct((rows, width), BF16),
            jax.ShapeDtypeStruct((rows, width), BF16),
            full(done.shape),
            full(lead.shape),
            full(gate_p.shape[1:]),
            full(up_p.shape[1:]),
            full(qkv_shape[1:]),
            full(out_shape[1:]),
        ),
        in_specs=[smem, smem] + [vm_spec()] * 9 + [any_spec()] * 11,
        out_specs=(vm_spec(),) + (any_spec(),) * 8,
        scratch_shapes=wires_scratch(6 + 4 * nfsdp + 18 + 3 * chunks + 4 + pairs)
        + [
            pltpu.SemaphoreType.DMA((17,)),
            pltpu.VMEM((5, rows, width), BF16),
            pltpu.VMEM(qkv_shape, BF16),
        ]
        + scatter_scratch(chunks, rows // chunks, width)
        + fsdp_scatter_scratch(gate_p.shape)
        + fsdp_scatter_scratch(up_p.shape)
        + fsdp_scatter_scratch(qkv_shape)
        + fsdp_scatter_scratch(out_shape)
        + [
            pltpu.VMEM(gate_p.shape[1:], BF16),
            pltpu.VMEM(up_p.shape[1:], BF16),
            pltpu.VMEM(qkv_shape[1:], BF16),
            pltpu.VMEM(out_shape[1:], BF16),
            pltpu.VMEM((tall, 3 * piece), BF16),
            pltpu.VMEM((rows, width), BF16),
            pltpu.VMEM((lines, 128), F32),
            pltpu.VMEM((2, lines, 128), F32),
            pltpu.VMEM((3, lines, 128), F32),
            pltpu.VMEM((lines, 128), F32),
            pltpu.VMEM((pairs - 1, lines, 128), F32),
            pltpu.VMEM((8, 128), F32),
        ],
        compiler_params=call_params(5, 64),
        name="back",
    )(starts, table, ids, gains, lse, gain_b, q, k, v, o, do, resid, rgrad, tok, y_p, out_p, gate_p, up_p, done, lead, n1, first)


def unpack_kernel(nseq, nfsdp, heads, *refs):
    srcs, small, outs = refs[:8], refs[8], refs[9:18]
    ga, gb, table, ins, offs = refs[18:23]
    vs, ts = refs[23:31], refs[31:]
    loads = [pltpu.make_async_copy(a, b, ins.at[n]) for n, (a, b) in enumerate(zip(srcs, vs))]
    for a in loads:
        a.start()
    lead_f, gate_f, up_f, down_f, qkv_f, out_f, y, dx = vs
    tq, tk, tv, to, tg, tu, td = ts
    gq, gk, gv, go, gg, gu, gd, gy, gx = outs
    copies = []

    def save(src, dst):
        copies.append(pltpu.make_async_copy(src, dst, offs.at[len(copies)]))
        copies[-1].start()

    block, piece = pack_piece(tg.shape[1], nfsdp, nseq)
    half = nfsdp // 2

    def columns(get):
        parts = []
        for f in range(nfsdp):
            for t in range(nseq):
                size = min(piece, block - t * piece)
                full, f_at = get(f)
                parts.append(full[t, :, f_at * piece : f_at * piece + size].astype(F32))
        return jnp.concatenate(parts, axis=1)

    loads[0].wait()
    loads[1].wait()
    tg[...] = columns(lambda f: (lead_f, f) if f < half else (gate_f, f - half))
    save(tg, gg)
    loads[2].wait()
    tu[...] = columns(lambda f: (up_f, f))
    save(tu, gu)
    loads[3].wait()
    size = down_f.shape[1]
    for t in range(nseq):
        n = min(size, td.shape[0] - t * size)
        td[t * size : t * size + n, :] = down_f[t, :n, :].astype(F32)
    save(td, gd)
    loads[4].wait()
    width = qkv_f.shape[2] // 3
    for n, (dst, out) in enumerate(((tq, gq), (tk, gk), (tv, gv))):
        dst[...] = jnp.concatenate([qkv_f[t, :, n * width : (n + 1) * width] for t in range(nseq)], axis=1).astype(F32)
        save(dst, out)
    loads[5].wait()
    to[...] = jnp.concatenate([out_f[t] for t in range(nseq)], axis=1).astype(F32)
    save(to, go)
    for n, (src, dst) in enumerate(((y, gy), (dx, gx))):
        loads[6 + n].wait()
        save(src, dst)
    where = lax.axis_index("fsdp")
    share = ga.shape[1]
    lines = nfsdp * share // 128
    for n, dst in enumerate((ga, gb)):
        line = jnp.concatenate([small[n * lines + a : n * lines + a + 1, :] for a in range(lines)], axis=1)
        for f in range(nfsdp):

            @pl.when(where == f)
            def _():
                dst[...] = line[:, f * share : (f + 1) * share]

    turned = small[2 * lines : 2 * lines + 8 * nseq, :].T
    table[...] = jnp.concatenate([turned[: table.shape[0], 8 * t : 8 * t + heads] for t in range(nseq)], axis=1)
    for a in copies:
        a.wait()


def unpack(srcs, small, like, blocks_like, table, nfsdp):
    nseq = srcs[0].shape[0]
    share = like[0].shape[0]
    vm = [vm_spec()] * 3
    return pl.pallas_call(
        functools.partial(unpack_kernel, nseq, nfsdp, table.shape[1] // nseq),
        out_shape=tuple(jax.ShapeDtypeStruct(a.shape, F32) for a in like)
        + tuple(jax.ShapeDtypeStruct(a.shape, BF16) for a in blocks_like)
        + (
            jax.ShapeDtypeStruct((1, share), F32),
            jax.ShapeDtypeStruct((1, share), F32),
            jax.ShapeDtypeStruct(table.shape, F32),
        ),
        in_specs=[any_spec()] * 8 + [vm_spec()],
        out_specs=tuple([any_spec()] * 9 + vm),
        scratch_shapes=[pltpu.SemaphoreType.DMA((8,)), pltpu.SemaphoreType.DMA((9,))]
        + [pltpu.VMEM(a.shape, BF16) for a in srcs]
        + [pltpu.VMEM(a.shape, F32) for a in like],
        compiler_params=pltpu.CompilerParams(vmem_limit_bytes=67043328),
        name="unpack",
    )(*srcs, small)


def reversed_ids(bucket_ids):
    span = bucket_ids.shape[0]
    ids = jnp.concatenate([bucket_ids[::-1], jnp.full((1,), -1, jnp.int32)])
    return ids[None, :]


def dot32(a, b):
    return jnp.dot(a, b, preferred_element_type=F32)


def dot_tn(a, b):
    return lax.dot_general(a, b, (((0,), (0,)), ((), ())), preferred_element_type=F32)


def gelu_both(u):
    inner = 0.7978845608028654 * (u + 0.044715 * u * u * u)
    t = jnp.tanh(inner)
    value = 0.5 * u * (1.0 + t)
    slope = 0.5 * (1.0 + t) + 0.5 * u * (1.0 - t * t) * 0.7978845608028654 * (1.0 + 3 * 0.044715 * u * u)
    return value, slope


def body(
    tokens,
    out_grad,
    attn_gain,
    w_query,
    w_key,
    w_value,
    w_out,
    mix_gain,
    w_gate,
    w_up,
    w_down,
    rel_table,
    bucket_ids,
    cont_start,
):
    nseq = lax.axis_size("seq")
    nfsdp = lax.axis_size("fsdp")
    inner = w_query.shape[1]

    ids = reversed_ids(bucket_ids)
    starts = cont_start[0]
    query, keys, values, mixed, lse, gains, normed, first, out_w, cot, gate_w, up_q, down_q = front(
        starts,
        rel_table,
        ids,
        jnp.stack([attn_gain.astype(F32), mix_gain.astype(F32)]),
        tokens[0],
        w_query,
        w_key,
        w_value,
        w_out,
        w_gate,
        w_up,
        w_down,
        out_grad[0],
        nseq,
        nfsdp,
    )
    out_w = out_w.reshape(nseq, inner, -1)
    mixed_rows, resid, normed_two, hidden, gate_grad, up_grad, up_w, down_w, down_grad = middle(
        mixed, out_w, tokens[0], gains, up_q, down_q, gate_w, cot, nfsdp
    )
    resid_grad, mixed_grad, gain_two_grad, down_grad, lead_grad, out_w_grad, gate_w_grad, up_w_grad, result = unmix(
        gains, mixed_rows, resid, out_grad[0], down_grad, gate_grad, up_grad, gate_w, up_w, out_w, normed_two, hidden, down_w
    )
    small, block_out, in_grad, down_grad, lead_grad, gate_w_grad, up_w_grad, qkv_grad, out_w_grad = back(
        starts,
        rel_table,
        ids,
        gains,
        lse,
        gain_two_grad,
        query,
        keys,
        values,
        mixed,
        mixed_grad,
        resid,
        resid_grad,
        tokens[0],
        result,
        out_w_grad,
        gate_w_grad,
        up_w_grad,
        down_grad,
        lead_grad,
        normed,
        first,
    )
    *shards, block_out, in_grad, gain_one_share, gain_two_share, table_grad = unpack(
        (lead_grad, gate_w_grad, up_w_grad, down_grad, qkv_grad, out_w_grad, block_out, in_grad),
        small,
        (w_query, w_key, w_value, w_out, w_gate, w_up, w_down),
        (block_out, in_grad),
        rel_table,
        nfsdp,
    )
    return (
        block_out[None],
        in_grad[None],
        gain_one_share[0],
        *shards[:4],
        gain_two_share[0],
        *shards[4:],
        table_grad,
    )


def solution(mesh):
    placed = (
        P("fsdp", "seq", None),
        P("fsdp", "seq", None),
        P("fsdp"),
        P("fsdp", None),
        P("fsdp", None),
        P("fsdp", None),
        P("fsdp", None),
        P("fsdp"),
        P("fsdp", None),
        P("fsdp", None),
        P("fsdp", None),
        P(),
        P(),
        P("fsdp", None),
    )
    results = placed[:1] * 2 + placed[2:11] + (P(),)
    return jax.shard_map(body, mesh=mesh, in_specs=placed, out_specs=results, check_vma=False)
```

```python
import functools
import jax
import jax.numpy as jnp
from jax import lax
from jax.experimental import pallas as pl
from jax.experimental.pallas import tpu as pltpu
from jax.sharding import PartitionSpec as P

HEAD_DIM = 64
PROMPT = 1024
CL = 256
F32 = jnp.float32
BF16 = jnp.bfloat16
MESH = pl.DeviceIdType.MESH
epsilon = 1e-06
STRIP = 2 * PROMPT - 128
FARW = PROMPT - 128 + CL
KC = 256


def nt(a, b):
    return lax.dot_general(a, b, (((1,), (1,)), ((), ())), preferred_element_type=F32)


def nn(a, b):
    return lax.dot_general(a, b, (((1,), (0,)), ((), ())), preferred_element_type=F32)


class Wires:
    def __init__(self, send, recv):
        self.send, self.recv, self.used = send, recv, 0

    def take(self, count):
        self.used += count
        return self.used - count

    def at(self, i, src, dst, where):
        return pltpu.make_async_remote_copy(
            src_ref=src,
            dst_ref=dst,
            send_sem=self.send.at[i],
            recv_sem=self.recv.at[i],
            device_id=where,
            device_id_type=MESH,
        )

    def go(self, src, dst, where):
        c = self.at(self.take(1), src, dst, where)
        c.start()
        return c


def seq_places():
    s = lax.axis_index("seq")
    near = s + 1 - 2 * lax.rem(s, 2)
    far = lax.rem(s + 2, 4)
    cross = lax.rem(near + 2, 4)
    return s, near, far, cross


def meet(places):
    barrier = pltpu.get_barrier_semaphore()
    for where in places:
        pl.semaphore_signal(barrier, inc=1, device_id=where, device_id_type=MESH)
    pl.semaphore_wait(barrier, len(places))


def rows_at(index, rows, offset=0, count=None):
    return pl.ds(pl.multiple_of(index * rows + offset, 16), rows if count is None else count)


class SeqGather:
    def __init__(self, wires, out_at, chunks):
        self.wires, self.out_at, self.chunks = wires, out_at, chunks
        self.s, self.near, self.far, self.cross = seq_places()
        self.base = wires.take(3 * chunks)

    def trip(self, kind, c, src=None):
        view = self.out_at(self.far if kind == 2 else self.s, c)
        where = {"seq": self.far if kind == 0 else self.near}
        return self.wires.at(self.base + 3 * c + kind, view if src is None else src, view, where)

    def send(self, c, src):
        self.trip(0, c, src).start()
        self.trip(1, c, src).start()

    def forward(self, c):
        self.trip(0, c).wait_recv()
        self.trip(2, c).start()

    def got_near(self, c):
        self.trip(1, c).wait_recv()

    def got_cross(self, c):
        self.trip(2, c).wait_recv()

    def drain(self):
        for c in range(self.chunks):
            for kind in range(3):
                self.trip(kind, c).wait_send()

    def finish(self):
        for c in range(self.chunks):
            self.got_near(c)
            self.got_cross(c)
        self.drain()


def fsdp_places():
    f = lax.axis_index("fsdp")
    return f // 2, lax.rem(f, 2), lax.axis_size("fsdp") // 2


def far_first(k):
    pair, _, pairs = fsdp_places()
    if pairs != 4:
        return k + 1
    first, second = 3 - (pair + 1) // 2, 1 + lax.rem(pair + 1, 3)
    return (first, second, 6 - first - second)[k]


def near_first(k):
    pairs = lax.axis_size("fsdp") // 2
    return pairs - far_first(pairs - 2 - k) if pairs == 4 else k + 1


def fsdp_peers():
    pair, side, pairs = fsdp_places()
    peers = [{"fsdp": lax.rem(pair + d, pairs) * 2 + side} for d in range(1, pairs)]
    return peers + [{"fsdp": pair * 2 + 1 - side}]


class FsdpGather:
    def __init__(self, wires, shard, full_at, local):
        self.wires, self.shard, self.full_at, self.local = wires, shard, full_at, local
        self.pair, self.side, self.pairs = fsdp_places()
        self.base = wires.take(2 * self.pairs)

    def source(self, d):
        return lax.rem(self.pair + self.pairs - d, self.pairs)

    def over(self):
        own = self.full_at(self.pair * 2 + self.side)
        return self.wires.at(self.base, self.shard, own, {"fsdp": self.pair * 2 + 1 - self.side})

    def out(self, d):
        own = self.full_at(self.pair * 2 + self.side)
        where = {"fsdp": lax.rem(self.pair + d, self.pairs) * 2 + self.side}
        return self.wires.at(self.base + d, self.shard, own, where)

    def onward(self, d):
        view = self.full_at(self.source(d) * 2 + self.side)
        return self.wires.at(self.base + self.pairs + d, view, view, {"fsdp": self.pair * 2 + 1 - self.side})

    def keep(self):
        return pltpu.make_async_copy(self.shard, self.full_at(self.pair * 2 + self.side), self.local)

    def start(self):
        self.over().start()
        for k in range(self.pairs - 1):
            self.out(far_first(k)).start()
        self.keep().start()

    def forward(self, k):
        d = near_first(k - 1)
        self.out(d).wait_recv()
        self.onward(d).start()

    def place(self, k):
        return 0 if k == 0 else near_first(k - 1)

    def complete(self, k):
        if k == 0:
            self.keep().wait()
            self.over().wait_recv()
        else:
            self.onward(near_first(k - 1)).wait_recv()

    def drain(self):
        self.over().wait_send()
        for d in range(1, self.pairs):
            self.out(d).wait_send()
            self.onward(d).wait_send()

    def finish(self):
        for k in range(self.pairs):
            self.complete(k)
        self.drain()


def gather_halves(wires, shard, full, size, local):
    half = shard.shape[1] // 2

    def one(n):
        cut = slice(n * half, (n + 1) * half)
        return FsdpGather(wires, shard.at[:, cut], lambda f: full.at[shard_rows(f, size), cut], local[n])

    return [one(0), one(1)]


class FsdpScatter:
    def __init__(self, wires, parts, bufs, result):
        self.wires, self.parts, self.result = wires, parts, result
        self.mine, self.got, self.landed, self.local = bufs
        self.pair, self.side, self.pairs = fsdp_places()
        self.base = wires.take(2 * self.pairs)

    def step_to(self, k):
        return far_first(k) if k < self.pairs - 1 else 0

    def owner(self, d):
        return lax.rem(self.pair + d, self.pairs) * 2

    def load(self, k):
        part = self.parts.at[self.owner(self.step_to(k)) + self.side]
        return pltpu.make_async_copy(part, self.mine.at[k % 2], self.local.at[k % 2])

    def swap(self, d):
        src = self.parts.at[self.owner(d) + 1 - self.side]
        return self.wires.at(self.base + d, src, self.got.at[d], {"fsdp": self.pair * 2 + 1 - self.side})

    def onward(self, d):
        where = {"fsdp": self.owner(d) + self.side}
        return self.wires.at(self.base + self.pairs + d, self.got.at[d], self.landed.at[d - 1], where)

    def start(self):
        for k in range(self.pairs):
            self.swap(self.step_to(k)).start()
        self.load(0).start()

    def step(self, k):
        d = self.step_to(k - 1)
        self.load(k).start()
        self.load(k - 1).wait()
        self.swap(d).wait_recv()
        self.got[d] = (self.mine[(k - 1) % 2].astype(F32) + self.got[d].astype(F32)).astype(BF16)
        self.onward(d).start()

    def finish(self):
        self.load(self.pairs - 1).wait()
        self.swap(0).wait_recv()
        total = self.mine[(self.pairs - 1) % 2].astype(F32) + self.got[0].astype(F32)
        for d in range(1, self.pairs):
            self.onward(d).wait_recv()
            total = total + self.landed[d - 1].astype(F32)
        self.result[...] = total.astype(BF16)

    def drain(self):
        for d in range(self.pairs):
            self.swap(d).wait_send()
        for d in range(1, self.pairs):
            self.onward(d).wait_send()


def fsdp_scatter_scratch(shape):
    pairs = shape[0] // 2
    return [
        pltpu.VMEM((2,) + shape[1:], BF16),
        pltpu.VMEM((pairs,) + shape[1:], BF16),
        pltpu.VMEM((pairs - 1,) + shape[1:], BF16),
        pltpu.SemaphoreType.DMA((2,)),
    ]


def blocks(a, count):
    return a.reshape((count, a.shape[0] // count) + a.shape[1:])


def shard_rows(f, size):
    return pl.ds(pl.multiple_of(f * size, 16 if size % 16 == 0 else 8 if size % 8 == 0 else size), size)


def vm_spec():
    return pl.BlockSpec(memory_space=pltpu.VMEM)


def any_spec():
    return pl.BlockSpec(memory_space=pl.ANY)


def wires_scratch(n):
    return [pltpu.SemaphoreType.DMA((n,)), pltpu.SemaphoreType.DMA((n,))]


def call_params(number, vmem=60):
    return pltpu.CompilerParams(collective_id=number, has_side_effects=True, vmem_limit_bytes=min(vmem << 20, 67043328))


def inverse_rms(v):
    return lax.rsqrt(jnp.mean(v * v, axis=-1, keepdims=True) + epsilon)


def norm_back(grad, v, r, gain):
    scaled = grad * gain
    return r * scaled - v * (r * r * r) * jnp.mean(v * scaled, axis=-1, keepdims=True)


class SeqScatter:
    def __init__(self, wires, chunks, *bufs):
        self.s, self.near, self.far, self.cross = seq_places()
        self.wires, self.chunks, self.bufs = wires, chunks, bufs
        self.base = wires.take(3 * chunks)

    def trip(self, kind, c):
        where = {"seq": self.far if kind == 1 else self.near}
        src, dst = self.bufs[2 * kind].at[c], self.bufs[2 * kind + 1].at[c]
        return self.wires.at(self.base + 3 * c + kind, src, dst, where)

    def cross_chunk(self, c, value):
        self.bufs[0][c] = value.astype(BF16)
        self.trip(0, c).start()

    def far_chunk(self, c, value):
        self.trip(0, c).wait_recv()
        self.bufs[2][c] = (value + self.bufs[1][c].astype(F32)).astype(BF16)
        self.trip(1, c).start()

    def near_chunk(self, c, value):
        self.bufs[4][c] = value.astype(BF16)
        self.trip(2, c).start()

    def own_chunk(self, c, value):
        self.trip(2, c).wait_recv()
        self.trip(1, c).wait_recv()
        return value + self.bufs[5][c].astype(F32) + self.bufs[3][c].astype(F32)

    def finish(self):
        for c in range(self.chunks):
            for kind in range(3):
                self.trip(kind, c).wait_send()


def scatter_scratch(chunks, rows, width):
    return [pltpu.VMEM((chunks, rows, width), BF16)] * 6


def unmix_kernel(
    chunks, gains, obuf, resid, cot, down_p, dg_h, du_h, gate_h, up_h, out_h, n2_h, hid_h, dw_h,
    rgrad, dmix, ggrad, shard, lead_s, out_p, gate_p, up_p, y_h,
    send, recv, b0, b1, b2, b3, b4, b5, attn, dob, p0, p1, p2, p3, l0, l1, l2, l3, lead_p,
    local, dg, du, gate_w, up_w, out_w, n2, hid, down_w, wgrad, wbuf, stage, ystage, sems,
):
    rows, width = resid.shape
    nseq, _, piece = obuf.shape
    nfsdp = gate_p.shape[0]
    units = dg.shape[1]
    first_half = units // 2
    s, near, far, cross = seq_places()
    loads = [
        pltpu.make_async_copy(src, dst, local.at[n])
        for n, (src, dst) in enumerate(
            (
                (gate_h, gate_w),
                (up_h, up_w),
                (dg_h, dg),
                (du_h, du),
                (n2_h, n2),
                (out_h, out_w),
                (hid_h, hid),
                (dw_h, down_w),
            )
        )
    ]
    for a in loads:
        a.start()
    meet([{"seq": near}, {"seq": far}, {"seq": cross}] + fsdp_peers())
    wires = Wires(send, recv)
    grads = FsdpScatter(wires, down_p, (p0, p1, p2, p3), shard)
    grads.start()
    leads = FsdpScatter(wires, lead_p, (l0, l1, l2, l3), lead_s)
    pairs = grads.pairs
    sums = SeqScatter(wires, chunks, b0, b1, b2, b3, b4, b5)
    size = rows // chunks
    for a in loads[:4]:
        a.wait()

    def part(t, c):
        at = rows_at(t, rows, c * size, size)
        return nt(dg[at, :], gate_w[...]) + nt(du[at, :], up_w[...])

    for c in range(chunks):
        sums.cross_chunk(c, part(cross, c))
    for c in range(chunks):
        sums.far_chunk(c, part(far, c))
    for c in range(chunks):
        sums.near_chunk(c, part(near, c))
    for c in range(chunks):
        rgrad[c * size : (c + 1) * size, :] = part(s, c)
    grads.step(1)
    loads[4].wait()
    depth = width // nfsdp
    wide = 384
    saves = []

    def weight_parts(side, out, begin, end, cut):
        for n in range(begin, end):
            slot = n % 2
            group = pl.ds(n * (wide // depth), wide // depth)
            if len(saves) > 1:
                saves[-2].wait()
            got = dot_tn(n2[:, n * wide : (n + 1) * wide], side[...])
            for m in range(wide // depth):
                low = got[m * depth : (m + 1) * depth, :].astype(BF16)
                if cut:
                    lead_p[n * (wide // depth) + m] = low[:, :cut]
                stage[slot, m, :, : units - cut] = low[:, cut:]
            a = pltpu.make_async_copy(stage.at[slot, :, :, : units - cut], out.at[group], sems.at[3 + slot])
            a.start()
            saves.append(a)

    weight_parts(dg, gate_p, 0, width // wide, first_half)
    if pairs > 2:
        grads.step(2)
    loads[5].wait()
    cols = out_w.shape[2]

    def own_rows(c, total):
        at = slice(c * size, (c + 1) * size)
        dn = sums.own_chunk(c, rgrad[at, :])
        h = resid[at, :]
        r = inverse_rms(h)
        rg = cot[at, :].astype(F32) + norm_back(dn, h, r, gains[1:2, :])
        rgrad[at, :] = rg
        low = rg.astype(BF16)
        attn[at, :] = low
        for t in range(nseq):
            acc = jnp.zeros((size, piece), F32)
            for u in range(nseq):
                acc = acc + nt(low[:, u * cols : (u + 1) * cols], out_w[u, t * piece : (t + 1) * piece, :])
            dob[t, at, :] = acc.astype(BF16)
        return total + jnp.sum(dn * h * r, axis=0, keepdims=True)

    base = wires.take(3 * chunks)

    def trip(n, t, c):
        at = pl.ds(c * size, size)
        return wires.at(base + 3 * c + n, dob.at[t, at, :], dmix.at[rows_at(s, rows, c * size, size), :], {"seq": t})

    total = jnp.zeros((1, width), F32)
    for c in range(chunks):
        total = own_rows(c, total)
        if c == 0:
            weight_parts(du, up_p, 0, 1, 0)
            leads.start()
        for n, t in enumerate((far, cross, near)):
            trip(n, t, c).start()
        dmix[rows_at(s, rows, c * size, size), :] = dob[s, pl.ds(c * size, size), :]
        if c == 0:
            weight_parts(du, up_p, 1, width // wide, 0)
            for d in range(3, pairs):
                grads.step(d)
    ggrad[...] = jnp.broadcast_to(total, ggrad.shape)
    wbase = wires.take(3)

    def wtrip(n):
        u = (cross, far, near)[n]
        return wires.at(wbase + n, wgrad.at[u], wbuf.at[n], {"seq": far if n == 1 else near})

    def wblock(u):
        for t in range(nseq):
            at = pl.ds(pl.multiple_of(u * cols, 128), cols)
            wgrad[u, t * piece : (t + 1) * piece, :] = dot_tn(obuf[t], attn[:, at]).astype(BF16)

    wblock(cross)
    wblock(far)
    wtrip(0).start()
    wblock(near)
    wtrip(0).wait_recv()
    wgrad[far] = (wgrad[far].astype(F32) + wbuf[0].astype(F32)).astype(BF16)
    wblock(s)
    wtrip(1).start()
    wtrip(2).start()
    leads.step(1)
    for a in loads[6:]:
        a.wait()
    ycopies = []
    for t in range(nseq):
        slot = t % 2
        if t > 1:
            ycopies[t - 2].wait()
        at = slice(t * rows, (t + 1) * rows)
        ystage[slot] = nn(hid[at, :], down_w[...]).astype(BF16)
        ycopies.append(pltpu.make_async_copy(ystage.at[slot], y_h.at[at, :], sems.at[slot]))
        ycopies[t].start()
        if t == 0:
            for d in range(2, pairs - 1):
                leads.step(d)
        if t == 1 and pairs > 2:
            leads.step(pairs - 1)
    for c in range(chunks):
        for n, t in enumerate((far, cross, near)):
            trip(n, t, c).wait()
    grads.finish()
    for n in range(1, 3):
        wtrip(n).wait_recv()
    wsum = wgrad[s].astype(F32) + wbuf[1].astype(F32) + wbuf[2].astype(F32)
    lines = out_p.shape[1]
    for f in range(nfsdp):
        out_p[f] = wsum[f * lines : (f + 1) * lines, :].astype(BF16)
    for n in range(3):
        wtrip(n).wait_send()
    sums.finish()
    grads.drain()
    leads.finish()
    leads.drain()
    for a in saves[-2:]:
        a.wait()
    for a in ycopies[-2:]:
        a.wait()


def unmix(gains, obuf, resid, cot, down_p, dg, du, gate_w, up_w, out_w, n2, hid, down_w, chunks=2):
    rows, width = resid.shape
    nseq, _, piece = obuf.shape
    nfsdp = down_p.shape[0]
    units = dg.shape[1]
    grad_shape = (nfsdp, width // nfsdp, units)
    half_shape = (nfsdp, width // nfsdp, units // 2)
    return pl.pallas_call(
        functools.partial(unmix_kernel, chunks),
        out_shape=(
            jax.ShapeDtypeStruct((rows, width), F32),
            jax.ShapeDtypeStruct((nseq * rows, piece), BF16),
            jax.ShapeDtypeStruct((8, width), F32),
            jax.ShapeDtypeStruct(down_p.shape[1:], BF16),
            jax.ShapeDtypeStruct(half_shape[1:], BF16),
            jax.ShapeDtypeStruct((nfsdp, out_w.shape[1] // nfsdp, out_w.shape[2]), BF16),
            jax.ShapeDtypeStruct(half_shape, BF16),
            jax.ShapeDtypeStruct(grad_shape, BF16),
            jax.ShapeDtypeStruct(n2.shape, BF16),
        ),
        in_specs=[vm_spec()] * 4 + [any_spec()] * 9,
        out_specs=(vm_spec(),) * 6 + (any_spec(),) * 3,
        scratch_shapes=wires_scratch(6 * chunks + 2 * nfsdp + 3)
        + scatter_scratch(chunks, rows // chunks, width)
        + [pltpu.VMEM((rows, width), BF16), pltpu.VMEM((nseq, rows, piece), BF16)]
        + fsdp_scatter_scratch(down_p.shape)
        + fsdp_scatter_scratch(half_shape)
        + [
            pltpu.VMEM(half_shape, BF16),
            pltpu.SemaphoreType.DMA((8,)),
            pltpu.VMEM(dg.shape, BF16),
            pltpu.VMEM(du.shape, BF16),
            pltpu.VMEM(gate_w.shape, BF16),
            pltpu.VMEM(up_w.shape, BF16),
            pltpu.VMEM(out_w.shape, BF16),
            pltpu.VMEM(n2.shape, BF16),
            pltpu.VMEM(hid.shape, BF16),
            pltpu.VMEM(down_w.shape, BF16),
            pltpu.VMEM(out_w.shape, BF16),
            pltpu.VMEM((3,) + out_w.shape[1:], BF16),
            pltpu.VMEM((2, 384 * nfsdp // width, width // nfsdp, units), BF16),
            pltpu.VMEM((2, rows, width), BF16),
            pltpu.SemaphoreType.DMA((5,)),
        ],
        compiler_params=call_params(4, 63),
        name="unmix",
    )(gains, obuf, resid, cot, down_p, dg, du, gate_w, up_w, out_w, n2, hid, down_w)


def build_strips(heads, first_head, starts, table, ids, strip, far):
    length = ids.shape[1]
    half = 2 * PROMPT
    for h in range(heads):
        row = jnp.zeros(ids.shape, F32)
        for b in range(table.shape[1]):
            row = jnp.where(ids[...] == b, table[first_head + h, b], row)
        row = jnp.broadcast_to(row, (8, length))
        base = jnp.broadcast_to(row[:1, PROMPT // 2 : PROMPT // 2 + half], (128, half))
        strip[h] = pltpu.roll(base, 1, 1, stride=1, stride_axis=0)[:, 128:]
        for c in range(2):
            moved = pltpu.roll(row, length - PROMPT // 2 - starts[c], 1)
            base = jnp.broadcast_to(moved[:1, : FARW + 128], (128, FARW + 128))
            far[h, c] = pltpu.roll(base, 1, 1, stride=1, stride_axis=0)[:, 128:]


def head_masks(width, heads):
    lane = lax.broadcasted_iota(jnp.int32, (1, width), 1)
    return [(lane >= h * HEAD_DIM) & (lane < (h + 1) * HEAD_DIM) for h in range(heads)]


def masked_copies(src, dst, heads):
    masks = head_masks(src.shape[1], heads)
    for h in range(heads):
        dst[h] = jnp.where(masks[h], src[...], jnp.zeros((), src.dtype))


def bias_chunk(strip, far, h, first_q, kstart, kind, c):
    parts = []
    for r in range(KC // 128):
        m = PROMPT - 128 - (kstart + 128 * r)
        if kind == "far":
            parts.append(far[h, c, :, m : m + CL])
        else:
            parts.append(strip[h, :, pl.ds(pl.multiple_of(first_q + m, 128), CL)])
    return jnp.concatenate(parts, axis=0)


def pack_piece(units, nfsdp, nseq):
    block = units // nfsdp
    return block, -(-block // (16 * nseq)) * 16


def pack_front(t, raw, first_q, out_q, gains):
    r_q, r_k, r_v, r_o = raw
    piece = first_q.shape[1] * 3 // 10
    depth = first_q.shape[0]
    cut = slice(t * piece, (t + 1) * piece)
    first_q[...] = jnp.concatenate(
        [r_q[:, cut], r_k[:, cut], r_v[:, cut], gains, jnp.zeros((depth, first_q.shape[1] - 3 * piece - 8), BF16)], axis=1
    )
    cols = out_q.shape[1]
    out_q[...] = r_o[:, t * cols : (t + 1) * cols]


def pack_cols(t, nseq, nfsdp, raw, packed):
    block, piece = pack_piece(raw.shape[1], nfsdp, nseq)
    pieces = []
    for f in range(nfsdp):
        begin = f * block + t * piece
        end = min(begin + piece, (f + 1) * block)
        pieces.append(raw[:, begin:end])
        if end - begin < piece:
            pieces.append(jnp.zeros((raw.shape[0], piece - end + begin), BF16))
    packed[...] = jnp.concatenate(pieces, axis=1)


def pack_down(t, raw, packed):
    piece = packed.shape[0]
    begin = t * piece
    end = min(begin + piece, raw.shape[0])
    packed[: end - begin, :] = raw[begin:end, :]
    if end - begin < piece:
        packed[end - begin :, :] = jnp.zeros((piece - end + begin, raw.shape[1]), BF16)


def forward_kernel(
    heads, nseq, starts, table, ids, gain_q, tok_h, w_q, w_k, w_v, w_o, w_g, w_u, w_d, cot_q,
    q, k, v, o, lse, gains, obuf, resid,
    n1_h, first_h, out_h, cot_h, gate_h, up_h, down_h, n2_h, hid_h, dg_h, du_h, parts_h,
    send, recv, local, first_q, out_q, gate_q, up_q, down_q, group, first, gate_w, up_w, down_w, tok, fsems, spare,
):
    rows, width = tok.shape
    units = gate_w.shape[1]
    piece = q.shape[1]
    mine, near, other, cross = seq_places()
    pair, side, pairs = fsdp_places()
    nfsdp = 2 * pairs
    half = rows // 2
    wires = Wires(send, recv)
    ring = SeqGather(wires, lambda t, c: group.at[rows_at(t, rows, c * half, half), :], 2)
    size = first_q.shape[0]
    lead = FsdpGather(wires, first_q, lambda f: first.at[shard_rows(f, size), :], local.at[7])
    late = FsdpGather(wires, out_q, lambda f: out_h.at[mine, f], local.at[8])
    gates = gather_halves(wires, gate_q, gate_w, gate_q.shape[0], (local.at[9], local.at[10]))
    ups = gather_halves(wires, up_q, up_w, up_q.shape[0], (local.at[11], local.at[12]))
    downs = gather_halves(wires, down_q, down_w, down_q.shape[0], (local.at[13], local.at[14]))
    wring = SeqGather(wires, lambda t, c: out_h.at[t], 1)
    cring = SeqGather(wires, lambda t, c: cot_h.at[rows_at(t, rows, c * half, half), :], 2)
    nring = SeqGather(wires, lambda t, c: group.at[rows_at(t, rows, c * half, half), :], 2)
    obase = wires.take(3)
    own = [
        pltpu.make_async_copy(tok_h, group.at[rows_at(mine, rows), :], local.at[15]),
        pltpu.make_async_copy(cot_q, cot_h.at[rows_at(mine, rows), :], local.at[16]),
        pltpu.make_async_copy(tok_h, tok, local.at[17]),
    ]

    def begin(r_q, r_k, r_v, r_o, r_g, r_u, r_d):
        loads = [
            pltpu.make_async_copy(src, dst, local.at[n])
            for n, (src, dst) in enumerate(
                ((w_q, r_q), (w_k, r_k), (w_v, r_v), (w_o, r_o), (w_g, r_g), (w_u, r_u), (w_d, r_d))
            )
        ]
        for a in loads:
            a.start()
        meet([{"seq": near}, {"seq": other}, {"seq": cross}] + fsdp_peers())
        for c in range(2):
            ring.send(c, tok_h.at[pl.ds(c * half, half), :])
        for a in own:
            a.start()
        for a in loads[:4]:
            a.wait()
        both = jnp.concatenate([gain_q[...], jnp.zeros((6, gain_q.shape[1]), F32)], axis=0).T.astype(BF16)
        for t in range(nseq):

            @pl.when(mine == t)
            def _():
                pack_front(t, (r_q, r_k, r_v, r_o), first_q, out_q, both)

        for a in loads[4:]:
            a.wait()
        lead.start()
        for t in range(nseq):

            @pl.when(mine == t)
            def _():
                pack_cols(t, nseq, nfsdp, r_g, gate_q)

        late.start()
        for t in range(nseq):

            @pl.when(mine == t)
            def _():
                pack_cols(t, nseq, nfsdp, r_u, up_q)
                pack_down(t, r_d, down_q)

    pl.run_scoped(begin, *[pltpu.VMEM(a.shape, BF16) for a in (w_q, w_k, w_v, w_o, w_g, w_u, w_d)])
    for a in gates + ups + downs:
        a.start()
    cring.send(0, cot_q.at[pl.ds(0, half), :])

    def attend(n1, strip, far, kh, vt, ot, s):
        build_strips(heads, mine * heads, starts, table, ids, strip, far)
        lse[...] = jnp.zeros(lse.shape, F32)
        for d in range(1, pairs):
            lead.forward(d)
            if d == pairs // 2:
                ring.forward(0)
        for d in range(1, pairs):
            late.forward(d)
        ring.forward(1)
        lead.finish()
        saves = [pltpu.make_async_copy(first, first_h, local.at[0])]
        saves[0].start()
        column = 3 * piece
        gains[...] = jnp.zeros(gains.shape, F32)
        for b in range(width // 256):
            base = column // 128 * 128
            band = first[b * 256 : (b + 1) * 256, base : base + 128].astype(F32).T
            for n in range(2):
                line = column - base + n
                gains[n : n + 1, b * 256 : (b + 1) * 256] = band[line : line + 1, :]

        def project(t):
            at = rows_at(t, rows)
            x = group[at, :].astype(F32)
            low = (x * inverse_rms(x) * gains[0:1, :]).astype(BF16)
            n1[at, :] = low
            r = nn(low, first[:, :column])
            q[at, :] = r[:, :piece].astype(BF16)
            k[at, :] = r[:, piece : 2 * piece].astype(BF16)
            v[at, :] = r[:, 2 * piece :].astype(BF16)

        own[0].wait()
        project(mine)
        for c in range(2):
            ring.got_near(c)
        project(near)
        project(other)
        for c in range(2):
            ring.got_cross(c)
        project(cross)
        saves.append(pltpu.make_async_copy(n1, n1_h, local.at[1]))
        saves[1].start()
        for d in range(pairs):
            late.complete(d)
        wring.send(0, out_h.at[mine])
        cring.send(1, cot_q.at[pl.ds(half, half), :])
        masked_copies(k, kh, heads)
        vt[...] = v[...].astype(F32).T.astype(BF16)

        def block(h, q0, bias_q0, chunks, c):
            qb = q[pl.ds(q0, CL), :]
            top = None
            for n, (k0, kind, kstart) in enumerate(chunks):
                sc = nt(kh[h, pl.ds(k0, KC), :], qb) + bias_chunk(strip, far, h, bias_q0, kstart, kind, c)
                s[n * KC : (n + 1) * KC, :] = sc
                m = jnp.max(sc, axis=0, keepdims=True)
                top = m if top is None else jnp.maximum(top, m)
            total = jnp.zeros((1, CL), F32)
            acc = jnp.zeros((HEAD_DIM, CL), F32)
            lines = pl.ds(pl.multiple_of(h * HEAD_DIM, HEAD_DIM), HEAD_DIM)
            for n, (k0, kind, kstart) in enumerate(chunks):
                e = jnp.exp(s[n * KC : (n + 1) * KC, :] - top)
                total = total + jnp.sum(e, axis=0, keepdims=True)
                acc = acc + nn(vt[lines, pl.ds(k0, KC)], e.astype(BF16))
            ot[lines, pl.ds(q0, CL)] = acc / total
            lse[pl.ds(h, 1), pl.ds(q0, CL)] = top + jnp.log(total)

        nblk = PROMPT // CL
        steps = [(a, d) for a in gates for d in range(1, pairs)]
        early, later, final = steps[: pairs - 1], steps[pairs - 1 : -1], steps[-1:]

        def prompt_body(i, carry):
            h, blk = i // nblk, i % nblk
            q0 = pl.multiple_of(blk * CL, CL)
            block(h, q0, q0, [(j * KC, "strip", j * KC) for j in range(PROMPT // KC)], None)
            for n, (a, d) in enumerate(early):

                @pl.when(i == max((heads * nblk - 2) * (n + 1) // len(early) - 2, 0))
                def _():
                    a.forward(d)

            return carry

        def cont_body(i, carry):
            h, c = i // 2, i % 2
            q0 = pl.multiple_of(PROMPT + c * CL, CL)
            chunks = [(j * KC, "far", j * KC) for j in range(PROMPT // KC)]
            chunks += [(q0 + j * KC, "strip", j * KC) for j in range(CL // KC)]
            block(h, q0, 0, chunks, c)
            for n, (a, d) in enumerate(later):

                @pl.when(i == max(2 * heads * (n + 1) // len(later) - 1, 0))
                def _():
                    a.forward(d)

            return carry

        lax.fori_loop(0, heads * nblk, prompt_body, 0)
        cring.forward(0)
        lax.fori_loop(0, heads * 2, cont_body, 0)
        o[...] = ot[...].T.astype(BF16)
        ring.drain()
        for n, t in enumerate((other, cross, near)):
            wires.at(obase + n, o.at[rows_at(t, rows), :], obuf.at[mine], {"seq": t}).start()
        obuf[mine] = o[rows_at(mine, rows), :]
        wring.forward(0)
        for a, d in final:
            a.forward(d)
        for a in saves:
            a.wait()

    tall = nseq * rows
    pl.run_scoped(
        attend,
        pltpu.VMEM((tall, width), BF16),
        pltpu.VMEM((heads, 128, STRIP), F32),
        pltpu.VMEM((heads, 2, 128, FARW), F32),
        pltpu.VMEM((heads, tall, piece), BF16),
        pltpu.VMEM((piece, tall), BF16),
        pltpu.VMEM((piece, tall), F32),
        pltpu.VMEM((PROMPT + CL, CL), F32),
    )
    todo = [(a, d) for a in ups + downs for d in range(1, pairs)]

    def pass_on(share):
        while todo and len(todo) > round((1 - share) * 4 * (pairs - 1)):
            a, d = todo.pop(0)
            a.forward(d)

    def feed(out_w, cot, ga, ub, hid, dg, du, parts):
        cols = out_w.shape[2]
        wring.got_near(0)
        wring.got_cross(0)
        lines = w_o.shape[0]
        fetch = []
        if lines % 16 == 0:
            fetch = [
                pltpu.make_async_copy(out_h.at[u, f], out_w.at[u, pl.ds(f * lines, lines), :], fsems.at[u * nfsdp + f])
                for u in range(nseq)
                for f in range(nfsdp)
            ]
        else:
            load = pltpu.make_async_copy(out_h, spare, local.at[2])
            load.start()
            load.wait()
            for u in range(nseq):
                joined = jnp.concatenate([spare[u, f].astype(F32) for f in range(nfsdp)], axis=0)
                out_w[u] = joined.astype(BF16)
        saves = []

        def save(src, dst):
            saves.append(pltpu.make_async_copy(src, dst, local.at[18 + len(saves)]))
            saves[-1].start()

        for a in fetch:
            a.start()
        for n, t in enumerate((other, cross, near)):
            wires.at(obase + n, o.at[rows_at(t, rows), :], obuf.at[mine], {"seq": t}).wait()
        for a in fetch:
            a.wait()
        pass_on(1 / 12)
        own[2].wait()
        for c in range(2):
            part = slice(c * half, (c + 1) * half)
            for u in range(nseq):
                acc = tok[part, u * cols : (u + 1) * cols].astype(F32)
                for t in range(nseq):
                    acc = acc + nn(obuf[t, part, :], out_w[u, t * piece : (t + 1) * piece, :])
                resid[part, u * cols : (u + 1) * cols] = acc
            h = resid[part, :]
            group[rows_at(mine, rows, c * half, half), :] = (h * inverse_rms(h) * gains[1:2, :]).astype(BF16)
            if c == 1:
                nring.send(0, group.at[rows_at(mine, rows, 0, half), :])
        nring.send(1, group.at[rows_at(mine, rows, half, half), :])
        cring.forward(1)
        for a in gates:
            for d in range(pairs):
                a.complete(d)
        save(gate_w, gate_h)

        def gate_rows(t):
            ga[rows_at(t, rows), :] = nn(group[rows_at(t, rows), :], gate_w[...])

        def act_rows(t):
            up = nn(group[rows_at(t, rows), :], up_w[...])
            active, slope = gelu_both(ga[rows_at(t, rows), :])
            hid[rows_at(t, rows), :] = (active * up).astype(BF16)
            ga[rows_at(t, rows), :] = slope * up
            ub[rows_at(t, rows), :] = active

        pass_on(2 / 12)
        gate_rows(mine)
        nring.got_near(0)
        nring.got_near(1)
        pass_on(3 / 12)
        gate_rows(near)
        pass_on(4 / 12)
        nring.forward(0)
        pass_on(6 / 12)
        nring.forward(1)
        own[1].wait()
        for c in range(2):
            cring.got_near(c)
            cring.got_cross(c)
        cload = pltpu.make_async_copy(cot_h, cot, local.at[3])
        cload.start()
        pass_on(7 / 12)
        gate_rows(other)
        for c in range(2):
            nring.got_cross(c)
        gate_rows(cross)
        save(group, n2_h)
        pass_on(8 / 12)
        for a in ups:
            for d in range(pairs):
                a.complete(d)
        save(up_w, up_h)
        act_rows(mine)
        act_rows(near)
        pass_on(9 / 12)
        act_rows(other)
        act_rows(cross)
        save(hid, hid_h)
        pass_on(10 / 12)
        cload.wait()
        width_f = units // nfsdp
        wide = max(256 // width_f, 1)
        pieces = []

        def down_part(n):
            slot = n % 2
            if n > 1:
                pieces[n - 2].wait()
            got = dot_tn(hid[:, n * wide * width_f : (n + 1) * wide * width_f], cot[...]).astype(BF16)
            for m in range(wide):
                parts[slot, m] = got[m * width_f : (m + 1) * width_f, :]
            pieces.append(pltpu.make_async_copy(parts.at[slot], parts_h.at[pl.ds(n * wide, wide)], local.at[4 + slot]))
            pieces[n].start()

        for n in range(nfsdp // wide):
            down_part(n)
            if n == 1:
                pass_on(11 / 12)

        def back_cols(at):
            for t in range(nseq):
                band = slice(t * rows, (t + 1) * rows)
                dh = nt(cot[band, :], down_w[at, :])
                dg[band, at] = (dh * ga[band, at]).astype(BF16)
                du[band, at] = (dh * ub[band, at]).astype(BF16)
            save(dg.at[:, at], dg_h.at[:, at])
            save(du.at[:, at], du_h.at[:, at])

        if (2 * width_f) % 128 == 0:

            def columns(d):
                for a in downs:
                    a.complete(d)
                start = downs[0].source(downs[0].place(d)) * 2 * width_f
                back_cols(pl.ds(pl.multiple_of(start, 2 * width_f), 2 * width_f))

            columns(0)
            pass_on(1)
            for d in range(1, pairs):
                columns(d)
        else:
            pass_on(1)
            for d in range(pairs):
                for a in downs:
                    a.complete(d)
            for n in range(units // 256):
                back_cols(slice(n * 256, (n + 1) * 256))
        save(down_w, down_h)
        nring.drain()
        wring.drain()
        cring.drain()
        lead_late = [late] + gates + ups + downs
        for a in lead_late:
            a.drain()
        for a in pieces[-2:] + saves:
            a.wait()

    pl.run_scoped(
        feed,
        pltpu.VMEM((nseq, w_o.shape[0] * nfsdp, width // nseq), BF16),
        pltpu.VMEM((tall, width), BF16),
        pltpu.VMEM((tall, units), F32),
        pltpu.VMEM((tall, units), F32),
        pltpu.VMEM((tall, units), BF16),
        pltpu.VMEM((tall, units), BF16),
        pltpu.VMEM((tall, units), BF16),
        pltpu.VMEM((2, max(256 * nfsdp // units, 1), units // nfsdp, width), BF16),
    )


def forward(starts, table, ids, gain_q, tok, w_q, w_k, w_v, w_o, w_g, w_u, w_d, cot, nseq, nfsdp):
    rows, width = tok.shape
    inner = w_q.shape[1]
    piece = inner // nseq
    heads = piece // HEAD_DIM
    tall = nseq * rows
    size = w_q.shape[0]
    unit = pack_piece(w_g.shape[1], nfsdp, nseq)[1]
    units = nfsdp * unit
    cols = width // nseq
    lead = piece * 10 // 3
    smem = pl.BlockSpec(memory_space=pltpu.SMEM)

    def low(*shape):
        return jax.ShapeDtypeStruct(shape, BF16)

    return pl.pallas_call(
        functools.partial(forward_kernel, heads, nseq),
        out_shape=(
            low(tall, piece),
            low(tall, piece),
            low(tall, piece),
            low(tall, piece),
            jax.ShapeDtypeStruct((8, tall), F32),
            jax.ShapeDtypeStruct((8, width), F32),
            low(nseq, rows, piece),
            jax.ShapeDtypeStruct((rows, width), F32),
            low(tall, width),
            low(width, lead),
            low(nseq, nfsdp, w_o.shape[0], cols),
            low(tall, width),
            low(width, units),
            low(width, units),
            low(units, width),
            low(tall, width),
            low(tall, units),
            low(tall, units),
            low(tall, units),
            low(nfsdp, unit, width),
        ),
        in_specs=[smem, smem, vm_spec(), vm_spec()] + [any_spec()] * 9,
        out_specs=(vm_spec(),) * 8 + (any_spec(),) * 12,
        scratch_shapes=wires_scratch(6 + 8 * nfsdp + 3 + 6 + 6 + 3)
        + [
            pltpu.SemaphoreType.DMA((18 + 5 + 2 * max(nfsdp // 2, units // 256),)),
            pltpu.VMEM((size, lead), BF16),
            pltpu.VMEM((w_o.shape[0], cols), BF16),
            pltpu.VMEM((size, units), BF16),
            pltpu.VMEM((size, units), BF16),
            pltpu.VMEM((unit, width), BF16),
            pltpu.VMEM((tall, width), BF16),
            pltpu.VMEM((width, lead), BF16),
            pltpu.VMEM((width, units), BF16),
            pltpu.VMEM((width, units), BF16),
            pltpu.VMEM((units, width), BF16),
            pltpu.VMEM((rows, width), BF16),
            pltpu.SemaphoreType.DMA((nseq * nfsdp,)),
            pltpu.VMEM((nseq, nfsdp) + w_o.shape[:1] + (cols,) if w_o.shape[0] % 16 else (1, 1, 8, 128), BF16),
        ],
        compiler_params=call_params(1, 64),
        name="forward",
    )(starts, table, ids, gain_q, tok, w_q, w_k, w_v, w_o, w_g, w_u, w_d, cot)


def back_kernel(
    heads, chunks, starts, table, ids, gains, lse, gain_b, q, k, v, o, do,
    resid_h, rgrad_h, tok_h, y_p, out_p, gate_p, up_p, done_h, lead_h, n1_h, first_h,
    small, y_h, in_h, down_f, lead_f, gate_f, up_f, qkv_f, out_f,
    send, recv, local, ybuf, qkv_p, b0, b1, b2, b3, b4, b5,
    g0, g1, g2, g3, u0, u1, u2, u3, q0_, q1_, q2_, q3_, o0, o1, o2, o3,
    gate_s, up_s, qkv_s, out_s, dqkv, tok, held, stage, one, two, three, tgrad,
):
    rows, width = tok.shape
    nseq = q.shape[0] // rows
    piece = q.shape[1]
    nfsdp = gate_p.shape[0]
    s, near, far_d, cross = seq_places()
    pair, side, pairs = fsdp_places()

    def y_block(t):
        return y_p.at[rows_at(t, rows), :]

    loads = [
        pltpu.make_async_copy(y_block(far_d), ybuf.at[2], local.at[0]),
        pltpu.make_async_copy(y_block(s), ybuf.at[3], local.at[1]),
    ]
    loads.append(pltpu.make_async_copy(tok_h, tok, local.at[5]))
    for a in loads:
        a.start()
    meet([{"seq": near}, {"seq": far_d}, {"seq": cross}] + fsdp_peers())
    wires = Wires(send, recv)
    hop = wires.go(y_block(cross), ybuf.at[0], {"seq": near})
    turn = wires.go(y_block(near), ybuf.at[1], {"seq": near})
    gates = FsdpScatter(wires, gate_p, (g0, g1, g2, g3), gate_s)
    ups = FsdpScatter(wires, up_p, (u0, u1, u2, u3), up_s)
    gates.start()
    ups.start()
    down_ring = SeqGather(wires, lambda t, c: down_f.at[t], 1)
    lead_ring = SeqGather(wires, lambda t, c: lead_f.at[t], 1)
    gate_ring = SeqGather(wires, lambda t, c: gate_f.at[t], 1)
    up_ring = SeqGather(wires, lambda t, c: up_f.at[t], 1)
    qkv_ring = SeqGather(wires, lambda t, c: qkv_f.at[t], 1)
    out_ring = SeqGather(wires, lambda t, c: out_f.at[t], 1)
    qkvs = FsdpScatter(wires, qkv_p, (q0_, q1_, q2_, q3_), qkv_s)
    outs = FsdpScatter(wires, out_p, (o0, o1, o2, o3), out_s)
    far_hop = wires.at(wires.take(1), ybuf.at[2], ybuf.at[4], {"seq": far_d})
    down_keep = pltpu.make_async_copy(done_h, down_f.at[s], local.at[6])
    down_keep.start()
    down_ring.send(0, done_h)
    lead_keep = pltpu.make_async_copy(lead_h, lead_f.at[s], local.at[10])
    lead_keep.start()
    lead_ring.send(0, lead_h)
    length = ids.shape[1]
    half = 2 * PROMPT

    def attend_back(strip, far, kh, vh, kt, delta, dqt, dk, dv, gstrip, gfar):
        build_strips(heads, s * heads, starts, table, ids, strip, far)
        loads[0].wait()
        hop.wait_recv()
        ybuf[2] = (ybuf[2].astype(F32) + ybuf[0].astype(F32)).astype(BF16)
        for src, dst in ((k, kh), (v, vh)):
            masked_copies(src, dst, heads)
        far_hop.start()
        kt[...] = k[...].astype(F32).T.astype(BF16)
        prod = (o[...].astype(F32) * do[...].astype(F32)).T
        for h in range(heads):
            delta[h : h + 1, :] = jnp.sum(prod[h * HEAD_DIM : (h + 1) * HEAD_DIM, :], axis=0, keepdims=True)
        dk[...] = jnp.zeros(dk.shape, F32)
        dv[...] = jnp.zeros(dv.shape, F32)
        gstrip[...] = jnp.zeros(gstrip.shape, F32)
        gfar[...] = jnp.zeros(gfar.shape, F32)
        lane = lax.broadcasted_iota(jnp.int32, (1, piece), 1)

        def block(h, q0, bias_q0, chunk_list, c):
            qb = q[pl.ds(q0, CL), :]
            dob = do[pl.ds(q0, CL), :]
            keep = lane // HEAD_DIM == h
            qhb = jnp.where(keep, qb, jnp.zeros((), BF16))
            dohb = jnp.where(keep, dob, jnp.zeros((), BF16))
            lrow = lse[pl.ds(h, 1), pl.ds(q0, CL)]
            drow = delta[pl.ds(h, 1), pl.ds(q0, CL)]
            acc = jnp.zeros((HEAD_DIM, CL), F32)
            for n, (k0, kind, kstart) in enumerate(chunk_list):
                ks = pl.ds(k0, KC)
                sc = nt(kh[h, ks, :], qb) + bias_chunk(strip, far, h, bias_q0, kstart, kind, c)
                pr = jnp.exp(sc - lrow)
                dp = nt(vh[h, ks, :], dob)
                ds = pr * (dp - drow)
                dsl = ds.astype(BF16)
                dv[ks, :] += nn(pr.astype(BF16), dohb)
                dk[ks, :] += nn(dsl, qhb)
                acc = acc + nn(kt[pl.ds(pl.multiple_of(h * HEAD_DIM, HEAD_DIM), HEAD_DIM), ks], dsl)
                for r in range(KC // 128):
                    m = PROMPT - 128 - (kstart + 128 * r)
                    part = ds[128 * r : 128 * (r + 1), :]
                    if kind == "far":
                        gfar[h, c, :, m : m + CL] += part
                    else:
                        gstrip[h, :, pl.ds(pl.multiple_of(bias_q0 + m, 128), CL)] += part
            dqt[pl.ds(pl.multiple_of(h * HEAD_DIM, HEAD_DIM), HEAD_DIM), pl.ds(q0, CL)] = acc

        nblk = PROMPT // CL

        def prompt_body(i, carry):
            h, blk = i // nblk, i % nblk
            q0 = pl.multiple_of(blk * CL, CL)
            block(h, q0, q0, [(j * KC, "strip", j * KC) for j in range(PROMPT // KC)], None)

            for k in range(1, pairs):

                @pl.when(i == heads * nblk * k // pairs)
                def _():
                    gates.step(k)

            return carry

        lax.fori_loop(0, heads * nblk, prompt_body, 0)

        def cont_body(i, carry):
            h, c = i // 2, i % 2
            q0 = pl.multiple_of(PROMPT + c * CL, CL)
            chunk_list = [(j * KC, "far", j * KC) for j in range(PROMPT // KC)]
            chunk_list += [(q0 + j * KC, "strip", j * KC) for j in range(CL // KC)]
            block(h, q0, 0, chunk_list, c)

            @pl.when(i == heads)
            def _():
                ups.step(1)

            return carry

        lax.fori_loop(0, heads * 2, cont_body, 0)
        dqkv[...] = jnp.concatenate([dqt[...].T, dk[...], dv[...]], axis=1).astype(BF16)
        buckets = table.shape[1]
        lines8 = lax.broadcasted_iota(jnp.int32, (buckets, length), 0)
        hot = ids[:1, :] == lines8
        tgrad[...] = jnp.zeros(tgrad.shape, F32)
        for h in range(heads):

            def unskew(g, span):
                full = jnp.concatenate([jnp.zeros((128, 128), F32), g], axis=1)
                eight = full[:8]
                for a in range(1, 16):
                    eight = eight + pltpu.roll(full[8 * a : 8 * a + 8], span - 8 * a, 1)
                vec = pltpu.roll(eight, span - 1, 1)[:1]
                for b in range(1, 8):
                    vec = vec + pltpu.roll(eight, span - 1 - b, 1)[b : b + 1]
                return jnp.concatenate([vec, jnp.zeros((1, length - span), F32)], axis=1)

            whole = jnp.broadcast_to(unskew(gstrip[h], half), (8, length))
            whole = pltpu.roll(whole, PROMPT // 2, 1)
            for c in range(2):
                moved = jnp.broadcast_to(unskew(gfar[h, c], FARW + 128), (8, length))
                whole = whole + pltpu.roll(moved, PROMPT // 2 + starts[c], 1)
            picked = jnp.where(hot, whole[:1, :], 0.0)
            column = jnp.broadcast_to(jnp.sum(picked, axis=1, keepdims=True), (buckets, 128))
            tgrad[h : h + 1, :buckets] = column.T[:1, :]

    tall = nseq * rows
    pl.run_scoped(
        attend_back,
        pltpu.VMEM((heads, 128, STRIP), F32),
        pltpu.VMEM((heads, 2, 128, FARW), F32),
        pltpu.VMEM((heads, tall, piece), BF16),
        pltpu.VMEM((heads, tall, piece), BF16),
        pltpu.VMEM((piece, tall), BF16),
        pltpu.VMEM((8, tall), F32),
        pltpu.VMEM((piece, tall), F32),
        pltpu.VMEM((tall, piece), F32),
        pltpu.VMEM((tall, piece), F32),
        pltpu.VMEM((heads, 128, STRIP), F32),
        pltpu.VMEM((heads, 2, 128, FARW), F32),
    )

    def rest(n1, hold, rgrad, resid, first):
        later = [
            pltpu.make_async_copy(n1_h, n1, local.at[7]),
            pltpu.make_async_copy(rgrad_h, rgrad, local.at[8]),
            pltpu.make_async_copy(resid_h, resid, local.at[9]),
        ]
        ready = pltpu.make_async_copy(first_h, first, local.at[4])
        ready.start()
        for a in later:
            a.start()
        sums = SeqScatter(wires, chunks, b0, b1, b2, b3, b4, b5)
        size = rows // chunks
        ready.wait()

        def part(t, c):
            return nt(dqkv[rows_at(t, rows, c * size, size), :], first[:, : 3 * piece])

        for c in range(chunks):
            sums.cross_chunk(c, part(cross, c))
        for c in range(chunks):
            sums.far_chunk(c, part(far_d, c))
        for k in range(2, pairs - 1):
            ups.step(k)
        later[0].wait()
        depth = width // nfsdp
        wide = 384
        for n in range(width // wide):
            got = dot_tn(n1[:, n * wide : (n + 1) * wide], dqkv[...])
            for m in range(wide // depth):
                qkv_p[n * (wide // depth) + m] = got[m * depth : (m + 1) * depth, :].astype(BF16)
        for c in range(chunks):
            sums.near_chunk(c, part(near, c))
        for c in range(chunks):
            hold[c * size : (c + 1) * size, :] = part(s, c)
        qkvs.start()
        if pairs > 2:
            ups.step(pairs - 1)
        gates.finish()
        outs.start()
        gate_keep = pltpu.make_async_copy(gate_s, gate_f.at[s], local.at[11])
        gate_keep.start()
        gate_ring.send(0, gate_s)
        down_ring.forward(0)
        lead_ring.forward(0)
        later[2].wait()
        loads[1].wait()
        turn.wait_recv()
        far_hop.wait_recv()
        total = ybuf[3].astype(F32) + ybuf[1].astype(F32) + ybuf[4].astype(F32)
        ybuf[3] = (resid[...] + total).astype(BF16)
        qkvs.step(1)
        loads[2].wait()
        later[1].wait()
        gsum = jnp.zeros((1, width), F32)
        y_keep = pltpu.make_async_copy(ybuf.at[3], y_h, local.at[12])
        y_keep.start()
        for c in range(chunks):
            at = slice(c * size, (c + 1) * size)
            dn = sums.own_chunk(c, hold[at, :])
            x = tok[at, :].astype(F32)
            r = inverse_rms(x)
            gsum = gsum + jnp.sum(dn * x * r, axis=0, keepdims=True)
            tok[at, :] = (rgrad[at, :] + norm_back(dn, x, r, gains[0:1, :])).astype(BF16)
            if c == 0:
                for k in range(2, pairs - 1):
                    qkvs.step(k)
                ups.finish()
                up_keep = pltpu.make_async_copy(up_s, up_f.at[s], local.at[14])
                up_keep.start()
                up_ring.send(0, up_s)
                if pairs > 2:
                    qkvs.step(pairs - 1)
        in_keep = pltpu.make_async_copy(tok, in_h, local.at[13])
        in_keep.start()
        held[...] = jnp.zeros(held.shape, F32)
        lanes = held.shape[1]
        lines = width // lanes
        for n in range(lines):
            held[n : n + 1, :] = gsum[:, n * lanes : (n + 1) * lanes]
            held[lines + n : lines + n + 1, :] = gain_b[:1, n * lanes : (n + 1) * lanes]
        held[pl.ds(2 * lines + s * 8, 8), :] = tgrad[...]
        outs.step(1)
        trips = [wires.go(held, one.at[n], {"seq": t}) for n, t in enumerate((near, far_d, cross))]
        gate_ring.forward(0)
        for k in range(2, pairs):
            outs.step(k)
        for a in trips:
            a.wait_recv()
        stage[0] = held[...] + one[0] + one[1] + one[2]
        up_ring.forward(0)
        trips.append(wires.go(stage.at[0], two, {"fsdp": pair * 2 + 1 - side}))
        trips[-1].wait_recv()
        stage[1] = stage[0] + two[...]
        zs = [
            wires.go(stage.at[1], three.at[d - 1], {"fsdp": lax.rem(pair + d, pairs) * 2 + side})
            for d in range(1, pairs)
        ]
        qkvs.finish()
        qkv_keep = pltpu.make_async_copy(qkv_s, qkv_f.at[s], local.at[15])
        qkv_keep.start()
        qkv_ring.send(0, qkv_s)
        outs.finish()
        out_keep = pltpu.make_async_copy(out_s, out_f.at[s], local.at[16])
        out_keep.start()
        out_ring.send(0, out_s)
        total = stage[1]
        for d, a in enumerate(zs):
            a.wait_recv()
            total = total + three[d]
        small[...] = total
        qkv_ring.forward(0)
        out_ring.forward(0)
        for a in (down_ring, lead_ring, gate_ring, up_ring, qkv_ring, out_ring):
            a.finish()
        sums.finish()
        for a in (gates, ups, qkvs, outs):
            a.drain()
        for a in (gate_keep, up_keep, qkv_keep, out_keep, y_keep, in_keep, down_keep, lead_keep):
            a.wait()
        for a in trips + zs + [hop, turn, far_hop]:
            a.wait_send()

    pl.run_scoped(
        rest,
        pltpu.VMEM((tall, width), BF16),
        pltpu.VMEM((rows, width), F32),
        pltpu.VMEM((rows, width), F32),
        pltpu.VMEM((rows, width), F32),
        pltpu.VMEM(first_h.shape, BF16),
    )


def back(starts, table, ids, gains, lse, gain_b, q, k, v, o, do, resid, rgrad, tok, y_p, out_p, gate_p, up_p, done, lead, n1, first, chunks=2):
    tall, piece = q.shape
    heads = piece // HEAD_DIM
    rows, width = tok.shape
    nseq = tall // rows
    nfsdp = gate_p.shape[0]
    pairs = nfsdp // 2
    lines = -(-(2 * width // 128 + 8 * nseq) // 8) * 8
    qkv_shape = (nfsdp, width // nfsdp, 3 * piece)
    out_shape = out_p.shape
    smem = pl.BlockSpec(memory_space=pltpu.SMEM)

    def full(a):
        return jax.ShapeDtypeStruct((nseq,) + tuple(a), BF16)

    return pl.pallas_call(
        functools.partial(back_kernel, heads, chunks),
        out_shape=(
            jax.ShapeDtypeStruct((lines, 128), F32),
            jax.ShapeDtypeStruct((rows, width), BF16),
            jax.ShapeDtypeStruct((rows, width), BF16),
            full(done.shape),
            full(lead.shape),
            full(gate_p.shape[1:]),
            full(up_p.shape[1:]),
            full(qkv_shape[1:]),
            full(out_shape[1:]),
        ),
        in_specs=[smem, smem] + [vm_spec()] * 9 + [any_spec()] * 11,
        out_specs=(vm_spec(),) + (any_spec(),) * 8,
        scratch_shapes=wires_scratch(6 + 4 * nfsdp + 18 + 3 * chunks + 4 + pairs)
        + [
            pltpu.SemaphoreType.DMA((17,)),
            pltpu.VMEM((5, rows, width), BF16),
            pltpu.VMEM(qkv_shape, BF16),
        ]
        + scatter_scratch(chunks, rows // chunks, width)
        + fsdp_scatter_scratch(gate_p.shape)
        + fsdp_scatter_scratch(up_p.shape)
        + fsdp_scatter_scratch(qkv_shape)
        + fsdp_scatter_scratch(out_shape)
        + [
            pltpu.VMEM(gate_p.shape[1:], BF16),
            pltpu.VMEM(up_p.shape[1:], BF16),
            pltpu.VMEM(qkv_shape[1:], BF16),
            pltpu.VMEM(out_shape[1:], BF16),
            pltpu.VMEM((tall, 3 * piece), BF16),
            pltpu.VMEM((rows, width), BF16),
            pltpu.VMEM((lines, 128), F32),
            pltpu.VMEM((2, lines, 128), F32),
            pltpu.VMEM((3, lines, 128), F32),
            pltpu.VMEM((lines, 128), F32),
            pltpu.VMEM((pairs - 1, lines, 128), F32),
            pltpu.VMEM((8, 128), F32),
        ],
        compiler_params=call_params(5, 64),
        name="back",
    )(starts, table, ids, gains, lse, gain_b, q, k, v, o, do, resid, rgrad, tok, y_p, out_p, gate_p, up_p, done, lead, n1, first)


def unpack_kernel(nseq, nfsdp, heads, *refs):
    srcs, small, outs = refs[:8], refs[8], refs[9:18]
    ga, gb, table, ins, offs = refs[18:23]
    vs, ts = refs[23:31], refs[31:]
    loads = [pltpu.make_async_copy(a, b, ins.at[n]) for n, (a, b) in enumerate(zip(srcs, vs))]
    for a in loads:
        a.start()
    lead_f, gate_f, up_f, down_f, qkv_f, out_f, y, dx = vs
    tq, tk, tv, to, tg, tu, td = ts
    gq, gk, gv, go, gg, gu, gd, gy, gx = outs
    copies = []

    def save(src, dst):
        copies.append(pltpu.make_async_copy(src, dst, offs.at[len(copies)]))
        copies[-1].start()

    block, piece = pack_piece(tg.shape[1], nfsdp, nseq)
    half = nfsdp // 2

    def columns(get):
        parts = []
        for f in range(nfsdp):
            for t in range(nseq):
                size = min(piece, block - t * piece)
                full, f_at = get(f)
                parts.append(full[t, :, f_at * piece : f_at * piece + size].astype(F32))
        return jnp.concatenate(parts, axis=1)

    loads[0].wait()
    loads[1].wait()
    tg[...] = columns(lambda f: (lead_f, f) if f < half else (gate_f, f - half))
    save(tg, gg)
    loads[2].wait()
    tu[...] = columns(lambda f: (up_f, f))
    save(tu, gu)
    loads[3].wait()
    size = down_f.shape[1]
    for t in range(nseq):
        n = min(size, td.shape[0] - t * size)
        td[t * size : t * size + n, :] = down_f[t, :n, :].astype(F32)
    save(td, gd)
    loads[4].wait()
    width = qkv_f.shape[2] // 3
    for n, (dst, out) in enumerate(((tq, gq), (tk, gk), (tv, gv))):
        dst[...] = jnp.concatenate([qkv_f[t, :, n * width : (n + 1) * width] for t in range(nseq)], axis=1).astype(F32)
        save(dst, out)
    loads[5].wait()
    to[...] = jnp.concatenate([out_f[t] for t in range(nseq)], axis=1).astype(F32)
    save(to, go)
    for n, (src, dst) in enumerate(((y, gy), (dx, gx))):
        loads[6 + n].wait()
        save(src, dst)
    where = lax.axis_index("fsdp")
    share = ga.shape[1]
    lines = nfsdp * share // 128
    for n, dst in enumerate((ga, gb)):
        line = jnp.concatenate([small[n * lines + a : n * lines + a + 1, :] for a in range(lines)], axis=1)
        for f in range(nfsdp):

            @pl.when(where == f)
            def _():
                dst[...] = line[:, f * share : (f + 1) * share]

    for t in range(nseq):
        at = 2 * lines + 8 * t
        table[t * heads : (t + 1) * heads, :] = small[at : at + heads, : table.shape[1]]
    for a in copies:
        a.wait()


def unpack(srcs, small, like, blocks_like, table, nfsdp):
    nseq = srcs[0].shape[0]
    share = like[0].shape[0]
    vm = [vm_spec()] * 3
    return pl.pallas_call(
        functools.partial(unpack_kernel, nseq, nfsdp, table.shape[0] // nseq),
        out_shape=tuple(jax.ShapeDtypeStruct(a.shape, F32) for a in like)
        + tuple(jax.ShapeDtypeStruct(a.shape, BF16) for a in blocks_like)
        + (
            jax.ShapeDtypeStruct((1, share), F32),
            jax.ShapeDtypeStruct((1, share), F32),
            jax.ShapeDtypeStruct(table.shape, F32),
        ),
        in_specs=[any_spec()] * 8 + [vm_spec()],
        out_specs=tuple([any_spec()] * 9 + vm),
        scratch_shapes=[pltpu.SemaphoreType.DMA((8,)), pltpu.SemaphoreType.DMA((9,))]
        + [pltpu.VMEM(a.shape, BF16) for a in srcs]
        + [pltpu.VMEM(a.shape, F32) for a in like],
        compiler_params=pltpu.CompilerParams(vmem_limit_bytes=67043328),
        name="unpack",
    )(*srcs, small)


def reversed_ids(bucket_ids):
    span = bucket_ids.shape[0]
    ids = jnp.concatenate([bucket_ids[::-1], jnp.full((1,), -1, jnp.int32)])
    return ids[None, :]


def dot32(a, b):
    return jnp.dot(a, b, preferred_element_type=F32)


def dot_tn(a, b):
    return lax.dot_general(a, b, (((0,), (0,)), ((), ())), preferred_element_type=F32)


def gelu_both(u):
    inner = 0.7978845608028654 * (u + 0.044715 * u * u * u)
    t = jnp.tanh(inner)
    value = 0.5 * u * (1.0 + t)
    slope = 0.5 * (1.0 + t) + 0.5 * u * (1.0 - t * t) * 0.7978845608028654 * (1.0 + 3 * 0.044715 * u * u)
    return value, slope


def body(
    tokens,
    out_grad,
    attn_gain,
    w_query,
    w_key,
    w_value,
    w_out,
    mix_gain,
    w_gate,
    w_up,
    w_down,
    rel_table,
    bucket_ids,
    cont_start,
):
    nseq = lax.axis_size("seq")
    nfsdp = lax.axis_size("fsdp")
    inner = w_query.shape[1]

    ids = reversed_ids(bucket_ids)
    starts = cont_start[0]
    (
        query,
        keys,
        values,
        mixed,
        lse,
        gains,
        mixed_rows,
        resid,
        normed,
        first,
        out_w,
        _,
        gate_w,
        up_w,
        down_w,
        normed_two,
        hidden,
        gate_grad,
        up_grad,
        down_grad,
    ) = forward(
        starts,
        rel_table.T,
        ids,
        jnp.stack([attn_gain.astype(F32), mix_gain.astype(F32)]),
        tokens[0],
        w_query,
        w_key,
        w_value,
        w_out,
        w_gate,
        w_up,
        w_down,
        out_grad[0],
        nseq,
        nfsdp,
    )
    out_w = out_w.reshape(nseq, inner, -1)
    resid_grad, mixed_grad, gain_two_grad, down_grad, lead_grad, out_w_grad, gate_w_grad, up_w_grad, result = unmix(
        gains, mixed_rows, resid, out_grad[0], down_grad, gate_grad, up_grad, gate_w, up_w, out_w, normed_two, hidden, down_w
    )
    small, block_out, in_grad, down_grad, lead_grad, gate_w_grad, up_w_grad, qkv_grad, out_w_grad = back(
        starts,
        rel_table.T,
        ids,
        gains,
        lse,
        gain_two_grad,
        query,
        keys,
        values,
        mixed,
        mixed_grad,
        resid,
        resid_grad,
        tokens[0],
        result,
        out_w_grad,
        gate_w_grad,
        up_w_grad,
        down_grad,
        lead_grad,
        normed,
        first,
    )
    *shards, block_out, in_grad, gain_one_share, gain_two_share, table_grad = unpack(
        (lead_grad, gate_w_grad, up_w_grad, down_grad, qkv_grad, out_w_grad, block_out, in_grad),
        small,
        (w_query, w_key, w_value, w_out, w_gate, w_up, w_down),
        (block_out, in_grad),
        rel_table.T,
        nfsdp,
    )
    return (
        block_out[None],
        in_grad[None],
        gain_one_share[0],
        *shards[:4],
        gain_two_share[0],
        *shards[4:],
        table_grad.T,
    )


def solution(mesh):
    placed = (
        P("fsdp", "seq", None),
        P("fsdp", "seq", None),
        P("fsdp"),
        P("fsdp", None),
        P("fsdp", None),
        P("fsdp", None),
        P("fsdp", None),
        P("fsdp"),
        P("fsdp", None),
        P("fsdp", None),
        P("fsdp", None),
        P(),
        P(),
        P("fsdp", None),
    )
    results = placed[:1] * 2 + placed[2:11] + (P(),)
    return jax.shard_map(body, mesh=mesh, in_specs=placed, out_specs=results, check_vma=False)
```

```python
import functools
import jax
import jax.numpy as jnp
from jax import lax
from jax.experimental import pallas as pl
from jax.experimental.pallas import tpu as pltpu
from jax.sharding import PartitionSpec as P

HEAD_DIM = 64
PROMPT = 1024
CL = 256
F32 = jnp.float32
BF16 = jnp.bfloat16
MESH = pl.DeviceIdType.MESH
epsilon = 1e-06
STRIP = 2 * PROMPT - 128
FARW = PROMPT - 128 + CL
KC = 256


def nt(a, b):
    return lax.dot_general(a, b, (((1,), (1,)), ((), ())), preferred_element_type=F32)


def nn(a, b):
    return lax.dot_general(a, b, (((1,), (0,)), ((), ())), preferred_element_type=F32)


class Wires:
    def __init__(self, send, recv):
        self.send, self.recv, self.used = send, recv, 0

    def take(self, count):
        self.used += count
        return self.used - count

    def at(self, i, src, dst, where):
        return pltpu.make_async_remote_copy(
            src_ref=src,
            dst_ref=dst,
            send_sem=self.send.at[i],
            recv_sem=self.recv.at[i],
            device_id=where,
            device_id_type=MESH,
        )

    def go(self, src, dst, where):
        c = self.at(self.take(1), src, dst, where)
        c.start()
        return c


def seq_places():
    s = lax.axis_index("seq")
    near = s + 1 - 2 * lax.rem(s, 2)
    far = lax.rem(s + 2, 4)
    cross = lax.rem(near + 2, 4)
    return s, near, far, cross


def greet(places):
    barrier = pltpu.get_barrier_semaphore()
    for where in places:
        pl.semaphore_signal(barrier, inc=1, device_id=where, device_id_type=MESH)


def meet(places):
    greet(places)
    pl.semaphore_wait(pltpu.get_barrier_semaphore(), len(places))


def rows_at(index, rows, offset=0, count=None):
    return pl.ds(pl.multiple_of(index * rows + offset, 16), rows if count is None else count)


class SeqGather:
    def __init__(self, wires, out_at, chunks):
        self.wires, self.out_at, self.chunks = wires, out_at, chunks
        self.s, self.near, self.far, self.cross = seq_places()
        self.base = wires.take(3 * chunks)

    def trip(self, kind, c, src=None):
        view = self.out_at(self.far if kind == 2 else self.s, c)
        where = {"seq": self.far if kind == 0 else self.near}
        return self.wires.at(self.base + 3 * c + kind, view if src is None else src, view, where)

    def send(self, c, src):
        self.trip(0, c, src).start()
        self.trip(1, c, src).start()

    def forward(self, c):
        self.trip(0, c).wait_recv()
        self.trip(2, c).start()

    def got_near(self, c):
        self.trip(1, c).wait_recv()

    def got_cross(self, c):
        self.trip(2, c).wait_recv()

    def drain(self):
        for c in range(self.chunks):
            for kind in range(3):
                self.trip(kind, c).wait_send()

    def finish(self):
        for c in range(self.chunks):
            self.got_near(c)
            self.got_cross(c)
        self.drain()


def fsdp_places():
    f = lax.axis_index("fsdp")
    return f // 2, lax.rem(f, 2), lax.axis_size("fsdp") // 2


def far_first(k):
    pair, _, pairs = fsdp_places()
    if pairs != 4:
        return k + 1
    first, second = 3 - (pair + 1) // 2, 1 + lax.rem(pair + 1, 3)
    return (first, second, 6 - first - second)[k]


def fsdp_peers():
    pair, side, pairs = fsdp_places()
    peers = [{"fsdp": lax.rem(pair + d, pairs) * 2 + side} for d in range(1, pairs)]
    return peers + [{"fsdp": pair * 2 + 1 - side}]


class FsdpGather:
    def __init__(self, wires, shard, full_at, local):
        self.wires, self.shard, self.full_at, self.local = wires, shard, full_at, local
        self.pair, self.side, self.pairs = fsdp_places()
        self.base = wires.take(2 * self.pairs)

    def source(self, d):
        return lax.rem(self.pair + self.pairs - d, self.pairs)

    def over(self):
        own = self.full_at(self.pair * 2 + self.side)
        return self.wires.at(self.base, self.shard, own, {"fsdp": self.pair * 2 + 1 - self.side})

    def out(self, d):
        own = self.full_at(self.pair * 2 + self.side)
        where = {"fsdp": lax.rem(self.pair + d, self.pairs) * 2 + self.side}
        return self.wires.at(self.base + d, self.shard, own, where)

    def onward(self, d):
        view = self.full_at(self.source(d) * 2 + self.side)
        return self.wires.at(self.base + self.pairs + d, view, view, {"fsdp": self.pair * 2 + 1 - self.side})

    def keep(self):
        return pltpu.make_async_copy(self.shard, self.full_at(self.pair * 2 + self.side), self.local)

    def start(self):
        for k in range(self.pairs - 1):
            self.out(k + 1).start()
        self.keep().start()

    def forward(self, k):
        self.out(k).wait_recv()
        self.onward(k).start()

    def complete(self, k):
        if k == 0:
            self.keep().wait()
            self.over().wait_recv()
        else:
            self.onward(k).wait_recv()

    def drain(self):
        self.over().wait_send()
        for d in range(1, self.pairs):
            self.out(d).wait_send()
            self.onward(d).wait_send()

    def finish(self):
        for k in range(self.pairs):
            self.complete(k)
        self.drain()


def gather_halves(wires, shard, full, size, local):
    half, wide = size // 2, shard.shape[1] // 2

    def one(n):
        if size % 32 == 0:
            rows = pl.ds(n * half, half)
            return FsdpGather(wires, shard.at[rows, :], lambda f: full.at[shard_rows(2 * f + n, half), :], local[n])
        cut = slice(n * wide, (n + 1) * wide)
        return FsdpGather(wires, shard.at[:, cut], lambda f: full.at[shard_rows(f, size), cut], local[n])

    return [one(0), one(1)]


class FsdpScatter:
    def __init__(self, wires, parts, bufs, result):
        self.wires, self.parts, self.result = wires, parts, result
        self.mine, self.got, self.landed, self.local = bufs
        self.pair, self.side, self.pairs = fsdp_places()
        self.base = wires.take(2 * self.pairs)

    def step_to(self, k):
        return far_first(k) if k < self.pairs - 1 else 0

    def owner(self, d):
        return lax.rem(self.pair + d, self.pairs) * 2

    def load(self, k):
        part = self.parts.at[self.owner(self.step_to(k)) + self.side]
        return pltpu.make_async_copy(part, self.mine.at[k % 2], self.local.at[k % 2])

    def swap(self, d):
        src = self.parts.at[self.owner(d) + 1 - self.side]
        return self.wires.at(self.base + d, src, self.got.at[d], {"fsdp": self.pair * 2 + 1 - self.side})

    def onward(self, d):
        where = {"fsdp": self.owner(d) + self.side}
        return self.wires.at(self.base + self.pairs + d, self.got.at[d], self.landed.at[d - 1], where)

    def start(self):
        for k in range(self.pairs):
            self.swap(self.step_to(k)).start()
        self.load(0).start()

    def step(self, k):
        d = self.step_to(k - 1)
        self.load(k).start()
        self.load(k - 1).wait()
        self.swap(d).wait_recv()
        self.got[d] = (self.mine[(k - 1) % 2].astype(F32) + self.got[d].astype(F32)).astype(BF16)
        self.onward(d).start()

    def finish(self):
        self.load(self.pairs - 1).wait()
        self.swap(0).wait_recv()
        total = self.mine[(self.pairs - 1) % 2].astype(F32) + self.got[0].astype(F32)
        for d in range(1, self.pairs):
            self.onward(d).wait_recv()
            total = total + self.landed[d - 1].astype(F32)
        self.result[...] = total.astype(BF16)

    def drain(self):
        for d in range(self.pairs):
            self.swap(d).wait_send()
        for d in range(1, self.pairs):
            self.onward(d).wait_send()


def fsdp_scatter_scratch(shape):
    pairs = shape[0] // 2
    return [
        pltpu.VMEM((2,) + shape[1:], BF16),
        pltpu.VMEM((pairs,) + shape[1:], BF16),
        pltpu.VMEM((pairs - 1,) + shape[1:], BF16),
        pltpu.SemaphoreType.DMA((2,)),
    ]


def blocks(a, count):
    return a.reshape((count, a.shape[0] // count) + a.shape[1:])


def shard_rows(f, size):
    return pl.ds(pl.multiple_of(f * size, 16 if size % 16 == 0 else 8 if size % 8 == 0 else size), size)


def vm_spec():
    return pl.BlockSpec(memory_space=pltpu.VMEM)


def any_spec():
    return pl.BlockSpec(memory_space=pl.ANY)


def wires_scratch(n):
    return [pltpu.SemaphoreType.DMA((n,)), pltpu.SemaphoreType.DMA((n,))]


def call_params(number, vmem=60):
    return pltpu.CompilerParams(collective_id=number, has_side_effects=True, vmem_limit_bytes=min(vmem << 20, 67043328))


def inverse_rms(v):
    return lax.rsqrt(jnp.mean(v * v, axis=-1, keepdims=True) + epsilon)


def norm_back(grad, v, r, gain):
    scaled = grad * gain
    return r * scaled - v * (r * r * r) * jnp.mean(v * scaled, axis=-1, keepdims=True)


class SeqScatter:
    def __init__(self, wires, chunks, *bufs):
        self.s, self.near, self.far, self.cross = seq_places()
        self.wires, self.chunks, self.bufs = wires, chunks, bufs
        self.base = wires.take(3 * chunks)

    def trip(self, kind, c):
        where = {"seq": self.far if kind == 1 else self.near}
        src, dst = self.bufs[2 * kind].at[c], self.bufs[2 * kind + 1].at[c]
        return self.wires.at(self.base + 3 * c + kind, src, dst, where)

    def cross_chunk(self, c, value):
        self.bufs[0][c] = value.astype(BF16)
        self.trip(0, c).start()

    def far_chunk(self, c, value):
        self.trip(0, c).wait_recv()
        self.bufs[2][c] = (value + self.bufs[1][c].astype(F32)).astype(BF16)
        self.trip(1, c).start()

    def near_chunk(self, c, value):
        self.bufs[4][c] = value.astype(BF16)
        self.trip(2, c).start()

    def own_chunk(self, c, value):
        self.trip(2, c).wait_recv()
        self.trip(1, c).wait_recv()
        return value + self.bufs[5][c].astype(F32) + self.bufs[3][c].astype(F32)

    def finish(self):
        for c in range(self.chunks):
            for kind in range(3):
                self.trip(kind, c).wait_send()


def scatter_scratch(chunks, rows, width):
    return [pltpu.VMEM((chunks, rows, width), BF16)] * 6


def unmix_kernel(
    chunks, gains, obuf, resid, cot, down_p, dg_h, du_h, gate_h, up_h, out_h, n2_h, hid_h, dw_h,
    rgrad_h, dmix_h, ggrad, shard, lead_s, out_p, gate_p, up_p, y_h,
    send, recv, b0, b1, b2, b3, b4, b5, attn, dob, p0, p1, p2, p3, l0, l1, l2, l3, lead_p,
    local, dg, du, gate_w, up_w, out_w, n2, hid, down_w, wgrad, wbuf, stage, ystage, sems, rgrad, dmix,
):
    rows, width = resid.shape
    nseq, _, piece = obuf.shape
    nfsdp = gate_p.shape[0]
    units = dg.shape[1]
    first_half = units // 2
    s, near, far, cross = seq_places()
    loads = [
        pltpu.make_async_copy(src, dst, local.at[n])
        for n, (src, dst) in enumerate(
            (
                (gate_h, gate_w),
                (up_h, up_w),
                (dg_h, dg),
                (du_h, du),
                (n2_h, n2),
                (out_h, out_w),
                (hid_h, hid),
                (dw_h, down_w),
            )
        )
    ]
    for a in loads:
        a.start()
    meet([{"seq": near}, {"seq": far}, {"seq": cross}] + fsdp_peers())
    wires = Wires(send, recv)
    grads = FsdpScatter(wires, down_p, (p0, p1, p2, p3), shard)
    grads.start()
    leads = FsdpScatter(wires, lead_p, (l0, l1, l2, l3), lead_s)
    pairs = grads.pairs
    sums = SeqScatter(wires, chunks, b0, b1, b2, b3, b4, b5)
    size = rows // chunks
    for a in loads[:4]:
        a.wait()

    def part(t, c):
        at = rows_at(t, rows, c * size, size)
        return nt(dg[at, :], gate_w[...]) + nt(du[at, :], up_w[...])

    for c in range(chunks):
        sums.cross_chunk(c, part(cross, c))
    for c in range(chunks):
        sums.far_chunk(c, part(far, c))
    for c in range(chunks):
        sums.near_chunk(c, part(near, c))
    for c in range(chunks):
        rgrad[c * size : (c + 1) * size, :] = part(s, c)
    grads.step(1)
    loads[4].wait()
    depth = width // nfsdp
    wide = 384
    saves = []

    def weight_parts(side, out, begin, end, cut):
        for n in range(begin, end):
            slot = n % 2
            group = pl.ds(n * (wide // depth), wide // depth)
            if len(saves) > 1:
                saves[-2].wait()
            got = dot_tn(n2[:, n * wide : (n + 1) * wide], side[...])
            for m in range(wide // depth):
                low = got[m * depth : (m + 1) * depth, :].astype(BF16)
                if cut:
                    lead_p[n * (wide // depth) + m] = low[:, :cut]
                stage[slot, m, :, : units - cut] = low[:, cut:]
            a = pltpu.make_async_copy(stage.at[slot, :, :, : units - cut], out.at[group], sems.at[3 + slot])
            a.start()
            saves.append(a)

    weight_parts(dg, gate_p, 0, width // wide, first_half)
    if pairs > 2:
        grads.step(2)
    loads[5].wait()
    cols = out_w.shape[2]

    def own_rows(c, total):
        at = slice(c * size, (c + 1) * size)
        dn = sums.own_chunk(c, rgrad[at, :])
        h = resid[at, :]
        r = inverse_rms(h)
        rg = cot[at, :].astype(F32) + norm_back(dn, h, r, gains[1:2, :])
        rgrad[at, :] = rg
        low = rg.astype(BF16)
        attn[at, :] = low
        for t in range(nseq):
            acc = jnp.zeros((size, piece), F32)
            for u in range(nseq):
                acc = acc + nt(low[:, u * cols : (u + 1) * cols], out_w[u, t * piece : (t + 1) * piece, :])
            dob[t, at, :] = acc.astype(BF16)
        return total + jnp.sum(dn * h * r, axis=0, keepdims=True)

    base = wires.take(3 * chunks)

    def trip(n, t, c):
        at = pl.ds(c * size, size)
        return wires.at(base + 3 * c + n, dob.at[t, at, :], dmix.at[rows_at(s, rows, c * size, size), :], {"seq": t})

    total = jnp.zeros((1, width), F32)
    for c in range(chunks):
        total = own_rows(c, total)
        if c == 0:
            weight_parts(du, up_p, 0, 1, 0)
            leads.start()
        for n, t in enumerate((far, cross, near)):
            trip(n, t, c).start()
        dmix[rows_at(s, rows, c * size, size), :] = dob[s, pl.ds(c * size, size), :]
        if c == 0:
            weight_parts(du, up_p, 1, width // wide, 0)
            for d in range(3, pairs):
                grads.step(d)
    ggrad[...] = jnp.broadcast_to(total, ggrad.shape)
    rsave = pltpu.make_async_copy(rgrad, rgrad_h, sems.at[2])
    rsave.start()
    leads.step(1)
    wbase = wires.take(3)

    def wtrip(n):
        u = (cross, far, near)[n]
        return wires.at(wbase + n, wgrad.at[u], wbuf.at[n], {"seq": far if n == 1 else near})

    def wblock(u):
        for t in range(nseq):
            at = pl.ds(pl.multiple_of(u * cols, 128), cols)
            wgrad[u, t * piece : (t + 1) * piece, :] = dot_tn(obuf[t], attn[:, at]).astype(BF16)

    wblock(cross)
    wblock(far)
    wtrip(0).start()
    for d in range(2, pairs - 1):
        leads.step(d)
    wblock(near)
    wtrip(0).wait_recv()
    wgrad[far] = (wgrad[far].astype(F32) + wbuf[0].astype(F32)).astype(BF16)
    wblock(s)
    wtrip(1).start()
    wtrip(2).start()
    for a in loads[6:]:
        a.wait()
    ycopies = []
    for t in range(nseq):
        slot = t % 2
        if t > 1:
            ycopies[t - 2].wait()
        at = slice(t * rows, (t + 1) * rows)
        ystage[slot] = nn(hid[at, :], down_w[...]).astype(BF16)
        ycopies.append(pltpu.make_async_copy(ystage.at[slot], y_h.at[at, :], sems.at[slot]))
        ycopies[t].start()
        if t == 1:
            leads.step(pairs - 1)
    for c in range(chunks):
        for n, t in enumerate((far, cross, near)):
            trip(n, t, c).wait()
    dsave = pltpu.make_async_copy(dmix, dmix_h, local.at[8])
    dsave.start()
    grads.finish()
    for n in range(1, 3):
        wtrip(n).wait_recv()
    wsum = wgrad[s].astype(F32) + wbuf[1].astype(F32) + wbuf[2].astype(F32)
    lines = out_p.shape[1]
    for f in range(nfsdp):
        out_p[f] = wsum[f * lines : (f + 1) * lines, :].astype(BF16)
    for n in range(3):
        wtrip(n).wait_send()
    sums.finish()
    grads.drain()
    leads.finish()
    leads.drain()
    for a in saves[-2:]:
        a.wait()
    for a in ycopies[-2:] + [rsave, dsave]:
        a.wait()


def unmix(gains, obuf, resid, cot, down_p, dg, du, gate_w, up_w, out_w, n2, hid, down_w, chunks=2):
    rows, width = resid.shape
    nseq, _, piece = obuf.shape
    nfsdp = down_p.shape[0]
    units = dg.shape[1]
    grad_shape = (nfsdp, width // nfsdp, units)
    half_shape = (nfsdp, width // nfsdp, units // 2)
    return pl.pallas_call(
        functools.partial(unmix_kernel, chunks),
        out_shape=(
            jax.ShapeDtypeStruct((rows, width), F32),
            jax.ShapeDtypeStruct((nseq * rows, piece), BF16),
            jax.ShapeDtypeStruct((8, width), F32),
            jax.ShapeDtypeStruct(down_p.shape[1:], BF16),
            jax.ShapeDtypeStruct(half_shape[1:], BF16),
            jax.ShapeDtypeStruct((nfsdp, out_w.shape[1] // nfsdp, out_w.shape[2]), BF16),
            jax.ShapeDtypeStruct(half_shape, BF16),
            jax.ShapeDtypeStruct(grad_shape, BF16),
            jax.ShapeDtypeStruct(n2.shape, BF16),
        ),
        in_specs=[vm_spec()] * 4 + [any_spec()] * 9,
        out_specs=(any_spec(),) * 2 + (vm_spec(),) * 4 + (any_spec(),) * 3,
        scratch_shapes=wires_scratch(6 * chunks + 2 * nfsdp + 3)
        + scatter_scratch(chunks, rows // chunks, width)
        + [pltpu.VMEM((rows, width), BF16), pltpu.VMEM((nseq, rows, piece), BF16)]
        + fsdp_scatter_scratch(down_p.shape)
        + fsdp_scatter_scratch(half_shape)
        + [
            pltpu.VMEM(half_shape, BF16),
            pltpu.SemaphoreType.DMA((9,)),
            pltpu.VMEM(dg.shape, BF16),
            pltpu.VMEM(du.shape, BF16),
            pltpu.VMEM(gate_w.shape, BF16),
            pltpu.VMEM(up_w.shape, BF16),
            pltpu.VMEM(out_w.shape, BF16),
            pltpu.VMEM(n2.shape, BF16),
            pltpu.VMEM(hid.shape, BF16),
            pltpu.VMEM(down_w.shape, BF16),
            pltpu.VMEM(out_w.shape, BF16),
            pltpu.VMEM((3,) + out_w.shape[1:], BF16),
            pltpu.VMEM((2, 384 * nfsdp // width, width // nfsdp, units), BF16),
            pltpu.VMEM((2, rows, width), BF16),
            pltpu.SemaphoreType.DMA((5,)),
            pltpu.VMEM((rows, width), F32),
            pltpu.VMEM((nseq * rows, piece), BF16),
        ],
        compiler_params=call_params(4, 63),
        name="unmix",
    )(gains, obuf, resid, cot, down_p, dg, du, gate_w, up_w, out_w, n2, hid, down_w)


def build_strips(heads, first_head, starts, table, ids, strip, far):
    length = ids.shape[1]
    half = 2 * PROMPT
    for h in range(heads):
        row = jnp.zeros(ids.shape, F32)
        for b in range(table.shape[1]):
            row = jnp.where(ids[...] == b, table[first_head + h, b], row)
        row = jnp.broadcast_to(row, (8, length))
        base = jnp.broadcast_to(row[:1, PROMPT // 2 : PROMPT // 2 + half], (128, half))
        strip[h] = pltpu.roll(base, 1, 1, stride=1, stride_axis=0)[:, 128:]
        for c in range(2):
            moved = pltpu.roll(row, length - PROMPT // 2 - starts[c], 1)
            base = jnp.broadcast_to(moved[:1, : FARW + 128], (128, FARW + 128))
            far[h, c] = pltpu.roll(base, 1, 1, stride=1, stride_axis=0)[:, 128:]


def head_masks(width, heads):
    lane = lax.broadcasted_iota(jnp.int32, (1, width), 1)
    return [(lane >= h * HEAD_DIM) & (lane < (h + 1) * HEAD_DIM) for h in range(heads)]


def masked_copies(src, dst, heads):
    masks = head_masks(src.shape[1], heads)
    for h in range(heads):
        dst[h] = jnp.where(masks[h], src[...], jnp.zeros((), src.dtype))


def bias_chunk(strip, far, h, first_q, kstart, kind, c):
    parts = []
    for r in range(KC // 128):
        m = PROMPT - 128 - (kstart + 128 * r)
        if kind == "far":
            parts.append(far[h, c, :, m : m + CL])
        else:
            parts.append(strip[h, :, pl.ds(pl.multiple_of(first_q + m, 128), CL)])
    return jnp.concatenate(parts, axis=0)


def pack_piece(units, nfsdp, nseq):
    block = units // nfsdp
    return block, -(-block // (16 * nseq)) * 16


def pack_front(t, raw, first_q, out_q, gains):
    r_q, r_k, r_v, r_o = raw
    piece = first_q.shape[1] * 3 // 10
    depth = first_q.shape[0]
    cut = slice(t * piece, (t + 1) * piece)
    first_q[...] = jnp.concatenate(
        [r_q[:, cut], r_k[:, cut], r_v[:, cut], gains, jnp.zeros((depth, first_q.shape[1] - 3 * piece - 8), BF16)], axis=1
    )
    cols = out_q.shape[1]
    out_q[...] = r_o[:, t * cols : (t + 1) * cols]


def pack_cols(t, nseq, nfsdp, raw, packed):
    block, piece = pack_piece(raw.shape[1], nfsdp, nseq)
    pieces = []
    for f in range(nfsdp):
        begin = f * block + t * piece
        end = min(begin + piece, (f + 1) * block)
        pieces.append(raw[:, begin:end])
        if end - begin < piece:
            pieces.append(jnp.zeros((raw.shape[0], piece - end + begin), BF16))
    packed[...] = jnp.concatenate(pieces, axis=1)


def pack_down(t, raw, packed):
    piece = packed.shape[0]
    begin = t * piece
    end = min(begin + piece, raw.shape[0])
    packed[: end - begin, :] = raw[begin:end, :]
    if end - begin < piece:
        packed[end - begin :, :] = jnp.zeros((piece - end + begin, raw.shape[1]), BF16)


def forward_kernel(
    heads, nseq, starts, table, ids, gain_q, tok_h, w_q, w_k, w_v, w_o, w_g, w_u, w_d, cot_q,
    lse, gains, q_h, k_h, v_h, o_h, obuf_h, resid_h,
    n1_h, first_h, out_h, cot_h, gate_h, up_h, down_h, n2_h, hid_h, dg_h, du_h, parts_h,
    send, recv, local, first_q, out_q, gate_q, up_q, down_q, group, first, gate_w, up_w, down_w, tok, fsems, spare, q, k, v, o, obuf, resid, osems,
):
    rows, width = tok.shape
    units = gate_w.shape[1]
    piece = q.shape[1]
    mine, near, other, cross = seq_places()
    pair, side, pairs = fsdp_places()
    nfsdp = 2 * pairs
    half = rows // 2
    wires = Wires(send, recv)
    ring = SeqGather(wires, lambda t, c: group.at[rows_at(t, rows, c * half, half), :], 2)
    size = first_q.shape[0]
    lead = FsdpGather(wires, first_q, lambda f: first.at[shard_rows(f, size), :], local.at[7])
    late = FsdpGather(wires, out_q, lambda f: out_h.at[mine, f], local.at[8])
    gates = gather_halves(wires, gate_q, gate_w, gate_q.shape[0], (local.at[9], local.at[10]))
    ups = gather_halves(wires, up_q, up_w, up_q.shape[0], (local.at[11], local.at[12]))
    downs = gather_halves(wires, down_q, down_w, down_q.shape[0], (local.at[13], local.at[14]))
    wring = SeqGather(wires, lambda t, c: out_h.at[t], 1)
    cring = SeqGather(wires, lambda t, c: cot_h.at[rows_at(t, rows, c * half, half), :], 2)
    nring = SeqGather(wires, lambda t, c: group.at[rows_at(t, rows, c * half, half), :], 2)
    obase = wires.take(3)
    own = [
        pltpu.make_async_copy(tok_h, group.at[rows_at(mine, rows), :], local.at[15]),
        pltpu.make_async_copy(cot_q, cot_h.at[rows_at(mine, rows), :], local.at[16]),
        pltpu.make_async_copy(tok_h, tok, local.at[17]),
    ]

    def begin(r_q, r_k, r_v, r_o, r_g, r_u, r_d):
        loads = [
            pltpu.make_async_copy(src, dst, local.at[n])
            for n, (src, dst) in enumerate(
                ((w_q, r_q), (w_k, r_k), (w_v, r_v), (w_o, r_o), (w_g, r_g), (w_u, r_u), (w_d, r_d))
            )
        ]
        for a in loads:
            a.start()
        peers = [{"seq": near}, {"seq": other}, {"seq": cross}] + fsdp_peers()
        greet(peers)
        for a in own:
            a.start()
        for a in loads[:4]:
            a.wait()
        both = jnp.concatenate([gain_q[...], jnp.zeros((6, gain_q.shape[1]), F32)], axis=0).T.astype(BF16)
        for t in range(nseq):

            @pl.when(mine == t)
            def _():
                pack_front(t, (r_q, r_k, r_v, r_o), first_q, out_q, both)

        pl.semaphore_wait(pltpu.get_barrier_semaphore(), len(peers))
        for c in range(2):
            ring.send(c, tok_h.at[pl.ds(c * half, half), :])
        lead.over().start()
        lead.start()
        for a in loads[4:]:
            a.wait()
        for t in range(nseq):

            @pl.when(mine == t)
            def _():
                pack_cols(t, nseq, nfsdp, r_g, gate_q)

        late.over().start()
        late.start()
        for t in range(nseq):

            @pl.when(mine == t)
            def _():
                pack_cols(t, nseq, nfsdp, r_u, up_q)
                pack_down(t, r_d, down_q)

    pl.run_scoped(begin, *[pltpu.VMEM(a.shape, BF16) for a in (w_q, w_k, w_v, w_o, w_g, w_u, w_d)])
    halves = gates + ups + downs
    for a in halves[:2]:
        a.over().start()
    for a in halves:
        a.start()

    def advance(n, d):
        halves[n].forward(d)
        if d == max(pairs - 2, 1) and n + 2 < len(halves):
            pass

    cring.send(0, cot_q.at[pl.ds(0, half), :])

    early_saves = []

    def attend(n1, strip, far, kh, vt, ot, s):
        build_strips(heads, mine * heads, starts, table, ids, strip, far)
        lse[...] = jnp.zeros(lse.shape, F32)
        for d in range(1, pairs):
            lead.forward(d)
            if d == pairs // 2:
                ring.forward(0)
        for d in range(1, pairs):
            late.forward(d)
        for a in halves[2:]:
            a.over().start()
        ring.forward(1)
        lead.finish()
        saves = [pltpu.make_async_copy(first, first_h, local.at[0])]
        saves[0].start()
        column = 3 * piece
        gains[...] = jnp.zeros(gains.shape, F32)
        for b in range(width // 256):
            base = column // 128 * 128
            band = first[b * 256 : (b + 1) * 256, base : base + 128].astype(F32).T
            for n in range(2):
                line = column - base + n
                gains[n : n + 1, b * 256 : (b + 1) * 256] = band[line : line + 1, :]

        def project(t):
            at = rows_at(t, rows)
            x = group[at, :].astype(F32)
            low = (x * inverse_rms(x) * gains[0:1, :]).astype(BF16)
            n1[at, :] = low
            r = nn(low, first[:, :column])
            q[at, :] = r[:, :piece].astype(BF16)
            k[at, :] = r[:, piece : 2 * piece].astype(BF16)
            v[at, :] = r[:, 2 * piece :].astype(BF16)

        own[0].wait()
        project(mine)
        for c in range(2):
            ring.got_near(c)
        project(near)
        project(other)
        for c in range(2):
            ring.got_cross(c)
        project(cross)
        saves.append(pltpu.make_async_copy(n1, n1_h, local.at[1]))
        saves[1].start()
        for d in range(pairs):
            late.complete(d)
        wring.send(0, out_h.at[mine])
        cring.send(1, cot_q.at[pl.ds(half, half), :])
        masked_copies(k, kh, heads)
        vt[...] = v[...].astype(F32).T.astype(BF16)

        def block(h, q0, bias_q0, chunks, c):
            qb = q[pl.ds(q0, CL), :]
            top = None
            for n, (k0, kind, kstart) in enumerate(chunks):
                sc = nt(kh[h, pl.ds(k0, KC), :], qb) + bias_chunk(strip, far, h, bias_q0, kstart, kind, c)
                s[n * KC : (n + 1) * KC, :] = sc
                m = jnp.max(sc, axis=0, keepdims=True)
                top = m if top is None else jnp.maximum(top, m)
            total = jnp.zeros((1, CL), F32)
            acc = jnp.zeros((HEAD_DIM, CL), F32)
            lines = pl.ds(pl.multiple_of(h * HEAD_DIM, HEAD_DIM), HEAD_DIM)
            for n, (k0, kind, kstart) in enumerate(chunks):
                e = jnp.exp(s[n * KC : (n + 1) * KC, :] - top)
                total = total + jnp.sum(e, axis=0, keepdims=True)
                acc = acc + nn(vt[lines, pl.ds(k0, KC)], e.astype(BF16))
            ot[lines, pl.ds(q0, CL)] = acc / total
            lse[pl.ds(h, 1), pl.ds(q0, CL)] = top + jnp.log(total)

        nblk = PROMPT // CL
        steps = [(n, d) for n in range(2) for d in range(1, pairs)]
        early, later, final = steps[: pairs - 1], steps[pairs - 1 : -1], steps[-1:]

        def prompt_body(i, carry):
            h, blk = i // nblk, i % nblk
            q0 = pl.multiple_of(blk * CL, CL)
            block(h, q0, q0, [(j * KC, "strip", j * KC) for j in range(PROMPT // KC)], None)
            for n, step in enumerate(early):

                @pl.when(i == max((heads * nblk - 2) * (n + 1) // len(early) - 2, 0))
                def _():
                    advance(*step)

            return carry

        def cont_body(i, carry):
            h, c = i // 2, i % 2
            q0 = pl.multiple_of(PROMPT + c * CL, CL)
            chunks = [(j * KC, "far", j * KC) for j in range(PROMPT // KC)]
            chunks += [(q0 + j * KC, "strip", j * KC) for j in range(CL // KC)]
            block(h, q0, 0, chunks, c)
            for n, step in enumerate(later):

                @pl.when(i == max(2 * heads * (n + 1) // len(later) - 1, 0))
                def _():
                    advance(*step)

            return carry

        lax.fori_loop(0, heads * nblk, prompt_body, 0)
        cring.forward(0)
        lax.fori_loop(0, heads * 2, cont_body, 0)
        o[...] = ot[...].T.astype(BF16)
        for n, (a, b) in enumerate(((q, q_h), (k, k_h), (v, v_h), (o, o_h))):
            early_saves.append(pltpu.make_async_copy(a, b, osems.at[n]))
            early_saves[n].start()
        ring.drain()
        for n, t in enumerate((other, cross, near)):
            wires.at(obase + n, o.at[rows_at(t, rows), :], obuf.at[mine], {"seq": t}).start()
        obuf[mine] = o[rows_at(mine, rows), :]
        wring.forward(0)
        for step in final:
            advance(*step)
        for a in saves:
            a.wait()

    tall = nseq * rows
    pl.run_scoped(
        attend,
        pltpu.VMEM((tall, width), BF16),
        pltpu.VMEM((heads, 128, STRIP), F32),
        pltpu.VMEM((heads, 2, 128, FARW), F32),
        pltpu.VMEM((heads, tall, piece), BF16),
        pltpu.VMEM((piece, tall), BF16),
        pltpu.VMEM((piece, tall), F32),
        pltpu.VMEM((PROMPT + CL, CL), F32),
    )
    todo = [(n, d) for n in range(2, 6) for d in range(1, pairs)]

    def pass_on(share):
        while todo and len(todo) > round((1 - share) * 4 * (pairs - 1)):
            advance(*todo.pop(0))

    def feed(out_w, cot, ga, ub, hid, dg, du, parts):
        cols = out_w.shape[2]
        wring.got_near(0)
        wring.got_cross(0)
        lines = w_o.shape[0]
        fetch = []
        if lines % 16 == 0:
            fetch = [
                pltpu.make_async_copy(out_h.at[u, f], out_w.at[u, pl.ds(f * lines, lines), :], fsems.at[u * nfsdp + f])
                for u in range(nseq)
                for f in range(nfsdp)
            ]
        else:
            load = pltpu.make_async_copy(out_h, spare, local.at[2])
            load.start()
            load.wait()
            for u in range(nseq):
                joined = jnp.concatenate([spare[u, f].astype(F32) for f in range(nfsdp)], axis=0)
                out_w[u] = joined.astype(BF16)
        saves = []

        def save(src, dst):
            saves.append(pltpu.make_async_copy(src, dst, local.at[18 + len(saves)]))
            saves[-1].start()

        for a in fetch:
            a.start()
        for n, t in enumerate((other, cross, near)):
            wires.at(obase + n, o.at[rows_at(t, rows), :], obuf.at[mine], {"seq": t}).wait()
        for a in fetch:
            a.wait()
        pass_on(1 / 12)
        own[2].wait()
        for c in range(2):
            part = slice(c * half, (c + 1) * half)
            for u in range(nseq):
                acc = tok[part, u * cols : (u + 1) * cols].astype(F32)
                for t in range(nseq):
                    acc = acc + nn(obuf[t, part, :], out_w[u, t * piece : (t + 1) * piece, :])
                resid[part, u * cols : (u + 1) * cols] = acc
            h = resid[part, :]
            group[rows_at(mine, rows, c * half, half), :] = (h * inverse_rms(h) * gains[1:2, :]).astype(BF16)
            if c == 1:
                nring.send(0, group.at[rows_at(mine, rows, 0, half), :])
        nring.send(1, group.at[rows_at(mine, rows, half, half), :])
        save(obuf, obuf_h)
        save(resid, resid_h)
        cring.forward(1)
        for a in gates:
            for d in range(pairs):
                a.complete(d)
        save(gate_w, gate_h)

        def gate_rows(t):
            ga[rows_at(t, rows), :] = nn(group[rows_at(t, rows), :], gate_w[...])

        def act_rows(t):
            up = nn(group[rows_at(t, rows), :], up_w[...])
            active, slope = gelu_both(ga[rows_at(t, rows), :])
            hid[rows_at(t, rows), :] = (active * up).astype(BF16)
            ga[rows_at(t, rows), :] = slope * up
            ub[rows_at(t, rows), :] = active

        pass_on(2 / 12)
        gate_rows(mine)
        nring.got_near(0)
        nring.got_near(1)
        pass_on(3 / 12)
        gate_rows(near)
        pass_on(4 / 12)
        nring.forward(0)
        pass_on(6 / 12)
        nring.forward(1)
        own[1].wait()
        for c in range(2):
            cring.got_near(c)
            cring.got_cross(c)
        cload = pltpu.make_async_copy(cot_h, cot, local.at[3])
        cload.start()
        pass_on(7 / 12)
        gate_rows(other)
        for c in range(2):
            nring.got_cross(c)
        gate_rows(cross)
        save(group, n2_h)
        pass_on(8 / 12)
        for a in ups:
            for d in range(pairs):
                a.complete(d)
        save(up_w, up_h)
        act_rows(mine)
        act_rows(near)
        pass_on(9 / 12)
        act_rows(other)
        act_rows(cross)
        save(hid, hid_h)
        pass_on(10 / 12)
        cload.wait()
        width_f = units // nfsdp
        wide = max(256 // width_f, 1)
        pieces = []

        def down_part(n):
            slot = n % 2
            if n > 1:
                pieces[n - 2].wait()
            got = dot_tn(hid[:, n * wide * width_f : (n + 1) * wide * width_f], cot[...]).astype(BF16)
            for m in range(wide):
                parts[slot, m] = got[m * width_f : (m + 1) * width_f, :]
            pieces.append(pltpu.make_async_copy(parts.at[slot], parts_h.at[pl.ds(n * wide, wide)], local.at[4 + slot]))
            pieces[n].start()

        for n in range(nfsdp // wide):
            down_part(n)
            if n == 1:
                pass_on(11 / 12)

        def back_cols(at):
            for t in range(nseq):
                band = slice(t * rows, (t + 1) * rows)
                dh = nt(cot[band, :], down_w[at, :])
                dg[band, at] = (dh * ga[band, at]).astype(BF16)
                du[band, at] = (dh * ub[band, at]).astype(BF16)
            save(dg.at[:, at], dg_h.at[:, at])
            save(du.at[:, at], du_h.at[:, at])

        if (2 * width_f) % 128 == 0:

            def columns(d):
                for a in downs:
                    a.complete(d)
                if d == pairs - 1:
                    save(down_w, down_h)
                start = downs[0].source(d) * 2 * width_f
                back_cols(pl.ds(pl.multiple_of(start, 2 * width_f), 2 * width_f))

            columns(0)
            pass_on(1)
            for d in range(1, pairs):
                columns(d)
        else:
            pass_on(1)
            for d in range(pairs):
                for a in downs:
                    a.complete(d)
            for n in range(units // 256):
                back_cols(slice(n * 256, (n + 1) * 256))
            save(down_w, down_h)
        nring.drain()
        wring.drain()
        cring.drain()
        lead_late = [late] + gates + ups + downs
        for a in lead_late:
            a.drain()
        for n, (a, b) in enumerate(((q, q_h), (k, k_h), (v, v_h), (o, o_h))):
            pltpu.make_async_copy(a, b, osems.at[n]).wait()
        for a in pieces[-2:] + saves:
            a.wait()

    pl.run_scoped(
        feed,
        pltpu.VMEM((nseq, w_o.shape[0] * nfsdp, width // nseq), BF16),
        pltpu.VMEM((tall, width), BF16),
        pltpu.VMEM((tall, units), F32),
        pltpu.VMEM((tall, units), F32),
        pltpu.VMEM((tall, units), BF16),
        pltpu.VMEM((tall, units), BF16),
        pltpu.VMEM((tall, units), BF16),
        pltpu.VMEM((2, max(256 * nfsdp // units, 1), units // nfsdp, width), BF16),
    )


def forward(starts, table, ids, gain_q, tok, w_q, w_k, w_v, w_o, w_g, w_u, w_d, cot, nseq, nfsdp):
    rows, width = tok.shape
    inner = w_q.shape[1]
    piece = inner // nseq
    heads = piece // HEAD_DIM
    tall = nseq * rows
    size = w_q.shape[0]
    unit = pack_piece(w_g.shape[1], nfsdp, nseq)[1]
    units = nfsdp * unit
    cols = width // nseq
    lead = piece * 10 // 3
    smem = pl.BlockSpec(memory_space=pltpu.SMEM)

    def low(*shape):
        return jax.ShapeDtypeStruct(shape, BF16)

    return pl.pallas_call(
        functools.partial(forward_kernel, heads, nseq),
        out_shape=(
            jax.ShapeDtypeStruct((8, tall), F32),
            jax.ShapeDtypeStruct((8, width), F32),
            low(tall, piece),
            low(tall, piece),
            low(tall, piece),
            low(tall, piece),
            low(nseq, rows, piece),
            jax.ShapeDtypeStruct((rows, width), F32),
            low(tall, width),
            low(width, lead),
            low(nseq, nfsdp, w_o.shape[0], cols),
            low(tall, width),
            low(width, units),
            low(width, units),
            low(units, width),
            low(tall, width),
            low(tall, units),
            low(tall, units),
            low(tall, units),
            low(nfsdp, unit, width),
        ),
        in_specs=[smem, smem, vm_spec(), vm_spec()] + [any_spec()] * 9,
        out_specs=(vm_spec(),) * 2 + (any_spec(),) * 18,
        scratch_shapes=wires_scratch(6 + 8 * nfsdp + 3 + 6 + 6 + 3)
        + [
            pltpu.SemaphoreType.DMA((18 + 7 + 2 * max(nfsdp // 2, units // 256),)),
            pltpu.VMEM((size, lead), BF16),
            pltpu.VMEM((w_o.shape[0], cols), BF16),
            pltpu.VMEM((size, units), BF16),
            pltpu.VMEM((size, units), BF16),
            pltpu.VMEM((unit, width), BF16),
            pltpu.VMEM((tall, width), BF16),
            pltpu.VMEM((width, lead), BF16),
            pltpu.VMEM((width, units), BF16),
            pltpu.VMEM((width, units), BF16),
            pltpu.VMEM((units, width), BF16),
            pltpu.VMEM((rows, width), BF16),
            pltpu.SemaphoreType.DMA((nseq * nfsdp,)),
            pltpu.VMEM((nseq, nfsdp) + w_o.shape[:1] + (cols,) if w_o.shape[0] % 16 else (1, 1, 8, 128), BF16),
            pltpu.VMEM((tall, piece), BF16),
            pltpu.VMEM((tall, piece), BF16),
            pltpu.VMEM((tall, piece), BF16),
            pltpu.VMEM((tall, piece), BF16),
            pltpu.VMEM((nseq, rows, piece), BF16),
            pltpu.VMEM((rows, width), F32),
            pltpu.SemaphoreType.DMA((4,)),
        ],
        compiler_params=call_params(1, 64),
        name="forward",
    )(starts, table, ids, gain_q, tok, w_q, w_k, w_v, w_o, w_g, w_u, w_d, cot)


def back_kernel(
    heads, chunks, starts, table, ids, gains, lse, gain_b, q, k, v, o, do,
    resid_h, rgrad_h, tok_h, y_p, out_p, gate_p, up_p, done_h, lead_h, n1_h, first_h,
    small, y_h, in_h, down_f, lead_f, gate_f, up_f, qkv_f, out_f,
    send, recv, local, ybuf, qkv_p, b0, b1, b2, b3, b4, b5,
    g0, g1, g2, g3, u0, u1, u2, u3, q0_, q1_, q2_, q3_, o0, o1, o2, o3,
    gate_s, up_s, qkv_s, out_s, dqkv, tok, held, stage, one, two, three, tgrad,
):
    rows, width = tok.shape
    nseq = q.shape[0] // rows
    piece = q.shape[1]
    nfsdp = gate_p.shape[0]
    s, near, far_d, cross = seq_places()
    pair, side, pairs = fsdp_places()

    def y_block(t):
        return y_p.at[rows_at(t, rows), :]

    loads = [
        pltpu.make_async_copy(y_block(far_d), ybuf.at[2], local.at[0]),
        pltpu.make_async_copy(y_block(s), ybuf.at[3], local.at[1]),
    ]
    loads.append(pltpu.make_async_copy(tok_h, tok, local.at[5]))
    for a in loads:
        a.start()
    meet([{"seq": near}, {"seq": far_d}, {"seq": cross}] + fsdp_peers())
    wires = Wires(send, recv)
    hop = wires.go(y_block(cross), ybuf.at[0], {"seq": near})
    turn = wires.go(y_block(near), ybuf.at[1], {"seq": near})
    gates = FsdpScatter(wires, gate_p, (g0, g1, g2, g3), gate_s)
    ups = FsdpScatter(wires, up_p, (u0, u1, u2, u3), up_s)
    gates.start()
    ups.start()
    down_ring = SeqGather(wires, lambda t, c: down_f.at[t], 1)
    lead_ring = SeqGather(wires, lambda t, c: lead_f.at[t], 1)
    gate_ring = SeqGather(wires, lambda t, c: gate_f.at[t], 1)
    up_ring = SeqGather(wires, lambda t, c: up_f.at[t], 1)
    qkv_ring = SeqGather(wires, lambda t, c: qkv_f.at[t], 1)
    out_ring = SeqGather(wires, lambda t, c: out_f.at[t], 1)
    qkvs = FsdpScatter(wires, qkv_p, (q0_, q1_, q2_, q3_), qkv_s)
    outs = FsdpScatter(wires, out_p, (o0, o1, o2, o3), out_s)
    far_hop = wires.at(wires.take(1), ybuf.at[2], ybuf.at[4], {"seq": far_d})
    down_keep = pltpu.make_async_copy(done_h, down_f.at[s], local.at[6])
    down_keep.start()
    down_ring.send(0, done_h)
    lead_keep = pltpu.make_async_copy(lead_h, lead_f.at[s], local.at[10])
    lead_keep.start()
    lead_ring.send(0, lead_h)
    length = ids.shape[1]
    half = 2 * PROMPT

    def attend_back(strip, far, kh, vh, kt, delta, dqt, dk, dv, gstrip, gfar):
        build_strips(heads, s * heads, starts, table, ids, strip, far)
        loads[0].wait()
        hop.wait_recv()
        ybuf[2] = (ybuf[2].astype(F32) + ybuf[0].astype(F32)).astype(BF16)
        for src, dst in ((k, kh), (v, vh)):
            masked_copies(src, dst, heads)
        far_hop.start()
        kt[...] = k[...].astype(F32).T.astype(BF16)
        prod = (o[...].astype(F32) * do[...].astype(F32)).T
        for h in range(heads):
            delta[h : h + 1, :] = jnp.sum(prod[h * HEAD_DIM : (h + 1) * HEAD_DIM, :], axis=0, keepdims=True)
        dk[...] = jnp.zeros(dk.shape, F32)
        dv[...] = jnp.zeros(dv.shape, F32)
        gstrip[...] = jnp.zeros(gstrip.shape, F32)
        gfar[...] = jnp.zeros(gfar.shape, F32)
        lane = lax.broadcasted_iota(jnp.int32, (1, piece), 1)

        def block(h, q0, bias_q0, chunk_list, c):
            qb = q[pl.ds(q0, CL), :]
            dob = do[pl.ds(q0, CL), :]
            keep = lane // HEAD_DIM == h
            qhb = jnp.where(keep, qb, jnp.zeros((), BF16))
            dohb = jnp.where(keep, dob, jnp.zeros((), BF16))
            lrow = lse[pl.ds(h, 1), pl.ds(q0, CL)]
            drow = delta[pl.ds(h, 1), pl.ds(q0, CL)]
            acc = jnp.zeros((HEAD_DIM, CL), F32)
            for n, (k0, kind, kstart) in enumerate(chunk_list):
                ks = pl.ds(k0, KC)
                sc = nt(kh[h, ks, :], qb) + bias_chunk(strip, far, h, bias_q0, kstart, kind, c)
                pr = jnp.exp(sc - lrow)
                dp = nt(vh[h, ks, :], dob)
                ds = pr * (dp - drow)
                dsl = ds.astype(BF16)
                dv[ks, :] += nn(pr.astype(BF16), dohb)
                dk[ks, :] += nn(dsl, qhb)
                acc = acc + nn(kt[pl.ds(pl.multiple_of(h * HEAD_DIM, HEAD_DIM), HEAD_DIM), ks], dsl)
                for r in range(KC // 128):
                    m = PROMPT - 128 - (kstart + 128 * r)
                    part = ds[128 * r : 128 * (r + 1), :]
                    if kind == "far":
                        gfar[h, c, :, m : m + CL] += part
                    else:
                        gstrip[h, :, pl.ds(pl.multiple_of(bias_q0 + m, 128), CL)] += part
            dqt[pl.ds(pl.multiple_of(h * HEAD_DIM, HEAD_DIM), HEAD_DIM), pl.ds(q0, CL)] = acc

        nblk = PROMPT // CL

        def prompt_body(i, carry):
            h, blk = i // nblk, i % nblk
            q0 = pl.multiple_of(blk * CL, CL)
            block(h, q0, q0, [(j * KC, "strip", j * KC) for j in range(PROMPT // KC)], None)

            for k in range(1, pairs):

                @pl.when(i == heads * nblk * k // pairs)
                def _():
                    gates.step(k)

            return carry

        lax.fori_loop(0, heads * nblk, prompt_body, 0)

        def cont_body(i, carry):
            h, c = i // 2, i % 2
            q0 = pl.multiple_of(PROMPT + c * CL, CL)
            chunk_list = [(j * KC, "far", j * KC) for j in range(PROMPT // KC)]
            chunk_list += [(q0 + j * KC, "strip", j * KC) for j in range(CL // KC)]
            block(h, q0, 0, chunk_list, c)

            @pl.when(i == heads)
            def _():
                ups.step(1)

            return carry

        lax.fori_loop(0, heads * 2, cont_body, 0)
        dqkv[...] = jnp.concatenate([dqt[...].T, dk[...], dv[...]], axis=1).astype(BF16)
        buckets = table.shape[1]
        lines8 = lax.broadcasted_iota(jnp.int32, (buckets, length), 0)
        hot = ids[:1, :] == lines8
        tgrad[...] = jnp.zeros(tgrad.shape, F32)
        for h in range(heads):

            def unskew(g, span):
                full = jnp.concatenate([jnp.zeros((128, 128), F32), g], axis=1)
                eight = full[:8]
                for a in range(1, 16):
                    eight = eight + pltpu.roll(full[8 * a : 8 * a + 8], span - 8 * a, 1)
                vec = pltpu.roll(eight, span - 1, 1)[:1]
                for b in range(1, 8):
                    vec = vec + pltpu.roll(eight, span - 1 - b, 1)[b : b + 1]
                return jnp.concatenate([vec, jnp.zeros((1, length - span), F32)], axis=1)

            whole = jnp.broadcast_to(unskew(gstrip[h], half), (8, length))
            whole = pltpu.roll(whole, PROMPT // 2, 1)
            for c in range(2):
                moved = jnp.broadcast_to(unskew(gfar[h, c], FARW + 128), (8, length))
                whole = whole + pltpu.roll(moved, PROMPT // 2 + starts[c], 1)
            picked = jnp.where(hot, whole[:1, :], 0.0)
            column = jnp.broadcast_to(jnp.sum(picked, axis=1, keepdims=True), (buckets, 128))
            tgrad[h : h + 1, :buckets] = column.T[:1, :]

    tall = nseq * rows
    pl.run_scoped(
        attend_back,
        pltpu.VMEM((heads, 128, STRIP), F32),
        pltpu.VMEM((heads, 2, 128, FARW), F32),
        pltpu.VMEM((heads, tall, piece), BF16),
        pltpu.VMEM((heads, tall, piece), BF16),
        pltpu.VMEM((piece, tall), BF16),
        pltpu.VMEM((8, tall), F32),
        pltpu.VMEM((piece, tall), F32),
        pltpu.VMEM((tall, piece), F32),
        pltpu.VMEM((tall, piece), F32),
        pltpu.VMEM((heads, 128, STRIP), F32),
        pltpu.VMEM((heads, 2, 128, FARW), F32),
    )

    def rest(n1, hold, rgrad, resid, first):
        later = [
            pltpu.make_async_copy(n1_h, n1, local.at[7]),
            pltpu.make_async_copy(rgrad_h, rgrad, local.at[8]),
            pltpu.make_async_copy(resid_h, resid, local.at[9]),
        ]
        ready = pltpu.make_async_copy(first_h, first, local.at[4])
        ready.start()
        for a in later:
            a.start()
        sums = SeqScatter(wires, chunks, b0, b1, b2, b3, b4, b5)
        size = rows // chunks
        ready.wait()

        def part(t, c):
            return nt(dqkv[rows_at(t, rows, c * size, size), :], first[:, : 3 * piece])

        for c in range(chunks):
            sums.cross_chunk(c, part(cross, c))
        for c in range(chunks):
            sums.far_chunk(c, part(far_d, c))
        for k in range(2, pairs - 1):
            ups.step(k)
        later[0].wait()
        depth = width // nfsdp
        wide = 384
        for n in range(width // wide):
            got = dot_tn(n1[:, n * wide : (n + 1) * wide], dqkv[...])
            for m in range(wide // depth):
                qkv_p[n * (wide // depth) + m] = got[m * depth : (m + 1) * depth, :].astype(BF16)
        for c in range(chunks):
            sums.near_chunk(c, part(near, c))
        for c in range(chunks):
            hold[c * size : (c + 1) * size, :] = part(s, c)
        qkvs.start()
        if pairs > 2:
            ups.step(pairs - 1)
        gates.finish()
        outs.start()
        gate_keep = pltpu.make_async_copy(gate_s, gate_f.at[s], local.at[11])
        gate_keep.start()
        gate_ring.send(0, gate_s)
        down_ring.forward(0)
        lead_ring.forward(0)
        later[2].wait()
        loads[1].wait()
        turn.wait_recv()
        far_hop.wait_recv()
        total = ybuf[3].astype(F32) + ybuf[1].astype(F32) + ybuf[4].astype(F32)
        ybuf[3] = (resid[...] + total).astype(BF16)
        qkvs.step(1)
        loads[2].wait()
        later[1].wait()
        gsum = jnp.zeros((1, width), F32)
        y_keep = pltpu.make_async_copy(ybuf.at[3], y_h, local.at[12])
        y_keep.start()
        for c in range(chunks):
            at = slice(c * size, (c + 1) * size)
            dn = sums.own_chunk(c, hold[at, :])
            x = tok[at, :].astype(F32)
            r = inverse_rms(x)
            gsum = gsum + jnp.sum(dn * x * r, axis=0, keepdims=True)
            tok[at, :] = (rgrad[at, :] + norm_back(dn, x, r, gains[0:1, :])).astype(BF16)
            if c == 0:
                for k in range(2, pairs - 1):
                    qkvs.step(k)
                ups.finish()
                up_keep = pltpu.make_async_copy(up_s, up_f.at[s], local.at[14])
                up_keep.start()
                up_ring.send(0, up_s)
                if pairs > 2:
                    qkvs.step(pairs - 1)
        in_keep = pltpu.make_async_copy(tok, in_h, local.at[13])
        in_keep.start()
        held[...] = jnp.zeros(held.shape, F32)
        lanes = held.shape[1]
        lines = width // lanes
        for n in range(lines):
            held[n : n + 1, :] = gsum[:, n * lanes : (n + 1) * lanes]
            held[lines + n : lines + n + 1, :] = gain_b[:1, n * lanes : (n + 1) * lanes]
        held[pl.ds(2 * lines + s * 8, 8), :] = tgrad[...]
        outs.step(1)
        trips = [wires.go(held, one.at[n], {"seq": t}) for n, t in enumerate((near, far_d, cross))]
        gate_ring.forward(0)
        for k in range(2, pairs):
            outs.step(k)
        for a in trips:
            a.wait_recv()
        stage[0] = held[...] + one[0] + one[1] + one[2]
        up_ring.forward(0)
        trips.append(wires.go(stage.at[0], two, {"fsdp": pair * 2 + 1 - side}))
        trips[-1].wait_recv()
        stage[1] = stage[0] + two[...]
        zs = [
            wires.go(stage.at[1], three.at[d - 1], {"fsdp": lax.rem(pair + d, pairs) * 2 + side})
            for d in range(1, pairs)
        ]
        qkvs.finish()
        qkv_keep = pltpu.make_async_copy(qkv_s, qkv_f.at[s], local.at[15])
        qkv_keep.start()
        qkv_ring.send(0, qkv_s)
        outs.finish()
        out_keep = pltpu.make_async_copy(out_s, out_f.at[s], local.at[16])
        out_keep.start()
        out_ring.send(0, out_s)
        total = stage[1]
        for d, a in enumerate(zs):
            a.wait_recv()
            total = total + three[d]
        small[...] = total
        qkv_ring.forward(0)
        out_ring.forward(0)
        for a in (down_ring, lead_ring, gate_ring, up_ring, qkv_ring, out_ring):
            a.finish()
        sums.finish()
        for a in (gates, ups, qkvs, outs):
            a.drain()
        for a in (gate_keep, up_keep, qkv_keep, out_keep, y_keep, in_keep, down_keep, lead_keep):
            a.wait()
        for a in trips + zs + [hop, turn, far_hop]:
            a.wait_send()

    pl.run_scoped(
        rest,
        pltpu.VMEM((tall, width), BF16),
        pltpu.VMEM((rows, width), F32),
        pltpu.VMEM((rows, width), F32),
        pltpu.VMEM((rows, width), F32),
        pltpu.VMEM(first_h.shape, BF16),
    )


def back(starts, table, ids, gains, lse, gain_b, q, k, v, o, do, resid, rgrad, tok, y_p, out_p, gate_p, up_p, done, lead, n1, first, chunks=2):
    tall, piece = q.shape
    heads = piece // HEAD_DIM
    rows, width = tok.shape
    nseq = tall // rows
    nfsdp = gate_p.shape[0]
    pairs = nfsdp // 2
    lines = -(-(2 * width // 128 + 8 * nseq) // 8) * 8
    qkv_shape = (nfsdp, width // nfsdp, 3 * piece)
    out_shape = out_p.shape
    smem = pl.BlockSpec(memory_space=pltpu.SMEM)

    def full(a):
        return jax.ShapeDtypeStruct((nseq,) + tuple(a), BF16)

    return pl.pallas_call(
        functools.partial(back_kernel, heads, chunks),
        out_shape=(
            jax.ShapeDtypeStruct((lines, 128), F32),
            jax.ShapeDtypeStruct((rows, width), BF16),
            jax.ShapeDtypeStruct((rows, width), BF16),
            full(done.shape),
            full(lead.shape),
            full(gate_p.shape[1:]),
            full(up_p.shape[1:]),
            full(qkv_shape[1:]),
            full(out_shape[1:]),
        ),
        in_specs=[smem, smem] + [vm_spec()] * 9 + [any_spec()] * 11,
        out_specs=(vm_spec(),) + (any_spec(),) * 8,
        scratch_shapes=wires_scratch(6 + 4 * nfsdp + 18 + 3 * chunks + 4 + pairs)
        + [
            pltpu.SemaphoreType.DMA((17,)),
            pltpu.VMEM((5, rows, width), BF16),
            pltpu.VMEM(qkv_shape, BF16),
        ]
        + scatter_scratch(chunks, rows // chunks, width)
        + fsdp_scatter_scratch(gate_p.shape)
        + fsdp_scatter_scratch(up_p.shape)
        + fsdp_scatter_scratch(qkv_shape)
        + fsdp_scatter_scratch(out_shape)
        + [
            pltpu.VMEM(gate_p.shape[1:], BF16),
            pltpu.VMEM(up_p.shape[1:], BF16),
            pltpu.VMEM(qkv_shape[1:], BF16),
            pltpu.VMEM(out_shape[1:], BF16),
            pltpu.VMEM((tall, 3 * piece), BF16),
            pltpu.VMEM((rows, width), BF16),
            pltpu.VMEM((lines, 128), F32),
            pltpu.VMEM((2, lines, 128), F32),
            pltpu.VMEM((3, lines, 128), F32),
            pltpu.VMEM((lines, 128), F32),
            pltpu.VMEM((pairs - 1, lines, 128), F32),
            pltpu.VMEM((8, 128), F32),
        ],
        compiler_params=call_params(5, 64),
        name="back",
    )(starts, table, ids, gains, lse, gain_b, q, k, v, o, do, resid, rgrad, tok, y_p, out_p, gate_p, up_p, done, lead, n1, first)


def unpack_kernel(nseq, nfsdp, heads, *refs):
    srcs, small, outs = refs[:8], refs[8], refs[9:18]
    ga, gb, table, ins, offs = refs[18:23]
    vs, ts = refs[23:31], refs[31:]
    loads = [pltpu.make_async_copy(a, b, ins.at[n]) for n, (a, b) in enumerate(zip(srcs, vs))]
    for a in loads:
        a.start()
    lead_f, gate_f, up_f, down_f, qkv_f, out_f, y, dx = vs
    tq, tk, tv, to, tg, tu, td = ts
    gq, gk, gv, go, gg, gu, gd, gy, gx = outs
    copies = []

    def save(src, dst):
        copies.append(pltpu.make_async_copy(src, dst, offs.at[len(copies)]))
        copies[-1].start()

    block, piece = pack_piece(tg.shape[1], nfsdp, nseq)
    half = nfsdp // 2

    def columns(get):
        parts = []
        for f in range(nfsdp):
            for t in range(nseq):
                size = min(piece, block - t * piece)
                full, f_at = get(f)
                parts.append(full[t, :, f_at * piece : f_at * piece + size].astype(F32))
        return jnp.concatenate(parts, axis=1)

    loads[0].wait()
    loads[1].wait()
    tg[...] = columns(lambda f: (lead_f, f) if f < half else (gate_f, f - half))
    save(tg, gg)
    loads[2].wait()
    tu[...] = columns(lambda f: (up_f, f))
    save(tu, gu)
    loads[3].wait()
    size = down_f.shape[1]
    for t in range(nseq):
        n = min(size, td.shape[0] - t * size)
        td[t * size : t * size + n, :] = down_f[t, :n, :].astype(F32)
    save(td, gd)
    loads[4].wait()
    width = qkv_f.shape[2] // 3
    for n, (dst, out) in enumerate(((tq, gq), (tk, gk), (tv, gv))):
        dst[...] = jnp.concatenate([qkv_f[t, :, n * width : (n + 1) * width] for t in range(nseq)], axis=1).astype(F32)
        save(dst, out)
    loads[5].wait()
    to[...] = jnp.concatenate([out_f[t] for t in range(nseq)], axis=1).astype(F32)
    save(to, go)
    for n, (src, dst) in enumerate(((y, gy), (dx, gx))):
        loads[6 + n].wait()
        save(src, dst)
    where = lax.axis_index("fsdp")
    share = ga.shape[1]
    lines = nfsdp * share // 128
    for n, dst in enumerate((ga, gb)):
        line = jnp.concatenate([small[n * lines + a : n * lines + a + 1, :] for a in range(lines)], axis=1)
        for f in range(nfsdp):

            @pl.when(where == f)
            def _():
                dst[...] = line[:, f * share : (f + 1) * share]

    for t in range(nseq):
        at = 2 * lines + 8 * t
        table[t * heads : (t + 1) * heads, :] = small[at : at + heads, : table.shape[1]]
    for a in copies:
        a.wait()


def unpack(srcs, small, like, blocks_like, table, nfsdp):
    nseq = srcs[0].shape[0]
    share = like[0].shape[0]
    vm = [vm_spec()] * 3
    return pl.pallas_call(
        functools.partial(unpack_kernel, nseq, nfsdp, table.shape[0] // nseq),
        out_shape=tuple(jax.ShapeDtypeStruct(a.shape, F32) for a in like)
        + tuple(jax.ShapeDtypeStruct(a.shape, BF16) for a in blocks_like)
        + (
            jax.ShapeDtypeStruct((1, share), F32),
            jax.ShapeDtypeStruct((1, share), F32),
            jax.ShapeDtypeStruct(table.shape, F32),
        ),
        in_specs=[any_spec()] * 8 + [vm_spec()],
        out_specs=tuple([any_spec()] * 9 + vm),
        scratch_shapes=[pltpu.SemaphoreType.DMA((8,)), pltpu.SemaphoreType.DMA((9,))]
        + [pltpu.VMEM(a.shape, BF16) for a in srcs]
        + [pltpu.VMEM(a.shape, F32) for a in like],
        compiler_params=pltpu.CompilerParams(vmem_limit_bytes=67043328),
        name="unpack",
    )(*srcs, small)


def reversed_ids(bucket_ids):
    span = bucket_ids.shape[0]
    ids = jnp.concatenate([bucket_ids[::-1], jnp.full((1,), -1, jnp.int32)])
    return ids[None, :]


def dot32(a, b):
    return jnp.dot(a, b, preferred_element_type=F32)


def dot_tn(a, b):
    return lax.dot_general(a, b, (((0,), (0,)), ((), ())), preferred_element_type=F32)


def gelu_both(u):
    inner = 0.7978845608028654 * (u + 0.044715 * u * u * u)
    t = jnp.tanh(inner)
    value = 0.5 * u * (1.0 + t)
    slope = 0.5 * (1.0 + t) + 0.5 * u * (1.0 - t * t) * 0.7978845608028654 * (1.0 + 3 * 0.044715 * u * u)
    return value, slope


def body(
    tokens,
    out_grad,
    attn_gain,
    w_query,
    w_key,
    w_value,
    w_out,
    mix_gain,
    w_gate,
    w_up,
    w_down,
    rel_table,
    bucket_ids,
    cont_start,
):
    nseq = lax.axis_size("seq")
    nfsdp = lax.axis_size("fsdp")
    inner = w_query.shape[1]

    ids = reversed_ids(bucket_ids)
    starts = cont_start[0]
    (
        lse,
        gains,
        query,
        keys,
        values,
        mixed,
        mixed_rows,
        resid,
        normed,
        first,
        out_w,
        _,
        gate_w,
        up_w,
        down_w,
        normed_two,
        hidden,
        gate_grad,
        up_grad,
        down_grad,
    ) = forward(
        starts,
        rel_table.T,
        ids,
        jnp.stack([attn_gain.astype(F32), mix_gain.astype(F32)]),
        tokens[0],
        w_query,
        w_key,
        w_value,
        w_out,
        w_gate,
        w_up,
        w_down,
        out_grad[0],
        nseq,
        nfsdp,
    )
    out_w = out_w.reshape(nseq, inner, -1)
    resid_grad, mixed_grad, gain_two_grad, down_grad, lead_grad, out_w_grad, gate_w_grad, up_w_grad, result = unmix(
        gains, mixed_rows, resid, out_grad[0], down_grad, gate_grad, up_grad, gate_w, up_w, out_w, normed_two, hidden, down_w
    )
    small, block_out, in_grad, down_grad, lead_grad, gate_w_grad, up_w_grad, qkv_grad, out_w_grad = back(
        starts,
        rel_table.T,
        ids,
        gains,
        lse,
        gain_two_grad,
        query,
        keys,
        values,
        mixed,
        mixed_grad,
        resid,
        resid_grad,
        tokens[0],
        result,
        out_w_grad,
        gate_w_grad,
        up_w_grad,
        down_grad,
        lead_grad,
        normed,
        first,
    )
    *shards, block_out, in_grad, gain_one_share, gain_two_share, table_grad = unpack(
        (lead_grad, gate_w_grad, up_w_grad, down_grad, qkv_grad, out_w_grad, block_out, in_grad),
        small,
        (w_query, w_key, w_value, w_out, w_gate, w_up, w_down),
        (block_out, in_grad),
        rel_table.T,
        nfsdp,
    )
    return (
        block_out[None],
        in_grad[None],
        gain_one_share[0],
        *shards[:4],
        gain_two_share[0],
        *shards[4:],
        table_grad.T,
    )


def solution(mesh):
    placed = (
        P("fsdp", "seq", None),
        P("fsdp", "seq", None),
        P("fsdp"),
        P("fsdp", None),
        P("fsdp", None),
        P("fsdp", None),
        P("fsdp", None),
        P("fsdp"),
        P("fsdp", None),
        P("fsdp", None),
        P("fsdp", None),
        P(),
        P(),
        P("fsdp", None),
    )
    results = placed[:1] * 2 + placed[2:11] + (P(),)
    return jax.shard_map(body, mesh=mesh, in_specs=placed, out_specs=results, check_vma=False)
```

```python
import functools
import jax
import jax.numpy as jnp
from jax import lax
from jax.experimental import pallas as pl
from jax.experimental.pallas import tpu as pltpu
from jax.sharding import PartitionSpec as P

HEAD_DIM = 64
PROMPT = 1024
CL = 256
F32 = jnp.float32
BF16 = jnp.bfloat16
MESH = pl.DeviceIdType.MESH
epsilon = 1e-06
STRIP = 2 * PROMPT - 128
FARW = PROMPT - 128 + CL
KC = 256


def nt(a, b):
    return lax.dot_general(a, b, (((1,), (1,)), ((), ())), preferred_element_type=F32)


def nn(a, b):
    return lax.dot_general(a, b, (((1,), (0,)), ((), ())), preferred_element_type=F32)


class Wires:
    def __init__(self, send, recv):
        self.send, self.recv, self.used = send, recv, 0

    def take(self, count):
        self.used += count
        return self.used - count

    def at(self, i, src, dst, where):
        return pltpu.make_async_remote_copy(
            src_ref=src,
            dst_ref=dst,
            send_sem=self.send.at[i],
            recv_sem=self.recv.at[i],
            device_id=where,
            device_id_type=MESH,
        )

    def go(self, src, dst, where):
        c = self.at(self.take(1), src, dst, where)
        c.start()
        return c


def seq_places():
    s = lax.axis_index("seq")
    near = s + 1 - 2 * lax.rem(s, 2)
    far = lax.rem(s + 2, 4)
    cross = lax.rem(near + 2, 4)
    return s, near, far, cross


def greet(places):
    barrier = pltpu.get_barrier_semaphore()
    for where in places:
        pl.semaphore_signal(barrier, inc=1, device_id=where, device_id_type=MESH)


def meet(places):
    greet(places)
    pl.semaphore_wait(pltpu.get_barrier_semaphore(), len(places))


def rows_at(index, rows, offset=0, count=None):
    return pl.ds(pl.multiple_of(index * rows + offset, 16), rows if count is None else count)


class SeqGather:
    def __init__(self, wires, out_at, chunks):
        self.wires, self.out_at, self.chunks = wires, out_at, chunks
        self.s, self.near, self.far, self.cross = seq_places()
        self.base = wires.take(3 * chunks)

    def trip(self, kind, c, src=None):
        view = self.out_at(self.far if kind == 2 else self.s, c)
        where = {"seq": self.far if kind == 0 else self.near}
        return self.wires.at(self.base + 3 * c + kind, view if src is None else src, view, where)

    def send(self, c, src):
        self.trip(0, c, src).start()
        self.trip(1, c, src).start()

    def forward(self, c):
        self.trip(0, c).wait_recv()
        self.trip(2, c).start()

    def got_near(self, c):
        self.trip(1, c).wait_recv()

    def got_cross(self, c):
        self.trip(2, c).wait_recv()

    def drain(self):
        for c in range(self.chunks):
            for kind in range(3):
                self.trip(kind, c).wait_send()

    def finish(self):
        for c in range(self.chunks):
            self.got_near(c)
            self.got_cross(c)
        self.drain()


def fsdp_places():
    f = lax.axis_index("fsdp")
    return f // 2, lax.rem(f, 2), lax.axis_size("fsdp") // 2


def far_first(k):
    pair, _, pairs = fsdp_places()
    if pairs != 4:
        return k + 1
    first, second = 3 - (pair + 1) // 2, 1 + lax.rem(pair + 1, 3)
    return (first, second, 6 - first - second)[k]


def fsdp_peers():
    pair, side, pairs = fsdp_places()
    peers = [{"fsdp": lax.rem(pair + d, pairs) * 2 + side} for d in range(1, pairs)]
    return peers + [{"fsdp": pair * 2 + 1 - side}]


class FsdpGather:
    def __init__(self, wires, shard, full_at, local):
        self.wires, self.shard, self.full_at, self.local = wires, shard, full_at, local
        self.pair, self.side, self.pairs = fsdp_places()
        self.base = wires.take(2 * self.pairs)

    def source(self, d):
        return lax.rem(self.pair + self.pairs - d, self.pairs)

    def over(self):
        own = self.full_at(self.pair * 2 + self.side)
        return self.wires.at(self.base, self.shard, own, {"fsdp": self.pair * 2 + 1 - self.side})

    def out(self, d):
        own = self.full_at(self.pair * 2 + self.side)
        where = {"fsdp": lax.rem(self.pair + d, self.pairs) * 2 + self.side}
        return self.wires.at(self.base + d, self.shard, own, where)

    def onward(self, d):
        view = self.full_at(self.source(d) * 2 + self.side)
        return self.wires.at(self.base + self.pairs + d, view, view, {"fsdp": self.pair * 2 + 1 - self.side})

    def keep(self):
        return pltpu.make_async_copy(self.shard, self.full_at(self.pair * 2 + self.side), self.local)

    def start(self):
        for k in range(self.pairs - 1):
            self.out(k + 1).start()
        self.keep().start()

    def forward(self, k):
        self.out(k).wait_recv()
        self.onward(k).start()

    def complete(self, k):
        if k == 0:
            self.keep().wait()
            self.over().wait_recv()
        else:
            self.onward(k).wait_recv()

    def drain(self):
        self.over().wait_send()
        for d in range(1, self.pairs):
            self.out(d).wait_send()
            self.onward(d).wait_send()

    def finish(self):
        for k in range(self.pairs):
            self.complete(k)
        self.drain()


def gather_halves(wires, shard, full, size, local):
    half, wide = size // 2, shard.shape[1] // 2

    def one(n):
        if size % 32 == 0:
            rows = pl.ds(n * half, half)
            return FsdpGather(wires, shard.at[rows, :], lambda f: full.at[shard_rows(2 * f + n, half), :], local[n])
        cut = slice(n * wide, (n + 1) * wide)
        return FsdpGather(wires, shard.at[:, cut], lambda f: full.at[shard_rows(f, size), cut], local[n])

    return [one(0), one(1)]


class FsdpScatter:
    def __init__(self, wires, parts, bufs, result):
        self.wires, self.parts_at, self.result = wires, parts if callable(parts) else lambda f: parts.at[f], result
        self.mine, self.got, self.landed, self.local = bufs
        self.pair, self.side, self.pairs = fsdp_places()
        self.base = wires.take(2 * self.pairs)

    def step_to(self, k):
        return far_first(k) if k < self.pairs - 1 else 0

    def owner(self, d):
        return lax.rem(self.pair + d, self.pairs) * 2

    def load(self, k):
        part = self.parts_at(self.owner(self.step_to(k)) + self.side)
        return pltpu.make_async_copy(part, self.mine.at[k % 2], self.local.at[k % 2])

    def swap(self, d):
        src = self.parts_at(self.owner(d) + 1 - self.side)
        return self.wires.at(self.base + d, src, self.got.at[d], {"fsdp": self.pair * 2 + 1 - self.side})

    def onward(self, d):
        where = {"fsdp": self.owner(d) + self.side}
        return self.wires.at(self.base + self.pairs + d, self.got.at[d], self.landed.at[d - 1], where)

    def start(self):
        for k in range(self.pairs):
            self.swap(self.step_to(k)).start()
        self.load(0).start()

    def step(self, k):
        d = self.step_to(k - 1)
        self.load(k).start()
        self.load(k - 1).wait()
        self.swap(d).wait_recv()
        self.got[d] = (self.mine[(k - 1) % 2].astype(F32) + self.got[d].astype(F32)).astype(BF16)
        self.onward(d).start()

    def finish(self):
        self.load(self.pairs - 1).wait()
        self.swap(0).wait_recv()
        total = self.mine[(self.pairs - 1) % 2].astype(F32) + self.got[0].astype(F32)
        for d in range(1, self.pairs):
            self.onward(d).wait_recv()
            total = total + self.landed[d - 1].astype(F32)
        self.result[...] = total.astype(BF16)

    def drain(self):
        for d in range(self.pairs):
            self.swap(d).wait_send()
        for d in range(1, self.pairs):
            self.onward(d).wait_send()


def fsdp_scatter_scratch(shape):
    pairs = shape[0] // 2
    return [
        pltpu.VMEM((2,) + shape[1:], BF16),
        pltpu.VMEM((pairs,) + shape[1:], BF16),
        pltpu.VMEM((pairs - 1,) + shape[1:], BF16),
        pltpu.SemaphoreType.DMA((2,)),
    ]


def blocks(a, count):
    return a.reshape((count, a.shape[0] // count) + a.shape[1:])


def shard_rows(f, size):
    return pl.ds(pl.multiple_of(f * size, 16 if size % 16 == 0 else 8 if size % 8 == 0 else size), size)


def vm_spec():
    return pl.BlockSpec(memory_space=pltpu.VMEM)


def any_spec():
    return pl.BlockSpec(memory_space=pl.ANY)


def wires_scratch(n):
    return [pltpu.SemaphoreType.DMA((n,)), pltpu.SemaphoreType.DMA((n,))]


def call_params(number, vmem=60):
    return pltpu.CompilerParams(collective_id=number, has_side_effects=True, vmem_limit_bytes=min(vmem << 20, 67043328))


def inverse_rms(v):
    return lax.rsqrt(jnp.mean(v * v, axis=-1, keepdims=True) + epsilon)


def norm_back(grad, v, r, gain):
    scaled = grad * gain
    return r * scaled - v * (r * r * r) * jnp.mean(v * scaled, axis=-1, keepdims=True)


class SeqScatter:
    def __init__(self, wires, chunks, *bufs):
        self.s, self.near, self.far, self.cross = seq_places()
        self.wires, self.chunks, self.bufs = wires, chunks, bufs
        self.base = wires.take(3 * chunks)

    def trip(self, kind, c):
        where = {"seq": self.far if kind == 1 else self.near}
        src, dst = self.bufs[2 * kind].at[c], self.bufs[2 * kind + 1].at[c]
        return self.wires.at(self.base + 3 * c + kind, src, dst, where)

    def cross_chunk(self, c, value):
        self.bufs[0][c] = value.astype(BF16)
        self.trip(0, c).start()

    def far_chunk(self, c, value):
        self.trip(0, c).wait_recv()
        self.bufs[2][c] = (value + self.bufs[1][c].astype(F32)).astype(BF16)
        self.trip(1, c).start()

    def near_chunk(self, c, value):
        self.bufs[4][c] = value.astype(BF16)
        self.trip(2, c).start()

    def own_chunk(self, c, value):
        self.trip(2, c).wait_recv()
        self.trip(1, c).wait_recv()
        return value + self.bufs[5][c].astype(F32) + self.bufs[3][c].astype(F32)

    def finish(self):
        for c in range(self.chunks):
            for kind in range(3):
                self.trip(kind, c).wait_send()


def scatter_scratch(chunks, rows, width):
    return [pltpu.VMEM((chunks, rows, width), BF16)] * 6


def unmix_kernel(
    chunks, gains, obuf, resid, cot, down_p, dg_h, du_h, gate_h, up_h, out_h, n2_h, hid_h, dw_h,
    rgrad_h, dmix_h, ggrad, shard, lead_s, out_p, gate_p, up_p, y_h,
    send, recv, b0, b1, b2, b3, b4, b5, attn, dob, p0, p1, p2, p3, r0, r1, r2, r3, l0, l1, l2, l3, lead_p,
    local, dg, du, gate_w, up_w, out_w, n2, hid, down_w, wgrad, wbuf, stage, ystage, sems, rgrad, dmix,
):
    rows, width = resid.shape
    nseq, _, piece = obuf.shape
    nfsdp = gate_p.shape[0]
    units = dg.shape[1]
    first_half = units // 2
    s, near, far, cross = seq_places()
    loads = [
        pltpu.make_async_copy(src, dst, local.at[n])
        for n, (src, dst) in enumerate(
            (
                (gate_h, gate_w),
                (up_h, up_w),
                (dg_h, dg),
                (du_h, du),
                (n2_h, n2),
                (out_h, out_w),
                (hid_h, hid),
                (dw_h, down_w),
            )
        )
    ]
    for a in loads:
        a.start()
    meet([{"seq": near}, {"seq": far}, {"seq": cross}] + fsdp_peers())
    wires = Wires(send, recv)
    def down_half(n, bufs):
        return FsdpScatter(wires, lambda f: down_p.at[2 * f + n], bufs, shard.at[n])

    grads = [down_half(0, (p0, p1, p2, p3)), down_half(1, (r0, r1, r2, r3))]
    for a in grads:
        a.start()
    leads = FsdpScatter(wires, lead_p, (l0, l1, l2, l3), lead_s)
    pairs = leads.pairs
    sums = SeqScatter(wires, chunks, b0, b1, b2, b3, b4, b5)
    size = rows // chunks
    for a in loads[:4]:
        a.wait()

    def part(t, c):
        at = rows_at(t, rows, c * size, size)
        return nt(dg[at, :], gate_w[...]) + nt(du[at, :], up_w[...])

    for c in range(chunks):
        sums.cross_chunk(c, part(cross, c))
    grads[0].step(1)
    for c in range(chunks):
        sums.far_chunk(c, part(far, c))
    for d in range(2, pairs - 1):
        grads[0].step(d)
    for c in range(chunks):
        sums.near_chunk(c, part(near, c))
    if pairs > 2:
        grads[0].step(pairs - 1)
    for c in range(chunks):
        rgrad[c * size : (c + 1) * size, :] = part(s, c)
    loads[4].wait()
    depth = width // nfsdp
    wide = 384
    saves = []

    def weight_parts(side, out, begin, end, cut):
        for n in range(begin, end):
            slot = n % 2
            group = pl.ds(n * (wide // depth), wide // depth)
            if len(saves) > 1:
                saves[-2].wait()
            got = dot_tn(n2[:, n * wide : (n + 1) * wide], side[...])
            for m in range(wide // depth):
                low = got[m * depth : (m + 1) * depth, :].astype(BF16)
                if cut:
                    lead_p[n * (wide // depth) + m] = low[:, :cut]
                stage[slot, m, :, : units - cut] = low[:, cut:]
            a = pltpu.make_async_copy(stage.at[slot, :, :, : units - cut], out.at[group], sems.at[3 + slot])
            a.start()
            saves.append(a)

    weight_parts(dg, gate_p, 0, width // wide, first_half)
    grads[1].step(1)
    loads[5].wait()
    cols = out_w.shape[2]

    def own_rows(c, total):
        at = slice(c * size, (c + 1) * size)
        dn = sums.own_chunk(c, rgrad[at, :])
        h = resid[at, :]
        r = inverse_rms(h)
        rg = cot[at, :].astype(F32) + norm_back(dn, h, r, gains[1:2, :])
        rgrad[at, :] = rg
        low = rg.astype(BF16)
        attn[at, :] = low
        for t in range(nseq):
            acc = jnp.zeros((size, piece), F32)
            for u in range(nseq):
                acc = acc + nt(low[:, u * cols : (u + 1) * cols], out_w[u, t * piece : (t + 1) * piece, :])
            dob[t, at, :] = acc.astype(BF16)
        return total + jnp.sum(dn * h * r, axis=0, keepdims=True)

    base = wires.take(3 * chunks)

    def trip(n, t, c):
        at = pl.ds(c * size, size)
        return wires.at(base + 3 * c + n, dob.at[t, at, :], dmix.at[rows_at(s, rows, c * size, size), :], {"seq": t})

    total = jnp.zeros((1, width), F32)
    for c in range(chunks):
        total = own_rows(c, total)
        if c == 0:
            leads.start()
            weight_parts(du, up_p, 0, 1, 0)
            for d in range(2, pairs - 1):
                grads[1].step(d)
        for n, t in enumerate((far, cross, near)):
            trip(n, t, c).start()
        dmix[rows_at(s, rows, c * size, size), :] = dob[s, pl.ds(c * size, size), :]
        if c == 0:
            weight_parts(du, up_p, 1, width // wide, 0)
            if pairs > 2:
                grads[1].step(pairs - 1)
    ggrad[...] = jnp.broadcast_to(total, ggrad.shape)
    rsave = pltpu.make_async_copy(rgrad, rgrad_h, sems.at[2])
    rsave.start()
    leads.step(1)
    wbase = wires.take(3)

    def wtrip(n):
        u = (cross, far, near)[n]
        return wires.at(wbase + n, wgrad.at[u], wbuf.at[n], {"seq": far if n == 1 else near})

    def wblock(u):
        for t in range(nseq):
            at = pl.ds(pl.multiple_of(u * cols, 128), cols)
            wgrad[u, t * piece : (t + 1) * piece, :] = dot_tn(obuf[t], attn[:, at]).astype(BF16)

    wblock(cross)
    wblock(far)
    wtrip(0).start()
    for d in range(2, pairs - 1):
        leads.step(d)
    wblock(near)
    wtrip(0).wait_recv()
    wgrad[far] = (wgrad[far].astype(F32) + wbuf[0].astype(F32)).astype(BF16)
    wblock(s)
    wtrip(1).start()
    wtrip(2).start()
    for a in loads[6:]:
        a.wait()
    ycopies = []
    for t in range(nseq):
        slot = t % 2
        if t > 1:
            ycopies[t - 2].wait()
        at = slice(t * rows, (t + 1) * rows)
        ystage[slot] = nn(hid[at, :], down_w[...]).astype(BF16)
        ycopies.append(pltpu.make_async_copy(ystage.at[slot], y_h.at[at, :], sems.at[slot]))
        ycopies[t].start()
        if t == 1:
            leads.step(pairs - 1)
    for c in range(chunks):
        for n, t in enumerate((far, cross, near)):
            trip(n, t, c).wait()
    dsave = pltpu.make_async_copy(dmix, dmix_h, local.at[8])
    dsave.start()
    for a in grads:
        a.finish()
    for n in range(1, 3):
        wtrip(n).wait_recv()
    wsum = wgrad[s].astype(F32) + wbuf[1].astype(F32) + wbuf[2].astype(F32)
    lines = out_p.shape[1]
    for f in range(nfsdp):
        out_p[f] = wsum[f * lines : (f + 1) * lines, :].astype(BF16)
    for n in range(3):
        wtrip(n).wait_send()
    sums.finish()
    for a in grads:
        a.drain()
    leads.finish()
    leads.drain()
    for a in saves[-2:]:
        a.wait()
    for a in ycopies[-2:] + [rsave, dsave]:
        a.wait()


def unmix(gains, obuf, resid, cot, down_p, dg, du, gate_w, up_w, out_w, n2, hid, down_w, chunks=2):
    rows, width = resid.shape
    nseq, _, piece = obuf.shape
    nfsdp = down_p.shape[0] // 2
    units = dg.shape[1]
    grad_shape = (nfsdp, width // nfsdp, units)
    half_shape = (nfsdp, width // nfsdp, units // 2)
    return pl.pallas_call(
        functools.partial(unmix_kernel, chunks),
        out_shape=(
            jax.ShapeDtypeStruct((rows, width), F32),
            jax.ShapeDtypeStruct((nseq * rows, piece), BF16),
            jax.ShapeDtypeStruct((8, width), F32),
            jax.ShapeDtypeStruct((2,) + down_p.shape[1:], BF16),
            jax.ShapeDtypeStruct(half_shape[1:], BF16),
            jax.ShapeDtypeStruct((nfsdp, out_w.shape[1] // nfsdp, out_w.shape[2]), BF16),
            jax.ShapeDtypeStruct(half_shape, BF16),
            jax.ShapeDtypeStruct(grad_shape, BF16),
            jax.ShapeDtypeStruct(n2.shape, BF16),
        ),
        in_specs=[vm_spec()] * 4 + [any_spec()] * 9,
        out_specs=(any_spec(),) * 2 + (vm_spec(),) * 4 + (any_spec(),) * 3,
        scratch_shapes=wires_scratch(6 * chunks + 3 * nfsdp + 3)
        + scatter_scratch(chunks, rows // chunks, width)
        + [pltpu.VMEM((rows, width), BF16), pltpu.VMEM((nseq, rows, piece), BF16)]
        + fsdp_scatter_scratch((nfsdp,) + down_p.shape[1:]) * 2
        + fsdp_scatter_scratch(half_shape)
        + [
            pltpu.VMEM(half_shape, BF16),
            pltpu.SemaphoreType.DMA((9,)),
            pltpu.VMEM(dg.shape, BF16),
            pltpu.VMEM(du.shape, BF16),
            pltpu.VMEM(gate_w.shape, BF16),
            pltpu.VMEM(up_w.shape, BF16),
            pltpu.VMEM(out_w.shape, BF16),
            pltpu.VMEM(n2.shape, BF16),
            pltpu.VMEM(hid.shape, BF16),
            pltpu.VMEM(down_w.shape, BF16),
            pltpu.VMEM(out_w.shape, BF16),
            pltpu.VMEM((3,) + out_w.shape[1:], BF16),
            pltpu.VMEM((2, 384 * nfsdp // width, width // nfsdp, units), BF16),
            pltpu.VMEM((2, rows, width), BF16),
            pltpu.SemaphoreType.DMA((5,)),
            pltpu.VMEM((rows, width), F32),
            pltpu.VMEM((nseq * rows, piece), BF16),
        ],
        compiler_params=call_params(4, 63),
        name="unmix",
    )(gains, obuf, resid, cot, down_p, dg, du, gate_w, up_w, out_w, n2, hid, down_w)


def build_strips(heads, first_head, starts, table, ids, strip, far):
    length = ids.shape[1]
    half = 2 * PROMPT
    for h in range(heads):
        row = jnp.zeros(ids.shape, F32)
        for b in range(table.shape[1]):
            row = jnp.where(ids[...] == b, table[first_head + h, b], row)
        row = jnp.broadcast_to(row, (8, length))
        base = jnp.broadcast_to(row[:1, PROMPT // 2 : PROMPT // 2 + half], (128, half))
        strip[h] = pltpu.roll(base, 1, 1, stride=1, stride_axis=0)[:, 128:]
        for c in range(2):
            moved = pltpu.roll(row, length - PROMPT // 2 - starts[c], 1)
            base = jnp.broadcast_to(moved[:1, : FARW + 128], (128, FARW + 128))
            far[h, c] = pltpu.roll(base, 1, 1, stride=1, stride_axis=0)[:, 128:]


def head_masks(width, heads):
    lane = lax.broadcasted_iota(jnp.int32, (1, width), 1)
    return [(lane >= h * HEAD_DIM) & (lane < (h + 1) * HEAD_DIM) for h in range(heads)]


def masked_copies(src, dst, heads):
    masks = head_masks(src.shape[1], heads)
    for h in range(heads):
        dst[h] = jnp.where(masks[h], src[...], jnp.zeros((), src.dtype))


def bias_chunk(strip, far, h, first_q, kstart, kind, c):
    parts = []
    for r in range(KC // 128):
        m = PROMPT - 128 - (kstart + 128 * r)
        if kind == "far":
            parts.append(far[h, c, :, m : m + CL])
        else:
            parts.append(strip[h, :, pl.ds(pl.multiple_of(first_q + m, 128), CL)])
    return jnp.concatenate(parts, axis=0)


def pack_piece(units, nfsdp, nseq):
    block = units // nfsdp
    return block, -(-block // (16 * nseq)) * 16


def pack_front(t, raw, first_q, out_q, gains):
    r_q, r_k, r_v, r_o = raw
    piece = first_q.shape[1] * 3 // 10
    depth = first_q.shape[0]
    cut = slice(t * piece, (t + 1) * piece)
    first_q[...] = jnp.concatenate(
        [r_q[:, cut], r_k[:, cut], r_v[:, cut], gains, jnp.zeros((depth, first_q.shape[1] - 3 * piece - 8), BF16)], axis=1
    )
    cols = out_q.shape[1]
    out_q[...] = r_o[:, t * cols : (t + 1) * cols]


def pack_cols(t, nseq, nfsdp, raw, packed):
    block, piece = pack_piece(raw.shape[1], nfsdp, nseq)
    pieces = []
    for f in range(nfsdp):
        begin = f * block + t * piece
        end = min(begin + piece, (f + 1) * block)
        pieces.append(raw[:, begin:end])
        if end - begin < piece:
            pieces.append(jnp.zeros((raw.shape[0], piece - end + begin), BF16))
    packed[...] = jnp.concatenate(pieces, axis=1)


def pack_down(t, raw, packed):
    piece = packed.shape[0]
    begin = t * piece
    end = min(begin + piece, raw.shape[0])
    packed[: end - begin, :] = raw[begin:end, :]
    if end - begin < piece:
        packed[end - begin :, :] = jnp.zeros((piece - end + begin, raw.shape[1]), BF16)


def forward_kernel(
    heads, nseq, starts, table, ids, gain_q, tok_h, w_q, w_k, w_v, w_o, w_g, w_u, w_d, cot_q,
    lse, gains, q_h, k_h, v_h, o_h, obuf_h, resid_h,
    n1_h, first_h, out_h, cot_h, gate_h, up_h, down_h, n2_h, hid_h, dg_h, du_h, parts_h,
    send, recv, local, first_q, out_q, gate_q, up_q, down_q, group, first, gate_w, up_w, down_w, tok, fsems, spare, q, k, v, o, obuf, resid, osems,
):
    rows, width = tok.shape
    units = gate_w.shape[1]
    piece = q.shape[1]
    mine, near, other, cross = seq_places()
    pair, side, pairs = fsdp_places()
    nfsdp = 2 * pairs
    half = rows // 2
    wires = Wires(send, recv)
    ring = SeqGather(wires, lambda t, c: group.at[rows_at(t, rows, c * half, half), :], 2)
    size = first_q.shape[0]
    lead = FsdpGather(wires, first_q, lambda f: first.at[shard_rows(f, size), :], local.at[7])
    late = FsdpGather(wires, out_q, lambda f: out_h.at[mine, f], local.at[8])
    gates = gather_halves(wires, gate_q, gate_w, gate_q.shape[0], (local.at[9], local.at[10]))
    ups = gather_halves(wires, up_q, up_w, up_q.shape[0], (local.at[11], local.at[12]))
    downs = gather_halves(wires, down_q, down_w, down_q.shape[0], (local.at[13], local.at[14]))
    wring = SeqGather(wires, lambda t, c: out_h.at[t], 1)
    cring = SeqGather(wires, lambda t, c: cot_h.at[rows_at(t, rows, c * half, half), :], 2)
    nring = SeqGather(wires, lambda t, c: group.at[rows_at(t, rows, c * half, half), :], 2)
    obase = wires.take(3)
    own = [
        pltpu.make_async_copy(tok_h, group.at[rows_at(mine, rows), :], local.at[15]),
        pltpu.make_async_copy(cot_q, cot_h.at[rows_at(mine, rows), :], local.at[16]),
        pltpu.make_async_copy(tok_h, tok, local.at[17]),
    ]

    def begin(r_q, r_k, r_v, r_o, r_g, r_u, r_d):
        loads = [
            pltpu.make_async_copy(src, dst, local.at[n])
            for n, (src, dst) in enumerate(
                ((w_q, r_q), (w_k, r_k), (w_v, r_v), (w_o, r_o), (w_g, r_g), (w_u, r_u), (w_d, r_d))
            )
        ]
        for a in loads:
            a.start()
        peers = [{"seq": near}, {"seq": other}, {"seq": cross}] + fsdp_peers()
        greet(peers)
        for a in own:
            a.start()
        for a in loads[:4]:
            a.wait()
        both = jnp.concatenate([gain_q[...], jnp.zeros((6, gain_q.shape[1]), F32)], axis=0).T.astype(BF16)
        for t in range(nseq):

            @pl.when(mine == t)
            def _():
                pack_front(t, (r_q, r_k, r_v, r_o), first_q, out_q, both)

        pl.semaphore_wait(pltpu.get_barrier_semaphore(), len(peers))
        for c in range(2):
            ring.send(c, tok_h.at[pl.ds(c * half, half), :])
        lead.over().start()
        lead.start()
        for a in loads[4:]:
            a.wait()
        for t in range(nseq):

            @pl.when(mine == t)
            def _():
                pack_cols(t, nseq, nfsdp, r_g, gate_q)

        late.over().start()
        late.start()
        for t in range(nseq):

            @pl.when(mine == t)
            def _():
                pack_cols(t, nseq, nfsdp, r_u, up_q)
                pack_down(t, r_d, down_q)

    pl.run_scoped(begin, *[pltpu.VMEM(a.shape, BF16) for a in (w_q, w_k, w_v, w_o, w_g, w_u, w_d)])
    halves = gates + ups + downs
    for a in halves[:2]:
        a.over().start()
    for a in halves:
        a.start()

    def advance(n, d):
        halves[n].forward(d)
        if d == max(pairs - 2, 1) and n + 2 < len(halves):
            pass

    cring.send(0, cot_q.at[pl.ds(0, half), :])

    early_saves = []

    def attend(n1, strip, far, kh, vt, ot, s):
        build_strips(heads, mine * heads, starts, table, ids, strip, far)
        lse[...] = jnp.zeros(lse.shape, F32)
        for d in range(1, pairs):
            lead.forward(d)
            if d == pairs // 2:
                ring.forward(0)
        for d in range(1, pairs):
            late.forward(d)
        for a in halves[2:]:
            a.over().start()
        ring.forward(1)
        lead.finish()
        saves = [pltpu.make_async_copy(first, first_h, local.at[0])]
        saves[0].start()
        column = 3 * piece
        gains[...] = jnp.zeros(gains.shape, F32)
        for b in range(width // 256):
            base = column // 128 * 128
            band = first[b * 256 : (b + 1) * 256, base : base + 128].astype(F32).T
            for n in range(2):
                line = column - base + n
                gains[n : n + 1, b * 256 : (b + 1) * 256] = band[line : line + 1, :]

        def project(t):
            at = rows_at(t, rows)
            x = group[at, :].astype(F32)
            low = (x * inverse_rms(x) * gains[0:1, :]).astype(BF16)
            n1[at, :] = low
            r = nn(low, first[:, :column])
            q[at, :] = r[:, :piece].astype(BF16)
            k[at, :] = r[:, piece : 2 * piece].astype(BF16)
            v[at, :] = r[:, 2 * piece :].astype(BF16)

        own[0].wait()
        project(mine)
        for c in range(2):
            ring.got_near(c)
        project(near)
        project(other)
        for c in range(2):
            ring.got_cross(c)
        project(cross)
        saves.append(pltpu.make_async_copy(n1, n1_h, local.at[1]))
        saves[1].start()
        for d in range(pairs):
            late.complete(d)
        wring.send(0, out_h.at[mine])
        cring.send(1, cot_q.at[pl.ds(half, half), :])
        masked_copies(k, kh, heads)
        vt[...] = v[...].astype(F32).T.astype(BF16)

        def block(h, q0, bias_q0, chunks, c):
            qb = q[pl.ds(q0, CL), :]
            top = None
            for n, (k0, kind, kstart) in enumerate(chunks):
                sc = nt(kh[h, pl.ds(k0, KC), :], qb) + bias_chunk(strip, far, h, bias_q0, kstart, kind, c)
                s[n * KC : (n + 1) * KC, :] = sc
                m = jnp.max(sc, axis=0, keepdims=True)
                top = m if top is None else jnp.maximum(top, m)
            total = jnp.zeros((1, CL), F32)
            acc = jnp.zeros((HEAD_DIM, CL), F32)
            lines = pl.ds(pl.multiple_of(h * HEAD_DIM, HEAD_DIM), HEAD_DIM)
            for n, (k0, kind, kstart) in enumerate(chunks):
                e = jnp.exp(s[n * KC : (n + 1) * KC, :] - top)
                total = total + jnp.sum(e, axis=0, keepdims=True)
                acc = acc + nn(vt[lines, pl.ds(k0, KC)], e.astype(BF16))
            ot[lines, pl.ds(q0, CL)] = acc / total
            lse[pl.ds(h, 1), pl.ds(q0, CL)] = top + jnp.log(total)

        nblk = PROMPT // CL
        steps = [(n, d) for n in range(2) for d in range(1, pairs)]
        early, later, final = steps[: pairs - 1], steps[pairs - 1 : -1], steps[-1:]

        def prompt_body(i, carry):
            h, blk = i // nblk, i % nblk
            q0 = pl.multiple_of(blk * CL, CL)
            block(h, q0, q0, [(j * KC, "strip", j * KC) for j in range(PROMPT // KC)], None)
            for n, step in enumerate(early):

                @pl.when(i == max((heads * nblk - 2) * (n + 1) // len(early) - 2, 0))
                def _():
                    advance(*step)

            return carry

        def cont_body(i, carry):
            h, c = i // 2, i % 2
            q0 = pl.multiple_of(PROMPT + c * CL, CL)
            chunks = [(j * KC, "far", j * KC) for j in range(PROMPT // KC)]
            chunks += [(q0 + j * KC, "strip", j * KC) for j in range(CL // KC)]
            block(h, q0, 0, chunks, c)
            for n, step in enumerate(later):

                @pl.when(i == max(2 * heads * (n + 1) // len(later) - 1, 0))
                def _():
                    advance(*step)

            return carry

        lax.fori_loop(0, heads * nblk, prompt_body, 0)
        cring.forward(0)
        lax.fori_loop(0, heads * 2, cont_body, 0)
        o[...] = ot[...].T.astype(BF16)
        for n, (a, b) in enumerate(((q, q_h), (k, k_h), (v, v_h), (o, o_h))):
            early_saves.append(pltpu.make_async_copy(a, b, osems.at[n]))
            early_saves[n].start()
        ring.drain()
        for n, t in enumerate((other, cross, near)):
            wires.at(obase + n, o.at[rows_at(t, rows), :], obuf.at[mine], {"seq": t}).start()
        obuf[mine] = o[rows_at(mine, rows), :]
        wring.forward(0)
        for step in final:
            advance(*step)
        for a in saves:
            a.wait()

    tall = nseq * rows
    pl.run_scoped(
        attend,
        pltpu.VMEM((tall, width), BF16),
        pltpu.VMEM((heads, 128, STRIP), F32),
        pltpu.VMEM((heads, 2, 128, FARW), F32),
        pltpu.VMEM((heads, tall, piece), BF16),
        pltpu.VMEM((piece, tall), BF16),
        pltpu.VMEM((piece, tall), F32),
        pltpu.VMEM((PROMPT + CL, CL), F32),
    )
    todo = [(n, d) for n in range(2, 6) for d in range(1, pairs)]

    def pass_on(share):
        while todo and len(todo) > round((1 - share) * 4 * (pairs - 1)):
            advance(*todo.pop(0))

    def feed(out_w, cot, ga, ub, hid, dg, du, parts):
        cols = out_w.shape[2]
        wring.got_near(0)
        wring.got_cross(0)
        lines = w_o.shape[0]
        fetch = []
        if lines % 16 == 0:
            fetch = [
                pltpu.make_async_copy(out_h.at[u, f], out_w.at[u, pl.ds(f * lines, lines), :], fsems.at[u * nfsdp + f])
                for u in range(nseq)
                for f in range(nfsdp)
            ]
        else:
            load = pltpu.make_async_copy(out_h, spare, local.at[2])
            load.start()
            load.wait()
            for u in range(nseq):
                joined = jnp.concatenate([spare[u, f].astype(F32) for f in range(nfsdp)], axis=0)
                out_w[u] = joined.astype(BF16)
        saves = []

        def save(src, dst):
            saves.append(pltpu.make_async_copy(src, dst, local.at[18 + len(saves)]))
            saves[-1].start()

        for a in fetch:
            a.start()
        for n, t in enumerate((other, cross, near)):
            wires.at(obase + n, o.at[rows_at(t, rows), :], obuf.at[mine], {"seq": t}).wait()
        for a in fetch:
            a.wait()
        pass_on(1 / 12)
        own[2].wait()
        for c in range(2):
            part = slice(c * half, (c + 1) * half)
            for u in range(nseq):
                acc = tok[part, u * cols : (u + 1) * cols].astype(F32)
                for t in range(nseq):
                    acc = acc + nn(obuf[t, part, :], out_w[u, t * piece : (t + 1) * piece, :])
                resid[part, u * cols : (u + 1) * cols] = acc
            h = resid[part, :]
            group[rows_at(mine, rows, c * half, half), :] = (h * inverse_rms(h) * gains[1:2, :]).astype(BF16)
            if c == 1:
                nring.send(0, group.at[rows_at(mine, rows, 0, half), :])
        nring.send(1, group.at[rows_at(mine, rows, half, half), :])
        save(obuf, obuf_h)
        save(resid, resid_h)
        cring.forward(1)
        for a in gates:
            for d in range(pairs):
                a.complete(d)
        save(gate_w, gate_h)

        def gate_rows(t):
            ga[rows_at(t, rows), :] = nn(group[rows_at(t, rows), :], gate_w[...])

        def act_rows(t):
            up = nn(group[rows_at(t, rows), :], up_w[...])
            active, slope = gelu_both(ga[rows_at(t, rows), :])
            hid[rows_at(t, rows), :] = (active * up).astype(BF16)
            ga[rows_at(t, rows), :] = slope * up
            ub[rows_at(t, rows), :] = active

        pass_on(2 / 12)
        gate_rows(mine)
        nring.got_near(0)
        nring.got_near(1)
        pass_on(3 / 12)
        gate_rows(near)
        pass_on(4 / 12)
        nring.forward(0)
        pass_on(6 / 12)
        nring.forward(1)
        own[1].wait()
        for c in range(2):
            cring.got_near(c)
            cring.got_cross(c)
        cload = pltpu.make_async_copy(cot_h, cot, local.at[3])
        cload.start()
        pass_on(7 / 12)
        gate_rows(other)
        for c in range(2):
            nring.got_cross(c)
        gate_rows(cross)
        save(group, n2_h)
        pass_on(8 / 12)
        for a in ups:
            for d in range(pairs):
                a.complete(d)
        save(up_w, up_h)
        act_rows(mine)
        act_rows(near)
        pass_on(9 / 12)
        act_rows(other)
        act_rows(cross)
        save(hid, hid_h)
        pass_on(10 / 12)
        cload.wait()
        width_f = units // nfsdp
        wide = max(256 // width_f, 1)
        pieces = []

        def down_part(n):
            slot = n % 2
            if n > 1:
                pieces[n - 2].wait()
            got = dot_tn(hid[:, n * wide * width_f : (n + 1) * wide * width_f], cot[...]).astype(BF16)
            for m in range(wide):
                parts[slot, m] = got[m * width_f : (m + 1) * width_f, :]
            pieces.append(pltpu.make_async_copy(parts.at[slot], parts_h.at[pl.ds(n * wide, wide)], local.at[4 + slot]))
            pieces[n].start()

        for n in range(nfsdp // wide):
            down_part(n)
            if n == 1:
                pass_on(11 / 12)

        def back_cols(at):
            for t in range(nseq):
                band = slice(t * rows, (t + 1) * rows)
                dh = nt(cot[band, :], down_w[at, :])
                dg[band, at] = (dh * ga[band, at]).astype(BF16)
                du[band, at] = (dh * ub[band, at]).astype(BF16)
            save(dg.at[:, at], dg_h.at[:, at])
            save(du.at[:, at], du_h.at[:, at])

        if (2 * width_f) % 128 == 0:

            def columns(d):
                for a in downs:
                    a.complete(d)
                if d == pairs - 1:
                    save(down_w, down_h)
                start = downs[0].source(d) * 2 * width_f
                back_cols(pl.ds(pl.multiple_of(start, 2 * width_f), 2 * width_f))

            columns(0)
            pass_on(1)
            for d in range(1, pairs):
                columns(d)
        else:
            pass_on(1)
            for d in range(pairs):
                for a in downs:
                    a.complete(d)
            for n in range(units // 256):
                back_cols(slice(n * 256, (n + 1) * 256))
            save(down_w, down_h)
        nring.drain()
        wring.drain()
        cring.drain()
        lead_late = [late] + gates + ups + downs
        for a in lead_late:
            a.drain()
        for n, (a, b) in enumerate(((q, q_h), (k, k_h), (v, v_h), (o, o_h))):
            pltpu.make_async_copy(a, b, osems.at[n]).wait()
        for a in pieces[-2:] + saves:
            a.wait()

    pl.run_scoped(
        feed,
        pltpu.VMEM((nseq, w_o.shape[0] * nfsdp, width // nseq), BF16),
        pltpu.VMEM((tall, width), BF16),
        pltpu.VMEM((tall, units), F32),
        pltpu.VMEM((tall, units), F32),
        pltpu.VMEM((tall, units), BF16),
        pltpu.VMEM((tall, units), BF16),
        pltpu.VMEM((tall, units), BF16),
        pltpu.VMEM((2, max(256 * nfsdp // units, 1), units // nfsdp, width), BF16),
    )


def forward(starts, table, ids, gain_q, tok, w_q, w_k, w_v, w_o, w_g, w_u, w_d, cot, nseq, nfsdp):
    rows, width = tok.shape
    inner = w_q.shape[1]
    piece = inner // nseq
    heads = piece // HEAD_DIM
    tall = nseq * rows
    size = w_q.shape[0]
    unit = pack_piece(w_g.shape[1], nfsdp, nseq)[1]
    units = nfsdp * unit
    cols = width // nseq
    lead = piece * 10 // 3
    smem = pl.BlockSpec(memory_space=pltpu.SMEM)

    def low(*shape):
        return jax.ShapeDtypeStruct(shape, BF16)

    return pl.pallas_call(
        functools.partial(forward_kernel, heads, nseq),
        out_shape=(
            jax.ShapeDtypeStruct((8, tall), F32),
            jax.ShapeDtypeStruct((8, width), F32),
            low(tall, piece),
            low(tall, piece),
            low(tall, piece),
            low(tall, piece),
            low(nseq, rows, piece),
            jax.ShapeDtypeStruct((rows, width), F32),
            low(tall, width),
            low(width, lead),
            low(nseq, nfsdp, w_o.shape[0], cols),
            low(tall, width),
            low(width, units),
            low(width, units),
            low(units, width),
            low(tall, width),
            low(tall, units),
            low(tall, units),
            low(tall, units),
            low(nfsdp, unit, width),
        ),
        in_specs=[smem, smem, vm_spec(), vm_spec()] + [any_spec()] * 9,
        out_specs=(vm_spec(),) * 2 + (any_spec(),) * 18,
        scratch_shapes=wires_scratch(6 + 8 * nfsdp + 3 + 6 + 6 + 3)
        + [
            pltpu.SemaphoreType.DMA((18 + 7 + 2 * max(nfsdp // 2, units // 256),)),
            pltpu.VMEM((size, lead), BF16),
            pltpu.VMEM((w_o.shape[0], cols), BF16),
            pltpu.VMEM((size, units), BF16),
            pltpu.VMEM((size, units), BF16),
            pltpu.VMEM((unit, width), BF16),
            pltpu.VMEM((tall, width), BF16),
            pltpu.VMEM((width, lead), BF16),
            pltpu.VMEM((width, units), BF16),
            pltpu.VMEM((width, units), BF16),
            pltpu.VMEM((units, width), BF16),
            pltpu.VMEM((rows, width), BF16),
            pltpu.SemaphoreType.DMA((nseq * nfsdp,)),
            pltpu.VMEM((nseq, nfsdp) + w_o.shape[:1] + (cols,) if w_o.shape[0] % 16 else (1, 1, 8, 128), BF16),
            pltpu.VMEM((tall, piece), BF16),
            pltpu.VMEM((tall, piece), BF16),
            pltpu.VMEM((tall, piece), BF16),
            pltpu.VMEM((tall, piece), BF16),
            pltpu.VMEM((nseq, rows, piece), BF16),
            pltpu.VMEM((rows, width), F32),
            pltpu.SemaphoreType.DMA((4,)),
        ],
        compiler_params=call_params(1, 64),
        name="forward",
    )(starts, table, ids, gain_q, tok, w_q, w_k, w_v, w_o, w_g, w_u, w_d, cot)


def back_kernel(
    heads, chunks, starts, table, ids, gains, lse, gain_b, q, k, v, o, do,
    resid_h, rgrad_h, tok_h, y_p, out_p, gate_p, up_p, done_h, lead_h, n1_h, first_h,
    small, y_h, in_h, down_f, lead_f, gate_f, up_f, qkv_f, out_f,
    send, recv, local, ybuf, qkv_p, b0, b1, b2, b3, b4, b5,
    g0, g1, g2, g3, u0, u1, u2, u3, q0_, q1_, q2_, q3_, o0, o1, o2, o3,
    gate_s, up_s, qkv_s, out_s, dqkv, tok, held, stage, one, two, three, tgrad,
):
    rows, width = tok.shape
    nseq = q.shape[0] // rows
    piece = q.shape[1]
    nfsdp = gate_p.shape[0]
    s, near, far_d, cross = seq_places()
    pair, side, pairs = fsdp_places()

    def y_block(t):
        return y_p.at[rows_at(t, rows), :]

    loads = [
        pltpu.make_async_copy(y_block(far_d), ybuf.at[2], local.at[0]),
        pltpu.make_async_copy(y_block(s), ybuf.at[3], local.at[1]),
    ]
    loads.append(pltpu.make_async_copy(tok_h, tok, local.at[5]))
    for a in loads:
        a.start()
    meet([{"seq": near}, {"seq": far_d}, {"seq": cross}] + fsdp_peers())
    wires = Wires(send, recv)
    hop = wires.go(y_block(cross), ybuf.at[0], {"seq": near})
    turn = wires.go(y_block(near), ybuf.at[1], {"seq": near})
    gates = FsdpScatter(wires, gate_p, (g0, g1, g2, g3), gate_s)
    ups = FsdpScatter(wires, up_p, (u0, u1, u2, u3), up_s)
    gates.start()
    ups.start()
    down_ring = SeqGather(wires, lambda t, c: down_f.at[t], 1)
    lead_ring = SeqGather(wires, lambda t, c: lead_f.at[t], 1)
    gate_ring = SeqGather(wires, lambda t, c: gate_f.at[t], 1)
    up_ring = SeqGather(wires, lambda t, c: up_f.at[t], 1)
    qkv_ring = SeqGather(wires, lambda t, c: qkv_f.at[t], 1)
    out_ring = SeqGather(wires, lambda t, c: out_f.at[t], 1)
    qkvs = FsdpScatter(wires, qkv_p, (q0_, q1_, q2_, q3_), qkv_s)
    outs = FsdpScatter(wires, out_p, (o0, o1, o2, o3), out_s)
    far_hop = wires.at(wires.take(1), ybuf.at[2], ybuf.at[4], {"seq": far_d})
    down_keep = pltpu.make_async_copy(done_h, down_f.at[s], local.at[6])
    down_keep.start()
    down_ring.send(0, done_h)
    lead_keep = pltpu.make_async_copy(lead_h, lead_f.at[s], local.at[10])
    lead_keep.start()
    lead_ring.send(0, lead_h)
    length = ids.shape[1]
    half = 2 * PROMPT

    def attend_back(strip, far, kh, vh, kt, delta, dqt, dk, dv, gstrip, gfar):
        build_strips(heads, s * heads, starts, table, ids, strip, far)
        loads[0].wait()
        hop.wait_recv()
        ybuf[2] = (ybuf[2].astype(F32) + ybuf[0].astype(F32)).astype(BF16)
        for src, dst in ((k, kh), (v, vh)):
            masked_copies(src, dst, heads)
        far_hop.start()
        kt[...] = k[...].astype(F32).T.astype(BF16)
        prod = (o[...].astype(F32) * do[...].astype(F32)).T
        for h in range(heads):
            delta[h : h + 1, :] = jnp.sum(prod[h * HEAD_DIM : (h + 1) * HEAD_DIM, :], axis=0, keepdims=True)
        dk[...] = jnp.zeros(dk.shape, F32)
        dv[...] = jnp.zeros(dv.shape, F32)
        gstrip[...] = jnp.zeros(gstrip.shape, F32)
        gfar[...] = jnp.zeros(gfar.shape, F32)
        lane = lax.broadcasted_iota(jnp.int32, (1, piece), 1)

        def block(h, q0, bias_q0, chunk_list, c):
            qb = q[pl.ds(q0, CL), :]
            dob = do[pl.ds(q0, CL), :]
            keep = lane // HEAD_DIM == h
            qhb = jnp.where(keep, qb, jnp.zeros((), BF16))
            dohb = jnp.where(keep, dob, jnp.zeros((), BF16))
            lrow = lse[pl.ds(h, 1), pl.ds(q0, CL)]
            drow = delta[pl.ds(h, 1), pl.ds(q0, CL)]
            acc = jnp.zeros((HEAD_DIM, CL), F32)
            for n, (k0, kind, kstart) in enumerate(chunk_list):
                ks = pl.ds(k0, KC)
                sc = nt(kh[h, ks, :], qb) + bias_chunk(strip, far, h, bias_q0, kstart, kind, c)
                pr = jnp.exp(sc - lrow)
                dp = nt(vh[h, ks, :], dob)
                ds = pr * (dp - drow)
                dsl = ds.astype(BF16)
                dv[ks, :] += nn(pr.astype(BF16), dohb)
                dk[ks, :] += nn(dsl, qhb)
                acc = acc + nn(kt[pl.ds(pl.multiple_of(h * HEAD_DIM, HEAD_DIM), HEAD_DIM), ks], dsl)
                for r in range(KC // 128):
                    m = PROMPT - 128 - (kstart + 128 * r)
                    part = ds[128 * r : 128 * (r + 1), :]
                    if kind == "far":
                        gfar[h, c, :, m : m + CL] += part
                    else:
                        gstrip[h, :, pl.ds(pl.multiple_of(bias_q0 + m, 128), CL)] += part
            dqt[pl.ds(pl.multiple_of(h * HEAD_DIM, HEAD_DIM), HEAD_DIM), pl.ds(q0, CL)] = acc

        nblk = PROMPT // CL

        def prompt_body(i, carry):
            h, blk = i // nblk, i % nblk
            q0 = pl.multiple_of(blk * CL, CL)
            block(h, q0, q0, [(j * KC, "strip", j * KC) for j in range(PROMPT // KC)], None)

            for k in range(1, pairs):

                @pl.when(i == heads * nblk * k // pairs)
                def _():
                    gates.step(k)

            return carry

        lax.fori_loop(0, heads * nblk, prompt_body, 0)

        def cont_body(i, carry):
            h, c = i // 2, i % 2
            q0 = pl.multiple_of(PROMPT + c * CL, CL)
            chunk_list = [(j * KC, "far", j * KC) for j in range(PROMPT // KC)]
            chunk_list += [(q0 + j * KC, "strip", j * KC) for j in range(CL // KC)]
            block(h, q0, 0, chunk_list, c)

            @pl.when(i == heads)
            def _():
                ups.step(1)

            return carry

        lax.fori_loop(0, heads * 2, cont_body, 0)
        dqkv[...] = jnp.concatenate([dqt[...].T, dk[...], dv[...]], axis=1).astype(BF16)
        buckets = table.shape[1]
        lines8 = lax.broadcasted_iota(jnp.int32, (buckets, length), 0)
        hot = ids[:1, :] == lines8
        tgrad[...] = jnp.zeros(tgrad.shape, F32)
        for h in range(heads):

            def unskew(g, span):
                full = jnp.concatenate([jnp.zeros((128, 128), F32), g], axis=1)
                eight = full[:8]
                for a in range(1, 16):
                    eight = eight + pltpu.roll(full[8 * a : 8 * a + 8], span - 8 * a, 1)
                vec = pltpu.roll(eight, span - 1, 1)[:1]
                for b in range(1, 8):
                    vec = vec + pltpu.roll(eight, span - 1 - b, 1)[b : b + 1]
                return jnp.concatenate([vec, jnp.zeros((1, length - span), F32)], axis=1)

            whole = jnp.broadcast_to(unskew(gstrip[h], half), (8, length))
            whole = pltpu.roll(whole, PROMPT // 2, 1)
            for c in range(2):
                moved = jnp.broadcast_to(unskew(gfar[h, c], FARW + 128), (8, length))
                whole = whole + pltpu.roll(moved, PROMPT // 2 + starts[c], 1)
            picked = jnp.where(hot, whole[:1, :], 0.0)
            column = jnp.broadcast_to(jnp.sum(picked, axis=1, keepdims=True), (buckets, 128))
            tgrad[h : h + 1, :buckets] = column.T[:1, :]

    tall = nseq * rows
    pl.run_scoped(
        attend_back,
        pltpu.VMEM((heads, 128, STRIP), F32),
        pltpu.VMEM((heads, 2, 128, FARW), F32),
        pltpu.VMEM((heads, tall, piece), BF16),
        pltpu.VMEM((heads, tall, piece), BF16),
        pltpu.VMEM((piece, tall), BF16),
        pltpu.VMEM((8, tall), F32),
        pltpu.VMEM((piece, tall), F32),
        pltpu.VMEM((tall, piece), F32),
        pltpu.VMEM((tall, piece), F32),
        pltpu.VMEM((heads, 128, STRIP), F32),
        pltpu.VMEM((heads, 2, 128, FARW), F32),
    )

    def rest(n1, hold, rgrad, resid, first):
        later = [
            pltpu.make_async_copy(n1_h, n1, local.at[7]),
            pltpu.make_async_copy(rgrad_h, rgrad, local.at[8]),
            pltpu.make_async_copy(resid_h, resid, local.at[9]),
        ]
        ready = pltpu.make_async_copy(first_h, first, local.at[4])
        ready.start()
        for a in later:
            a.start()
        sums = SeqScatter(wires, chunks, b0, b1, b2, b3, b4, b5)
        size = rows // chunks
        ready.wait()

        def part(t, c):
            return nt(dqkv[rows_at(t, rows, c * size, size), :], first[:, : 3 * piece])

        for c in range(chunks):
            sums.cross_chunk(c, part(cross, c))
        for c in range(chunks):
            sums.far_chunk(c, part(far_d, c))
        for k in range(2, pairs - 1):
            ups.step(k)
        later[0].wait()
        depth = width // nfsdp
        wide = 384
        for n in range(width // wide):
            got = dot_tn(n1[:, n * wide : (n + 1) * wide], dqkv[...])
            for m in range(wide // depth):
                qkv_p[n * (wide // depth) + m] = got[m * depth : (m + 1) * depth, :].astype(BF16)
        for c in range(chunks):
            sums.near_chunk(c, part(near, c))
        for c in range(chunks):
            hold[c * size : (c + 1) * size, :] = part(s, c)
        qkvs.start()
        if pairs > 2:
            ups.step(pairs - 1)
        gates.finish()
        outs.start()
        gate_keep = pltpu.make_async_copy(gate_s, gate_f.at[s], local.at[11])
        gate_keep.start()
        gate_ring.send(0, gate_s)
        down_ring.forward(0)
        lead_ring.forward(0)
        later[2].wait()
        loads[1].wait()
        turn.wait_recv()
        far_hop.wait_recv()
        total = ybuf[3].astype(F32) + ybuf[1].astype(F32) + ybuf[4].astype(F32)
        ybuf[3] = (resid[...] + total).astype(BF16)
        qkvs.step(1)
        loads[2].wait()
        later[1].wait()
        gsum = jnp.zeros((1, width), F32)
        y_keep = pltpu.make_async_copy(ybuf.at[3], y_h, local.at[12])
        y_keep.start()
        for c in range(chunks):
            at = slice(c * size, (c + 1) * size)
            dn = sums.own_chunk(c, hold[at, :])
            x = tok[at, :].astype(F32)
            r = inverse_rms(x)
            gsum = gsum + jnp.sum(dn * x * r, axis=0, keepdims=True)
            tok[at, :] = (rgrad[at, :] + norm_back(dn, x, r, gains[0:1, :])).astype(BF16)
            if c == 0:
                for k in range(2, pairs - 1):
                    qkvs.step(k)
                ups.finish()
                up_keep = pltpu.make_async_copy(up_s, up_f.at[s], local.at[14])
                up_keep.start()
                up_ring.send(0, up_s)
                if pairs > 2:
                    qkvs.step(pairs - 1)
        in_keep = pltpu.make_async_copy(tok, in_h, local.at[13])
        in_keep.start()
        held[...] = jnp.zeros(held.shape, F32)
        lanes = held.shape[1]
        lines = width // lanes
        for n in range(lines):
            held[n : n + 1, :] = gsum[:, n * lanes : (n + 1) * lanes]
            held[lines + n : lines + n + 1, :] = gain_b[:1, n * lanes : (n + 1) * lanes]
        held[pl.ds(2 * lines + s * 8, 8), :] = tgrad[...]
        outs.step(1)
        trips = [wires.go(held, one.at[n], {"seq": t}) for n, t in enumerate((near, far_d, cross))]
        gate_ring.forward(0)
        for k in range(2, pairs):
            outs.step(k)
        for a in trips:
            a.wait_recv()
        stage[0] = held[...] + one[0] + one[1] + one[2]
        up_ring.forward(0)
        trips.append(wires.go(stage.at[0], two, {"fsdp": pair * 2 + 1 - side}))
        trips[-1].wait_recv()
        stage[1] = stage[0] + two[...]
        zs = [
            wires.go(stage.at[1], three.at[d - 1], {"fsdp": lax.rem(pair + d, pairs) * 2 + side})
            for d in range(1, pairs)
        ]
        qkvs.finish()
        qkv_keep = pltpu.make_async_copy(qkv_s, qkv_f.at[s], local.at[15])
        qkv_keep.start()
        qkv_ring.send(0, qkv_s)
        outs.finish()
        out_keep = pltpu.make_async_copy(out_s, out_f.at[s], local.at[16])
        out_keep.start()
        out_ring.send(0, out_s)
        total = stage[1]
        for d, a in enumerate(zs):
            a.wait_recv()
            total = total + three[d]
        small[...] = total
        qkv_ring.forward(0)
        out_ring.forward(0)
        for a in (down_ring, lead_ring, gate_ring, up_ring, qkv_ring, out_ring):
            a.finish()
        sums.finish()
        for a in (gates, ups, qkvs, outs):
            a.drain()
        for a in (gate_keep, up_keep, qkv_keep, out_keep, y_keep, in_keep, down_keep, lead_keep):
            a.wait()
        for a in trips + zs + [hop, turn, far_hop]:
            a.wait_send()

    pl.run_scoped(
        rest,
        pltpu.VMEM((tall, width), BF16),
        pltpu.VMEM((rows, width), F32),
        pltpu.VMEM((rows, width), F32),
        pltpu.VMEM((rows, width), F32),
        pltpu.VMEM(first_h.shape, BF16),
    )


def back(starts, table, ids, gains, lse, gain_b, q, k, v, o, do, resid, rgrad, tok, y_p, out_p, gate_p, up_p, done, lead, n1, first, chunks=2):
    tall, piece = q.shape
    heads = piece // HEAD_DIM
    rows, width = tok.shape
    nseq = tall // rows
    nfsdp = gate_p.shape[0]
    pairs = nfsdp // 2
    lines = -(-(2 * width // 128 + 8 * nseq) // 8) * 8
    qkv_shape = (nfsdp, width // nfsdp, 3 * piece)
    out_shape = out_p.shape
    smem = pl.BlockSpec(memory_space=pltpu.SMEM)

    def full(a):
        return jax.ShapeDtypeStruct((nseq,) + tuple(a), BF16)

    return pl.pallas_call(
        functools.partial(back_kernel, heads, chunks),
        out_shape=(
            jax.ShapeDtypeStruct((lines, 128), F32),
            jax.ShapeDtypeStruct((rows, width), BF16),
            jax.ShapeDtypeStruct((rows, width), BF16),
            full(done.shape),
            full(lead.shape),
            full(gate_p.shape[1:]),
            full(up_p.shape[1:]),
            full(qkv_shape[1:]),
            full(out_shape[1:]),
        ),
        in_specs=[smem, smem] + [vm_spec()] * 9 + [any_spec()] * 11,
        out_specs=(vm_spec(),) + (any_spec(),) * 8,
        scratch_shapes=wires_scratch(6 + 4 * nfsdp + 18 + 3 * chunks + 4 + pairs)
        + [
            pltpu.SemaphoreType.DMA((17,)),
            pltpu.VMEM((5, rows, width), BF16),
            pltpu.VMEM(qkv_shape, BF16),
        ]
        + scatter_scratch(chunks, rows // chunks, width)
        + fsdp_scatter_scratch(gate_p.shape)
        + fsdp_scatter_scratch(up_p.shape)
        + fsdp_scatter_scratch(qkv_shape)
        + fsdp_scatter_scratch(out_shape)
        + [
            pltpu.VMEM(gate_p.shape[1:], BF16),
            pltpu.VMEM(up_p.shape[1:], BF16),
            pltpu.VMEM(qkv_shape[1:], BF16),
            pltpu.VMEM(out_shape[1:], BF16),
            pltpu.VMEM((tall, 3 * piece), BF16),
            pltpu.VMEM((rows, width), BF16),
            pltpu.VMEM((lines, 128), F32),
            pltpu.VMEM((2, lines, 128), F32),
            pltpu.VMEM((3, lines, 128), F32),
            pltpu.VMEM((lines, 128), F32),
            pltpu.VMEM((pairs - 1, lines, 128), F32),
            pltpu.VMEM((8, 128), F32),
        ],
        compiler_params=call_params(5, 64),
        name="back",
    )(starts, table, ids, gains, lse, gain_b, q, k, v, o, do, resid, rgrad, tok, y_p, out_p, gate_p, up_p, done, lead, n1, first)


def unpack_kernel(nseq, nfsdp, heads, *refs):
    srcs, small, outs = refs[:8], refs[8], refs[9:18]
    ga, gb, table, ins, offs = refs[18:23]
    vs, ts = refs[23:31], refs[31:]
    loads = [pltpu.make_async_copy(a, b, ins.at[n]) for n, (a, b) in enumerate(zip(srcs, vs))]
    for a in loads:
        a.start()
    lead_f, gate_f, up_f, down_f, qkv_f, out_f, y, dx = vs
    tq, tk, tv, to, tg, tu, td = ts
    gq, gk, gv, go, gg, gu, gd, gy, gx = outs
    copies = []

    def save(src, dst):
        copies.append(pltpu.make_async_copy(src, dst, offs.at[len(copies)]))
        copies[-1].start()

    block, piece = pack_piece(tg.shape[1], nfsdp, nseq)
    half = nfsdp // 2

    def columns(get):
        parts = []
        for f in range(nfsdp):
            for t in range(nseq):
                size = min(piece, block - t * piece)
                full, f_at = get(f)
                parts.append(full[t, :, f_at * piece : f_at * piece + size].astype(F32))
        return jnp.concatenate(parts, axis=1)

    loads[0].wait()
    loads[1].wait()
    tg[...] = columns(lambda f: (lead_f, f) if f < half else (gate_f, f - half))
    save(tg, gg)
    loads[2].wait()
    tu[...] = columns(lambda f: (up_f, f))
    save(tu, gu)
    loads[3].wait()
    size = down_f.shape[1]
    for t in range(nseq):
        n = min(size, td.shape[0] - t * size)
        td[t * size : t * size + n, :] = down_f[t, :n, :].astype(F32)
    save(td, gd)
    loads[4].wait()
    width = qkv_f.shape[2] // 3
    for n, (dst, out) in enumerate(((tq, gq), (tk, gk), (tv, gv))):
        dst[...] = jnp.concatenate([qkv_f[t, :, n * width : (n + 1) * width] for t in range(nseq)], axis=1).astype(F32)
        save(dst, out)
    loads[5].wait()
    to[...] = jnp.concatenate([out_f[t] for t in range(nseq)], axis=1).astype(F32)
    save(to, go)
    for n, (src, dst) in enumerate(((y, gy), (dx, gx))):
        loads[6 + n].wait()
        save(src, dst)
    where = lax.axis_index("fsdp")
    share = ga.shape[1]
    lines = nfsdp * share // 128
    for n, dst in enumerate((ga, gb)):
        line = jnp.concatenate([small[n * lines + a : n * lines + a + 1, :] for a in range(lines)], axis=1)
        for f in range(nfsdp):

            @pl.when(where == f)
            def _():
                dst[...] = line[:, f * share : (f + 1) * share]

    for t in range(nseq):
        at = 2 * lines + 8 * t
        table[t * heads : (t + 1) * heads, :] = small[at : at + heads, : table.shape[1]]
    for a in copies:
        a.wait()


def unpack(srcs, small, like, blocks_like, table, nfsdp):
    nseq = srcs[0].shape[0]
    share = like[0].shape[0]
    vm = [vm_spec()] * 3
    return pl.pallas_call(
        functools.partial(unpack_kernel, nseq, nfsdp, table.shape[0] // nseq),
        out_shape=tuple(jax.ShapeDtypeStruct(a.shape, F32) for a in like)
        + tuple(jax.ShapeDtypeStruct(a.shape, BF16) for a in blocks_like)
        + (
            jax.ShapeDtypeStruct((1, share), F32),
            jax.ShapeDtypeStruct((1, share), F32),
            jax.ShapeDtypeStruct(table.shape, F32),
        ),
        in_specs=[any_spec()] * 8 + [vm_spec()],
        out_specs=tuple([any_spec()] * 9 + vm),
        scratch_shapes=[pltpu.SemaphoreType.DMA((8,)), pltpu.SemaphoreType.DMA((9,))]
        + [pltpu.VMEM(a.shape, BF16) for a in srcs]
        + [pltpu.VMEM(a.shape, F32) for a in like],
        compiler_params=pltpu.CompilerParams(vmem_limit_bytes=67043328),
        name="unpack",
    )(*srcs, small)


def reversed_ids(bucket_ids):
    span = bucket_ids.shape[0]
    ids = jnp.concatenate([bucket_ids[::-1], jnp.full((1,), -1, jnp.int32)])
    return ids[None, :]


def dot32(a, b):
    return jnp.dot(a, b, preferred_element_type=F32)


def dot_tn(a, b):
    return lax.dot_general(a, b, (((0,), (0,)), ((), ())), preferred_element_type=F32)


def gelu_both(u):
    inner = 0.7978845608028654 * (u + 0.044715 * u * u * u)
    t = jnp.tanh(inner)
    value = 0.5 * u * (1.0 + t)
    slope = 0.5 * (1.0 + t) + 0.5 * u * (1.0 - t * t) * 0.7978845608028654 * (1.0 + 3 * 0.044715 * u * u)
    return value, slope


def body(
    tokens,
    out_grad,
    attn_gain,
    w_query,
    w_key,
    w_value,
    w_out,
    mix_gain,
    w_gate,
    w_up,
    w_down,
    rel_table,
    bucket_ids,
    cont_start,
):
    nseq = lax.axis_size("seq")
    nfsdp = lax.axis_size("fsdp")
    inner = w_query.shape[1]

    ids = reversed_ids(bucket_ids)
    starts = cont_start[0]
    (
        lse,
        gains,
        query,
        keys,
        values,
        mixed,
        mixed_rows,
        resid,
        normed,
        first,
        out_w,
        _,
        gate_w,
        up_w,
        down_w,
        normed_two,
        hidden,
        gate_grad,
        up_grad,
        down_grad,
    ) = forward(
        starts,
        rel_table.T,
        ids,
        jnp.stack([attn_gain.astype(F32), mix_gain.astype(F32)]),
        tokens[0],
        w_query,
        w_key,
        w_value,
        w_out,
        w_gate,
        w_up,
        w_down,
        out_grad[0],
        nseq,
        nfsdp,
    )
    out_w = out_w.reshape(nseq, inner, -1)
    resid_grad, mixed_grad, gain_two_grad, down_grad, lead_grad, out_w_grad, gate_w_grad, up_w_grad, result = unmix(
        gains, mixed_rows, resid, out_grad[0], blocks(down_grad.reshape(-1, down_grad.shape[2]), 2 * nfsdp), gate_grad, up_grad, gate_w, up_w, out_w, normed_two, hidden, down_w
    )
    down_grad = down_grad.reshape(-1, down_grad.shape[2])
    small, block_out, in_grad, down_grad, lead_grad, gate_w_grad, up_w_grad, qkv_grad, out_w_grad = back(
        starts,
        rel_table.T,
        ids,
        gains,
        lse,
        gain_two_grad,
        query,
        keys,
        values,
        mixed,
        mixed_grad,
        resid,
        resid_grad,
        tokens[0],
        result,
        out_w_grad,
        gate_w_grad,
        up_w_grad,
        down_grad,
        lead_grad,
        normed,
        first,
    )
    *shards, block_out, in_grad, gain_one_share, gain_two_share, table_grad = unpack(
        (lead_grad, gate_w_grad, up_w_grad, down_grad, qkv_grad, out_w_grad, block_out, in_grad),
        small,
        (w_query, w_key, w_value, w_out, w_gate, w_up, w_down),
        (block_out, in_grad),
        rel_table.T,
        nfsdp,
    )
    return (
        block_out[None],
        in_grad[None],
        gain_one_share[0],
        *shards[:4],
        gain_two_share[0],
        *shards[4:],
        table_grad.T,
    )


def solution(mesh):
    placed = (
        P("fsdp", "seq", None),
        P("fsdp", "seq", None),
        P("fsdp"),
        P("fsdp", None),
        P("fsdp", None),
        P("fsdp", None),
        P("fsdp", None),
        P("fsdp"),
        P("fsdp", None),
        P("fsdp", None),
        P("fsdp", None),
        P(),
        P(),
        P("fsdp", None),
    )
    results = placed[:1] * 2 + placed[2:11] + (P(),)
    return jax.shard_map(body, mesh=mesh, in_specs=placed, out_specs=results, check_vma=False)
```

```python
import functools
import jax
import jax.numpy as jnp
from jax import lax
from jax.experimental import pallas as pl
from jax.experimental.pallas import tpu as pltpu
from jax.sharding import PartitionSpec as P

HEAD_DIM = 64
PROMPT = 1024
CL = 256
F32 = jnp.float32
BF16 = jnp.bfloat16
MESH = pl.DeviceIdType.MESH
epsilon = 1e-06
STRIP = 2 * PROMPT - 128
FARW = PROMPT - 128 + CL
KC = 256


def nt(a, b):
    return lax.dot_general(a, b, (((1,), (1,)), ((), ())), preferred_element_type=F32)


def nn(a, b):
    return lax.dot_general(a, b, (((1,), (0,)), ((), ())), preferred_element_type=F32)


class Wires:
    def __init__(self, send, recv):
        self.send, self.recv, self.used = send, recv, 0

    def take(self, count):
        self.used += count
        return self.used - count

    def at(self, i, src, dst, where):
        return pltpu.make_async_remote_copy(
            src_ref=src,
            dst_ref=dst,
            send_sem=self.send.at[i],
            recv_sem=self.recv.at[i],
            device_id=where,
            device_id_type=MESH,
        )

    def go(self, src, dst, where):
        c = self.at(self.take(1), src, dst, where)
        c.start()
        return c


def seq_places():
    s = lax.axis_index("seq")
    near = s + 1 - 2 * lax.rem(s, 2)
    far = lax.rem(s + 2, 4)
    cross = lax.rem(near + 2, 4)
    return s, near, far, cross


def greet(places):
    barrier = pltpu.get_barrier_semaphore()
    for where in places:
        pl.semaphore_signal(barrier, inc=1, device_id=where, device_id_type=MESH)


def meet(places):
    greet(places)
    pl.semaphore_wait(pltpu.get_barrier_semaphore(), len(places))


def rows_at(index, rows, offset=0, count=None):
    return pl.ds(pl.multiple_of(index * rows + offset, 16), rows if count is None else count)


class SeqGather:
    def __init__(self, wires, out_at, chunks):
        self.wires, self.out_at, self.chunks = wires, out_at, chunks
        self.s, self.near, self.far, self.cross = seq_places()
        self.base = wires.take(3 * chunks)

    def trip(self, kind, c, src=None):
        view = self.out_at(self.far if kind == 2 else self.s, c)
        where = {"seq": self.far if kind == 0 else self.near}
        return self.wires.at(self.base + 3 * c + kind, view if src is None else src, view, where)

    def send(self, c, src):
        self.trip(0, c, src).start()
        self.trip(1, c, src).start()

    def forward(self, c):
        self.trip(0, c).wait_recv()
        self.trip(2, c).start()

    def got_near(self, c):
        self.trip(1, c).wait_recv()

    def got_cross(self, c):
        self.trip(2, c).wait_recv()

    def drain(self):
        for c in range(self.chunks):
            for kind in range(3):
                self.trip(kind, c).wait_send()

    def finish(self):
        for c in range(self.chunks):
            self.got_near(c)
            self.got_cross(c)
        self.drain()


def fsdp_places():
    f = lax.axis_index("fsdp")
    return f // 2, lax.rem(f, 2), lax.axis_size("fsdp") // 2


def far_first(k):
    pair, _, pairs = fsdp_places()
    if pairs != 4:
        return k + 1
    first, second = 3 - (pair + 1) // 2, 1 + lax.rem(pair + 1, 3)
    return (first, second, 6 - first - second)[k]


def fsdp_peers():
    pair, side, pairs = fsdp_places()
    peers = [{"fsdp": lax.rem(pair + d, pairs) * 2 + side} for d in range(1, pairs)]
    return peers + [{"fsdp": pair * 2 + 1 - side}]


class FsdpGather:
    def __init__(self, wires, shard, full_at, local):
        self.wires, self.shard, self.full_at, self.local = wires, shard, full_at, local
        self.pair, self.side, self.pairs = fsdp_places()
        self.base = wires.take(2 * self.pairs)

    def source(self, d):
        return lax.rem(self.pair + self.pairs - d, self.pairs)

    def over(self):
        own = self.full_at(self.pair * 2 + self.side)
        return self.wires.at(self.base, self.shard, own, {"fsdp": self.pair * 2 + 1 - self.side})

    def out(self, d):
        own = self.full_at(self.pair * 2 + self.side)
        where = {"fsdp": lax.rem(self.pair + d, self.pairs) * 2 + self.side}
        return self.wires.at(self.base + d, self.shard, own, where)

    def onward(self, d):
        view = self.full_at(self.source(d) * 2 + self.side)
        return self.wires.at(self.base + self.pairs + d, view, view, {"fsdp": self.pair * 2 + 1 - self.side})

    def keep(self):
        return pltpu.make_async_copy(self.shard, self.full_at(self.pair * 2 + self.side), self.local)

    def start(self):
        for k in range(self.pairs - 1):
            self.out(k + 1).start()
        self.keep().start()

    def forward(self, k):
        self.out(k).wait_recv()
        self.onward(k).start()

    def complete(self, k):
        if k == 0:
            self.keep().wait()
            self.over().wait_recv()
        else:
            self.onward(k).wait_recv()

    def drain(self):
        self.over().wait_send()
        for d in range(1, self.pairs):
            self.out(d).wait_send()
            self.onward(d).wait_send()

    def finish(self):
        for k in range(self.pairs):
            self.complete(k)
        self.drain()


def gather_halves(wires, shard, full, size, local):
    half, wide = size // 2, shard.shape[1] // 2

    def one(n):
        if size % 32 == 0:
            rows = pl.ds(n * half, half)
            return FsdpGather(wires, shard.at[rows, :], lambda f: full.at[shard_rows(2 * f + n, half), :], local[n])
        cut = slice(n * wide, (n + 1) * wide)
        return FsdpGather(wires, shard.at[:, cut], lambda f: full.at[shard_rows(f, size), cut], local[n])

    return [one(0), one(1)]


class FsdpScatter:
    def __init__(self, wires, parts, bufs, result):
        self.wires, self.parts_at, self.result = wires, parts if callable(parts) else lambda f: parts.at[f], result
        self.mine, self.got, self.landed, self.local = bufs
        self.pair, self.side, self.pairs = fsdp_places()
        self.base = wires.take(2 * self.pairs)

    def step_to(self, k):
        return far_first(k) if k < self.pairs - 1 else 0

    def owner(self, d):
        return lax.rem(self.pair + d, self.pairs) * 2

    def load(self, k):
        part = self.parts_at(self.owner(self.step_to(k)) + self.side)
        return pltpu.make_async_copy(part, self.mine.at[k % 2], self.local.at[k % 2])

    def swap(self, d):
        src = self.parts_at(self.owner(d) + 1 - self.side)
        return self.wires.at(self.base + d, src, self.got.at[d], {"fsdp": self.pair * 2 + 1 - self.side})

    def onward(self, d):
        where = {"fsdp": self.owner(d) + self.side}
        return self.wires.at(self.base + self.pairs + d, self.got.at[d], self.landed.at[d - 1], where)

    def start(self):
        for k in range(self.pairs):
            self.swap(self.step_to(k)).start()
        self.load(0).start()

    def step(self, k):
        d = self.step_to(k - 1)
        self.load(k).start()
        self.load(k - 1).wait()
        self.swap(d).wait_recv()
        self.got[d] = (self.mine[(k - 1) % 2].astype(F32) + self.got[d].astype(F32)).astype(BF16)
        self.onward(d).start()

    def finish(self):
        self.load(self.pairs - 1).wait()
        self.swap(0).wait_recv()
        total = self.mine[(self.pairs - 1) % 2].astype(F32) + self.got[0].astype(F32)
        for d in range(1, self.pairs):
            self.onward(d).wait_recv()
            total = total + self.landed[d - 1].astype(F32)
        self.result[...] = total.astype(BF16)

    def drain(self):
        for d in range(self.pairs):
            self.swap(d).wait_send()
        for d in range(1, self.pairs):
            self.onward(d).wait_send()


def fsdp_scatter_scratch(shape):
    pairs = shape[0] // 2
    return [
        pltpu.VMEM((2,) + shape[1:], BF16),
        pltpu.VMEM((pairs,) + shape[1:], BF16),
        pltpu.VMEM((pairs - 1,) + shape[1:], BF16),
        pltpu.SemaphoreType.DMA((2,)),
    ]


def blocks(a, count):
    return a.reshape((count, a.shape[0] // count) + a.shape[1:])


def shard_rows(f, size):
    return pl.ds(pl.multiple_of(f * size, 16 if size % 16 == 0 else 8 if size % 8 == 0 else size), size)


def vm_spec():
    return pl.BlockSpec(memory_space=pltpu.VMEM)


def any_spec():
    return pl.BlockSpec(memory_space=pl.ANY)


def wires_scratch(n):
    return [pltpu.SemaphoreType.DMA((n,)), pltpu.SemaphoreType.DMA((n,))]


def call_params(number, vmem=60):
    return pltpu.CompilerParams(collective_id=number, has_side_effects=True, vmem_limit_bytes=min(vmem << 20, 67043328))


def inverse_rms(v):
    return lax.rsqrt(jnp.mean(v * v, axis=-1, keepdims=True) + epsilon)


def norm_back(grad, v, r, gain):
    scaled = grad * gain
    return r * scaled - v * (r * r * r) * jnp.mean(v * scaled, axis=-1, keepdims=True)


class SeqScatter:
    def __init__(self, wires, chunks, *bufs):
        self.s, self.near, self.far, self.cross = seq_places()
        self.wires, self.chunks, self.bufs = wires, chunks, bufs
        self.base = wires.take(3 * chunks)

    def trip(self, kind, c):
        where = {"seq": self.far if kind == 1 else self.near}
        src, dst = self.bufs[2 * kind].at[c], self.bufs[2 * kind + 1].at[c]
        return self.wires.at(self.base + 3 * c + kind, src, dst, where)

    def cross_chunk(self, c, value):
        self.bufs[0][c] = value.astype(BF16)
        self.trip(0, c).start()

    def far_chunk(self, c, value):
        self.trip(0, c).wait_recv()
        self.bufs[2][c] = (value + self.bufs[1][c].astype(F32)).astype(BF16)
        self.trip(1, c).start()

    def near_chunk(self, c, value):
        self.bufs[4][c] = value.astype(BF16)
        self.trip(2, c).start()

    def own_chunk(self, c, value):
        self.trip(2, c).wait_recv()
        self.trip(1, c).wait_recv()
        return value + self.bufs[5][c].astype(F32) + self.bufs[3][c].astype(F32)

    def finish(self):
        for c in range(self.chunks):
            for kind in range(3):
                self.trip(kind, c).wait_send()


def scatter_scratch(chunks, rows, width):
    return [pltpu.VMEM((chunks, rows, width), BF16)] * 6


def unmix_kernel(
    chunks, gains, obuf, resid, cot, down_p, dg_h, du_h, gate_h, up_h, out_h, n2_h, hid_h, dw_h,
    rgrad_h, dmix_h, ggrad, shard, lead_s, out_p, gate_p, up_p, y_h,
    send, recv, b0, b1, b2, b3, b4, b5, attn, dob, p0, p1, p2, p3, r0, r1, r2, r3, l0, l1, l2, l3, lead_p,
    local, dg, du, gate_w, up_w, out_w, n2, hid, down_w, wgrad, wbuf, stage, ystage, sems, rgrad, dmix,
):
    rows, width = resid.shape
    nseq, _, piece = obuf.shape
    nfsdp = gate_p.shape[0]
    units = dg.shape[1]
    first_half = units // 2
    s, near, far, cross = seq_places()
    loads = [
        pltpu.make_async_copy(src, dst, local.at[n])
        for n, (src, dst) in enumerate(
            (
                (gate_h, gate_w),
                (up_h, up_w),
                (dg_h, dg),
                (du_h, du),
                (n2_h, n2),
                (out_h, out_w),
                (hid_h, hid),
                (dw_h, down_w),
            )
        )
    ]
    for a in loads:
        a.start()
    meet([{"seq": near}, {"seq": far}, {"seq": cross}] + fsdp_peers())
    wires = Wires(send, recv)
    def down_half(n, bufs):
        return FsdpScatter(wires, lambda f: down_p.at[2 * f + n], bufs, shard.at[n])

    grads = [down_half(0, (p0, p1, p2, p3)), down_half(1, (r0, r1, r2, r3))]
    for a in grads:
        a.start()
    leads = FsdpScatter(wires, lead_p, (l0, l1, l2, l3), lead_s)
    pairs = leads.pairs
    sums = SeqScatter(wires, chunks, b0, b1, b2, b3, b4, b5)
    size = rows // chunks
    for a in loads[:4]:
        a.wait()

    def part(t, c):
        at = rows_at(t, rows, c * size, size)
        return nt(dg[at, :], gate_w[...]) + nt(du[at, :], up_w[...])

    for c in range(chunks):
        sums.cross_chunk(c, part(cross, c))
    grads[0].step(1)
    for c in range(chunks):
        sums.far_chunk(c, part(far, c))
    for d in range(2, pairs - 1):
        grads[0].step(d)
    for c in range(chunks):
        sums.near_chunk(c, part(near, c))
    if pairs > 2:
        grads[0].step(pairs - 1)
    for c in range(chunks):
        rgrad[c * size : (c + 1) * size, :] = part(s, c)
    loads[4].wait()
    depth = width // nfsdp
    wide = 384
    saves = []

    def weight_parts(side, out, begin, end, cut):
        for n in range(begin, end):
            slot = n % 2
            group = pl.ds(n * (wide // depth), wide // depth)
            if len(saves) > 1:
                saves[-2].wait()
            got = dot_tn(n2[:, n * wide : (n + 1) * wide], side[...])
            for m in range(wide // depth):
                low = got[m * depth : (m + 1) * depth, :].astype(BF16)
                if cut:
                    lead_p[n * (wide // depth) + m] = low[:, :cut]
                stage[slot, m, :, : units - cut] = low[:, cut:]
            a = pltpu.make_async_copy(stage.at[slot, :, :, : units - cut], out.at[group], sems.at[3 + slot])
            a.start()
            saves.append(a)

    weight_parts(dg, gate_p, 0, width // wide, first_half)
    grads[1].step(1)
    loads[5].wait()
    cols = out_w.shape[2]

    def own_rows(c, total):
        at = slice(c * size, (c + 1) * size)
        dn = sums.own_chunk(c, rgrad[at, :])
        h = resid[at, :]
        r = inverse_rms(h)
        rg = cot[at, :].astype(F32) + norm_back(dn, h, r, gains[1:2, :])
        rgrad[at, :] = rg
        low = rg.astype(BF16)
        attn[at, :] = low
        for t in range(nseq):
            acc = jnp.zeros((size, piece), F32)
            for u in range(nseq):
                acc = acc + nt(low[:, u * cols : (u + 1) * cols], out_w[u, t * piece : (t + 1) * piece, :])
            dob[t, at, :] = acc.astype(BF16)
        return total + jnp.sum(dn * h * r, axis=0, keepdims=True)

    base = wires.take(3 * chunks)

    def trip(n, t, c):
        at = pl.ds(c * size, size)
        return wires.at(base + 3 * c + n, dob.at[t, at, :], dmix.at[rows_at(s, rows, c * size, size), :], {"seq": t})

    total = jnp.zeros((1, width), F32)
    for c in range(chunks):
        total = own_rows(c, total)
        if c == 0:
            leads.start()
            weight_parts(du, up_p, 0, 1, 0)
            for d in range(2, pairs - 1):
                grads[1].step(d)
        for n, t in enumerate((far, cross, near)):
            trip(n, t, c).start()
        dmix[rows_at(s, rows, c * size, size), :] = dob[s, pl.ds(c * size, size), :]
        if c == 0:
            weight_parts(du, up_p, 1, width // wide, 0)
            if pairs > 2:
                grads[1].step(pairs - 1)
    ggrad[...] = jnp.broadcast_to(total, ggrad.shape)
    rsave = pltpu.make_async_copy(rgrad, rgrad_h, sems.at[2])
    rsave.start()
    leads.step(1)
    wbase = wires.take(3)

    def wtrip(n):
        u = (cross, far, near)[n]
        return wires.at(wbase + n, wgrad.at[u], wbuf.at[n], {"seq": far if n == 1 else near})

    def wblock(u):
        for t in range(nseq):
            at = pl.ds(pl.multiple_of(u * cols, 128), cols)
            wgrad[u, t * piece : (t + 1) * piece, :] = dot_tn(obuf[t], attn[:, at]).astype(BF16)

    wblock(cross)
    wblock(far)
    wtrip(0).start()
    for d in range(2, pairs - 1):
        leads.step(d)
    wblock(near)
    wtrip(0).wait_recv()
    wgrad[far] = (wgrad[far].astype(F32) + wbuf[0].astype(F32)).astype(BF16)
    wblock(s)
    wtrip(1).start()
    wtrip(2).start()
    for a in loads[6:]:
        a.wait()
    ycopies = []
    for t in range(nseq):
        slot = t % 2
        if t > 1:
            ycopies[t - 2].wait()
        at = slice(t * rows, (t + 1) * rows)
        ystage[slot] = nn(hid[at, :], down_w[...]).astype(BF16)
        ycopies.append(pltpu.make_async_copy(ystage.at[slot], y_h.at[at, :], sems.at[slot]))
        ycopies[t].start()
        if t == 1:
            leads.step(pairs - 1)
    for c in range(chunks):
        for n, t in enumerate((far, cross, near)):
            trip(n, t, c).wait()
    dsave = pltpu.make_async_copy(dmix, dmix_h, local.at[8])
    dsave.start()
    for a in grads:
        a.finish()
    for n in range(1, 3):
        wtrip(n).wait_recv()
    wsum = wgrad[s].astype(F32) + wbuf[1].astype(F32) + wbuf[2].astype(F32)
    lines = out_p.shape[1]
    for f in range(nfsdp):
        out_p[f] = wsum[f * lines : (f + 1) * lines, :].astype(BF16)
    for n in range(3):
        wtrip(n).wait_send()
    sums.finish()
    for a in grads:
        a.drain()
    leads.finish()
    leads.drain()
    for a in saves[-2:]:
        a.wait()
    for a in ycopies[-2:] + [rsave, dsave]:
        a.wait()


def unmix(gains, obuf, resid, cot, down_p, dg, du, gate_w, up_w, out_w, n2, hid, down_w, chunks=2):
    rows, width = resid.shape
    nseq, _, piece = obuf.shape
    nfsdp = down_p.shape[0] // 2
    units = dg.shape[1]
    grad_shape = (nfsdp, width // nfsdp, units)
    half_shape = (nfsdp, width // nfsdp, units // 2)
    return pl.pallas_call(
        functools.partial(unmix_kernel, chunks),
        out_shape=(
            jax.ShapeDtypeStruct((rows, width), F32),
            jax.ShapeDtypeStruct((nseq * rows, piece), BF16),
            jax.ShapeDtypeStruct((8, width), F32),
            jax.ShapeDtypeStruct((2,) + down_p.shape[1:], BF16),
            jax.ShapeDtypeStruct(half_shape[1:], BF16),
            jax.ShapeDtypeStruct((nfsdp, out_w.shape[1] // nfsdp, out_w.shape[2]), BF16),
            jax.ShapeDtypeStruct(half_shape, BF16),
            jax.ShapeDtypeStruct(grad_shape, BF16),
            jax.ShapeDtypeStruct(n2.shape, BF16),
        ),
        in_specs=[vm_spec()] * 4 + [any_spec()] * 9,
        out_specs=(any_spec(),) * 2 + (vm_spec(),) * 4 + (any_spec(),) * 3,
        scratch_shapes=wires_scratch(6 * chunks + 3 * nfsdp + 3)
        + scatter_scratch(chunks, rows // chunks, width)
        + [pltpu.VMEM((rows, width), BF16), pltpu.VMEM((nseq, rows, piece), BF16)]
        + fsdp_scatter_scratch((nfsdp,) + down_p.shape[1:]) * 2
        + fsdp_scatter_scratch(half_shape)
        + [
            pltpu.VMEM(half_shape, BF16),
            pltpu.SemaphoreType.DMA((9,)),
            pltpu.VMEM(dg.shape, BF16),
            pltpu.VMEM(du.shape, BF16),
            pltpu.VMEM(gate_w.shape, BF16),
            pltpu.VMEM(up_w.shape, BF16),
            pltpu.VMEM(out_w.shape, BF16),
            pltpu.VMEM(n2.shape, BF16),
            pltpu.VMEM(hid.shape, BF16),
            pltpu.VMEM(down_w.shape, BF16),
            pltpu.VMEM(out_w.shape, BF16),
            pltpu.VMEM((3,) + out_w.shape[1:], BF16),
            pltpu.VMEM((2, 384 * nfsdp // width, width // nfsdp, units), BF16),
            pltpu.VMEM((2, rows, width), BF16),
            pltpu.SemaphoreType.DMA((5,)),
            pltpu.VMEM((rows, width), F32),
            pltpu.VMEM((nseq * rows, piece), BF16),
        ],
        compiler_params=call_params(4, 63),
        name="unmix",
    )(gains, obuf, resid, cot, down_p, dg, du, gate_w, up_w, out_w, n2, hid, down_w)


def build_strips(heads, first_head, starts, table, ids, strip, far):
    length = ids.shape[1]
    half = 2 * PROMPT
    for h in range(heads):
        row = jnp.zeros(ids.shape, F32)
        for b in range(table.shape[1]):
            row = jnp.where(ids[...] == b, table[first_head + h, b], row)
        row = jnp.broadcast_to(row, (8, length))
        base = jnp.broadcast_to(row[:1, PROMPT // 2 : PROMPT // 2 + half], (128, half))
        strip[h] = pltpu.roll(base, 1, 1, stride=1, stride_axis=0)[:, 128:]
        for c in range(2):
            moved = pltpu.roll(row, length - PROMPT // 2 - starts[c], 1)
            base = jnp.broadcast_to(moved[:1, : FARW + 128], (128, FARW + 128))
            far[h, c] = pltpu.roll(base, 1, 1, stride=1, stride_axis=0)[:, 128:]


def head_masks(width, heads):
    lane = lax.broadcasted_iota(jnp.int32, (1, width), 1)
    return [(lane >= h * HEAD_DIM) & (lane < (h + 1) * HEAD_DIM) for h in range(heads)]


def masked_copies(src, dst, heads):
    masks = head_masks(src.shape[1], heads)
    for h in range(heads):
        dst[h] = jnp.where(masks[h], src[...], jnp.zeros((), src.dtype))


def bias_chunk(strip, far, h, first_q, kstart, kind, c):
    parts = []
    for r in range(KC // 128):
        m = PROMPT - 128 - (kstart + 128 * r)
        if kind == "far":
            parts.append(far[h, c, :, m : m + CL])
        else:
            parts.append(strip[h, :, pl.ds(pl.multiple_of(first_q + m, 128), CL)])
    return jnp.concatenate(parts, axis=0)


def pack_piece(units, nfsdp, nseq):
    block = units // nfsdp
    return block, -(-block // (16 * nseq)) * 16


def pack_front(t, raw, first_q, out_q, gains):
    r_q, r_k, r_v, r_o = raw
    piece = first_q.shape[1] * 3 // 10
    depth = first_q.shape[0]
    cut = slice(t * piece, (t + 1) * piece)
    first_q[...] = jnp.concatenate(
        [r_q[:, cut], r_k[:, cut], r_v[:, cut], gains, jnp.zeros((depth, first_q.shape[1] - 3 * piece - 8), BF16)], axis=1
    )
    cols = out_q.shape[1]
    out_q[...] = r_o[:, t * cols : (t + 1) * cols]


def pack_cols(t, nseq, nfsdp, raw, packed):
    block, piece = pack_piece(raw.shape[1], nfsdp, nseq)
    pieces = []
    for f in range(nfsdp):
        begin = f * block + t * piece
        end = min(begin + piece, (f + 1) * block)
        pieces.append(raw[:, begin:end])
        if end - begin < piece:
            pieces.append(jnp.zeros((raw.shape[0], piece - end + begin), BF16))
    packed[...] = jnp.concatenate(pieces, axis=1)


def pack_down(t, raw, packed):
    piece = packed.shape[0]
    begin = t * piece
    end = min(begin + piece, raw.shape[0])
    packed[: end - begin, :] = raw[begin:end, :]
    if end - begin < piece:
        packed[end - begin :, :] = jnp.zeros((piece - end + begin, raw.shape[1]), BF16)


def forward_kernel(
    heads, nseq, starts, table, ids, gain_q, tok_h, w_q, w_k, w_v, w_o, w_g, w_u, w_d, cot_q,
    lse, gains, q_h, k_h, v_h, o_h, obuf_h, resid_h,
    n1_h, first_h, out_h, cot_h, gate_h, up_h, down_h, n2_h, hid_h, dg_h, du_h, parts_h,
    send, recv, local, first_q, out_q, gate_q, up_q, down_q, group, first, gate_w, up_w, down_w, tok, fsems, spare, q, k, v, o, obuf, resid, osems,
):
    rows, width = tok.shape
    units = gate_w.shape[1]
    piece = q.shape[1]
    mine, near, other, cross = seq_places()
    pair, side, pairs = fsdp_places()
    nfsdp = 2 * pairs
    half = rows // 2
    wires = Wires(send, recv)
    ring = SeqGather(wires, lambda t, c: group.at[rows_at(t, rows, c * half, half), :], 2)
    size = first_q.shape[0]
    lead = FsdpGather(wires, first_q, lambda f: first.at[shard_rows(f, size), :], local.at[7])
    late = FsdpGather(wires, out_q, lambda f: out_h.at[mine, f], local.at[8])
    gates = gather_halves(wires, gate_q, gate_w, gate_q.shape[0], (local.at[9], local.at[10]))
    ups = gather_halves(wires, up_q, up_w, up_q.shape[0], (local.at[11], local.at[12]))
    downs = gather_halves(wires, down_q, down_w, down_q.shape[0], (local.at[13], local.at[14]))
    wring = SeqGather(wires, lambda t, c: out_h.at[t], 1)
    cring = SeqGather(wires, lambda t, c: cot_h.at[rows_at(t, rows, c * half, half), :], 2)
    nring = SeqGather(wires, lambda t, c: group.at[rows_at(t, rows, c * half, half), :], 2)
    obase = wires.take(3)
    own = [
        pltpu.make_async_copy(tok_h, group.at[rows_at(mine, rows), :], local.at[15]),
        pltpu.make_async_copy(cot_q, cot_h.at[rows_at(mine, rows), :], local.at[16]),
        pltpu.make_async_copy(tok_h, tok, local.at[17]),
    ]

    def begin(r_q, r_k, r_v, r_o, r_g, r_u, r_d):
        loads = [
            pltpu.make_async_copy(src, dst, local.at[n])
            for n, (src, dst) in enumerate(
                ((w_q, r_q), (w_k, r_k), (w_v, r_v), (w_o, r_o), (w_g, r_g), (w_u, r_u), (w_d, r_d))
            )
        ]
        for a in loads:
            a.start()
        peers = [{"seq": near}, {"seq": other}, {"seq": cross}] + fsdp_peers()
        greet(peers)
        for a in own:
            a.start()
        for a in loads[:4]:
            a.wait()
        both = jnp.concatenate([gain_q[...], jnp.zeros((6, gain_q.shape[1]), F32)], axis=0).T.astype(BF16)
        for t in range(nseq):

            @pl.when(mine == t)
            def _():
                pack_front(t, (r_q, r_k, r_v, r_o), first_q, out_q, both)

        pl.semaphore_wait(pltpu.get_barrier_semaphore(), len(peers))
        for c in range(2):
            ring.send(c, tok_h.at[pl.ds(c * half, half), :])
        lead.over().start()
        lead.start()
        for a in loads[4:]:
            a.wait()
        for t in range(nseq):

            @pl.when(mine == t)
            def _():
                pack_cols(t, nseq, nfsdp, r_g, gate_q)

        late.over().start()
        late.start()
        for t in range(nseq):

            @pl.when(mine == t)
            def _():
                pack_cols(t, nseq, nfsdp, r_u, up_q)
                pack_down(t, r_d, down_q)

    pl.run_scoped(begin, *[pltpu.VMEM(a.shape, BF16) for a in (w_q, w_k, w_v, w_o, w_g, w_u, w_d)])
    halves = gates + ups + downs
    for a in halves[:2]:
        a.over().start()
    for a in halves:
        a.start()

    def advance(n, d):
        halves[n].forward(d)
        if d == max(pairs - 2, 1) and n + 2 < len(halves):
            pass

    cring.send(0, cot_q.at[pl.ds(0, half), :])

    early_saves = []

    def attend(n1, strip, far, kh, vt, ot, s):
        build_strips(heads, mine * heads, starts, table, ids, strip, far)
        lse[...] = jnp.zeros(lse.shape, F32)
        for d in range(1, pairs):
            lead.forward(d)
            if d == pairs // 2:
                ring.forward(0)
        for d in range(1, pairs):
            late.forward(d)
        for a in halves[2:]:
            a.over().start()
        ring.forward(1)
        lead.finish()
        saves = [pltpu.make_async_copy(first, first_h, local.at[0])]
        saves[0].start()
        column = 3 * piece
        gains[...] = jnp.zeros(gains.shape, F32)
        for b in range(width // 256):
            base = column // 128 * 128
            band = first[b * 256 : (b + 1) * 256, base : base + 128].astype(F32).T
            for n in range(2):
                line = column - base + n
                gains[n : n + 1, b * 256 : (b + 1) * 256] = band[line : line + 1, :]

        def project(t):
            at = rows_at(t, rows)
            x = group[at, :].astype(F32)
            low = (x * inverse_rms(x) * gains[0:1, :]).astype(BF16)
            n1[at, :] = low
            r = nn(low, first[:, :column])
            q[at, :] = r[:, :piece].astype(BF16)
            k[at, :] = r[:, piece : 2 * piece].astype(BF16)
            v[at, :] = r[:, 2 * piece :].astype(BF16)

        own[0].wait()
        project(mine)
        for c in range(2):
            ring.got_near(c)
        project(near)
        project(other)
        for c in range(2):
            ring.got_cross(c)
        project(cross)
        saves.append(pltpu.make_async_copy(n1, n1_h, local.at[1]))
        saves[1].start()
        for d in range(pairs):
            late.complete(d)
        wring.send(0, out_h.at[mine])
        cring.send(1, cot_q.at[pl.ds(half, half), :])
        masked_copies(k, kh, heads)
        vt[...] = v[...].astype(F32).T.astype(BF16)

        def block(h, q0, bias_q0, chunks, c):
            qb = q[pl.ds(q0, CL), :]
            top = None
            for n, (k0, kind, kstart) in enumerate(chunks):
                sc = nt(kh[h, pl.ds(k0, KC), :], qb) + bias_chunk(strip, far, h, bias_q0, kstart, kind, c)
                s[n * KC : (n + 1) * KC, :] = sc
                m = jnp.max(sc, axis=0, keepdims=True)
                top = m if top is None else jnp.maximum(top, m)
            total = jnp.zeros((1, CL), F32)
            acc = jnp.zeros((HEAD_DIM, CL), F32)
            lines = pl.ds(pl.multiple_of(h * HEAD_DIM, HEAD_DIM), HEAD_DIM)
            for n, (k0, kind, kstart) in enumerate(chunks):
                e = jnp.exp(s[n * KC : (n + 1) * KC, :] - top)
                total = total + jnp.sum(e, axis=0, keepdims=True)
                acc = acc + nn(vt[lines, pl.ds(k0, KC)], e.astype(BF16))
            ot[lines, pl.ds(q0, CL)] = acc / total
            lse[pl.ds(h, 1), pl.ds(q0, CL)] = top + jnp.log(total)

        nblk = PROMPT // CL
        steps = [(n, d) for n in range(2) for d in range(1, pairs)]
        early, later, final = steps[: pairs - 1], steps[pairs - 1 : -1], steps[-1:]

        def prompt_body(i, carry):
            h, blk = i // nblk, i % nblk
            q0 = pl.multiple_of(blk * CL, CL)
            block(h, q0, q0, [(j * KC, "strip", j * KC) for j in range(PROMPT // KC)], None)
            for n, step in enumerate(early):

                @pl.when(i == max((heads * nblk - 2) * (n + 1) // len(early) - 2, 0))
                def _():
                    advance(*step)

            return carry

        def cont_body(i, carry):
            h, c = i // 2, i % 2
            q0 = pl.multiple_of(PROMPT + c * CL, CL)
            chunks = [(j * KC, "far", j * KC) for j in range(PROMPT // KC)]
            chunks += [(q0 + j * KC, "strip", j * KC) for j in range(CL // KC)]
            block(h, q0, 0, chunks, c)
            for n, step in enumerate(later):

                @pl.when(i == max(2 * heads * (n + 1) // len(later) - 1, 0))
                def _():
                    advance(*step)

            return carry

        lax.fori_loop(0, heads * nblk, prompt_body, 0)
        cring.forward(0)
        lax.fori_loop(0, heads * 2, cont_body, 0)
        o[...] = ot[...].T.astype(BF16)
        for n, (a, b) in enumerate(((q, q_h), (k, k_h), (v, v_h), (o, o_h))):
            early_saves.append(pltpu.make_async_copy(a, b, osems.at[n]))
            early_saves[n].start()
        ring.drain()
        for n, t in enumerate((other, cross, near)):
            wires.at(obase + n, o.at[rows_at(t, rows), :], obuf.at[mine], {"seq": t}).start()
        obuf[mine] = o[rows_at(mine, rows), :]
        wring.forward(0)
        for step in final:
            advance(*step)
        for a in saves:
            a.wait()

    tall = nseq * rows
    pl.run_scoped(
        attend,
        pltpu.VMEM((tall, width), BF16),
        pltpu.VMEM((heads, 128, STRIP), F32),
        pltpu.VMEM((heads, 2, 128, FARW), F32),
        pltpu.VMEM((heads, tall, piece), BF16),
        pltpu.VMEM((piece, tall), BF16),
        pltpu.VMEM((piece, tall), F32),
        pltpu.VMEM((PROMPT + CL, CL), F32),
    )
    todo = [(n, d) for n in range(2, 6) for d in range(1, pairs)]

    def pass_on(share):
        while todo and len(todo) > round((1 - share) * 4 * (pairs - 1)):
            advance(*todo.pop(0))

    def feed(out_w, cot, ga, ub, hid, dg, du, parts):
        cols = out_w.shape[2]
        wring.got_near(0)
        wring.got_cross(0)
        lines = w_o.shape[0]
        fetch = []
        if lines % 16 == 0:
            fetch = [
                pltpu.make_async_copy(out_h.at[u, f], out_w.at[u, pl.ds(f * lines, lines), :], fsems.at[u * nfsdp + f])
                for u in range(nseq)
                for f in range(nfsdp)
            ]
        else:
            load = pltpu.make_async_copy(out_h, spare, local.at[2])
            load.start()
            load.wait()
            for u in range(nseq):
                joined = jnp.concatenate([spare[u, f].astype(F32) for f in range(nfsdp)], axis=0)
                out_w[u] = joined.astype(BF16)
        saves = []

        def save(src, dst):
            saves.append(pltpu.make_async_copy(src, dst, local.at[18 + len(saves)]))
            saves[-1].start()

        for a in fetch:
            a.start()
        for n, t in enumerate((other, cross, near)):
            wires.at(obase + n, o.at[rows_at(t, rows), :], obuf.at[mine], {"seq": t}).wait()
        for a in fetch:
            a.wait()
        pass_on(1 / 12)
        own[2].wait()
        for c in range(2):
            part = slice(c * half, (c + 1) * half)
            for u in range(nseq):
                acc = tok[part, u * cols : (u + 1) * cols].astype(F32)
                for t in range(nseq):
                    acc = acc + nn(obuf[t, part, :], out_w[u, t * piece : (t + 1) * piece, :])
                resid[part, u * cols : (u + 1) * cols] = acc
            h = resid[part, :]
            group[rows_at(mine, rows, c * half, half), :] = (h * inverse_rms(h) * gains[1:2, :]).astype(BF16)
            if c == 1:
                nring.send(0, group.at[rows_at(mine, rows, 0, half), :])
        nring.send(1, group.at[rows_at(mine, rows, half, half), :])
        save(obuf, obuf_h)
        save(resid, resid_h)
        cring.forward(1)
        for a in gates:
            for d in range(pairs):
                a.complete(d)
        save(gate_w, gate_h)

        def gate_rows(t):
            ga[rows_at(t, rows), :] = nn(group[rows_at(t, rows), :], gate_w[...])

        def act_rows(t):
            up = nn(group[rows_at(t, rows), :], up_w[...])
            active, slope = gelu_both(ga[rows_at(t, rows), :])
            hid[rows_at(t, rows), :] = (active * up).astype(BF16)
            ga[rows_at(t, rows), :] = slope * up
            ub[rows_at(t, rows), :] = active

        pass_on(2 / 12)
        gate_rows(mine)
        nring.got_near(0)
        nring.got_near(1)
        pass_on(3 / 12)
        gate_rows(near)
        pass_on(4 / 12)
        nring.forward(0)
        pass_on(6 / 12)
        nring.forward(1)
        own[1].wait()
        for c in range(2):
            cring.got_near(c)
            cring.got_cross(c)
        cload = pltpu.make_async_copy(cot_h, cot, local.at[3])
        cload.start()
        pass_on(7 / 12)
        gate_rows(other)
        for c in range(2):
            nring.got_cross(c)
        gate_rows(cross)
        save(group, n2_h)
        pass_on(8 / 12)
        for a in ups:
            for d in range(pairs):
                a.complete(d)
        save(up_w, up_h)
        act_rows(mine)
        act_rows(near)
        pass_on(9 / 12)
        act_rows(other)
        act_rows(cross)
        save(hid, hid_h)
        pass_on(10 / 12)
        cload.wait()
        width_f = units // nfsdp
        wide = max(256 // width_f, 1)
        pieces = []

        def down_part(n):
            slot = n % 2
            if n > 1:
                pieces[n - 2].wait()
            got = dot_tn(hid[:, n * wide * width_f : (n + 1) * wide * width_f], cot[...]).astype(BF16)
            for m in range(wide):
                parts[slot, m] = got[m * width_f : (m + 1) * width_f, :]
            pieces.append(pltpu.make_async_copy(parts.at[slot], parts_h.at[pl.ds(n * wide, wide)], local.at[4 + slot]))
            pieces[n].start()

        for n in range(nfsdp // wide):
            down_part(n)
            if n == 1:
                pass_on(11 / 12)

        def back_cols(at):
            for t in range(nseq):
                band = slice(t * rows, (t + 1) * rows)
                dh = nt(cot[band, :], down_w[at, :])
                dg[band, at] = (dh * ga[band, at]).astype(BF16)
                du[band, at] = (dh * ub[band, at]).astype(BF16)
            save(dg.at[:, at], dg_h.at[:, at])
            save(du.at[:, at], du_h.at[:, at])

        if (2 * width_f) % 128 == 0:

            def columns(d):
                for a in downs:
                    a.complete(d)
                if d == pairs - 1:
                    save(down_w, down_h)
                start = downs[0].source(d) * 2 * width_f
                back_cols(pl.ds(pl.multiple_of(start, 2 * width_f), 2 * width_f))

            columns(0)
            pass_on(1)
            for d in range(1, pairs):
                columns(d)
        else:
            pass_on(1)
            for d in range(pairs):
                for a in downs:
                    a.complete(d)
            for n in range(units // 256):
                back_cols(slice(n * 256, (n + 1) * 256))
            save(down_w, down_h)
        nring.drain()
        wring.drain()
        cring.drain()
        lead_late = [late] + gates + ups + downs
        for a in lead_late:
            a.drain()
        for n, (a, b) in enumerate(((q, q_h), (k, k_h), (v, v_h), (o, o_h))):
            pltpu.make_async_copy(a, b, osems.at[n]).wait()
        for a in pieces[-2:] + saves:
            a.wait()

    pl.run_scoped(
        feed,
        pltpu.VMEM((nseq, w_o.shape[0] * nfsdp, width // nseq), BF16),
        pltpu.VMEM((tall, width), BF16),
        pltpu.VMEM((tall, units), F32),
        pltpu.VMEM((tall, units), F32),
        pltpu.VMEM((tall, units), BF16),
        pltpu.VMEM((tall, units), BF16),
        pltpu.VMEM((tall, units), BF16),
        pltpu.VMEM((2, max(256 * nfsdp // units, 1), units // nfsdp, width), BF16),
    )


def forward(starts, table, ids, gain_q, tok, w_q, w_k, w_v, w_o, w_g, w_u, w_d, cot, nseq, nfsdp):
    rows, width = tok.shape
    inner = w_q.shape[1]
    piece = inner // nseq
    heads = piece // HEAD_DIM
    tall = nseq * rows
    size = w_q.shape[0]
    unit = pack_piece(w_g.shape[1], nfsdp, nseq)[1]
    units = nfsdp * unit
    cols = width // nseq
    lead = piece * 10 // 3
    smem = pl.BlockSpec(memory_space=pltpu.SMEM)

    def low(*shape):
        return jax.ShapeDtypeStruct(shape, BF16)

    return pl.pallas_call(
        functools.partial(forward_kernel, heads, nseq),
        out_shape=(
            jax.ShapeDtypeStruct((8, tall), F32),
            jax.ShapeDtypeStruct((8, width), F32),
            low(tall, piece),
            low(tall, piece),
            low(tall, piece),
            low(tall, piece),
            low(nseq, rows, piece),
            jax.ShapeDtypeStruct((rows, width), F32),
            low(tall, width),
            low(width, lead),
            low(nseq, nfsdp, w_o.shape[0], cols),
            low(tall, width),
            low(width, units),
            low(width, units),
            low(units, width),
            low(tall, width),
            low(tall, units),
            low(tall, units),
            low(tall, units),
            low(nfsdp, unit, width),
        ),
        in_specs=[smem, smem, vm_spec(), vm_spec()] + [any_spec()] * 9,
        out_specs=(vm_spec(),) * 2 + (any_spec(),) * 18,
        scratch_shapes=wires_scratch(6 + 8 * nfsdp + 3 + 6 + 6 + 3)
        + [
            pltpu.SemaphoreType.DMA((18 + 7 + 2 * max(nfsdp // 2, units // 256),)),
            pltpu.VMEM((size, lead), BF16),
            pltpu.VMEM((w_o.shape[0], cols), BF16),
            pltpu.VMEM((size, units), BF16),
            pltpu.VMEM((size, units), BF16),
            pltpu.VMEM((unit, width), BF16),
            pltpu.VMEM((tall, width), BF16),
            pltpu.VMEM((width, lead), BF16),
            pltpu.VMEM((width, units), BF16),
            pltpu.VMEM((width, units), BF16),
            pltpu.VMEM((units, width), BF16),
            pltpu.VMEM((rows, width), BF16),
            pltpu.SemaphoreType.DMA((nseq * nfsdp,)),
            pltpu.VMEM((nseq, nfsdp) + w_o.shape[:1] + (cols,) if w_o.shape[0] % 16 else (1, 1, 8, 128), BF16),
            pltpu.VMEM((tall, piece), BF16),
            pltpu.VMEM((tall, piece), BF16),
            pltpu.VMEM((tall, piece), BF16),
            pltpu.VMEM((tall, piece), BF16),
            pltpu.VMEM((nseq, rows, piece), BF16),
            pltpu.VMEM((rows, width), F32),
            pltpu.SemaphoreType.DMA((4,)),
        ],
        compiler_params=call_params(1, 64),
        name="forward",
    )(starts, table, ids, gain_q, tok, w_q, w_k, w_v, w_o, w_g, w_u, w_d, cot)


def back_kernel(
    heads, chunks, starts, table, ids, gains, lse, gain_b, q, k, v, o, do,
    resid_h, rgrad_h, tok_h, y_p, out_p, gate_p, up_p, done_h, lead_h, n1_h, first_h,
    small, y_h, in_h, down_f, lead_f, gate_f, up_f, qkv_f, out_f,
    send, recv, local, ybuf, qkv_p, b0, b1, b2, b3, b4, b5,
    g0, g1, g2, g3, u0, u1, u2, u3, q0_, q1_, q2_, q3_, o0, o1, o2, o3,
    gate_s, up_s, qkv_s, out_s, dqkv, tok, held, stage, one, two, three, tgrad,
):
    rows, width = tok.shape
    nseq = q.shape[0] // rows
    piece = q.shape[1]
    nfsdp = gate_p.shape[0]
    s, near, far_d, cross = seq_places()
    pair, side, pairs = fsdp_places()

    def y_block(t):
        return y_p.at[rows_at(t, rows), :]

    loads = [
        pltpu.make_async_copy(y_block(far_d), ybuf.at[2], local.at[0]),
        pltpu.make_async_copy(y_block(s), ybuf.at[3], local.at[1]),
    ]
    loads.append(pltpu.make_async_copy(tok_h, tok, local.at[5]))
    for a in loads:
        a.start()
    meet([{"seq": near}, {"seq": far_d}, {"seq": cross}] + fsdp_peers())
    wires = Wires(send, recv)
    hop = wires.go(y_block(cross), ybuf.at[0], {"seq": near})
    turn = wires.go(y_block(near), ybuf.at[1], {"seq": near})
    gates = FsdpScatter(wires, gate_p, (g0, g1, g2, g3), gate_s)
    ups = FsdpScatter(wires, up_p, (u0, u1, u2, u3), up_s)
    gates.start()
    ups.start()
    down_ring = SeqGather(wires, lambda t, c: down_f.at[t], 1)
    lead_ring = SeqGather(wires, lambda t, c: lead_f.at[t], 1)
    gate_ring = SeqGather(wires, lambda t, c: gate_f.at[t], 1)
    up_ring = SeqGather(wires, lambda t, c: up_f.at[t], 1)
    qkv_ring = SeqGather(wires, lambda t, c: qkv_f.at[t], 1)
    out_ring = SeqGather(wires, lambda t, c: out_f.at[t], 1)
    qkvs = FsdpScatter(wires, qkv_p, (q0_, q1_, q2_, q3_), qkv_s)
    outs = FsdpScatter(wires, out_p, (o0, o1, o2, o3), out_s)
    far_hop = wires.at(wires.take(1), ybuf.at[2], ybuf.at[4], {"seq": far_d})
    down_keep = pltpu.make_async_copy(done_h, down_f.at[s], local.at[6])
    down_keep.start()
    down_ring.send(0, done_h)
    lead_keep = pltpu.make_async_copy(lead_h, lead_f.at[s], local.at[10])
    lead_keep.start()
    lead_ring.send(0, lead_h)
    length = ids.shape[1]
    half = 2 * PROMPT

    def attend_back(strip, far, kh, vh, kt, delta, dqt, dk, dv, gstrip, gfar):
        build_strips(heads, s * heads, starts, table, ids, strip, far)
        loads[0].wait()
        hop.wait_recv()
        ybuf[2] = (ybuf[2].astype(F32) + ybuf[0].astype(F32)).astype(BF16)
        for src, dst in ((k, kh), (v, vh)):
            masked_copies(src, dst, heads)
        far_hop.start()
        kt[...] = k[...].astype(F32).T.astype(BF16)
        prod = (o[...].astype(F32) * do[...].astype(F32)).T
        for h in range(heads):
            delta[h : h + 1, :] = jnp.sum(prod[h * HEAD_DIM : (h + 1) * HEAD_DIM, :], axis=0, keepdims=True)
        dk[...] = jnp.zeros(dk.shape, F32)
        dv[...] = jnp.zeros(dv.shape, F32)
        gstrip[...] = jnp.zeros(gstrip.shape, F32)
        gfar[...] = jnp.zeros(gfar.shape, F32)
        lane = lax.broadcasted_iota(jnp.int32, (1, piece), 1)

        def block(h, q0, bias_q0, chunk_list, c):
            qb = q[pl.ds(q0, CL), :]
            dob = do[pl.ds(q0, CL), :]
            keep = lane // HEAD_DIM == h
            qhb = jnp.where(keep, qb, jnp.zeros((), BF16))
            dohb = jnp.where(keep, dob, jnp.zeros((), BF16))
            lrow = lse[pl.ds(h, 1), pl.ds(q0, CL)]
            drow = delta[pl.ds(h, 1), pl.ds(q0, CL)]
            acc = jnp.zeros((HEAD_DIM, CL), F32)
            for n, (k0, kind, kstart) in enumerate(chunk_list):
                ks = pl.ds(k0, KC)
                sc = nt(kh[h, ks, :], qb) + bias_chunk(strip, far, h, bias_q0, kstart, kind, c)
                pr = jnp.exp(sc - lrow)
                dp = nt(vh[h, ks, :], dob)
                ds = pr * (dp - drow)
                dsl = ds.astype(BF16)
                dv[ks, :] += nn(pr.astype(BF16), dohb)
                dk[ks, :] += nn(dsl, qhb)
                acc = acc + nn(kt[pl.ds(pl.multiple_of(h * HEAD_DIM, HEAD_DIM), HEAD_DIM), ks], dsl)
                for r in range(KC // 128):
                    m = PROMPT - 128 - (kstart + 128 * r)
                    part = ds[128 * r : 128 * (r + 1), :]
                    if kind == "far":
                        gfar[h, c, :, m : m + CL] += part
                    else:
                        gstrip[h, :, pl.ds(pl.multiple_of(bias_q0 + m, 128), CL)] += part
            dqt[pl.ds(pl.multiple_of(h * HEAD_DIM, HEAD_DIM), HEAD_DIM), pl.ds(q0, CL)] = acc

        nblk = PROMPT // CL

        def prompt_body(i, carry):
            h, blk = i // nblk, i % nblk
            q0 = pl.multiple_of(blk * CL, CL)
            block(h, q0, q0, [(j * KC, "strip", j * KC) for j in range(PROMPT // KC)], None)

            for k in range(1, pairs):

                @pl.when(i == heads * nblk * k // pairs)
                def _():
                    gates.step(k)

            return carry

        lax.fori_loop(0, heads * nblk, prompt_body, 0)

        def cont_body(i, carry):
            h, c = i // 2, i % 2
            q0 = pl.multiple_of(PROMPT + c * CL, CL)
            chunk_list = [(j * KC, "far", j * KC) for j in range(PROMPT // KC)]
            chunk_list += [(q0 + j * KC, "strip", j * KC) for j in range(CL // KC)]
            block(h, q0, 0, chunk_list, c)

            @pl.when(i == heads)
            def _():
                ups.step(1)

            return carry

        lax.fori_loop(0, heads * 2, cont_body, 0)
        dqkv[...] = jnp.concatenate([dqt[...].T, dk[...], dv[...]], axis=1).astype(BF16)
        buckets = table.shape[1]
        lines8 = lax.broadcasted_iota(jnp.int32, (buckets, length), 0)
        hot = ids[:1, :] == lines8
        tgrad[...] = jnp.zeros(tgrad.shape, F32)
        for h in range(heads):

            def unskew(g, span):
                full = jnp.concatenate([jnp.zeros((128, 128), F32), g], axis=1)
                eight = full[:8]
                for a in range(1, 16):
                    eight = eight + pltpu.roll(full[8 * a : 8 * a + 8], span - 8 * a, 1)
                vec = pltpu.roll(eight, span - 1, 1)[:1]
                for b in range(1, 8):
                    vec = vec + pltpu.roll(eight, span - 1 - b, 1)[b : b + 1]
                return jnp.concatenate([vec, jnp.zeros((1, length - span), F32)], axis=1)

            whole = jnp.broadcast_to(unskew(gstrip[h], half), (8, length))
            whole = pltpu.roll(whole, PROMPT // 2, 1)
            for c in range(2):
                moved = jnp.broadcast_to(unskew(gfar[h, c], FARW + 128), (8, length))
                whole = whole + pltpu.roll(moved, PROMPT // 2 + starts[c], 1)
            picked = jnp.where(hot, whole[:1, :], 0.0)
            column = jnp.broadcast_to(jnp.sum(picked, axis=1, keepdims=True), (buckets, 128))
            tgrad[h : h + 1, :buckets] = column.T[:1, :]

    tall = nseq * rows
    pl.run_scoped(
        attend_back,
        pltpu.VMEM((heads, 128, STRIP), F32),
        pltpu.VMEM((heads, 2, 128, FARW), F32),
        pltpu.VMEM((heads, tall, piece), BF16),
        pltpu.VMEM((heads, tall, piece), BF16),
        pltpu.VMEM((piece, tall), BF16),
        pltpu.VMEM((8, tall), F32),
        pltpu.VMEM((piece, tall), F32),
        pltpu.VMEM((tall, piece), F32),
        pltpu.VMEM((tall, piece), F32),
        pltpu.VMEM((heads, 128, STRIP), F32),
        pltpu.VMEM((heads, 2, 128, FARW), F32),
    )

    def rest(n1, hold, rgrad, resid, first):
        later = [
            pltpu.make_async_copy(n1_h, n1, local.at[7]),
            pltpu.make_async_copy(rgrad_h, rgrad, local.at[8]),
            pltpu.make_async_copy(resid_h, resid, local.at[9]),
        ]
        ready = pltpu.make_async_copy(first_h, first, local.at[4])
        ready.start()
        for a in later:
            a.start()
        sums = SeqScatter(wires, chunks, b0, b1, b2, b3, b4, b5)
        size = rows // chunks
        ready.wait()

        def part(t, c):
            return nt(dqkv[rows_at(t, rows, c * size, size), :], first[:, : 3 * piece])

        for c in range(chunks):
            sums.cross_chunk(c, part(cross, c))
        for c in range(chunks):
            sums.far_chunk(c, part(far_d, c))
        for k in range(2, pairs - 1):
            ups.step(k)
        later[0].wait()
        depth = width // nfsdp
        wide = 384
        for n in range(width // wide):
            got = dot_tn(n1[:, n * wide : (n + 1) * wide], dqkv[...])
            for m in range(wide // depth):
                qkv_p[n * (wide // depth) + m] = got[m * depth : (m + 1) * depth, :].astype(BF16)
        for c in range(chunks):
            sums.near_chunk(c, part(near, c))
        for c in range(chunks):
            hold[c * size : (c + 1) * size, :] = part(s, c)
        qkvs.start()
        if pairs > 2:
            ups.step(pairs - 1)
        gates.finish()
        outs.start()
        gate_keep = pltpu.make_async_copy(gate_s, gate_f.at[s], local.at[11])
        gate_keep.start()
        gate_ring.send(0, gate_s)
        down_ring.forward(0)
        lead_ring.forward(0)
        later[2].wait()
        loads[1].wait()
        turn.wait_recv()
        far_hop.wait_recv()
        total = ybuf[3].astype(F32) + ybuf[1].astype(F32) + ybuf[4].astype(F32)
        ybuf[3] = (resid[...] + total).astype(BF16)
        qkvs.step(1)
        loads[2].wait()
        later[1].wait()
        gsum = jnp.zeros((1, width), F32)
        y_keep = pltpu.make_async_copy(ybuf.at[3], y_h, local.at[12])
        y_keep.start()
        for c in range(chunks):
            at = slice(c * size, (c + 1) * size)
            dn = sums.own_chunk(c, hold[at, :])
            x = tok[at, :].astype(F32)
            r = inverse_rms(x)
            gsum = gsum + jnp.sum(dn * x * r, axis=0, keepdims=True)
            tok[at, :] = (rgrad[at, :] + norm_back(dn, x, r, gains[0:1, :])).astype(BF16)
            if c == 0:
                for k in range(2, pairs - 1):
                    qkvs.step(k)
                ups.finish()
                up_keep = pltpu.make_async_copy(up_s, up_f.at[s], local.at[14])
                up_keep.start()
                up_ring.send(0, up_s)
                if pairs > 2:
                    qkvs.step(pairs - 1)
        in_keep = pltpu.make_async_copy(tok, in_h, local.at[13])
        in_keep.start()
        held[...] = jnp.zeros(held.shape, F32)
        lanes = held.shape[1]
        lines = width // lanes
        for n in range(lines):
            held[n : n + 1, :] = gsum[:, n * lanes : (n + 1) * lanes]
            held[lines + n : lines + n + 1, :] = gain_b[:1, n * lanes : (n + 1) * lanes]
        held[pl.ds(2 * lines + s * 8, 8), :] = tgrad[...]
        outs.step(1)
        trips = [wires.go(held, one.at[n], {"seq": t}) for n, t in enumerate((near, far_d, cross))]
        gate_ring.forward(0)
        for k in range(2, pairs):
            outs.step(k)
        for a in trips:
            a.wait_recv()
        stage[0] = held[...] + one[0] + one[1] + one[2]
        up_ring.forward(0)
        trips.append(wires.go(stage.at[0], two, {"fsdp": pair * 2 + 1 - side}))
        trips[-1].wait_recv()
        stage[1] = stage[0] + two[...]
        zs = [
            wires.go(stage.at[1], three.at[d - 1], {"fsdp": lax.rem(pair + d, pairs) * 2 + side})
            for d in range(1, pairs)
        ]
        qkvs.finish()
        qkv_keep = pltpu.make_async_copy(qkv_s, qkv_f.at[s], local.at[15])
        qkv_keep.start()
        qkv_ring.send(0, qkv_s)
        outs.finish()
        out_keep = pltpu.make_async_copy(out_s, out_f.at[s], local.at[16])
        out_keep.start()
        out_ring.send(0, out_s)
        total = stage[1]
        for d, a in enumerate(zs):
            a.wait_recv()
            total = total + three[d]
        small[...] = total
        qkv_ring.forward(0)
        out_ring.forward(0)
        for a in (down_ring, lead_ring, gate_ring, up_ring, qkv_ring, out_ring):
            a.finish()
        sums.finish()
        for a in (gates, ups, qkvs, outs):
            a.drain()
        for a in (gate_keep, up_keep, qkv_keep, out_keep, y_keep, in_keep, down_keep, lead_keep):
            a.wait()
        for a in trips + zs + [hop, turn, far_hop]:
            a.wait_send()

    pl.run_scoped(
        rest,
        pltpu.VMEM((tall, width), BF16),
        pltpu.VMEM((rows, width), F32),
        pltpu.VMEM((rows, width), F32),
        pltpu.VMEM((rows, width), F32),
        pltpu.VMEM(first_h.shape, BF16),
    )


def back(starts, table, ids, gains, lse, gain_b, q, k, v, o, do, resid, rgrad, tok, y_p, out_p, gate_p, up_p, done, lead, n1, first, chunks=2):
    tall, piece = q.shape
    heads = piece // HEAD_DIM
    rows, width = tok.shape
    nseq = tall // rows
    nfsdp = gate_p.shape[0]
    pairs = nfsdp // 2
    lines = -(-(2 * width // 128 + 8 * nseq) // 8) * 8
    qkv_shape = (nfsdp, width // nfsdp, 3 * piece)
    out_shape = out_p.shape
    smem = pl.BlockSpec(memory_space=pltpu.SMEM)

    def full(a):
        return jax.ShapeDtypeStruct((nseq,) + tuple(a), BF16)

    return pl.pallas_call(
        functools.partial(back_kernel, heads, chunks),
        out_shape=(
            jax.ShapeDtypeStruct((lines, 128), F32),
            jax.ShapeDtypeStruct((rows, width), BF16),
            jax.ShapeDtypeStruct((rows, width), BF16),
            full(done.shape),
            full(lead.shape),
            full(gate_p.shape[1:]),
            full(up_p.shape[1:]),
            full(qkv_shape[1:]),
            full(out_shape[1:]),
        ),
        in_specs=[smem, smem] + [vm_spec()] * 9 + [any_spec()] * 11,
        out_specs=(vm_spec(),) + (any_spec(),) * 8,
        scratch_shapes=wires_scratch(6 + 4 * nfsdp + 18 + 3 * chunks + 4 + pairs)
        + [
            pltpu.SemaphoreType.DMA((17,)),
            pltpu.VMEM((5, rows, width), BF16),
            pltpu.VMEM(qkv_shape, BF16),
        ]
        + scatter_scratch(chunks, rows // chunks, width)
        + fsdp_scatter_scratch(gate_p.shape)
        + fsdp_scatter_scratch(up_p.shape)
        + fsdp_scatter_scratch(qkv_shape)
        + fsdp_scatter_scratch(out_shape)
        + [
            pltpu.VMEM(gate_p.shape[1:], BF16),
            pltpu.VMEM(up_p.shape[1:], BF16),
            pltpu.VMEM(qkv_shape[1:], BF16),
            pltpu.VMEM(out_shape[1:], BF16),
            pltpu.VMEM((tall, 3 * piece), BF16),
            pltpu.VMEM((rows, width), BF16),
            pltpu.VMEM((lines, 128), F32),
            pltpu.VMEM((2, lines, 128), F32),
            pltpu.VMEM((3, lines, 128), F32),
            pltpu.VMEM((lines, 128), F32),
            pltpu.VMEM((pairs - 1, lines, 128), F32),
            pltpu.VMEM((8, 128), F32),
        ],
        compiler_params=call_params(5, 64),
        name="back",
    )(starts, table, ids, gains, lse, gain_b, q, k, v, o, do, resid, rgrad, tok, y_p, out_p, gate_p, up_p, done, lead, n1, first)


def unpack_kernel(nseq, nfsdp, heads, *refs):
    srcs, small, outs = refs[:8], refs[8], refs[9:18]
    ga, gb, table, ins, offs = refs[18:23]
    vs, ts = refs[23:31], refs[31:]
    loads = [pltpu.make_async_copy(a, b, ins.at[n]) for n, (a, b) in enumerate(zip(srcs, vs))]
    for n in (6, 7, 3, 0, 1, 2, 4, 5):
        loads[n].start()
    lead_f, gate_f, up_f, down_f, qkv_f, out_f, y, dx = vs
    tq, tk, tv, to, tg, tu, td = ts
    gq, gk, gv, go, gg, gu, gd, gy, gx = outs
    copies = []

    def save(src, dst):
        copies.append(pltpu.make_async_copy(src, dst, offs.at[len(copies)]))
        copies[-1].start()

    block, piece = pack_piece(tg.shape[1], nfsdp, nseq)
    half = nfsdp // 2

    def columns(get):
        parts = []
        for f in range(nfsdp):
            for t in range(nseq):
                size = min(piece, block - t * piece)
                full, f_at = get(f)
                parts.append(full[t, :, f_at * piece : f_at * piece + size].astype(F32))
        return jnp.concatenate(parts, axis=1)

    for n, (src, dst) in enumerate(((y, gy), (dx, gx))):
        loads[6 + n].wait()
        save(src, dst)
    loads[3].wait()
    size = down_f.shape[1]
    for t in range(nseq):
        n = min(size, td.shape[0] - t * size)
        td[t * size : t * size + n, :] = down_f[t, :n, :].astype(F32)
    save(td, gd)
    loads[0].wait()
    loads[1].wait()
    tg[...] = columns(lambda f: (lead_f, f) if f < half else (gate_f, f - half))
    save(tg, gg)
    loads[2].wait()
    tu[...] = columns(lambda f: (up_f, f))
    save(tu, gu)
    loads[4].wait()
    width = qkv_f.shape[2] // 3
    for n, (dst, out) in enumerate(((tq, gq), (tk, gk), (tv, gv))):
        dst[...] = jnp.concatenate([qkv_f[t, :, n * width : (n + 1) * width] for t in range(nseq)], axis=1).astype(F32)
        save(dst, out)
    loads[5].wait()
    to[...] = jnp.concatenate([out_f[t] for t in range(nseq)], axis=1).astype(F32)
    save(to, go)
    where = lax.axis_index("fsdp")
    share = ga.shape[1]
    lines = nfsdp * share // 128
    for n, dst in enumerate((ga, gb)):
        line = jnp.concatenate([small[n * lines + a : n * lines + a + 1, :] for a in range(lines)], axis=1)
        for f in range(nfsdp):

            @pl.when(where == f)
            def _():
                dst[...] = line[:, f * share : (f + 1) * share]

    for t in range(nseq):
        at = 2 * lines + 8 * t
        table[t * heads : (t + 1) * heads, :] = small[at : at + heads, : table.shape[1]]
    for a in copies:
        a.wait()


def unpack(srcs, small, like, blocks_like, table, nfsdp):
    nseq = srcs[0].shape[0]
    share = like[0].shape[0]
    vm = [vm_spec()] * 3
    return pl.pallas_call(
        functools.partial(unpack_kernel, nseq, nfsdp, table.shape[0] // nseq),
        out_shape=tuple(jax.ShapeDtypeStruct(a.shape, F32) for a in like)
        + tuple(jax.ShapeDtypeStruct(a.shape, BF16) for a in blocks_like)
        + (
            jax.ShapeDtypeStruct((1, share), F32),
            jax.ShapeDtypeStruct((1, share), F32),
            jax.ShapeDtypeStruct(table.shape, F32),
        ),
        in_specs=[any_spec()] * 8 + [vm_spec()],
        out_specs=tuple([any_spec()] * 9 + vm),
        scratch_shapes=[pltpu.SemaphoreType.DMA((8,)), pltpu.SemaphoreType.DMA((9,))]
        + [pltpu.VMEM(a.shape, BF16) for a in srcs]
        + [pltpu.VMEM(a.shape, F32) for a in like],
        compiler_params=pltpu.CompilerParams(vmem_limit_bytes=67043328),
        name="unpack",
    )(*srcs, small)


def reversed_ids(bucket_ids):
    span = bucket_ids.shape[0]
    ids = jnp.concatenate([bucket_ids[::-1], jnp.full((1,), -1, jnp.int32)])
    return ids[None, :]


def dot32(a, b):
    return jnp.dot(a, b, preferred_element_type=F32)


def dot_tn(a, b):
    return lax.dot_general(a, b, (((0,), (0,)), ((), ())), preferred_element_type=F32)


def gelu_both(u):
    inner = 0.7978845608028654 * (u + 0.044715 * u * u * u)
    t = jnp.tanh(inner)
    value = 0.5 * u * (1.0 + t)
    slope = 0.5 * (1.0 + t) + 0.5 * u * (1.0 - t * t) * 0.7978845608028654 * (1.0 + 3 * 0.044715 * u * u)
    return value, slope


def body(
    tokens,
    out_grad,
    attn_gain,
    w_query,
    w_key,
    w_value,
    w_out,
    mix_gain,
    w_gate,
    w_up,
    w_down,
    rel_table,
    bucket_ids,
    cont_start,
):
    nseq = lax.axis_size("seq")
    nfsdp = lax.axis_size("fsdp")
    inner = w_query.shape[1]

    ids = reversed_ids(bucket_ids)
    starts = cont_start[0]
    (
        lse,
        gains,
        query,
        keys,
        values,
        mixed,
        mixed_rows,
        resid,
        normed,
        first,
        out_w,
        _,
        gate_w,
        up_w,
        down_w,
        normed_two,
        hidden,
        gate_grad,
        up_grad,
        down_grad,
    ) = forward(
        starts,
        rel_table.T,
        ids,
        jnp.stack([attn_gain, mix_gain]).astype(F32),
        tokens[0],
        w_query,
        w_key,
        w_value,
        w_out,
        w_gate,
        w_up,
        w_down,
        out_grad[0],
        nseq,
        nfsdp,
    )
    out_w = out_w.reshape(nseq, inner, -1)
    resid_grad, mixed_grad, gain_two_grad, down_grad, lead_grad, out_w_grad, gate_w_grad, up_w_grad, result = unmix(
        gains, mixed_rows, resid, out_grad[0], blocks(down_grad.reshape(-1, down_grad.shape[2]), 2 * nfsdp), gate_grad, up_grad, gate_w, up_w, out_w, normed_two, hidden, down_w
    )
    down_grad = down_grad.reshape(-1, down_grad.shape[2])
    small, block_out, in_grad, down_grad, lead_grad, gate_w_grad, up_w_grad, qkv_grad, out_w_grad = back(
        starts,
        rel_table.T,
        ids,
        gains,
        lse,
        gain_two_grad,
        query,
        keys,
        values,
        mixed,
        mixed_grad,
        resid,
        resid_grad,
        tokens[0],
        result,
        out_w_grad,
        gate_w_grad,
        up_w_grad,
        down_grad,
        lead_grad,
        normed,
        first,
    )
    *shards, block_out, in_grad, gain_one_share, gain_two_share, table_grad = unpack(
        (lead_grad, gate_w_grad, up_w_grad, down_grad, qkv_grad, out_w_grad, block_out, in_grad),
        small,
        (w_query, w_key, w_value, w_out, w_gate, w_up, w_down),
        (block_out, in_grad),
        rel_table.T,
        nfsdp,
    )
    return (
        block_out[None],
        in_grad[None],
        gain_one_share[0],
        *shards[:4],
        gain_two_share[0],
        *shards[4:],
        table_grad.T,
    )


def solution(mesh):
    placed = (
        P("fsdp", "seq", None),
        P("fsdp", "seq", None),
        P("fsdp"),
        P("fsdp", None),
        P("fsdp", None),
        P("fsdp", None),
        P("fsdp", None),
        P("fsdp"),
        P("fsdp", None),
        P("fsdp", None),
        P("fsdp", None),
        P(),
        P(),
        P("fsdp", None),
    )
    results = placed[:1] * 2 + placed[2:11] + (P(),)
    return jax.shard_map(body, mesh=mesh, in_specs=placed, out_specs=results, check_vma=False)
```
